32 devices in a mesh: narrow: 4 (over y, x), wide: 8 (over z, core).
Axes of the slice: x: 2, y: 2, z: 4, core: 2. Of those that a mesh axis runs over, the one named last changes fastest.
Arguments:
- inputs_one: bfloat16 [32, 1024, 512], P(('narrow', 'wide')), may hold values from -6 to 6
- inputs_two: bfloat16 [32, 1024, 512], P(('narrow', 'wide')), may hold values from -6 to 6
- memory: bfloat16 [32, 1024, 512], P(('narrow', 'wide')), may hold values from -6 to 6
- cotangent_one: bfloat16 [32, 1024, 512], P(('narrow', 'wide')), may hold values from -6 to 6
- cotangent_two: bfloat16 [32, 1024, 512], P(('narrow', 'wide')), may hold values from -6 to 6
- target_ids: int32 [32, 1024], P(('narrow', 'wide')), may hold values from -1 to 3, as said below
- memory_ids: int32 [32, 1024], P(('narrow', 'wide')), may hold values from -1 to 3, as said below
- norm_gain: bfloat16 [3, 512], P(None, 'wide'), may hold values from 0.5 to 1.5
- norm_shift: bfloat16 [3, 512], P(None, 'wide'), may hold values from -1.796875 to 1.796875
- self_qkv: bfloat16 [512, 1536], P('wide'), may hold values from -0.25 to 0.25
- self_out: bfloat16 [512, 512], P('wide'), may hold values from -1 to 1
- cross_query: bfloat16 [512, 512], P('wide'), may hold values from -0.25 to 0.25
- cross_kv: bfloat16 [512, 1024], P('wide'), may hold values from -0.25 to 0.25
- cross_out: bfloat16 [512, 512], P('wide'), may hold values from -1 to 1
- ffn_in: bfloat16 [512, 2048], P('wide'), may hold values from -0.25 to 0.25
- ffn_out: bfloat16 [2048, 512], P('wide'), may hold values from -0.125 to 0.125
Outputs:
- out_one: bfloat16 [32, 1024, 512], P(('narrow', 'wide'))
- out_two: bfloat16 [32, 1024, 512], P(('narrow', 'wide'))
- grad_in_one: float32 [32, 1024, 512], P(('narrow', 'wide'))
- grad_in_two: float32 [32, 1024, 512], P(('narrow', 'wide'))
- grad_memory: float32 [32, 1024, 512], P(('narrow', 'wide'))
- grad_norm_gain: float32 [3, 512], P(None, 'wide')
- grad_norm_shift: float32 [3, 512], P(None, 'wide')
- grad_self_qkv: float32 [512, 1536], P('wide')
- grad_self_out: float32 [512, 512], P('wide')
- grad_cross_query: float32 [512, 512], P('wide')
- grad_cross_kv: float32 [512, 1024], P('wide')
- grad_cross_out: float32 [512, 512], P('wide')
- grad_ffn_in: float32 [512, 2048], P('wide')
- grad_ffn_out: float32 [2048, 512], P('wide')
The draws below stay inside these ranges and needn't reach their ends.
Inputs may be any that keep to these rules, and one draw needn't show every extreme that they name: `target_ids`: in every row, the ids are 0 to 3 in increasing order, each document one or more slots, followed by one or more padding slots of id -1; every id from -1 to 3 occurs in every row. `memory_ids`: in every row, the ids are 0 to 3 in increasing order, each document one or more slots, followed by one or more padding slots of id -1; every id from -1 to 3 occurs in every row.
All inputs are finite; a program needn't handle non-finite values.
Results may differ from the reference program's by a relative error of at most 0.023.
Values may be sent and summed in bfloat16 or wider, within the bound.
A program may use at most 256 MiB of HBM per device.

```python
import jax
import jax.numpy as jnp
from jax import lax

D = 512
HEAD_DIM = 64
FF = 2048
LEN = 1024
NSEG = 4
BATCH = 32


def segment_ids(key, salt_value):
    base_len = LEN * 7 // (10 * NSEG)
    spread = LEN * 2 // (10 * NSEG) + 2
    lengths = base_len + jax.random.randint(jax.random.fold_in(key, salt_value), (BATCH, NSEG), 0, spread)
    bounds = jnp.cumsum(lengths, axis=1).astype(jnp.int32)
    position = jnp.arange(LEN, dtype=jnp.int32)
    segment = jnp.sum((position[None, :, None] >= bounds[:, None, :]).astype(jnp.int32), axis=2)
    return jnp.where(segment >= NSEG, -1, segment).astype(jnp.int32)


def draw_target_ids(key, part):
    return segment_ids(key, 11)


def draw_memory_ids(key, part):
    return segment_ids(key, 23)


def steps_of(own_key, extent, shards, smallest, largest):
    loudness = 1.0
    for dim, blocks in shards:
        draws = jax.random.uniform(jax.random.fold_in(jax.random.fold_in(own_key, 6), dim), (blocks,), jnp.float32, smallest / len(shards), largest / len(shards))
        loudness = loudness * jnp.repeat(jnp.exp(draws), extent[dim] // blocks).reshape((-1,) + (1,) * (len(extent) - 1 - dim))
    return loudness


def scatter_about(stream_key, dims, deviation, reach, pieces=(), held_as=jnp.bfloat16):
    array = deviation * jax.random.normal(stream_key, dims, jnp.float32)
    if pieces:
        array = array * steps_of(stream_key, dims, pieces, -0.22, 0.18)
    return jnp.clip(array, -reach, reach).astype(held_as)


def setup_inputs(seed: int = 0) -> dict:
    arg_keys = jax.random.split(jax.random.key(seed), 17)
    inputs_one = scatter_about(arg_keys[0], (BATCH, LEN, D), 1.0, 6.0, ((0, 32),))
    inputs_two = scatter_about(arg_keys[1], (BATCH, LEN, D), 1.0, 6.0, ((0, 32),))
    memory = scatter_about(arg_keys[2], (BATCH, LEN, D), 1.0, 6.0, ((0, 32),))
    cotangent_one = scatter_about(arg_keys[3], (BATCH, LEN, D), 1.0, 6.0, ((0, 32),))
    cotangent_two = scatter_about(arg_keys[4], (BATCH, LEN, D), 1.0, 6.0, ((0, 32),))
    target_ids = draw_target_ids(jax.random.fold_in(arg_keys[16], 71), 0)
    memory_ids = draw_memory_ids(jax.random.fold_in(arg_keys[16], 71), 0)
    norm_gain = jnp.clip(1.0 + 0.1 * jax.random.normal(arg_keys[7], (3, D), jnp.float32), 0.5, 1.5).astype(jnp.bfloat16)
    norm_shift = scatter_about(arg_keys[8], (3, D), 0.3, 1.796875, ((1, 8),))
    self_qkv = scatter_about(arg_keys[9], (D, 3 * D), D ** -0.5, 0.25, ((0, 8),))
    self_out = scatter_about(arg_keys[10], (D, D), (D // 16) ** -0.5, 1.0, ((0, 8),))
    cross_query = scatter_about(arg_keys[11], (D, D), D ** -0.5, 0.25, ((0, 8),))
    cross_kv = scatter_about(arg_keys[12], (D, 2 * D), D ** -0.5, 0.25, ((0, 8),))
    cross_out = scatter_about(arg_keys[13], (D, D), (D // 16) ** -0.5, 1.0, ((0, 8),))
    ffn_in = scatter_about(arg_keys[14], (D, FF), D ** -0.5, 0.25, ((0, 8),))
    ffn_out = scatter_about(arg_keys[15], (FF, D), FF ** -0.5, 0.125, ((0, 8),))
    return dict(inputs_one=inputs_one, inputs_two=inputs_two, memory=memory, cotangent_one=cotangent_one, cotangent_two=cotangent_two, target_ids=target_ids, memory_ids=memory_ids, norm_gain=norm_gain, norm_shift=norm_shift, self_qkv=self_qkv, self_out=self_out, cross_query=cross_query, cross_kv=cross_kv, cross_out=cross_out, ffn_in=ffn_in, ffn_out=ffn_out)


@jax.custom_vjp
def low(v):
    return lax.optimization_barrier(v.astype(jnp.bfloat16)).astype(jnp.float32)

@jax.custom_vjp
def low_back(v):
    return v

def low_keep(v):
    return (low(v), None)

def low_pass(kept, grad):
    return (grad,)

def back_keep(v):
    return (v, None)

def back_low(kept, grad):
    return (low(grad),)
low.defvjp(low_keep, low_pass)
low_back.defvjp(back_keep, back_low)

def layer_norm(values, gain, shift):
    centre = lax.optimization_barrier(jnp.mean(values, -1, keepdims=True))
    centred = values - centre
    spread = lax.optimization_barrier(jnp.mean(centred * centred, -1, keepdims=True))
    return centred * lax.rsqrt(spread + 1e-05) * gain + shift

def smooth_gate(values):
    return jax.nn.gelu(values, approximate=True)

def product(left, right):
    return jnp.dot(left, right, precision=lax.Precision.HIGHEST)

def attend(query, keys, values, allowed):
    scale = query.shape[-1] ** (-0.5)
    scores = low_back(jnp.einsum('qhe,khe->hqk', query, keys, precision=lax.Precision.HIGHEST) * scale)
    scores = jnp.where(allowed[None], scores, -1e+30)
    highest = lax.optimization_barrier(jnp.max(scores, -1, keepdims=True))
    expon = jnp.exp(scores - highest)
    probs = expon / lax.optimization_barrier(jnp.sum(expon, -1, keepdims=True))
    return jnp.einsum('hqk,khe->qhe', low(probs), values, precision=lax.Precision.HIGHEST)

def one_step(inputs, mem_keys, mem_values, target_row, memory_row, weights):
    gain, shift, w_qkv, w_self, w_query, w_kv, w_cross, w_in, w_out = weights
    length = inputs.shape[0]
    model_width = inputs.shape[1]

    def heads_of(tensor):
        return tensor.reshape(length, model_width // HEAD_DIM, HEAD_DIM)
    normed = low(layer_norm(inputs, gain[0], shift[0]))
    joined = low(low_back(product(normed, w_qkv)))
    self_mask = target_row[:, None] == target_row[None, :]
    attended = attend(heads_of(joined[:, :model_width]), heads_of(joined[:, model_width:2 * model_width]), heads_of(joined[:, 2 * model_width:]), self_mask)
    mixed = low(low_back(attended.reshape(length, model_width)))
    after_self = inputs + low_back(product(mixed, w_self))
    normed_two = low(layer_norm(after_self, gain[1], shift[1]))
    asked = low(low_back(product(normed_two, w_query)))
    cross_mask = target_row[:, None] == memory_row[None, :]
    fetched = attend(heads_of(asked), mem_keys, mem_values, cross_mask)
    fetched = low(low_back(fetched.reshape(length, model_width)))
    after_cross = after_self + low_back(product(fetched, w_cross))
    normed_three = low(layer_norm(after_cross, gain[2], shift[2]))
    hidden = low(smooth_gate(low_back(product(normed_three, w_in))))
    return after_cross + low_back(product(hidden, w_out))

def layer_pair(first_in, second_in, memory_vals, target_row, memory_row, weights):
    length = memory_vals.shape[0]
    model_width = memory_vals.shape[1]
    cross_pair = low(low_back(product(memory_vals, weights[5])))
    mem_keys = cross_pair[:, :model_width].reshape(length, model_width // HEAD_DIM, HEAD_DIM)
    mem_values = cross_pair[:, model_width:].reshape(length, model_width // HEAD_DIM, HEAD_DIM)
    first_out = one_step(first_in, mem_keys, mem_values, target_row, memory_row, weights)
    second_out = one_step(second_in, mem_keys, mem_values, target_row, memory_row, weights)
    return (first_out, second_out)

def reference(inputs_one, inputs_two, memory, cotangent_one, cotangent_two, target_ids, memory_ids, norm_gain, norm_shift, self_qkv, self_out, cross_query, cross_kv, cross_out, ffn_in, ffn_out):
    weights = tuple((item.astype(jnp.float32) for item in (norm_gain, norm_shift, self_qkv, self_out, cross_query, cross_kv, cross_out, ffn_in, ffn_out)))
    starting = jax.tree.map(jnp.zeros_like, weights)

    def per_row(running, row_items):
        first_in, second_in, memory_row_vals, first_cot, second_cot, target_row, memory_row = row_items

        def layer_fn(first_val, second_val, memory_val, weight_vals):
            return layer_pair(first_val, second_val, memory_val, target_row, memory_row, weight_vals)
        outputs, pull = jax.vjp(layer_fn, first_in.astype(jnp.float32), second_in.astype(jnp.float32), memory_row_vals.astype(jnp.float32), weights)
        grad_first, grad_second, grad_mem, grad_weights = pull((first_cot.astype(jnp.float32), second_cot.astype(jnp.float32)))
        running = jax.tree.map(jnp.add, running, grad_weights)
        return (running, (outputs[0].astype(jnp.bfloat16), outputs[1].astype(jnp.bfloat16), grad_first, grad_second, grad_mem))
    summed, stacked = lax.scan(per_row, starting, (inputs_one, inputs_two, memory, cotangent_one, cotangent_two, target_ids, memory_ids))
    return (stacked[0], stacked[1], stacked[2], stacked[3], stacked[4], summed[0], summed[1], summed[2], summed[3], summed[4], summed[5], summed[6], summed[7], summed[8])
```

```python
import functools

import jax
import jax.numpy as jnp
from jax import lax
from jax.experimental import pallas as pl
from jax.experimental.pallas import tpu as pltpu
from jax.sharding import PartitionSpec as P

HEAD_DIM = 64
TILE = 256
SEGMENTS = 5
MASKED = -1e30
VMEM_LIMIT = 60 * 1024 * 1024
BF16 = jnp.bfloat16
F32 = jnp.float32


def lower(values):
    return values.astype(BF16)


def dot(left, right):
    return lax.dot_general(left, right, (((1,), (0,)), ((), ())), preferred_element_type=F32)


def dot_bt(left, right):
    return lax.dot_general(left, right, (((1,), (1,)), ((), ())), preferred_element_type=F32)


def dot_at(left, right):
    return lax.dot_general(left, right, (((0,), (0,)), ((), ())), preferred_element_type=F32)


def standardise(values):
    centred = values - jnp.mean(values, -1, keepdims=True)
    inverse = lax.rsqrt(jnp.mean(centred * centred, -1, keepdims=True) + 1e-05)
    return centred * inverse, inverse


def norm_back(xhat, inverse, gain, incoming):
    dz = incoming * gain
    inner = jnp.mean(dz * xhat, -1, keepdims=True)
    return (dz - jnp.mean(dz, -1, keepdims=True) - xhat * inner) * inverse


def fold_rows(values):
    rows, width = values.shape
    return jnp.sum(values.reshape(rows // 8, 8, width), axis=0)


def segment_bounds(ids):
    order = jnp.where(ids < 0, SEGMENTS - 1, ids).reshape(1, -1)
    level = lax.broadcasted_iota(jnp.int32, (8, 1), 0)
    return jnp.sum((order < level).astype(jnp.int32), axis=1)


def lane_index(rows):
    return lax.broadcasted_iota(jnp.int32, (rows, 128), 1)


def row_index(rows):
    return lax.broadcasted_iota(jnp.int32, (rows, 128), 0)


def stack_heads(pair, first):
    zero = jnp.zeros_like(pair)
    return jnp.concatenate([jnp.where(first, pair, zero), jnp.where(first, zero, pair)], axis=0)


def each_query_tile(bounds, q_row, k_row, length, visit):
    def per_segment(s, carry):
        q_low, q_high = bounds[q_row, s], bounds[q_row, s + 1]
        k_low, k_high = bounds[k_row, s], bounds[k_row, s + 1]
        q_base, k_base = (q_low // 16) * 16, (k_low // 16) * 16
        q_tiles = (q_high - q_base + TILE - 1) // TILE
        k_tiles = (k_high - k_base + TILE - 1) // TILE

        def per_tile(i, inner):
            low = jnp.maximum(q_low, q_base + i * TILE)
            start = pl.multiple_of(jnp.minimum(q_base + i * TILE, length - TILE), 16)
            visit(start, low, q_high, k_base, k_low, k_high, k_tiles)
            return inner

        return lax.fori_loop(0, q_tiles, per_tile, carry)

    lax.fori_loop(0, SEGMENTS, per_segment, 0)


def key_tile(j, k_base, k_low, k_high, length):
    low = jnp.maximum(k_low, k_base + j * TILE)
    start = pl.multiple_of(jnp.minimum(k_base + j * TILE, length - TILE), 16)
    rows = row_index(TILE) + start
    return start, (rows >= low) & (rows < k_high)


def attend(bounds, q_row, k_row, query, keys, values, out_ref, stat_ref):
    (q_ref, q_col), (k_ref, k_col), (v_ref, v_col) = query, keys, values
    length, width = out_ref.shape
    first = lane_index(TILE) < HEAD_DIM
    lanes = lane_index(TILE)
    unit = jnp.where(lane_index(2 * TILE) == 0, 1.0, 0.0).astype(BF16)
    ones = jnp.ones((TILE, 128), BF16)

    def visit(start, low, high, k_base, k_low, k_high, k_tiles):
        rows = row_index(TILE) + start
        keep = (rows >= low) & (rows < high)
        span = pl.ds(start, TILE)

        def piece(p, k_start, inside):
            cols = p * 128
            bias = jnp.where((lanes == 0) & jnp.logical_not(inside), MASKED, 0.0).astype(BF16)
            queries = stack_heads(q_ref[span, q_col + cols : q_col + cols + 128], first)
            k_span = pl.ds(k_start, TILE)
            pair_k = k_ref[k_span, k_col + cols : k_col + cols + 128]
            pair_v = v_ref[k_span, v_col + cols : v_col + cols + 128]
            scores = dot_bt(
                jnp.concatenate([queries, unit], axis=1), jnp.concatenate([pair_k, bias], axis=1)
            )
            return scores, jnp.concatenate([pair_v, ones], axis=1)

        def finish(p, highest, total):
            cols = p * 128
            mass = total[:, 128:]
            result = total[:, :128] / mass
            log_total = highest + jnp.log(mass)
            merged = lower(jnp.where(first, result[:TILE], result[TILE:]))
            out_ref[span, cols : cols + 128] = jnp.where(
                keep, merged, out_ref[span, cols : cols + 128]
            )
            old = stat_ref[span, :]
            new = jnp.where(lanes == 2 * p, log_total[:TILE], old)
            new = jnp.where(lanes == 2 * p + 1, log_total[TILE:], new)
            stat_ref[span, :] = jnp.where(keep, new, old)

        @pl.when(k_tiles == 1)
        def _():
            k_start, inside = key_tile(0, k_base, k_low, k_high, length)
            for p in range(width // 128):
                scores, wide_v = piece(p, k_start, inside)
                highest = jnp.max(scores, -1, keepdims=True)
                finish(p, highest, dot(lower(jnp.exp(scores - highest)), wide_v))

        @pl.when(k_tiles > 1)
        def _():
            for p in range(width // 128):

                def per_key(j, carry):
                    highest, total = carry
                    k_start, inside = key_tile(j, k_base, k_low, k_high, length)
                    scores, wide_v = piece(p, k_start, inside)
                    newest = jnp.maximum(highest, jnp.max(scores, -1, keepdims=True))
                    expon = lower(jnp.exp(scores - newest))
                    return newest, total * jnp.exp(highest - newest) + dot(expon, wide_v)

                empty = (jnp.full((2 * TILE, 1), MASKED, F32), jnp.zeros((2 * TILE, 256), F32))
                finish(p, *lax.fori_loop(0, k_tiles, per_key, empty))

    each_query_tile(bounds, q_row, k_row, length, visit)


def spread_lanes(column, lanes, lead):
    high = lower(column).astype(F32)
    rest = column - high
    middle = lower(rest).astype(F32)
    spread = jnp.where(lanes == 1, high, jnp.where(lanes == 2, middle, rest - middle))
    return lower(jnp.where(lanes == 0, lead, jnp.where(lanes < 4, -spread, 0.0)))


def attend_back(bounds, q_row, k_row, query, keys, values, do_ref, out_ref, stat_ref, dq, dk, dv):
    (q_ref, q_col), (k_ref, k_col), (v_ref, v_col) = query, keys, values
    (dq_ref, dq_col), (dk_ref, dk_col), (dv_ref, dv_col) = dq, dk, dv
    length, width = do_ref.shape
    first = lane_index(TILE) < HEAD_DIM
    lanes = lane_index(TILE)
    lanes_two = lane_index(2 * TILE)

    def visit(start, low, high, k_base, k_low, k_high, k_tiles):
        rows = row_index(TILE) + start
        keep = (rows >= low) & (rows < high)
        span = pl.ds(start, TILE)

        def per_key(j, carry):
            k_start, inside = key_tile(j, k_base, k_low, k_high, length)
            k_span = pl.ds(k_start, TILE)
            tail = jnp.where(lanes == 0, jnp.where(inside, 0.0, MASKED), 0.0)
            tail = lower(jnp.where((lanes > 0) & (lanes < 4), 1.0, tail))
            for p in range(width // 128):
                cols = p * 128
                pair_q = q_ref[span, q_col + cols : q_col + cols + 128]
                pair_k = k_ref[k_span, k_col + cols : k_col + cols + 128]
                pair_v = v_ref[k_span, v_col + cols : v_col + cols + 128]
                pair_do = jnp.where(keep, do_ref[span, cols : cols + 128], jnp.zeros((), BF16))
                inner = pair_do.astype(F32) * out_ref[span, cols : cols + 128].astype(F32)
                centre = jnp.concatenate(
                    [
                        jnp.sum(jnp.where(first, inner, 0.0), -1, keepdims=True),
                        jnp.sum(jnp.where(first, 0.0, inner), -1, keepdims=True),
                    ],
                    axis=0,
                )
                stat = jnp.where(keep, stat_ref[span, :], -MASKED)
                log_total = jnp.concatenate(
                    [stat[:, 2 * p : 2 * p + 1], stat[:, 2 * p + 1 : 2 * p + 2]], axis=0
                )
                queries = stack_heads(pair_q, first)
                grads = stack_heads(pair_do, first)
                probs = jnp.exp(
                    dot_bt(
                        jnp.concatenate([pair_k, tail], axis=1),
                        jnp.concatenate([queries, spread_lanes(log_total, lanes_two, 1.0)], axis=1),
                    )
                )
                slope = dot_bt(
                    jnp.concatenate([pair_v, tail], axis=1),
                    jnp.concatenate([grads, spread_lanes(centre, lanes_two, 0.0)], axis=1),
                )
                ds = lower(probs * slope)
                dv_ref[k_span, dv_col + cols : dv_col + cols + 128] += dot(lower(probs), grads)
                dk_ref[k_span, dk_col + cols : dk_col + cols + 128] += dot(ds, queries)
                turned = dot(pair_k.T, ds)
                turned = jnp.concatenate(
                    [turned[:HEAD_DIM, :TILE], turned[HEAD_DIM:, TILE:]], axis=0
                )
                dq_ref[span, dq_col + cols : dq_col + cols + 128] += turned.T
            return carry

        lax.fori_loop(0, k_tiles, per_key, 0)

    each_query_tile(bounds, q_row, k_row, length, visit)


def project_kernel(x1, x2, mem, gain, shift, w_qkv, w_kv, xs, qkv, kv):
    width = x1.shape[1]
    both = jnp.concatenate([x1[...], x2[...]], axis=0)
    half = x1.shape[0]
    xs[0] = both[:half]
    xs[1] = both[half:]
    xhat, _ = standardise(both.astype(F32))
    h1 = lower(xhat * gain[0:1, :] + shift[0:1, :])
    for c in range(w_qkv.shape[1] // width):
        cols = slice(c * width, (c + 1) * width)
        part = dot(h1, w_qkv[:, cols])
        if c == 0:
            part = part * HEAD_DIM ** (-0.5)
        part = lower(part)
        qkv[0, :, cols] = part[:half]
        qkv[1, :, cols] = part[half:]
    kv[...] = lower(dot(mem[...], w_kv[...]))


def forward_kernel(
    bounds, xs, qkv, kv, gain, shift, w_self, w_query, a1, y1, q2, a2, stat1, stat2
):
    length, width = a1.shape[1:]
    attend(
        bounds,
        0,
        0,
        (qkv.at[0], 0),
        (qkv.at[0], width),
        (qkv.at[0], 2 * width),
        a1.at[0],
        stat1.at[0],
    )

    def rows(i, carry):
        span = pl.ds(pl.multiple_of(i * TILE, TILE), TILE)
        after = xs[0, span, :].astype(F32) + dot(a1[0, span, :], w_self[...])
        y1[0, span, :] = after
        xhat, _ = standardise(after)
        h2 = lower(xhat * gain[1:2, :] + shift[1:2, :])
        q2[0, span, :] = lower(dot(h2, w_query[...]) * HEAD_DIM ** (-0.5))
        return carry

    lax.fori_loop(0, length // TILE, rows, 0)
    attend(bounds, 0, 1, (q2.at[0], 0), (kv, 0), (kv, width), a2.at[0], stat2.at[0])


def feed_kernel(
    per_step, y1, a2, g1, g2, gain, shift, w_cross, w_in, w_out,
    o1, o2, h3, r, du, e2, dy2, do2, dnorm,
):
    i = pl.program_id(0)
    width = w_cross.shape[0]
    is_first = i < per_step
    grad = jnp.where(is_first, g1[...], g2[...])
    after = y1[0] + dot(a2[0], w_cross[...])
    xhat, inverse = standardise(after)
    normed = lower(xhat * gain[2:3, :] + shift[2:3, :])
    h3[0] = normed
    result = after
    dh3 = jnp.zeros_like(after)
    slope = (2.0 / jnp.pi) ** 0.5
    for c in range(w_in.shape[1] // width):
        cols = slice(c * width, (c + 1) * width)
        u = dot(normed, w_in[:, cols])
        dr = dot_bt(grad, w_out[cols, :])
        square = u * u
        t = jnp.tanh(slope * (u + 0.044715 * (square * u)))
        half = 0.5 * (1.0 + t)
        hidden = lower(u * half)
        r[0, :, cols] = hidden
        gate = half + 0.5 * u * (1.0 - t * t) * (slope * (1.0 + 3 * 0.044715 * square))
        pre = lower(dr * gate)
        du[0, :, cols] = pre
        result = result + dot(hidden, w_out[cols, :])
        dh3 = dh3 + dot_bt(pre, w_in[:, cols])

    @pl.when(is_first)
    def _():
        o1[...] = lower(result)

    @pl.when(jnp.logical_not(is_first))
    def _():
        o2[...] = lower(result)

    @pl.when(i == 0)
    def _():
        dnorm[...] = jnp.zeros_like(dnorm)

    dnorm[0] += fold_rows(dh3 * xhat)
    dnorm[1] += fold_rows(dh3)
    back = grad.astype(F32) + norm_back(xhat, inverse, gain[2:3, :], dh3)
    dy2[0] = back
    low = lower(back)
    e2[0] = low
    do2[0] = lower(dot_bt(low, w_cross[...]))


def feed_grad_kernel(h3, a2, e2, g1, g2, du, r, d_in, d_out, d_cross, turned):
    c = pl.program_id(0)
    half = g1.shape[0]

    @pl.when(c == 0)
    def _():
        turned[...] = h3[...].T
        d_cross[...] = lower(dot(a2[...].T, e2[...]))

    d_in[...] = lower(dot(turned[...], du[...]))
    d_out[...] = lower(dot_at(r[:half, :], g1[...]) + dot_at(r[half:, :], g2[...]))


def cross_back_kernel(
    bounds, q2, kv, a1, a2, stat2, do2, y1, dy2, mem, gain, shift, w_query, w_self, w_kv,
    dy1, do1, d_query, d_self, d_kv, d_mem, dnorm,
    dq_sum, dkv_sum, h2, low_q, low_e,
):
    step = pl.program_id(0)
    length, width = q2.shape[1:]

    @pl.when(step == 0)
    def _():
        dkv_sum[...] = jnp.zeros_like(dkv_sum)
        dnorm[...] = jnp.zeros_like(dnorm)

    dq_sum[...] = jnp.zeros_like(dq_sum)
    attend_back(
        bounds, 0, 1, (q2.at[0], 0), (kv, 0), (kv, width), do2.at[0], a2.at[0], stat2.at[0],
        (dq_sum, 0), (dkv_sum, 0), (dkv_sum, width),
    )

    def rows(i, carry):
        span = pl.ds(pl.multiple_of(i * TILE, TILE), TILE)
        grad_q = lower(dq_sum[span, :] * HEAD_DIM ** (-0.5))
        low_q[step, span, :] = grad_q
        xhat, inverse = standardise(y1[0, span, :])
        h2[step, span, :] = lower(xhat * gain[1:2, :] + shift[1:2, :])
        dh2 = dot_bt(grad_q, w_query[...])
        dnorm[0] += fold_rows(dh2 * xhat)
        dnorm[1] += fold_rows(dh2)
        back = dy2[0, span, :] + norm_back(xhat, inverse, gain[1:2, :], dh2)
        dy1[0, span, :] = back
        low = lower(back)
        low_e[step, span, :] = low
        do1[0, span, :] = lower(dot_bt(low, w_self[...]))
        return carry

    lax.fori_loop(0, length // TILE, rows, 0)

    @pl.when(step == 1)
    def _():
        d_query[...] = lower(dot(h2[0].T, low_q[0]) + dot(h2[1].T, low_q[1]))
        d_self[...] = lower(dot(a1[0].T, low_e[0]) + dot(a1[1].T, low_e[1]))
        pair = lower(dkv_sum[...])
        d_kv[...] = lower(dot(mem[...].T, pair))
        d_mem[...] = dot_bt(pair, w_kv[...])


def self_back_kernel(
    bounds, xs, qkv, a1, stat1, do1, dy1, gain, shift, w_qkv,
    gi1, gi2, d_qkv, dnorm,
    sums, h1, low,
):
    step = pl.program_id(0)
    length, width = do1.shape[1:]

    @pl.when(step == 0)
    def _():
        dnorm[...] = jnp.zeros_like(dnorm)

    sums[...] = jnp.zeros_like(sums)
    attend_back(
        bounds, 0, 0, (qkv.at[0], 0), (qkv.at[0], width), (qkv.at[0], 2 * width),
        do1.at[0], a1.at[0], stat1.at[0], (sums, 0), (sums, width), (sums, 2 * width),
    )

    def rows(i, carry):
        span = pl.ds(pl.multiple_of(i * TILE, TILE), TILE)
        low[step, span, :width] = lower(sums[span, :width] * HEAD_DIM ** (-0.5))
        low[step, span, width:] = lower(sums[span, width:])
        xhat, inverse = standardise(xs[0, span, :].astype(F32))
        h1[step, span, :] = lower(xhat * gain[0:1, :] + shift[0:1, :])
        dh1 = dot_bt(low[step, span, :], w_qkv[...])
        dnorm[0] += fold_rows(dh1 * xhat)
        dnorm[1] += fold_rows(dh1)
        back = dy1[0, span, :] + norm_back(xhat, inverse, gain[0:1, :], dh1)

        @pl.when(step == 0)
        def _():
            gi1[span, :] = back

        @pl.when(step == 1)
        def _():
            gi2[span, :] = back

        return carry

    lax.fori_loop(0, length // TILE, rows, 0)

    @pl.when(step == 1)
    def _():
        d_qkv[...] = lower(dot(h1[0].T, low[0]) + dot(h1[1].T, low[1]))


def whole(shape):
    zeros = (0,) * len(shape)
    return pl.BlockSpec(shape, lambda *_: zeros, pipeline_mode=pl.Buffered(1))


def fixed(shape):
    zeros = (0,) * len(shape)
    return pl.BlockSpec(shape, lambda *_: zeros)


def by_step(shape):
    return pl.BlockSpec((1,) + shape, lambda t, *_: (t, 0, 0))


def params():
    return pltpu.CompilerParams(
        vmem_limit_bytes=VMEM_LIMIT, dimension_semantics=("arbitrary",)
    )


def struct(shape, dtype):
    return jax.ShapeDtypeStruct(shape, dtype)


def local_step(x1, x2, mem, g1, g2, target_ids, memory_ids, gain, shift, weights):
    w_qkv, w_self, w_query, w_kv, w_cross, w_in, w_out = weights
    length, width = x1.shape
    hidden = w_in.shape[1]
    tiles = length // TILE
    bounds = jnp.stack([segment_bounds(target_ids), segment_bounds(memory_ids)])
    norm_spec = whole((3, width))
    row_tile = pl.BlockSpec((TILE, width), lambda i: (i, 0))

    xs, qkv, kv = pl.pallas_call(
        project_kernel,
        grid=(tiles,),
        in_specs=[row_tile, row_tile, row_tile, norm_spec, norm_spec, whole(w_qkv.shape), whole(w_kv.shape)],
        out_specs=[
            pl.BlockSpec((2, TILE, width), lambda i: (0, i, 0)),
            pl.BlockSpec((2, TILE, 3 * width), lambda i: (0, i, 0)),
            pl.BlockSpec((TILE, 2 * width), lambda i: (i, 0)),
        ],
        out_shape=[
            struct((2, length, width), BF16),
            struct((2, length, 3 * width), BF16),
            struct((length, 2 * width), BF16),
        ],
        compiler_params=params(),
        name="project",
    )(x1, x2, mem, gain, shift, w_qkv, w_kv)

    step_low = by_step((length, width))
    a1, y1, q2, a2, stat1, stat2 = pl.pallas_call(
        forward_kernel,
        grid_spec=pltpu.PrefetchScalarGridSpec(
            num_scalar_prefetch=1,
            grid=(2,),
            in_specs=[
                step_low, by_step((length, 3 * width)), whole(kv.shape), norm_spec, norm_spec,
                whole(w_self.shape), whole(w_query.shape),
            ],
            out_specs=[step_low] * 4 + [by_step((length, 128))] * 2,
        ),
        out_shape=[
            struct((2, length, width), BF16),
            struct((2, length, width), F32),
            struct((2, length, width), BF16),
            struct((2, length, width), BF16),
            struct((2, length, 128), F32),
            struct((2, length, 128), F32),
        ],
        compiler_params=params(),
        name="attend_forward",
    )(bounds, xs, qkv, kv, gain, shift, w_self, w_query)

    step_tile = pl.BlockSpec((1, TILE, width), lambda i: (i // tiles, i % tiles, 0))
    step_wide = pl.BlockSpec((1, TILE, hidden), lambda i: (i // tiles, i % tiles, 0))
    early = pl.BlockSpec((TILE, width), lambda i: (jnp.minimum(i, tiles - 1), 0))
    late = pl.BlockSpec((TILE, width), lambda i: (jnp.maximum(i - tiles, 0), 0))
    o1, o2, h3, r, du, e2, dy2, do2, dnorm2 = pl.pallas_call(
        functools.partial(feed_kernel, tiles),
        grid=(2 * tiles,),
        in_specs=[
            step_tile, step_tile, early, late, norm_spec, norm_spec,
            whole(w_cross.shape), whole(w_in.shape), whole(w_out.shape),
        ],
        out_specs=[
            early, late, step_tile, step_wide, step_wide, step_tile, step_tile, step_tile,
            fixed((2, 8, width)),
        ],
        out_shape=[
            struct((length, width), BF16),
            struct((length, width), BF16),
            struct((2, length, width), BF16),
            struct((2, length, hidden), BF16),
            struct((2, length, hidden), BF16),
            struct((2, length, width), BF16),
            struct((2, length, width), F32),
            struct((2, length, width), BF16),
            struct((2, 8, width), F32),
        ],
        compiler_params=params(),
        name="feed_forward_back",
    )(y1, a2, g1, g2, gain, shift, w_cross, w_in, w_out)

    flat = (2 * length, width)
    chunk = pl.BlockSpec((2 * length, width), lambda c: (0, c))
    d_in, d_out, d_cross = pl.pallas_call(
        feed_grad_kernel,
        grid=(hidden // width,),
        in_specs=[whole(flat), whole(flat), whole(flat), whole((length, width)), whole((length, width)), chunk, chunk],
        out_specs=[
            pl.BlockSpec((width, width), lambda c: (0, c)),
            pl.BlockSpec((width, width), lambda c: (c, 0)),
            fixed((width, width)),
        ],
        out_shape=[
            struct((width, hidden), BF16),
            struct((hidden, width), BF16),
            struct((width, width), BF16),
        ],
        scratch_shapes=[pltpu.VMEM((width, 2 * length), BF16)],
        compiler_params=params(),
        name="feed_weight_grads",
    )(h3.reshape(flat), a2.reshape(flat), e2.reshape(flat), g1, g2, du.reshape(2 * length, hidden), r.reshape(2 * length, hidden))

    dy1, do1, d_query, d_self, d_kv, d_mem, dnorm1 = pl.pallas_call(
        cross_back_kernel,
        grid_spec=pltpu.PrefetchScalarGridSpec(
            num_scalar_prefetch=1,
            grid=(2,),
            in_specs=[
                step_low, whole(kv.shape), whole(a1.shape), step_low, by_step((length, 128)), step_low,
                step_low, step_low, whole(mem.shape), norm_spec, norm_spec,
                whole(w_query.shape), whole(w_self.shape), whole(w_kv.shape),
            ],
            out_specs=[
                step_low, step_low, fixed((width, width)), fixed((width, width)), fixed((width, 2 * width)),
                fixed((length, width)), fixed((2, 8, width)),
            ],
            scratch_shapes=[
                pltpu.VMEM((length, width), F32),
                pltpu.VMEM((length, 2 * width), F32),
                pltpu.VMEM((2, length, width), BF16),
                pltpu.VMEM((2, length, width), BF16),
                pltpu.VMEM((2, length, width), BF16),
            ],
        ),
        out_shape=[
            struct((2, length, width), F32),
            struct((2, length, width), BF16),
            struct((width, width), BF16),
            struct((width, width), BF16),
            struct((width, 2 * width), BF16),
            struct((length, width), F32),
            struct((2, 8, width), F32),
        ],
        compiler_params=params(),
        name="cross_back",
    )(bounds, q2, kv, a1, a2, stat2, do2, y1, dy2, mem, gain, shift, w_query, w_self, w_kv)

    gi1, gi2, d_qkv, dnorm0 = pl.pallas_call(
        self_back_kernel,
        grid_spec=pltpu.PrefetchScalarGridSpec(
            num_scalar_prefetch=1,
            grid=(2,),
            in_specs=[
                step_low, by_step((length, 3 * width)), step_low, by_step((length, 128)), step_low, step_low,
                norm_spec, norm_spec, whole(w_qkv.shape),
            ],
            out_specs=[
                fixed((length, width)), fixed((length, width)), fixed((width, 3 * width)), fixed((2, 8, width)),
            ],
            scratch_shapes=[
                pltpu.VMEM((length, 3 * width), F32),
                pltpu.VMEM((2, length, width), BF16),
                pltpu.VMEM((2, length, 3 * width), BF16),
            ],
        ),
        out_shape=[
            struct((length, width), F32),
            struct((length, width), F32),
            struct((width, 3 * width), BF16),
            struct((2, 8, width), F32),
        ],
        compiler_params=params(),
        name="self_back",
    )(bounds, xs, qkv, a1, stat1, do1, dy1, gain, shift, w_qkv)

    dnorm = jnp.sum(jnp.stack([dnorm0, dnorm1, dnorm2]), axis=2)
    return o1, o2, gi1, gi2, d_mem, dnorm, (d_qkv, d_self, d_query, d_kv, d_cross, d_in, d_out)


def body(
    inputs_one, inputs_two, memory, cotangent_one, cotangent_two, target_ids, memory_ids,
    norm_gain, norm_shift, self_qkv, self_out, cross_query, cross_kv, cross_out, ffn_in, ffn_out,
):
    shape = inputs_one.shape
    length, width = shape[1:]
    norms = lax.all_gather(jnp.concatenate([norm_gain, norm_shift]), "wide", axis=1, tiled=True).astype(F32)
    weights = tuple(
        lax.all_gather(item, "wide", axis=0, tiled=True)
        for item in (self_qkv, self_out, cross_query, cross_kv, cross_out, ffn_in, ffn_out)
    )
    o1, o2, gi1, gi2, d_mem, dnorm, grads = local_step(
        inputs_one.reshape(length, width),
        inputs_two.reshape(length, width),
        memory.reshape(length, width),
        cotangent_one.reshape(length, width),
        cotangent_two.reshape(length, width),
        target_ids,
        memory_ids,
        norms[:3],
        norms[3:],
        weights,
    )
    shares = [lax.psum_scatter(item, "wide", scatter_dimension=0, tiled=True) for item in grads]
    norm_rows = jnp.concatenate([dnorm[:, 0], dnorm[:, 1]])
    norm_share = lax.psum_scatter(norm_rows.astype(BF16), "wide", scatter_dimension=1, tiled=True)
    totals = [lax.psum(item, "narrow").astype(F32) for item in shares + [norm_share]]
    return (
        o1.reshape(shape), o2.reshape(shape), gi1.reshape(shape), gi2.reshape(shape), d_mem.reshape(shape),
        totals[7][:3], totals[7][3:],
        totals[0], totals[1], totals[2], totals[3], totals[4], totals[5], totals[6],
    )


def solution(mesh):
    rows = P(("narrow", "wide"), None, None)
    ids = P(("narrow", "wide"), None)
    norm, weight = P(None, "wide"), P("wide", None)
    return jax.shard_map(
        body,
        mesh=mesh,
        in_specs=(rows,) * 5 + (ids,) * 2 + (norm,) * 2 + (weight,) * 7,
        out_specs=(rows,) * 5 + (norm,) * 2 + (weight,) * 7,
        check_vma=False,
    )
```

```python
import functools

import jax
import jax.numpy as jnp
from jax import lax
from jax.experimental import pallas as pl
from jax.experimental.pallas import tpu as pltpu
from jax.sharding import PartitionSpec as P

HEAD_DIM = 64
TILE = 256
SEGMENTS = 5
MASKED = -1e30
VMEM_LIMIT = 60 * 1024 * 1024
BF16 = jnp.bfloat16
F32 = jnp.float32
MESH = pl.DeviceIdType.MESH


def lower(values):
    return values.astype(BF16)


def dot(left, right):
    return lax.dot_general(left, right, (((1,), (0,)), ((), ())), preferred_element_type=F32)


def dot_bt(left, right):
    return lax.dot_general(left, right, (((1,), (1,)), ((), ())), preferred_element_type=F32)


def dot_at(left, right):
    return lax.dot_general(left, right, (((0,), (0,)), ((), ())), preferred_element_type=F32)


def standardise(values):
    centred = values - jnp.mean(values, -1, keepdims=True)
    inverse = lax.rsqrt(jnp.mean(centred * centred, -1, keepdims=True) + 1e-05)
    return centred * inverse, inverse


def norm_back(xhat, inverse, gain, incoming):
    dz = incoming * gain
    inner = jnp.mean(dz * xhat, -1, keepdims=True)
    return (dz - jnp.mean(dz, -1, keepdims=True) - xhat * inner) * inverse


def fold_rows(values):
    rows, width = values.shape
    return jnp.sum(values.reshape(rows // 8, 8, width), axis=0)


def segment_bounds(ids):
    order = jnp.where(ids < 0, SEGMENTS - 1, ids).reshape(1, -1)
    level = lax.broadcasted_iota(jnp.int32, (8, 1), 0)
    return jnp.sum((order < level).astype(jnp.int32), axis=1)


def lane_index(rows):
    return lax.broadcasted_iota(jnp.int32, (rows, 128), 1)


def row_index(rows):
    return lax.broadcasted_iota(jnp.int32, (rows, 128), 0)


def stack_heads(pair, first):
    zero = jnp.zeros_like(pair)
    return jnp.concatenate([jnp.where(first, pair, zero), jnp.where(first, zero, pair)], axis=0)


def each_query_tile(bounds, q_row, k_row, length, visit):
    def per_segment(s, carry):
        q_low, q_high = bounds[q_row, s], bounds[q_row, s + 1]
        k_low, k_high = bounds[k_row, s], bounds[k_row, s + 1]
        q_base, k_base = (q_low // 16) * 16, (k_low // 16) * 16
        q_tiles = (q_high - q_base + TILE - 1) // TILE
        k_tiles = (k_high - k_base + TILE - 1) // TILE

        def per_tile(i, inner):
            low = jnp.maximum(q_low, q_base + i * TILE)
            start = pl.multiple_of(jnp.minimum(q_base + i * TILE, length - TILE), 16)
            visit(start, low, q_high, k_base, k_low, k_high, k_tiles)
            return inner

        return lax.fori_loop(0, q_tiles, per_tile, carry)

    lax.fori_loop(0, SEGMENTS, per_segment, 0)


def key_tile(j, k_base, k_low, k_high, length):
    low = jnp.maximum(k_low, k_base + j * TILE)
    start = pl.multiple_of(jnp.minimum(k_base + j * TILE, length - TILE), 16)
    rows = row_index(TILE) + start
    return start, (rows >= low) & (rows < k_high)


def attend(bounds, q_row, k_row, query, keys, values, out_ref, stat_ref):
    (q_ref, q_col), (k_ref, k_col), (v_ref, v_col) = query, keys, values
    length, width = out_ref.shape
    first = lane_index(TILE) < HEAD_DIM
    lanes = lane_index(TILE)
    unit = jnp.where(lane_index(2 * TILE) == 0, 1.0, 0.0).astype(BF16)
    ones = jnp.ones((TILE, 128), BF16)

    def visit(start, low, high, k_base, k_low, k_high, k_tiles):
        rows = row_index(TILE) + start
        keep = (rows >= low) & (rows < high)
        span = pl.ds(start, TILE)

        def piece(p, k_start, inside):
            cols = p * 128
            bias = jnp.where((lanes == 0) & jnp.logical_not(inside), MASKED, 0.0).astype(BF16)
            queries = stack_heads(q_ref[span, q_col + cols : q_col + cols + 128], first)
            k_span = pl.ds(k_start, TILE)
            pair_k = k_ref[k_span, k_col + cols : k_col + cols + 128]
            pair_v = v_ref[k_span, v_col + cols : v_col + cols + 128]
            scores = dot_bt(
                jnp.concatenate([queries, unit], axis=1), jnp.concatenate([pair_k, bias], axis=1)
            )
            return scores, jnp.concatenate([pair_v, ones], axis=1)

        def finish(p, highest, total):
            cols = p * 128
            mass = total[:, 128:]
            result = total[:, :128] / mass
            log_total = highest + jnp.log(mass)
            merged = lower(jnp.where(first, result[:TILE], result[TILE:]))
            out_ref[span, cols : cols + 128] = jnp.where(
                keep, merged, out_ref[span, cols : cols + 128]
            )
            old = stat_ref[span, :]
            new = jnp.where(lanes == 2 * p, log_total[:TILE], old)
            new = jnp.where(lanes == 2 * p + 1, log_total[TILE:], new)
            stat_ref[span, :] = jnp.where(keep, new, old)

        @pl.when(k_tiles == 1)
        def _():
            k_start, inside = key_tile(0, k_base, k_low, k_high, length)
            for p in range(width // 128):
                scores, wide_v = piece(p, k_start, inside)
                highest = jnp.max(scores, -1, keepdims=True)
                finish(p, highest, dot(lower(jnp.exp(scores - highest)), wide_v))

        @pl.when(k_tiles > 1)
        def _():
            for p in range(width // 128):

                def per_key(j, carry):
                    highest, total = carry
                    k_start, inside = key_tile(j, k_base, k_low, k_high, length)
                    scores, wide_v = piece(p, k_start, inside)
                    newest = jnp.maximum(highest, jnp.max(scores, -1, keepdims=True))
                    expon = lower(jnp.exp(scores - newest))
                    return newest, total * jnp.exp(highest - newest) + dot(expon, wide_v)

                empty = (jnp.full((2 * TILE, 1), MASKED, F32), jnp.zeros((2 * TILE, 256), F32))
                finish(p, *lax.fori_loop(0, k_tiles, per_key, empty))

    each_query_tile(bounds, q_row, k_row, length, visit)


def spread_lanes(column, lanes, lead):
    high = lower(column).astype(F32)
    rest = column - high
    middle = lower(rest).astype(F32)
    spread = jnp.where(lanes == 1, high, jnp.where(lanes == 2, middle, rest - middle))
    return lower(jnp.where(lanes == 0, lead, jnp.where(lanes < 4, -spread, 0.0)))


def attend_back(bounds, q_row, k_row, query, keys, values, do_ref, out_ref, stat_ref, dq, dk, dv):
    (q_ref, q_col), (k_ref, k_col), (v_ref, v_col) = query, keys, values
    (dq_ref, dq_col), (dk_ref, dk_col), (dv_ref, dv_col) = dq, dk, dv
    length, width = do_ref.shape
    first = lane_index(TILE) < HEAD_DIM
    lanes = lane_index(TILE)
    lanes_two = lane_index(2 * TILE)

    def visit(start, low, high, k_base, k_low, k_high, k_tiles):
        rows = row_index(TILE) + start
        keep = (rows >= low) & (rows < high)
        span = pl.ds(start, TILE)

        def per_key(j, carry):
            k_start, inside = key_tile(j, k_base, k_low, k_high, length)
            k_span = pl.ds(k_start, TILE)
            tail = jnp.where(lanes == 0, jnp.where(inside, 0.0, MASKED), 0.0)
            tail = lower(jnp.where((lanes > 0) & (lanes < 4), 1.0, tail))
            for p in range(width // 128):
                cols = p * 128
                pair_q = q_ref[span, q_col + cols : q_col + cols + 128]
                pair_k = k_ref[k_span, k_col + cols : k_col + cols + 128]
                pair_v = v_ref[k_span, v_col + cols : v_col + cols + 128]
                pair_do = jnp.where(keep, do_ref[span, cols : cols + 128], jnp.zeros((), BF16))
                inner = pair_do.astype(F32) * out_ref[span, cols : cols + 128].astype(F32)
                centre = jnp.concatenate(
                    [
                        jnp.sum(jnp.where(first, inner, 0.0), -1, keepdims=True),
                        jnp.sum(jnp.where(first, 0.0, inner), -1, keepdims=True),
                    ],
                    axis=0,
                )
                stat = jnp.where(keep, stat_ref[span, :], -MASKED)
                log_total = jnp.concatenate(
                    [stat[:, 2 * p : 2 * p + 1], stat[:, 2 * p + 1 : 2 * p + 2]], axis=0
                )
                queries = stack_heads(pair_q, first)
                grads = stack_heads(pair_do, first)
                probs = jnp.exp(
                    dot_bt(
                        jnp.concatenate([pair_k, tail], axis=1),
                        jnp.concatenate([queries, spread_lanes(log_total, lanes_two, 1.0)], axis=1),
                    )
                )
                slope = dot_bt(
                    jnp.concatenate([pair_v, tail], axis=1),
                    jnp.concatenate([grads, spread_lanes(centre, lanes_two, 0.0)], axis=1),
                )
                ds = lower(probs * slope)
                dv_ref[k_span, dv_col + cols : dv_col + cols + 128] += dot(lower(probs), grads)
                dk_ref[k_span, dk_col + cols : dk_col + cols + 128] += dot(ds, queries)
                turned = dot(pair_k.T, ds)
                turned = jnp.concatenate(
                    [turned[:HEAD_DIM, :TILE], turned[HEAD_DIM:, TILE:]], axis=0
                )
                dq_ref[span, dq_col + cols : dq_col + cols + 128] += turned.T
            return carry

        lax.fori_loop(0, k_tiles, per_key, 0)

    each_query_tile(bounds, q_row, k_row, length, visit)


def forward_kernel(
    bounds, xs, qkv, kv, gain, shift, w_self, w_query, a1, y1, q2, a2, stat1, stat2
):
    length, width = a1.shape[1:]
    attend(
        bounds,
        0,
        0,
        (qkv.at[0], 0),
        (qkv.at[0], width),
        (qkv.at[0], 2 * width),
        a1.at[0],
        stat1.at[0],
    )

    def rows(i, carry):
        span = pl.ds(pl.multiple_of(i * TILE, TILE), TILE)
        after = xs[0, span, :].astype(F32) + dot(a1[0, span, :], w_self[...])
        y1[0, span, :] = after
        xhat, _ = standardise(after)
        h2 = lower(xhat * gain[1:2, :] + shift[1:2, :])
        q2[0, span, :] = lower(dot(h2, w_query[...]) * HEAD_DIM ** (-0.5))
        return carry

    lax.fori_loop(0, length // TILE, rows, 0)
    attend(bounds, 0, 1, (q2.at[0], 0), (kv, 0), (kv, width), a2.at[0], stat2.at[0])


def feed_kernel(
    per_step, y1, a2, g1, g2, gain, shift, w_cross, w_in, w_out,
    o1, o2, h3, r, du, e2, dy2, do2, dnorm,
):
    i = pl.program_id(0)
    width = w_cross.shape[0]
    is_first = i < per_step
    grad = jnp.where(is_first, g1[...], g2[...])
    after = y1[0] + dot(a2[0], w_cross[...])
    xhat, inverse = standardise(after)
    normed = lower(xhat * gain[2:3, :] + shift[2:3, :])
    h3[0] = normed
    result = after
    dh3 = jnp.zeros_like(after)
    slope = (2.0 / jnp.pi) ** 0.5
    for c in range(w_in.shape[1] // width):
        cols = slice(c * width, (c + 1) * width)
        u = dot(normed, w_in[:, cols])
        dr = dot_bt(grad, w_out[cols, :])
        square = u * u
        t = jnp.tanh(slope * (u + 0.044715 * (square * u)))
        half = 0.5 * (1.0 + t)
        hidden = lower(u * half)
        r[0, :, cols] = hidden
        gate = half + 0.5 * u * (1.0 - t * t) * (slope * (1.0 + 3 * 0.044715 * square))
        pre = lower(dr * gate)
        du[0, :, cols] = pre
        result = result + dot(hidden, w_out[cols, :])
        dh3 = dh3 + dot_bt(pre, w_in[:, cols])

    @pl.when(is_first)
    def _():
        o1[...] = lower(result)

    @pl.when(jnp.logical_not(is_first))
    def _():
        o2[...] = lower(result)

    @pl.when(i == 0)
    def _():
        dnorm[...] = jnp.zeros_like(dnorm)

    dnorm[0] += fold_rows(dh3 * xhat)
    dnorm[1] += fold_rows(dh3)
    back = grad.astype(F32) + norm_back(xhat, inverse, gain[2:3, :], dh3)
    dy2[0] = back
    low = lower(back)
    e2[0] = low
    do2[0] = lower(dot_bt(low, w_cross[...]))


def feed_grad_kernel(small, h3, a2, e2, g1, g2, du, r, joint, turned, d_in, d_out, d_cross, sem):
    c = pl.program_id(0)
    last = pl.num_programs(0) - 1
    half, width = g1.shape
    hidden = d_out.shape[2]
    group = hidden // width
    rows = width // group
    slot = lax.rem(c, 2)

    def copies(at, chunk):
        return (
            pltpu.make_async_copy(
                d_in.at[at], joint.at[:, pl.ds(pl.multiple_of(chunk * width, width), width)], sem.at[0, at]
            ),
            pltpu.make_async_copy(
                d_out.at[at],
                joint.at[pl.ds(pl.multiple_of(chunk * rows, rows), rows), hidden + width :],
                sem.at[1, at],
            ),
        )

    cross = pltpu.make_async_copy(d_cross, joint.at[:, hidden : hidden + width], sem.at[2, 0])

    @pl.when(c >= 2)
    def _():
        for copy in copies(slot, c - 2):
            copy.wait()

    @pl.when(c == 0)
    def _():
        turned[...] = h3[...].T
        d_cross[...] = lower(dot(a2[...].T, e2[...]))
        cross.start()

    d_in[slot] = lower(dot(turned[...], du[...]))
    part = lower(dot_at(r[:half, :], g1[...]) + dot_at(r[half:, :], g2[...]))
    for w in range(width // (group * small)):
        for j in range(group):
            at = (w * group + j) * small
            d_out[slot, w * small : (w + 1) * small, j * width : (j + 1) * width] = part[at : at + small]
    for copy in copies(slot, c):
        copy.start()

    @pl.when(c == last)
    def _():
        for copy in copies(1 - slot, c - 1) + copies(slot, c):
            copy.wait()
        cross.wait()


def cross_back_kernel(
    bounds, q2, kv, a1, a2, stat2, do2, y1, dy2, mem, gain, shift, w_query, w_self, w_kv,
    dy1, do1, d_query, d_self, d_kv, d_mem, dnorm,
    dq_sum, dkv_sum, h2, low_q, low_e,
):
    step = pl.program_id(0)
    length, width = q2.shape[1:]

    @pl.when(step == 0)
    def _():
        dkv_sum[...] = jnp.zeros_like(dkv_sum)
        dnorm[...] = jnp.zeros_like(dnorm)

    dq_sum[...] = jnp.zeros_like(dq_sum)
    attend_back(
        bounds, 0, 1, (q2.at[0], 0), (kv, 0), (kv, width), do2.at[0], a2.at[0], stat2.at[0],
        (dq_sum, 0), (dkv_sum, 0), (dkv_sum, width),
    )

    def rows(i, carry):
        span = pl.ds(pl.multiple_of(i * TILE, TILE), TILE)
        grad_q = lower(dq_sum[span, :] * HEAD_DIM ** (-0.5))
        low_q[step, span, :] = grad_q
        xhat, inverse = standardise(y1[0, span, :])
        h2[step, span, :] = lower(xhat * gain[1:2, :] + shift[1:2, :])
        dh2 = dot_bt(grad_q, w_query[...])
        dnorm[0] += fold_rows(dh2 * xhat)
        dnorm[1] += fold_rows(dh2)
        back = dy2[0, span, :] + norm_back(xhat, inverse, gain[1:2, :], dh2)
        dy1[0, span, :] = back
        low = lower(back)
        low_e[step, span, :] = low
        do1[0, span, :] = lower(dot_bt(low, w_self[...]))
        return carry

    lax.fori_loop(0, length // TILE, rows, 0)

    @pl.when(step == 1)
    def _():
        d_query[...] = lower(dot(h2[0].T, low_q[0]) + dot(h2[1].T, low_q[1]))
        d_self[...] = lower(dot(a1[0].T, low_e[0]) + dot(a1[1].T, low_e[1]))
        pair = lower(dkv_sum[...])
        d_kv[...] = lower(dot(mem[...].T, pair))
        d_mem[...] = dot_bt(pair, w_kv[...])


def self_back_kernel(bounds, qkv, a1, stat1, do1, low, sums):
    width = do1.shape[2]
    sums[...] = jnp.zeros_like(sums)
    attend_back(
        bounds, 0, 0, (qkv.at[0], 0), (qkv.at[0], width), (qkv.at[0], 2 * width),
        do1.at[0], a1.at[0], stat1.at[0], (sums, 0), (sums, width), (sums, 2 * width),
    )
    low[0, :, :width] = lower(sums[:, :width] * HEAD_DIM ** (-0.5))
    low[0, :, width:] = lower(sums[:, width:])


def flip(index, mask):
    out, bit = index, 1
    while bit <= mask:
        if mask & bit:
            out = out + bit - 2 * bit * lax.rem(lax.div(index, bit), 2)
        bit *= 2
    return out


class Links:
    def __init__(self, sizes, send, recv):
        self.members, wides = sizes
        self.lines = wides // 2
        self.group = min(4, self.members)
        self.narrow, self.wide = lax.axis_index("narrow"), lax.axis_index("wide")
        self.line, self.core = lax.div(self.wide, 2), lax.rem(self.wide, 2)
        self.part = lax.rem(self.narrow, self.group)
        self.send, self.recv, self.used = send, recv, 0

    def core_peer(self):
        return (self.narrow, flip(self.wide, 1))

    def plane_peer(self, mask):
        return (flip(self.narrow, mask), self.wide)

    def line_peer(self, mask):
        return (self.narrow, 2 * flip(self.line, mask) + self.core)

    def far_masks(self):
        masks, mask = [], self.group
        while mask < self.members:
            masks.append(mask)
            mask *= 2
        return masks

    def barrier(self, far):
        semaphore = pltpu.get_barrier_semaphore()
        peers = [self.core_peer()]
        peers += [self.plane_peer(m) for m in range(1, self.group)]
        peers += [self.line_peer(m) for m in range(1, self.lines)]
        if far:
            peers += [self.plane_peer(m) for m in self.far_masks()]
        for peer in peers:
            pl.semaphore_signal(semaphore, inc=1, device_id=peer, device_id_type=MESH)
        pl.semaphore_wait(semaphore, len(peers))

    def push(self, src, dst, peer):
        slot = self.used
        self.used += 1
        copy = pltpu.make_async_remote_copy(
            src_ref=src,
            dst_ref=dst,
            send_sem=self.send.at[slot],
            recv_sem=self.recv.at[slot],
            device_id=peer,
            device_id_type=MESH,
        )
        copy.start()
        return copy

    def quarter(self, part, cols):
        size = cols // self.group
        return pl.ds(pl.multiple_of(part * size, size), size)


def wait_all(copies):
    for copy in copies:
        copy.wait()


class Gathered:
    def __init__(self, links, shard, full, local_sem):
        self.links, self.shard, self.full = links, shard, full
        self.cols = shard.shape[-1]
        self.local = pltpu.make_async_copy(shard, full.at[links.line, links.core], local_sem)

    def start_line(self):
        links = self.links
        self.local.start()
        mine = links.quarter(links.part, self.cols)
        self.copies = [
            links.push(
                self.shard.at[:, mine], self.full.at[links.line, links.core, :, mine], links.line_peer(m)
            )
            for m in range(1, links.lines)
        ]

    def start_plane(self):
        links = self.links
        wait_all(self.copies)
        mine = links.quarter(links.part, self.cols)
        self.copies = []
        for k in range(1, links.lines):
            place = self.full.at[flip(links.line, k), links.core, :, mine]
            for m in range(1, links.group):
                self.copies.append(links.push(place, place, links.plane_peer(m)))

    def start_core(self):
        links = self.links
        wait_all(self.copies)
        self.local.wait()
        place = self.full.at[:, links.core]
        self.copies = [links.push(place, place, links.core_peer())]

    def finish(self):
        wait_all(self.copies)


def gather_slots(sizes, pieces):
    lines, group = sizes[1] // 2, min(4, sizes[0])
    return pieces * (lines - 1 + (lines - 1) * (group - 1) + 1) + lines


def gather_kernel(
    sizes, x1, x2, mem, norm, s_qkv, s_kv, s_self, s_query, s_cross, s_in, s_out,
    xs, qkv, kv, norms, f_qkv, f_kv, f_self, f_query, f_cross, f_in, f_out,
    h1, v_qkv, v_kv, o_qkv, o_kv, norm_all, send, recv, local,
):
    links = Links(sizes, send, recv)
    length, width = x1.shape
    used = [0]

    def local_copy(src, dst):
        copy = pltpu.make_async_copy(src, dst, local.at[used[0]])
        used[0] += 1
        copy.start()
        return copy

    def slot():
        used[0] += 1
        return local.at[used[0] - 1]

    def piece(shard, full):
        return Gathered(links, shard, full, slot())

    links.barrier(False)
    pieces = []
    for c in range(3):
        cols = slice(c * width, (c + 1) * width)
        pieces.append(piece(s_qkv.at[:, cols], v_qkv.at[c]))
    for c in range(2):
        cols = slice(c * width, (c + 1) * width)
        pieces.append(piece(s_kv.at[:, cols], v_kv.at[c]))
    pieces.append(piece(s_self, f_self))
    pieces.append(piece(s_query, f_query))
    pieces.append(piece(s_cross, f_cross))
    half = s_in.shape[1] // 2
    for c in range(2):
        cols = slice(c * half, (c + 1) * half)
        pieces.append(piece(s_in.at[:, cols], f_in.at[:, :, :, cols]))
    half = s_out.shape[0] // 2
    for c in range(2):
        rows = slice(c * half, (c + 1) * half)
        pieces.append(piece(s_out.at[rows], f_out.at[:, :, rows]))

    norm_all[links.line, links.core] = norm[...]
    own = norm_all.at[links.line, links.core]
    norm_copies = [links.push(own, own, links.line_peer(m)) for m in range(1, links.lines)]
    for p in range(2):
        pieces[p].start_line()
    outgoing = [local_copy(x1, xs.at[0]), local_copy(x2, xs.at[1])]
    pieces[2].start_line()
    wait_all(norm_copies)
    place = norm_all.at[:, links.core]
    norm_copy = links.push(place, place, links.core_peer())
    pieces[0].start_plane()
    norm_copy.wait()
    every = norm_all[...]
    total = every[0, 0]
    for k in range(1, 2 * links.lines):
        total = total + every[k // 2, k % 2]
    norms[...] = total
    gain, shift = total[0:1, :], total[3:4, :]

    def normalise(t, x):
        def rows(i, carry):
            span = pl.ds(pl.multiple_of(i * TILE, TILE), TILE)
            xhat, _ = standardise(x[span, :].astype(F32))
            h1[t, span, :] = lower(xhat * gain + shift)
            return carry

        lax.fori_loop(0, length // TILE, rows, 0)

    def project(c):
        def run():
            weight = v_qkv[c].reshape(width, width)
            scale = HEAD_DIM ** (-0.5) if c == 0 else 1.0
            for t in range(2):

                def rows(i, carry, t=t):
                    span = pl.ds(pl.multiple_of(i * 2 * TILE, 2 * TILE), 2 * TILE)
                    o_qkv[c, t, span, :] = lower(dot(h1[t, span, :], weight) * scale)
                    return carry

                lax.fori_loop(0, length // (2 * TILE), rows, 0)
            cols = slice(c * width, (c + 1) * width)
            outgoing.append(local_copy(o_qkv.at[c], qkv.at[:, :, cols]))
            outgoing.append(local_copy(v_qkv.at[c], f_qkv.at[:, :, :, cols]))

        return run

    def project_memory(c):
        def run():
            weight = v_kv[c].reshape(width, width)

            def rows(i, carry):
                span = pl.ds(pl.multiple_of(i * 2 * TILE, 2 * TILE), 2 * TILE)
                o_kv[c, span, :] = lower(dot(mem[span, :], weight))
                return carry

            lax.fori_loop(0, length // (2 * TILE), rows, 0)
            cols = slice(c * width, (c + 1) * width)
            outgoing.append(local_copy(o_kv.at[c], kv.at[:, cols]))
            outgoing.append(local_copy(v_kv.at[c], f_kv.at[:, :, :, cols]))

        return run

    work = {c: project(c) for c in range(3)} | {3 + c: project_memory(c) for c in range(2)}
    count = len(pieces)
    for t in range(3, count + 6):
        if t < count:
            pieces[t].start_line()
        if 1 <= t - 2 < count:
            pieces[t - 2].start_plane()
        if t == 3:
            normalise(0, x1)
        if t == 4:
            normalise(1, x2)
        if 0 <= t - 4 < count:
            pieces[t - 4].start_core()
        if 0 <= t - 5 < count:
            pieces[t - 5].finish()
            if t - 5 in work:
                work[t - 5]()
    wait_all(outgoing)


class Reduced:
    def __init__(self, links, bufs, out, source=None, shard=None):
        self.links, self.out, self.source, self.shard = links, out, source, shard
        self.crecv, self.chip, self.precv, self.plane, self.lrecv, self.mine, self.xrecv, self.full = bufs
        self.cols = self.full.shape[-1]

    def start_core(self):
        links = self.links
        self.copies = [links.push(self.source.at[:, 1 - links.core], self.crecv, links.core_peer())]

    def start_plane(self):
        links = self.links
        if self.source is not None:
            wait_all(self.copies)
            for k in range(links.lines):
                self.chip[k] = lower(
                    self.source[k, links.core].astype(F32) + self.crecv[k].astype(F32)
                )
        self.copies = [
            links.push(
                self.chip.at[:, :, links.quarter(flip(links.part, m), self.cols)],
                self.precv.at[m - 1],
                links.plane_peer(m),
            )
            for m in range(1, links.group)
        ]

    def start_line(self):
        links = self.links
        wait_all(self.copies)
        total = self.chip[:, :, links.quarter(links.part, self.cols)].astype(F32)
        for m in range(1, links.group):
            total = total + self.precv[m - 1].astype(F32)
        self.plane[...] = lower(total)
        if self.source is None:
            self.copies = []
            return
        self.copies = [
            links.push(self.plane.at[flip(links.line, m)], self.lrecv.at[m - 1], links.line_peer(m))
            for m in range(1, links.lines)
        ]

    def start_gather(self):
        links = self.links
        wait_all(self.copies)
        if self.source is None:
            total = self.plane[0].astype(F32)
        else:
            total = self.plane[links.line].astype(F32)
            for m in range(1, links.lines):
                total = total + self.lrecv[m - 1].astype(F32)
        for i, mask in enumerate(links.far_masks()):
            self.xrecv[2 * i] = lower(total)
            links.push(self.xrecv.at[2 * i], self.xrecv.at[2 * i + 1], links.plane_peer(mask)).wait()
            total = self.xrecv[2 * i].astype(F32) + self.xrecv[2 * i + 1].astype(F32)
        self.mine[...] = lower(total)
        place = self.full.at[:, links.quarter(links.part, self.cols)]
        place[...] = self.mine[...]
        self.copies = [links.push(self.mine, place, links.plane_peer(m)) for m in range(1, links.group)]

    def finish(self):
        wait_all(self.copies)
        self.out[...] = self.full[...].astype(F32)


def reduced_scratch(sizes, rows, cols, wide_too):
    members, wides = sizes
    lines, group = wides // 2, min(4, members)
    part = cols // group
    depth = lines if wide_too else 1
    far = max(2, 2 * (members // group - 1))
    small = (1, 16, 128)
    return [
        pltpu.VMEM((lines, rows, cols) if wide_too else small, BF16),
        pltpu.VMEM((depth, rows, cols), BF16),
        pltpu.VMEM((group - 1, depth, rows, part), BF16),
        pltpu.VMEM((depth, rows, part), BF16),
        pltpu.VMEM((lines - 1, rows, part) if wide_too else small, BF16),
        pltpu.VMEM((rows, part), BF16),
        pltpu.VMEM((far, rows, part), BF16),
        pltpu.VMEM((rows, cols), BF16),
    ]


def reduce_slots(sizes, jobs):
    members, wides = sizes
    lines, group = wides // 2, min(4, members)
    return (jobs + 1) * (1 + 2 * (group - 1) + lines - 1 + members // group)


BUFS = 8


def finish_kernel(
    sizes, low_hbm, xs_hbm, dy1_hbm, norms, w_qkv, d_self, d_query, d_kv, c_in, c_out, c_cross, dnorm1, dnorm2,
    gi1, gi2, t_qkv, t_self, t_query, t_kv, t_in, t_out, t_cross, t_norm,
    low, xs, dy1, h1, grads, norm_slots, *rest,
):
    send, recv, local = rest[-3:]
    bufs = rest[:-3]
    links = Links(sizes, send, recv)
    _, length, width = xs.shape
    loads = [
        pltpu.make_async_copy(xs_hbm, xs, local.at[0]),
        pltpu.make_async_copy(low_hbm, low, local.at[1]),
        pltpu.make_async_copy(dy1_hbm, dy1, local.at[2]),
    ]
    for copy in loads:
        copy.start()
    links.barrier(True)

    taken = [0]

    def job(out, **kind):
        at = taken[0] * BUFS
        taken[0] += 1
        return Reduced(links, bufs[at : at + BUFS], out, **kind)

    others = [
        job(t_kv, source=d_kv), job(t_self, source=d_self), job(t_query, source=d_query),
    ]
    heads = [job(t_qkv.at[:, c * width : (c + 1) * width], source=grads.at[c]) for c in range(3)]
    shards = [job(t_in, shard=c_in), job(t_out, shard=c_out), job(t_cross, shard=c_cross)]
    for one in others:
        one.start_core()
    for one in shards:
        one.chip[0] = one.shard[...]
        one.start_plane()
    gain, shift = norms[0:1, :], norms[3:4, :]
    loads[0].wait()
    for t in range(2):
        for i in range(length // TILE):
            xhat, _ = standardise(xs[t, i * TILE : (i + 1) * TILE, :].astype(F32))
            at = t * length + i * TILE
            h1[:, at : at + TILE] = lower(xhat * gain + shift).T
    for one in others:
        one.start_plane()
    loads[1].wait()
    for c in range(3):
        cols = slice(c * width, (c + 1) * width)
        value = dot(h1[:, :length], low[0, :, cols]) + dot(h1[:, length:], low[1, :, cols])
        grads[c] = lower(value).reshape(grads.shape[1:])
        heads[c].start_core()
        if c > 0:
            heads[c - 1].start_plane()
    heads[2].start_plane()
    loads[2].wait()
    stores = []
    dgain = jnp.zeros((8, width), F32)
    dshift = jnp.zeros((8, width), F32)
    steps = [
        lambda: [one.start_line() for one in others],
        lambda: [one.start_line() for one in shards],
        lambda: [one.start_gather() for one in others],
        lambda: [one.start_gather() for one in shards],
        lambda: heads[0].start_line(),
        lambda: heads[1].start_line(),
        lambda: heads[2].start_line(),
        lambda: [one.finish() for one in others],
    ]
    weight = w_qkv[...]
    for t in range(2):
        for i in range(length // TILE):
            span = slice(i * TILE, (i + 1) * TILE)
            xhat, inverse = standardise(xs[t, span, :].astype(F32))
            dh1 = dot_bt(low[t, span, :], weight)
            dgain = dgain + fold_rows(dh1 * xhat)
            dshift = dshift + fold_rows(dh1)
            dy1[t, span, :] = dy1[t, span, :] + norm_back(xhat, inverse, gain, dh1)
            out = (gi1, gi2)[t]
            number = t * (length // TILE) + i
            copy = pltpu.make_async_copy(dy1.at[t, span, :], out.at[span, :], local.at[3 + number])
            copy.start()
            stores.append(copy)
            if number < len(steps):
                steps[number]()
    rows = [jnp.sum(item, axis=0, keepdims=True) for item in (dgain, dnorm1[0], dnorm2[0], dshift, dnorm1[1], dnorm2[1])]
    total = jnp.concatenate(rows + [jnp.zeros((2, width), F32)], axis=0)

    def swap(first, count, own, peers, total):
        norm_slots[first + own] = total
        place = norm_slots.at[first + own]
        wait_all([links.push(place, place, peer) for peer in peers])
        out = norm_slots[first]
        for k in range(1, count):
            out = out + norm_slots[first + k]
        return out

    total = swap(0, 2, links.core, [links.core_peer()], total)
    for one in heads:
        one.start_gather()
    total = swap(2, links.group, links.part, [links.plane_peer(m) for m in range(1, links.group)], total)
    first = 2 + links.group
    total = swap(first, links.lines, links.line, [links.line_peer(m) for m in range(1, links.lines)], total)
    first += links.lines
    for mask in links.far_masks():
        side = lax.rem(lax.div(links.narrow, mask), 2)
        total = swap(first, 2, side, [links.plane_peer(mask)], total)
        first += 2
    t_norm[...] = total
    for one in shards + heads:
        one.finish()
    wait_all(stores)


def whole(shape):
    zeros = (0,) * len(shape)
    return pl.BlockSpec(shape, lambda *_: zeros, pipeline_mode=pl.Buffered(1))


def fixed(shape):
    zeros = (0,) * len(shape)
    return pl.BlockSpec(shape, lambda *_: zeros)


def by_step(shape):
    return pl.BlockSpec((1,) + shape, lambda t, *_: (t, 0, 0))


def params():
    return pltpu.CompilerParams(
        vmem_limit_bytes=VMEM_LIMIT, dimension_semantics=("arbitrary",)
    )


def struct(shape, dtype):
    return jax.ShapeDtypeStruct(shape, dtype)


def local_step(sizes, x1, x2, mem, g1, g2, target_ids, memory_ids, norm, shards):
    length, width = x1.shape
    members, wides = sizes
    lines = wides // 2
    small = width // wides
    hidden = shards[5].shape[1]
    tiles = length // TILE
    bounds = jnp.stack([segment_bounds(target_ids), segment_bounds(memory_ids)])
    vmem = pl.BlockSpec(memory_space=pltpu.VMEM)
    anywhere = pl.BlockSpec(memory_space=pl.ANY)

    def full(shape):
        return struct((lines, 2, shape[0], shape[1]), BF16)

    pieces = 12
    slots = gather_slots(sizes, pieces)
    results = pl.pallas_call(
        functools.partial(gather_kernel, sizes),
        in_specs=[vmem] * 4 + [anywhere] * 7,
        out_specs=[anywhere] * 3 + [vmem] + [anywhere] * 7,
        out_shape=[
            struct((2, length, width), BF16),
            struct((2, length, 3 * width), BF16),
            struct((length, 2 * width), BF16),
            struct((8, width), F32),
        ]
        + [full(item.shape) for item in shards],
        scratch_shapes=[
            pltpu.VMEM((2, length, width), BF16),
            pltpu.VMEM((3, lines, 2, small, width), BF16),
            pltpu.VMEM((2, lines, 2, small, width), BF16),
            pltpu.VMEM((3, 2, length, width), BF16),
            pltpu.VMEM((2, length, width), BF16),
            pltpu.VMEM((lines, 2, 8, width), F32),
            pltpu.SemaphoreType.DMA((slots,)),
            pltpu.SemaphoreType.DMA((slots,)),
            pltpu.SemaphoreType.DMA((pieces + 12,)),
        ],
        compiler_params=pltpu.CompilerParams(
            vmem_limit_bytes=VMEM_LIMIT, collective_id=0, has_side_effects=True
        ),
        name="gather_project",
    )(x1, x2, mem, norm, *shards)
    xs, qkv, kv, norms = results[:4]
    w_qkv, w_kv, w_self, w_query, w_cross, w_in, w_out = (
        item.reshape(-1, item.shape[-1]) for item in results[4:]
    )
    gain, shift = norms[:3], norms[3:6]
    norm_spec = whole((3, width))
    step_low = by_step((length, width))
    a1, y1, q2, a2, stat1, stat2 = pl.pallas_call(
        forward_kernel,
        grid_spec=pltpu.PrefetchScalarGridSpec(
            num_scalar_prefetch=1,
            grid=(2,),
            in_specs=[
                step_low, by_step((length, 3 * width)), whole(kv.shape), norm_spec, norm_spec,
                whole(w_self.shape), whole(w_query.shape),
            ],
            out_specs=[step_low] * 4 + [by_step((length, 128))] * 2,
        ),
        out_shape=[
            struct((2, length, width), BF16),
            struct((2, length, width), F32),
            struct((2, length, width), BF16),
            struct((2, length, width), BF16),
            struct((2, length, 128), F32),
            struct((2, length, 128), F32),
        ],
        compiler_params=params(),
        name="attend_forward",
    )(bounds, xs, qkv, kv, gain, shift, w_self, w_query)

    step_tile = pl.BlockSpec((1, TILE, width), lambda i: (i // tiles, i % tiles, 0))
    step_wide = pl.BlockSpec((1, TILE, hidden), lambda i: (i // tiles, i % tiles, 0))
    early = pl.BlockSpec((TILE, width), lambda i: (jnp.minimum(i, tiles - 1), 0))
    late = pl.BlockSpec((TILE, width), lambda i: (jnp.maximum(i - tiles, 0), 0))
    o1, o2, h3, r, du, e2, dy2, do2, dnorm2 = pl.pallas_call(
        functools.partial(feed_kernel, tiles),
        grid=(2 * tiles,),
        in_specs=[
            step_tile, step_tile, early, late, norm_spec, norm_spec,
            whole(w_cross.shape), whole(w_in.shape), whole(w_out.shape),
        ],
        out_specs=[
            early, late, step_tile, step_wide, step_wide, step_tile, step_tile, step_tile,
            fixed((2, 8, width)),
        ],
        out_shape=[
            struct((length, width), BF16),
            struct((length, width), BF16),
            struct((2, length, width), BF16),
            struct((2, length, hidden), BF16),
            struct((2, length, hidden), BF16),
            struct((2, length, width), BF16),
            struct((2, length, width), F32),
            struct((2, length, width), BF16),
            struct((2, 8, width), F32),
        ],
        compiler_params=params(),
        name="feed_forward_back",
    )(y1, a2, g1, g2, gain, shift, w_cross, w_in, w_out)

    flat = (2 * length, width)
    chunk = pl.BlockSpec((2 * length, width), lambda c: (0, c))
    joint = pl.pallas_call(
        functools.partial(feed_grad_kernel, small),
        grid=(hidden // width,),
        in_specs=[whole(flat), whole(flat), whole(flat), whole((length, width)), whole((length, width)), chunk, chunk],
        out_specs=anywhere,
        out_shape=struct((width, 2 * hidden + width), BF16),
        scratch_shapes=[
            pltpu.VMEM((width, 2 * length), BF16),
            pltpu.VMEM((2, width, width), BF16),
            pltpu.VMEM((2, width * width // hidden, hidden), BF16),
            pltpu.VMEM((width, width), BF16),
            pltpu.SemaphoreType.DMA((3, 2)),
        ],
        compiler_params=params(),
        name="feed_weight_grads",
    )(h3.reshape(flat), a2.reshape(flat), e2.reshape(flat), g1, g2, du.reshape(2 * length, hidden), r.reshape(2 * length, hidden))
    share = lax.psum_scatter(joint, "wide", scatter_dimension=0, tiled=True)
    c_in = share[:, :hidden]
    c_cross = share[:, hidden : hidden + width]
    c_out = share[:, hidden + width :]

    dy1, do1, d_query, d_self, d_kv, d_mem, dnorm1 = pl.pallas_call(
        cross_back_kernel,
        grid_spec=pltpu.PrefetchScalarGridSpec(
            num_scalar_prefetch=1,
            grid=(2,),
            in_specs=[
                step_low, whole(kv.shape), whole(a1.shape), step_low, by_step((length, 128)), step_low,
                step_low, step_low, whole(mem.shape), norm_spec, norm_spec,
                whole(w_query.shape), whole(w_self.shape), whole(w_kv.shape),
            ],
            out_specs=[
                step_low, step_low, fixed((width, width)), fixed((width, width)), fixed((width, 2 * width)),
                fixed((length, width)), fixed((2, 8, width)),
            ],
            scratch_shapes=[
                pltpu.VMEM((length, width), F32),
                pltpu.VMEM((length, 2 * width), F32),
                pltpu.VMEM((2, length, width), BF16),
                pltpu.VMEM((2, length, width), BF16),
                pltpu.VMEM((2, length, width), BF16),
            ],
        ),
        out_shape=[
            struct((2, length, width), F32),
            struct((2, length, width), BF16),
            struct((width, width), BF16),
            struct((width, width), BF16),
            struct((width, 2 * width), BF16),
            struct((length, width), F32),
            struct((2, 8, width), F32),
        ],
        compiler_params=params(),
        name="cross_back",
    )(bounds, q2, kv, a1, a2, stat2, do2, y1, dy2, mem, gain, shift, w_query, w_self, w_kv)

    low = pl.pallas_call(
        self_back_kernel,
        grid_spec=pltpu.PrefetchScalarGridSpec(
            num_scalar_prefetch=1,
            grid=(2,),
            in_specs=[by_step((length, 3 * width)), step_low, by_step((length, 128)), step_low],
            out_specs=by_step((length, 3 * width)),
            scratch_shapes=[pltpu.VMEM((length, 3 * width), F32)],
        ),
        out_shape=struct((2, length, 3 * width), BF16),
        compiler_params=params(),
        name="self_back",
    )(bounds, qkv, a1, stat1, do1)

    def split(item):
        return item.reshape(lines, 2, small, item.shape[1])

    scratch = [
        pltpu.VMEM((2, length, 3 * width), BF16),
        pltpu.VMEM((2, length, width), BF16),
        pltpu.VMEM((2, length, width), F32),
        pltpu.VMEM((width, 2 * length), BF16),
        pltpu.VMEM((3, lines, 2, small, width), BF16),
        pltpu.VMEM((2 + 4 + lines + 2 * max(1, members // 4 - 1), 8, width), F32),
    ]
    for cols in (2 * width, width, width, width, width, width):
        scratch += reduced_scratch(sizes, small, cols, True)
    for cols in (hidden, hidden, width):
        scratch += reduced_scratch(sizes, small, cols, False)
    slots = reduce_slots(sizes, 9)
    scratch += [
        pltpu.SemaphoreType.DMA((slots,)),
        pltpu.SemaphoreType.DMA((slots,)),
        pltpu.SemaphoreType.DMA((3 + 2 * tiles,)),
    ]
    gi1, gi2, t_qkv, t_self, t_query, t_kv, t_in, t_out, t_cross, t_norm = pl.pallas_call(
        functools.partial(finish_kernel, sizes),
        in_specs=[anywhere] * 3 + [vmem] * 10,
        out_specs=[anywhere] * 2 + [vmem] * 8,
        out_shape=[
            struct((length, width), F32),
            struct((length, width), F32),
            struct((small, 3 * width), F32),
            struct((small, width), F32),
            struct((small, width), F32),
            struct((small, 2 * width), F32),
            struct((small, hidden), F32),
            struct((small, hidden), F32),
            struct((small, width), F32),
            struct((8, width), F32),
        ],
        scratch_shapes=scratch,
        compiler_params=pltpu.CompilerParams(
            vmem_limit_bytes=VMEM_LIMIT, collective_id=1, has_side_effects=True
        ),
        name="finish_reduce",
    )(low, xs, dy1, norms, w_qkv, split(d_self), split(d_query), split(d_kv), c_in, c_out, c_cross, dnorm1, dnorm2)
    t_out = t_out.reshape(small, hidden // width, width).swapaxes(0, 1).reshape(-1, width)
    return o1, o2, gi1, gi2, d_mem, t_norm, (t_qkv, t_self, t_query, t_kv, t_cross, t_in, t_out)


def body(
    sizes, inputs_one, inputs_two, memory, cotangent_one, cotangent_two, target_ids, memory_ids,
    norm_gain, norm_shift, self_qkv, self_out, cross_query, cross_kv, cross_out, ffn_in, ffn_out,
):
    shape = inputs_one.shape
    length, width = shape[1:]
    small = width // sizes[1]
    at = lax.axis_index("wide") * small
    norm = jnp.concatenate([norm_gain, norm_shift]).astype(F32)
    norm = lax.dynamic_update_slice(jnp.zeros((8, width), F32), norm, (0, at))
    o1, o2, gi1, gi2, d_mem, t_norm, grads = local_step(
        sizes,
        inputs_one.reshape(length, width),
        inputs_two.reshape(length, width),
        memory.reshape(length, width),
        cotangent_one.reshape(length, width),
        cotangent_two.reshape(length, width),
        target_ids,
        memory_ids,
        norm,
        (self_qkv, cross_kv, self_out, cross_query, cross_out, ffn_in, ffn_out),
    )
    mine = lax.dynamic_slice(t_norm, (0, at), (8, small))
    d_qkv, d_self, d_query, d_kv, d_cross, d_in, d_out = grads
    return (
        o1.reshape(shape), o2.reshape(shape), gi1.reshape(shape), gi2.reshape(shape), d_mem.reshape(shape),
        mine[:3], mine[3:6], d_qkv, d_self, d_query, d_kv, d_cross, d_in, d_out,
    )


def solution(mesh):
    rows = P(("narrow", "wide"), None, None)
    ids = P(("narrow", "wide"), None)
    norm, weight = P(None, "wide"), P("wide", None)
    return jax.shard_map(
        functools.partial(body, (mesh.shape["narrow"], mesh.shape["wide"])),
        mesh=mesh,
        in_specs=(rows,) * 5 + (ids,) * 2 + (norm,) * 2 + (weight,) * 7,
        out_specs=(rows,) * 5 + (norm,) * 2 + (weight,) * 7,
        check_vma=False,
    )
```

```python
import functools

import jax
import jax.numpy as jnp
from jax import lax
from jax.experimental import pallas as pl
from jax.experimental.pallas import tpu as pltpu
from jax.sharding import PartitionSpec as P

HEAD_DIM = 64
TILE = 256
SMALL = 128
SEGMENTS = 5
MASKED = -1e30
VMEM_LIMIT = 60 * 1024 * 1024
BF16 = jnp.bfloat16
F32 = jnp.float32
MESH = pl.DeviceIdType.MESH


def lower(values):
    return values.astype(BF16)


def dot(left, right):
    return lax.dot_general(left, right, (((1,), (0,)), ((), ())), preferred_element_type=F32)


def dot_bt(left, right):
    return lax.dot_general(left, right, (((1,), (1,)), ((), ())), preferred_element_type=F32)


def dot_at(left, right):
    return lax.dot_general(left, right, (((0,), (0,)), ((), ())), preferred_element_type=F32)


def standardise(values):
    centred = values - jnp.mean(values, -1, keepdims=True)
    inverse = lax.rsqrt(jnp.mean(centred * centred, -1, keepdims=True) + 1e-05)
    return centred * inverse, inverse


def norm_back(xhat, inverse, gain, incoming):
    dz = incoming * gain
    inner = jnp.mean(dz * xhat, -1, keepdims=True)
    return (dz - jnp.mean(dz, -1, keepdims=True) - xhat * inner) * inverse


def fold_rows(values):
    rows, width = values.shape
    return jnp.sum(values.reshape(rows // 8, 8, width), axis=0)


def segment_bounds(ids):
    order = jnp.where(ids < 0, SEGMENTS - 1, ids).reshape(1, -1)
    level = lax.broadcasted_iota(jnp.int32, (8, 1), 0)
    return jnp.sum((order < level).astype(jnp.int32), axis=1)


def lane_index(rows):
    return lax.broadcasted_iota(jnp.int32, (rows, 128), 1)


def row_index(rows):
    return lax.broadcasted_iota(jnp.int32, (rows, 128), 0)


def stack_heads(pair, first):
    zero = jnp.zeros_like(pair)
    return jnp.concatenate([jnp.where(first, pair, zero), jnp.where(first, zero, pair)], axis=0)


def tiles_of(low, high, length, visit):
    base = (low // 16) * 16
    span = high - base
    whole_tiles = (span + TILE - 1 - SMALL) // TILE
    rest = span - whole_tiles * TILE

    def per_tile(i, carry):
        begin = base + i * TILE
        visit(TILE, pl.multiple_of(jnp.minimum(begin, length - TILE), 16), jnp.maximum(low, begin))
        return carry

    lax.fori_loop(0, whole_tiles, per_tile, 0)

    @pl.when(rest > 0)
    def _():
        begin = base + whole_tiles * TILE
        visit(SMALL, pl.multiple_of(jnp.minimum(begin, length - SMALL), 16), jnp.maximum(low, begin))


def each_segment(bounds, q_row, k_row, visit):
    def per_segment(s, carry):
        visit(bounds[q_row, s], bounds[q_row, s + 1], bounds[k_row, s], bounds[k_row, s + 1])
        return carry

    lax.fori_loop(0, SEGMENTS, per_segment, 0)


def inside_rows(size, start, low, high):
    rows = row_index(size) + start
    return (rows >= low) & (rows < high)


def attend(bounds, q_row, k_row, query, keys, values, out_ref, tail_ref):
    (q_ref, q_col), (k_ref, k_col), (v_ref, v_col) = query, keys, values
    length, width = out_ref.shape
    pairs = range(width // 128)

    def visit(size, start, low, high, k_low, k_high):
        lanes = lane_index(size)
        first = lanes < HEAD_DIM
        owner, place = lanes // 4, lanes % 4
        unit = jnp.where(lane_index(2 * size) == 0, 1.0, 0.0).astype(BF16)
        keep = inside_rows(size, start, low, high)
        span = pl.ds(start, size)
        k_base = (k_low // 16) * 16
        k_tiles = (k_high - k_base + TILE - 1) // TILE

        def piece(p, k_size, k_start, low_k):
            cols = p * 128
            inside = inside_rows(k_size, k_start, low_k, k_high)
            shut = (lane_index(k_size) == 0) & jnp.logical_not(inside)
            bias = jnp.where(shut, MASKED, 0.0).astype(BF16)
            queries = stack_heads(q_ref[span, q_col + cols : q_col + cols + 128], first)
            k_span = pl.ds(k_start, k_size)
            pair_k = k_ref[k_span, k_col + cols : k_col + cols + 128]
            pair_v = v_ref[k_span, v_col + cols : v_col + cols + 128]
            scores = dot_bt(
                jnp.concatenate([queries, unit], axis=1), jnp.concatenate([pair_k, bias], axis=1)
            )
            ones = jnp.ones((k_size, 128), BF16)
            return scores, jnp.concatenate([pair_v, ones], axis=1)

        def finish(p, highest, total, stats):
            cols = p * 128
            top, bottom = total[:size], total[size:]
            mass = jnp.where(first, top[:, 128:], bottom[:, 128:])
            merged = lower(jnp.where(first, top[:, :128], bottom[:, :128]) / mass)
            out_ref[span, cols : cols + 128] = jnp.where(
                keep, merged, out_ref[span, cols : cols + 128]
            )
            peak, sums = stats
            for h, half in ((0, slice(0, size)), (1, slice(size, 2 * size))):
                here = owner == 2 * p + h
                peak = jnp.where(here, highest[half], peak)
                sums = jnp.where(here, total[half, 128:], sums)
            return peak, sums

        def close(results):
            stats = (jnp.zeros((size, 128), F32), jnp.ones((size, 128), F32))
            for p, (highest, total) in enumerate(results):
                stats = finish(p, highest, total, stats)
            peak, sums = stats
            tail = split_lanes(peak + jnp.log(sums), place, 1.0)
            tail_ref[span, :] = jnp.where(keep, tail, tail_ref[span, :])

        def direct(k_size):
            k_start = pl.multiple_of(jnp.minimum(k_base, length - k_size), 16)
            items = [piece(p, k_size, k_start, k_low) for p in pairs]
            tops = [jnp.max(item[0], -1, keepdims=True) for item in items]
            probs = [lower(jnp.exp(item[0] - top)) for item, top in zip(items, tops)]
            close([(top, dot(prob, item[1])) for top, prob, item in zip(tops, probs, items)])

        @pl.when(k_tiles == 1)
        def _():
            direct(TILE)

        @pl.when(k_tiles == 2)
        def _():
            direct(2 * TILE)

        @pl.when(k_tiles > 2)
        def _():
            results = []
            for p in pairs:

                def per_key(j, carry, p=p):
                    highest, total = carry
                    begin = k_base + j * TILE
                    k_start = pl.multiple_of(jnp.minimum(begin, length - TILE), 16)
                    scores, wide_v = piece(p, TILE, k_start, jnp.maximum(k_low, begin))
                    newest = jnp.maximum(highest, jnp.max(scores, -1, keepdims=True))
                    expon = lower(jnp.exp(scores - newest))
                    return newest, total * jnp.exp(highest - newest) + dot(expon, wide_v)

                empty = (jnp.full((2 * size, 1), MASKED, F32), jnp.zeros((2 * size, 256), F32))
                results.append(lax.fori_loop(0, k_tiles, per_key, empty))
            close(results)

    def segment(q_low, q_high, k_low, k_high):
        tiles_of(
            q_low, q_high, length, lambda size, start, low: visit(size, start, low, q_high, k_low, k_high)
        )

    each_segment(bounds, q_row, k_row, segment)


def split_lanes(values, place, lead):
    high = lower(values).astype(F32)
    rest = values - high
    middle = lower(rest).astype(F32)
    spread = jnp.where(place == 1, high, jnp.where(place == 2, middle, rest - middle))
    return lower(jnp.where(place == 0, lead, -spread))


def attend_back(bounds, q_row, k_row, query, keys, values, do_ref, out_ref, tail_ref, dq, dk, dv):
    (q_ref, q_col), (k_ref, k_col), (v_ref, v_col) = query, keys, values
    (dq_ref, dq_col), (dk_ref, dk_col), (dv_ref, dv_col) = dq, dk, dv
    length, width = do_ref.shape
    pairs = width // 128
    zero = jnp.zeros((), BF16)
    lane = lane_index(width)
    collect = (lane % 4 > 0) & (lane // 4 == row_index(width) // HEAD_DIM)
    collect = jnp.where(collect, 1.0, 0.0).astype(BF16)

    def visit(size, start, low, high, k_low, k_high):
        lanes = lane_index(size)
        first = lanes < HEAD_DIM
        owner, place = lanes // 4, lanes % 4
        closed = lower(jnp.where(place == 0, 1.0, jnp.where(place == 1, MASKED, 0.0)))
        keep = inside_rows(size, start, low, high)
        span = pl.ds(start, size)
        tail_q = jnp.where(keep, tail_ref[span, :], closed)
        centre = jnp.zeros((size, 128), F32)
        for p in range(pairs):
            cols = slice(p * 128, (p + 1) * 128)
            grad = jnp.where(keep, do_ref[span, cols], zero)
            inner = grad.astype(F32) * out_ref[span, cols].astype(F32)
            coarse = lower(inner)
            fine = lower(inner - coarse.astype(F32))
            centre = centre + dot(
                jnp.concatenate([coarse, fine], axis=1),
                jnp.concatenate([collect[cols], collect[cols]], axis=0),
            )
        tail_g = split_lanes(centre, place, 0.0)

        def per_key(k_size, k_start, low_k):
            k_span = pl.ds(k_start, k_size)
            inside = inside_rows(k_size, k_start, low_k, k_high)
            lead = lane_index(k_size) % 4 == 0
            tail = lower(jnp.where(lead, jnp.where(inside, 0.0, MASKED), 1.0))

            def load(p):
                cols = p * 128
                pair_q = q_ref[span, q_col + cols : q_col + cols + 128]
                pair_k = k_ref[k_span, k_col + cols : k_col + cols + 128]
                pair_v = v_ref[k_span, v_col + cols : v_col + cols + 128]
                pair_do = jnp.where(keep, do_ref[span, cols : cols + 128], zero)
                queries = stack_heads(pair_q, first)
                grads = stack_heads(pair_do, first)
                ends = [
                    jnp.concatenate(
                        [jnp.where(owner == 2 * p, item, zero), jnp.where(owner == 2 * p + 1, item, zero)],
                        axis=0,
                    )
                    for item in (tail_q, tail_g)
                ]
                scores = dot_bt(
                    jnp.concatenate([pair_k, tail], axis=1),
                    jnp.concatenate([queries, ends[0]], axis=1),
                )
                slope = dot_bt(
                    jnp.concatenate([pair_v, tail], axis=1),
                    jnp.concatenate([grads, ends[1]], axis=1),
                )
                return pair_k, queries, grads, scores, slope

            def middle(item):
                pair_k, queries, grads, scores, slope = item
                probs = jnp.exp(scores)
                return pair_k, queries, grads, lower(probs), lower(probs * slope)

            def store(p, pair_k, queries, grads, probs, ds):
                cols = p * 128
                dv_ref[k_span, dv_col + cols : dv_col + cols + 128] += dot(probs, grads)
                dk_ref[k_span, dk_col + cols : dk_col + cols + 128] += dot(ds, queries)
                turned = [dot_at(ds[:, :size], pair_k), dot_at(ds[:, size:], pair_k)]
                dq_ref[span, dq_col + cols : dq_col + cols + 128] += jnp.where(first, turned[0], turned[1])

            ahead = load(0)
            for p in range(pairs):
                item = ahead
                if p + 1 < pairs:
                    ahead = load(p + 1)
                store(p, *middle(item))

        tiles_of(k_low, k_high, length, per_key)

    def segment(q_low, q_high, k_low, k_high):
        tiles_of(
            q_low, q_high, length, lambda size, start, low: visit(size, start, low, q_high, k_low, k_high)
        )

    each_segment(bounds, q_row, k_row, segment)


def forward_kernel(
    bounds, xs, qkv, kv, norms, w_self, w_query, a1, y1, q2, a2, stat1, stat2
):
    length, width = a1.shape[1:]
    attend(
        bounds,
        0,
        0,
        (qkv.at[0], 0),
        (qkv.at[0], width),
        (qkv.at[0], 2 * width),
        a1.at[0],
        stat1.at[0],
    )

    def rows(i):
        span = slice(i * TILE, (i + 1) * TILE)
        after = xs[0, span, :].astype(F32) + dot(a1[0, span, :], w_self[...])
        y1[0, span, :] = after
        xhat, _ = standardise(after)
        h2 = lower(xhat * norms[1:2, :] + norms[4:5, :])
        q2[0, span, :] = lower(dot(h2, w_query[...]) * HEAD_DIM ** (-0.5))

    for i in range(length // TILE):
        rows(i)
    attend(bounds, 0, 1, (q2.at[0], 0), (kv, 0), (kv, width), a2.at[0], stat2.at[0])


def feed_kernel(
    per_step, y1, a2, g1, g2, norms, w_cross, w_in, w_out,
    o1, o2, h3, r, du, e2, dy2, do2, dnorm,
):
    i = pl.program_id(0)
    width = w_cross.shape[0]
    is_first = i < per_step
    grad = jnp.where(is_first, g1[...], g2[...])
    after = y1[0] + dot(a2[0], w_cross[...])
    xhat, inverse = standardise(after)
    normed = lower(xhat * norms[2:3, :] + norms[5:6, :])
    h3[0] = normed
    result = after
    dh3 = jnp.zeros_like(after)
    slope = (2.0 / jnp.pi) ** 0.5
    for c in range(w_in.shape[1] // width):
        cols = slice(c * width, (c + 1) * width)
        u = dot(normed, w_in[:, cols])
        dr = dot_bt(grad, w_out[cols, :])
        square = u * u
        t = jnp.tanh(slope * (u + 0.044715 * (square * u)))
        half = 0.5 * (1.0 + t)
        hidden = lower(u * half)
        r[0, :, cols] = hidden
        gate = half + 0.5 * u * (1.0 - t * t) * (slope * (1.0 + 3 * 0.044715 * square))
        pre = lower(dr * gate)
        du[0, :, cols] = pre
        result = result + dot(hidden, w_out[cols, :])
        dh3 = dh3 + dot_bt(pre, w_in[:, cols])

    @pl.when(is_first)
    def _():
        o1[...] = lower(result)

    @pl.when(jnp.logical_not(is_first))
    def _():
        o2[...] = lower(result)

    @pl.when(i == 0)
    def _():
        dnorm[...] = jnp.zeros_like(dnorm)

    dnorm[0] += fold_rows(dh3 * xhat)
    dnorm[1] += fold_rows(dh3)
    back = grad.astype(F32) + norm_back(xhat, inverse, norms[2:3, :], dh3)
    dy2[0] = back
    low = lower(back)
    e2[0] = low
    do2[0] = lower(dot_bt(low, w_cross[...]))


def feed_grad_kernel(small, h3, a2, e2, g1, g2, du, r, joint, turned, d_in, d_out, d_cross, sem):
    c = pl.program_id(0)
    last = pl.num_programs(0) - 1
    half, width = g1.shape
    hidden = d_out.shape[2]
    group = hidden // width
    rows = width // group
    slot = lax.rem(c, 2)

    def copies(at, chunk):
        return (
            pltpu.make_async_copy(
                d_in.at[at], joint.at[:, pl.ds(pl.multiple_of(chunk * width, width), width)], sem.at[0, at]
            ),
            pltpu.make_async_copy(
                d_out.at[at],
                joint.at[pl.ds(pl.multiple_of(chunk * rows, rows), rows), hidden + width :],
                sem.at[1, at],
            ),
        )

    cross = pltpu.make_async_copy(d_cross, joint.at[:, hidden : hidden + width], sem.at[2, 0])

    @pl.when(c >= 2)
    def _():
        for copy in copies(slot, c - 2):
            copy.wait()

    @pl.when(c == 0)
    def _():
        turned[...] = h3[...].T
        d_cross[...] = lower(dot(a2[...].T, e2[...]))
        cross.start()

    d_in[slot] = lower(dot(turned[...], du[...]))
    part = lower(dot_at(r[:half, :], g1[...]) + dot_at(r[half:, :], g2[...]))
    for w in range(width // (group * small)):
        for j in range(group):
            at = (w * group + j) * small
            d_out[slot, w * small : (w + 1) * small, j * width : (j + 1) * width] = part[at : at + small]
    for copy in copies(slot, c):
        copy.start()

    @pl.when(c == last)
    def _():
        for copy in copies(1 - slot, c - 1) + copies(slot, c):
            copy.wait()
        cross.wait()


def cross_back_kernel(
    bounds, q2, kv, a1, a2, stat2, do2, y1, dy2, mem_turned, norms, w_query, w_self, w_kv,
    dy1, do1, d_query, d_self, d_kv, d_mem, dnorm,
    dq_sum, dkv_sum, h2, low_q, low_e,
):
    step = pl.program_id(0)
    length, width = q2.shape[1:]

    @pl.when(step == 0)
    def _():
        dkv_sum[...] = jnp.zeros_like(dkv_sum)
        dnorm[...] = jnp.zeros_like(dnorm)

    dq_sum[...] = jnp.zeros_like(dq_sum)
    attend_back(
        bounds, 0, 1, (q2.at[0], 0), (kv, 0), (kv, width), do2.at[0], a2.at[0], stat2.at[0],
        (dq_sum, 0), (dkv_sum, 0), (dkv_sum, width),
    )

    def rows(i):
        span = slice(i * TILE, (i + 1) * TILE)
        grad_q = lower(dq_sum[span, :] * HEAD_DIM ** (-0.5))
        low_q[step, span, :] = grad_q
        xhat, inverse = standardise(y1[0, span, :])
        h2[step, span, :] = lower(xhat * norms[1:2, :] + norms[4:5, :])
        dh2 = dot_bt(grad_q, w_query[...])
        dnorm[0] += fold_rows(dh2 * xhat)
        dnorm[1] += fold_rows(dh2)
        back = dy2[0, span, :] + norm_back(xhat, inverse, norms[1:2, :], dh2)
        dy1[0, span, :] = back
        low = lower(back)
        low_e[step, span, :] = low
        do1[0, span, :] = lower(dot_bt(low, w_self[...]))

    for i in range(length // TILE):
        rows(i)

    @pl.when(step == 1)
    def _():
        d_query[...] = lower(dot(h2[0].T, low_q[0]) + dot(h2[1].T, low_q[1]))
        d_self[...] = lower(dot(a1[0].T, low_e[0]) + dot(a1[1].T, low_e[1]))
        pair = lower(dkv_sum[...])
        d_kv[...] = lower(dot(mem_turned[...], pair))
        d_mem[...] = dot_bt(pair, w_kv[...])


def self_back_kernel(bounds, qkv, a1, stat1, do1, low, sums):
    width = do1.shape[2]
    sums[...] = jnp.zeros_like(sums)
    attend_back(
        bounds, 0, 0, (qkv.at[0], 0), (qkv.at[0], width), (qkv.at[0], 2 * width),
        do1.at[0], a1.at[0], stat1.at[0], (sums, 0), (sums, width), (sums, 2 * width),
    )
    low[0, :, :width] = lower(sums[:, :width] * HEAD_DIM ** (-0.5))
    low[0, :, width:] = lower(sums[:, width:])


def flip(index, mask):
    out, bit = index, 1
    while bit <= mask:
        if mask & bit:
            out = out + bit - 2 * bit * lax.rem(lax.div(index, bit), 2)
        bit *= 2
    return out


class Links:
    def __init__(self, sizes, send, recv):
        self.members, wides = sizes
        self.lines = wides // 2
        self.group = min(4, self.members)
        self.narrow, self.wide = lax.axis_index("narrow"), lax.axis_index("wide")
        self.line, self.core = lax.div(self.wide, 2), lax.rem(self.wide, 2)
        self.part = lax.rem(self.narrow, self.group)
        self.send, self.recv, self.used = send, recv, 0

    def core_peer(self):
        return (self.narrow, flip(self.wide, 1))

    def plane_peer(self, mask):
        return (flip(self.narrow, mask), self.wide)

    def line_peer(self, mask):
        return (self.narrow, 2 * flip(self.line, mask) + self.core)

    def far_masks(self):
        masks, mask = [], self.group
        while mask < self.members:
            masks.append(mask)
            mask *= 2
        return masks

    def barrier(self, far):
        semaphore = pltpu.get_barrier_semaphore()
        peers = [self.core_peer()]
        peers += [self.plane_peer(m) for m in range(1, self.group)]
        peers += [self.line_peer(m) for m in range(1, self.lines)]
        if far:
            peers += [self.plane_peer(m) for m in self.far_masks()]
        for peer in peers:
            pl.semaphore_signal(semaphore, inc=1, device_id=peer, device_id_type=MESH)
        pl.semaphore_wait(semaphore, len(peers))

    def push(self, src, dst, peer):
        slot = self.used
        self.used += 1
        copy = pltpu.make_async_remote_copy(
            src_ref=src,
            dst_ref=dst,
            send_sem=self.send.at[slot],
            recv_sem=self.recv.at[slot],
            device_id=peer,
            device_id_type=MESH,
        )
        copy.start()
        return copy

    def quarter(self, part, cols):
        size = cols // self.group
        return pl.ds(pl.multiple_of(part * size, size), size)


def wait_all(copies):
    for copy in copies:
        copy.wait()


class Gathered:
    def __init__(self, links, shard, full, local_sem):
        self.links, self.shard, self.full = links, shard, full
        self.cols = shard.shape[-1]
        self.local = pltpu.make_async_copy(shard, full.at[links.line, links.core], local_sem)

    def start_line(self):
        links = self.links
        self.local.start()
        mine = links.quarter(links.part, self.cols)
        self.copies = [
            links.push(
                self.shard.at[:, mine], self.full.at[links.line, links.core, :, mine], links.line_peer(m)
            )
            for m in range(1, links.lines)
        ]

    def start_plane(self):
        links = self.links
        wait_all(self.copies)
        mine = links.quarter(links.part, self.cols)
        self.copies = []
        for k in range(1, links.lines):
            place = self.full.at[flip(links.line, k), links.core, :, mine]
            for m in range(1, links.group):
                self.copies.append(links.push(place, place, links.plane_peer(m)))

    def start_core(self):
        links = self.links
        wait_all(self.copies)
        self.local.wait()
        place = self.full.at[:, links.core]
        self.copies = [links.push(place, place, links.core_peer())]

    def finish(self):
        wait_all(self.copies)


def gather_slots(sizes, pieces):
    lines, group = sizes[1] // 2, min(4, sizes[0])
    return pieces * (lines - 1 + (lines - 1) * (group - 1) + 1) + lines


def gather_kernel(
    sizes, x1, x2, mem, norm, s_qkv, s_kv, s_self, s_query, s_cross, s_in,
    xs, qkv, kv, norms, h1_turned, mem_turned, f_qkv, f_kv, f_self, f_query, f_cross, f_in,
    h1, turned, turned_mem, v_qkv, v_kv, o_qkv, o_kv, norm_all, send, recv, local,
):
    links = Links(sizes, send, recv)
    length, width = x1.shape
    used = [0]

    def local_copy(src, dst):
        copy = pltpu.make_async_copy(src, dst, local.at[used[0]])
        used[0] += 1
        copy.start()
        return copy

    def slot():
        used[0] += 1
        return local.at[used[0] - 1]

    def piece(shard, full):
        return Gathered(links, shard, full, slot())

    links.barrier(False)
    pieces = []
    for c in range(3):
        cols = slice(c * width, (c + 1) * width)
        pieces.append(piece(s_qkv.at[:, cols], v_qkv.at[c]))
    for c in range(2):
        cols = slice(c * width, (c + 1) * width)
        pieces.append(piece(s_kv.at[:, cols], v_kv.at[c]))
    pieces.append(piece(s_self, f_self))
    pieces.append(piece(s_query, f_query))
    pieces.append(piece(s_cross, f_cross))
    half = s_in.shape[1] // 2
    for c in range(2):
        cols = slice(c * half, (c + 1) * half)
        pieces.append(piece(s_in.at[:, cols], f_in.at[:, :, :, cols]))

    norm_all[links.line, links.core] = norm[...]
    own = norm_all.at[links.line, links.core]
    norm_copies = [links.push(own, own, links.line_peer(m)) for m in range(1, links.lines)]
    for p in range(2):
        pieces[p].start_line()
    outgoing = [local_copy(x1, xs.at[0]), local_copy(x2, xs.at[1])]
    pieces[2].start_line()
    wait_all(norm_copies)
    place = norm_all.at[:, links.core]
    norm_copy = links.push(place, place, links.core_peer())
    pieces[0].start_plane()
    norm_copy.wait()
    every = norm_all[...]
    total = every[0, 0]
    for k in range(1, 2 * links.lines):
        total = total + every[k // 2, k % 2]
    norms[...] = total
    gain, shift = total[0:1, :], total[3:4, :]

    def normalise(t, x):
        for i in range(length // TILE):
            span = slice(i * TILE, (i + 1) * TILE)
            xhat, _ = standardise(x[span, :].astype(F32))
            h1[t, span, :] = lower(xhat * gain + shift)

    def turn():
        turned[:, :length] = h1[0].T
        turned[:, length:] = h1[1].T
        turned_mem[...] = mem[...].T
        outgoing.append(local_copy(turned, h1_turned))
        outgoing.append(local_copy(turned_mem, mem_turned))

    def project(c):
        def run():
            weight = v_qkv[c].reshape(width, width)
            scale = HEAD_DIM ** (-0.5) if c == 0 else 1.0
            for t in range(2):

                def rows(i, carry, t=t):
                    span = pl.ds(pl.multiple_of(i * 2 * TILE, 2 * TILE), 2 * TILE)
                    o_qkv[c, t, span, :] = lower(dot(h1[t, span, :], weight) * scale)
                    return carry

                lax.fori_loop(0, length // (2 * TILE), rows, 0)
            cols = slice(c * width, (c + 1) * width)
            outgoing.append(local_copy(o_qkv.at[c], qkv.at[:, :, cols]))
            outgoing.append(local_copy(v_qkv.at[c], f_qkv.at[:, :, :, cols]))

        return run

    def project_memory(c):
        def run():
            weight = v_kv[c].reshape(width, width)

            def rows(i, carry):
                span = pl.ds(pl.multiple_of(i * 2 * TILE, 2 * TILE), 2 * TILE)
                o_kv[c, span, :] = lower(dot(mem[span, :], weight))
                return carry

            lax.fori_loop(0, length // (2 * TILE), rows, 0)
            cols = slice(c * width, (c + 1) * width)
            outgoing.append(local_copy(o_kv.at[c], kv.at[:, cols]))
            outgoing.append(local_copy(v_kv.at[c], f_kv.at[:, :, :, cols]))

        return run

    work = {c: project(c) for c in range(3)} | {3 + c: project_memory(c) for c in range(2)}
    count = len(pieces)
    for t in range(3, count + 6):
        if t < count:
            pieces[t].start_line()
        if 1 <= t - 2 < count:
            pieces[t - 2].start_plane()
        if t == 3:
            normalise(0, x1)
        if t == 4:
            normalise(1, x2)
        if 0 <= t - 4 < count:
            pieces[t - 4].start_core()
        if 0 <= t - 5 < count:
            pieces[t - 5].finish()
            if t - 5 in work:
                work[t - 5]()
            if t - 5 == 5:
                turn()
    wait_all(outgoing)


class Reduced:
    def __init__(self, links, bufs, out, source=None, shard=None):
        self.links, self.out, self.source, self.shard = links, out, source, shard
        self.crecv, self.chip, self.precv, self.plane, self.lrecv, self.mine, self.xrecv, self.full = bufs
        self.cols = self.full.shape[-1]

    def start_core(self):
        links = self.links
        self.copies = [links.push(self.source.at[:, 1 - links.core], self.crecv, links.core_peer())]

    def start_plane(self):
        links = self.links
        if self.source is not None:
            wait_all(self.copies)
            for k in range(links.lines):
                self.chip[k] = lower(
                    self.source[k, links.core].astype(F32) + self.crecv[k].astype(F32)
                )
        self.copies = [
            links.push(
                self.chip.at[:, :, links.quarter(flip(links.part, m), self.cols)],
                self.precv.at[m - 1],
                links.plane_peer(m),
            )
            for m in range(1, links.group)
        ]

    def start_line(self):
        links = self.links
        wait_all(self.copies)
        total = self.chip[:, :, links.quarter(links.part, self.cols)].astype(F32)
        for m in range(1, links.group):
            total = total + self.precv[m - 1].astype(F32)
        self.plane[...] = lower(total)
        if self.source is None:
            self.copies = []
            return
        self.copies = [
            links.push(self.plane.at[flip(links.line, m)], self.lrecv.at[m - 1], links.line_peer(m))
            for m in range(1, links.lines)
        ]

    def start_gather(self):
        links = self.links
        wait_all(self.copies)
        if self.source is None:
            total = self.plane[0].astype(F32)
        else:
            total = self.plane[links.line].astype(F32)
            for m in range(1, links.lines):
                total = total + self.lrecv[m - 1].astype(F32)
        for i, mask in enumerate(links.far_masks()):
            self.xrecv[2 * i] = lower(total)
            links.push(self.xrecv.at[2 * i], self.xrecv.at[2 * i + 1], links.plane_peer(mask)).wait()
            total = self.xrecv[2 * i].astype(F32) + self.xrecv[2 * i + 1].astype(F32)
        self.mine[...] = lower(total)
        place = self.full.at[:, links.quarter(links.part, self.cols)]
        place[...] = self.mine[...]
        self.copies = [links.push(self.mine, place, links.plane_peer(m)) for m in range(1, links.group)]

    def finish(self):
        wait_all(self.copies)
        self.out[...] = self.full[...]


def reduced_scratch(sizes, rows, cols, wide_too):
    members, wides = sizes
    lines, group = wides // 2, min(4, members)
    part = cols // group
    depth = lines if wide_too else 1
    far = max(2, 2 * (members // group - 1))
    small = (1, 16, 128)
    return [
        pltpu.VMEM((lines, rows, cols) if wide_too else small, BF16),
        pltpu.VMEM((depth, rows, cols), BF16),
        pltpu.VMEM((group - 1, depth, rows, part), BF16),
        pltpu.VMEM((depth, rows, part), BF16),
        pltpu.VMEM((lines - 1, rows, part) if wide_too else small, BF16),
        pltpu.VMEM((rows, part), BF16),
        pltpu.VMEM((far, rows, part), BF16),
        pltpu.VMEM((rows, cols), BF16),
    ]


def reduce_slots(sizes, jobs):
    members, wides = sizes
    lines, group = wides // 2, min(4, members)
    return (jobs + 1) * (1 + 2 * (group - 1) + lines - 1 + members // group)


BUFS = 8


def finish_kernel(
    sizes, low_hbm, h1_hbm, xs_hbm, dy1_hbm, norms, w_qkv, d_self, d_query, d_kv, share, dnorm1, dnorm2,
    gi1, gi2, t_qkv, t_self, t_query, t_kv, t_in, t_out, t_cross, t_norm,
    low, xs, dy1, h1, grads, norm_slots, *rest,
):
    send, recv, local = rest[-3:]
    bufs = rest[:-3]
    links = Links(sizes, send, recv)
    _, length, width = xs.shape
    loads = [
        pltpu.make_async_copy(h1_hbm, h1, local.at[0]),
        pltpu.make_async_copy(low_hbm, low, local.at[1]),
        pltpu.make_async_copy(xs_hbm, xs, local.at[2]),
        pltpu.make_async_copy(dy1_hbm, dy1, local.at[3]),
    ]
    for copy in loads:
        copy.start()
    links.barrier(True)

    taken = [0]

    def job(out, **kind):
        at = taken[0] * BUFS
        taken[0] += 1
        return Reduced(links, bufs[at : at + BUFS], out, **kind)

    others = [
        job(t_kv, source=d_kv), job(t_self, source=d_self), job(t_query, source=d_query),
    ]
    heads = [job(t_qkv.at[:, c * width : (c + 1) * width], source=grads.at[c]) for c in range(3)]
    hidden = t_in.shape[1]
    shards = [
        job(t_in, shard=share.at[:, :hidden]),
        job(t_out, shard=share.at[:, hidden + width :]),
        job(t_cross, shard=share.at[:, hidden : hidden + width]),
    ]
    for one in others:
        one.start_core()
    gain = norms[0:1, :]
    loads[0].wait()
    loads[1].wait()
    for c in range(3):
        cols = slice(c * width, (c + 1) * width)
        value = dot(h1[:, :length], low[0, :, cols]) + dot(h1[:, length:], low[1, :, cols])
        grads[c] = lower(value).reshape(grads.shape[1:])
        heads[c].start_core()
        if c > 0:
            heads[c - 1].start_plane()
        if c == 0:
            for one in others:
                one.start_plane()
    heads[2].start_plane()
    for one in shards:
        one.chip[0] = one.shard[...]
        one.start_plane()
    loads[2].wait()
    loads[3].wait()
    stores = []
    dgain = jnp.zeros((8, width), F32)
    dshift = jnp.zeros((8, width), F32)
    steps = [
        lambda: [one.start_line() for one in others],
        lambda: heads[0].start_line(),
        lambda: heads[1].start_line(),
        lambda: heads[2].start_line(),
        lambda: [one.start_gather() for one in others],
        lambda: [one.start_line() for one in shards],
        lambda: [one.start_gather() for one in shards],
        lambda: [one.finish() for one in others],
    ]
    weight = w_qkv[...]
    for t in range(2):
        for i in range(length // TILE):
            span = slice(i * TILE, (i + 1) * TILE)
            xhat, inverse = standardise(xs[t, span, :].astype(F32))
            dh1 = dot_bt(low[t, span, :], weight)
            dgain = dgain + fold_rows(dh1 * xhat)
            dshift = dshift + fold_rows(dh1)
            dy1[t, span, :] = dy1[t, span, :] + norm_back(xhat, inverse, gain, dh1)
            out = (gi1, gi2)[t]
            number = t * (length // TILE) + i
            copy = pltpu.make_async_copy(dy1.at[t, span, :], out.at[span, :], local.at[4 + number])
            copy.start()
            stores.append(copy)
            if number < len(steps):
                steps[number]()
    rows = [jnp.sum(item, axis=0, keepdims=True) for item in (dgain, dnorm1[0], dnorm2[0], dshift, dnorm1[1], dnorm2[1])]
    total = jnp.concatenate(rows + [jnp.zeros((2, width), F32)], axis=0)

    def swap(first, count, own, peers, total):
        norm_slots[first + own] = total
        place = norm_slots.at[first + own]
        wait_all([links.push(place, place, peer) for peer in peers])
        out = norm_slots[first]
        for k in range(1, count):
            out = out + norm_slots[first + k]
        return out

    total = swap(0, 2, links.core, [links.core_peer()], total)
    for one in heads:
        one.start_gather()
    total = swap(2, links.group, links.part, [links.plane_peer(m) for m in range(1, links.group)], total)
    first = 2 + links.group
    total = swap(first, links.lines, links.line, [links.line_peer(m) for m in range(1, links.lines)], total)
    first += links.lines
    for mask in links.far_masks():
        side = lax.rem(lax.div(links.narrow, mask), 2)
        total = swap(first, 2, side, [links.plane_peer(mask)], total)
        first += 2
    t_norm[...] = total
    for one in shards + heads:
        one.finish()
    wait_all(stores)


def emit_kernel(
    wides, f1, f2, b_qkv, b_self, b_query, b_kv, b_in, b_out, b_cross, t_norm,
    gi1, gi2, gain, shift, t_qkv, t_self, t_query, t_kv, t_in, t_out, t_cross,
):
    gi1[...] = f1[...]
    gi2[...] = f2[...]
    width = gi1.shape[1]
    small = b_out.shape[0]

    @pl.when(pl.program_id(0) == 0)
    def _():
        for src, dst in (
            (b_qkv, t_qkv), (b_self, t_self), (b_query, t_query), (b_kv, t_kv), (b_in, t_in), (b_cross, t_cross),
        ):
            dst[...] = src[...].astype(F32)
        for j in range(b_out.shape[1] // width):
            t_out[j * small : (j + 1) * small, :] = b_out[:, j * width : (j + 1) * width].astype(F32)
        at = lax.axis_index("wide") * small
        mine = pltpu.roll(t_norm[...], lax.rem(width - at, width), 1)
        gain[...] = mine[:3, :small]
        shift[...] = mine[3:6, :small]


def whole(shape):
    zeros = (0,) * len(shape)
    return pl.BlockSpec(shape, lambda *_: zeros, pipeline_mode=pl.Buffered(1))


def fixed(shape):
    zeros = (0,) * len(shape)
    return pl.BlockSpec(shape, lambda *_: zeros)


def by_step(shape):
    return pl.BlockSpec((1,) + shape, lambda t, *_: (t, 0, 0))


def params():
    return pltpu.CompilerParams(
        vmem_limit_bytes=VMEM_LIMIT, dimension_semantics=("arbitrary",)
    )


def struct(shape, dtype):
    return jax.ShapeDtypeStruct(shape, dtype)


def call_forward(bounds, xs, qkv, kv, norms, w_self, w_query):
    length, width = xs.shape[1:]
    norm_spec = whole((8, width))
    step_low = by_step((length, width))
    return pl.pallas_call(
        forward_kernel,
        grid_spec=pltpu.PrefetchScalarGridSpec(
            num_scalar_prefetch=1,
            grid=(2,),
            in_specs=[
                step_low, by_step((length, 3 * width)), whole(kv.shape), norm_spec,
                whole(w_self.shape), whole(w_query.shape),
            ],
            out_specs=[step_low] * 4 + [by_step((length, 128))] * 2,
        ),
        out_shape=[
            struct((2, length, width), BF16),
            struct((2, length, width), F32),
            struct((2, length, width), BF16),
            struct((2, length, width), BF16),
            struct((2, length, 128), BF16),
            struct((2, length, 128), BF16),
        ],
        compiler_params=params(),
        name="attend_forward",
    )(bounds, xs, qkv, kv, norms, w_self, w_query)


def call_cross_back(bounds, q2, kv, a1, a2, stat2, do2, y1, dy2, mem_turned, norms, w_query, w_self, w_kv):
    length, width = q2.shape[1:]
    norm_spec = whole((8, width))
    step_low = by_step((length, width))
    return pl.pallas_call(
        cross_back_kernel,
        grid_spec=pltpu.PrefetchScalarGridSpec(
            num_scalar_prefetch=1,
            grid=(2,),
            in_specs=[
                step_low, whole(kv.shape), whole(a1.shape), step_low, by_step((length, 128)), step_low,
                step_low, step_low, whole(mem_turned.shape), norm_spec,
                whole(w_query.shape), whole(w_self.shape), whole(w_kv.shape),
            ],
            out_specs=[
                step_low, step_low, fixed((width, width)), fixed((width, width)), fixed((width, 2 * width)),
                fixed((length, width)), fixed((2, 8, width)),
            ],
            scratch_shapes=[
                pltpu.VMEM((length, width), F32),
                pltpu.VMEM((length, 2 * width), F32),
                pltpu.VMEM((2, length, width), BF16),
                pltpu.VMEM((2, length, width), BF16),
                pltpu.VMEM((2, length, width), BF16),
            ],
        ),
        out_shape=[
            struct((2, length, width), F32),
            struct((2, length, width), BF16),
            struct((width, width), BF16),
            struct((width, width), BF16),
            struct((width, 2 * width), BF16),
            struct((length, width), F32),
            struct((2, 8, width), F32),
        ],
        compiler_params=params(),
        name="cross_back",
    )(bounds, q2, kv, a1, a2, stat2, do2, y1, dy2, mem_turned, norms, w_query, w_self, w_kv)


def call_self_back(bounds, qkv, a1, stat1, do1):
    length, width = do1.shape[1:]
    norm_spec = whole((8, width))
    step_low = by_step((length, width))
    return pl.pallas_call(
        self_back_kernel,
        grid_spec=pltpu.PrefetchScalarGridSpec(
            num_scalar_prefetch=1,
            grid=(2,),
            in_specs=[by_step((length, 3 * width)), step_low, by_step((length, 128)), step_low],
            out_specs=by_step((length, 3 * width)),
            scratch_shapes=[pltpu.VMEM((length, 3 * width), F32)],
        ),
        out_shape=struct((2, length, 3 * width), BF16),
        compiler_params=params(),
        name="self_back",
    )(bounds, qkv, a1, stat1, do1)


def local_step(sizes, x1, x2, mem, g1, g2, target_ids, memory_ids, norm, shards):
    length, width = x1.shape
    members, wides = sizes
    lines = wides // 2
    small = width // wides
    hidden = shards[5].shape[1]
    w_out = lax.all_gather(shards[6], "wide", axis=0, tiled=True)
    shards = shards[:6]
    tiles = length // TILE
    bounds = jnp.stack([segment_bounds(target_ids), segment_bounds(memory_ids)])
    vmem = pl.BlockSpec(memory_space=pltpu.VMEM)
    anywhere = pl.BlockSpec(memory_space=pl.ANY)

    def full(shape):
        return struct((lines, 2, shape[0], shape[1]), BF16)

    pieces = 10
    slots = gather_slots(sizes, pieces)
    results = pl.pallas_call(
        functools.partial(gather_kernel, sizes),
        in_specs=[vmem] * 4 + [anywhere] * 6,
        out_specs=[anywhere] * 3 + [vmem] + [anywhere] * 8,
        out_shape=[
            struct((2, length, width), BF16),
            struct((2, length, 3 * width), BF16),
            struct((length, 2 * width), BF16),
            struct((8, width), F32),
            struct((width, 2 * length), BF16),
            struct((width, length), BF16),
        ]
        + [full(item.shape) for item in shards],
        scratch_shapes=[
            pltpu.VMEM((2, length, width), BF16),
            pltpu.VMEM((width, 2 * length), BF16),
            pltpu.VMEM((width, length), BF16),
            pltpu.VMEM((3, lines, 2, small, width), BF16),
            pltpu.VMEM((2, lines, 2, small, width), BF16),
            pltpu.VMEM((3, 2, length, width), BF16),
            pltpu.VMEM((2, length, width), BF16),
            pltpu.VMEM((lines, 2, 8, width), F32),
            pltpu.SemaphoreType.DMA((slots,)),
            pltpu.SemaphoreType.DMA((slots,)),
            pltpu.SemaphoreType.DMA((pieces + 14,)),
        ],
        compiler_params=pltpu.CompilerParams(
            vmem_limit_bytes=VMEM_LIMIT, collective_id=0, has_side_effects=True
        ),
        name="gather_project",
    )(x1, x2, mem, norm, *shards)
    xs, qkv, kv, norms, h1_turned, mem_turned = results[:6]
    w_qkv, w_kv, w_self, w_query, w_cross, w_in = (
        item.reshape(-1, item.shape[-1]) for item in results[6:]
    )
    norm_spec = whole((8, width))
    step_low = by_step((length, width))
    a1, y1, q2, a2, stat1, stat2 = call_forward(bounds, xs, qkv, kv, norms, w_self, w_query)

    step_tile = pl.BlockSpec((1, TILE, width), lambda i: (i // tiles, i % tiles, 0))
    step_wide = pl.BlockSpec((1, TILE, hidden), lambda i: (i // tiles, i % tiles, 0))
    early = pl.BlockSpec((TILE, width), lambda i: (jnp.minimum(i, tiles - 1), 0))
    late = pl.BlockSpec((TILE, width), lambda i: (jnp.maximum(i - tiles, 0), 0))
    o1, o2, h3, r, du, e2, dy2, do2, dnorm2 = pl.pallas_call(
        functools.partial(feed_kernel, tiles),
        grid=(2 * tiles,),
        in_specs=[
            step_tile, step_tile, early, late, norm_spec,
            whole(w_cross.shape), whole(w_in.shape), whole(w_out.shape),
        ],
        out_specs=[
            early, late, step_tile, step_wide, step_wide, step_tile, step_tile, step_tile,
            fixed((2, 8, width)),
        ],
        out_shape=[
            struct((length, width), BF16),
            struct((length, width), BF16),
            struct((2, length, width), BF16),
            struct((2, length, hidden), BF16),
            struct((2, length, hidden), BF16),
            struct((2, length, width), BF16),
            struct((2, length, width), F32),
            struct((2, length, width), BF16),
            struct((2, 8, width), F32),
        ],
        compiler_params=params(),
        name="feed_forward_back",
    )(y1, a2, g1, g2, norms, w_cross, w_in, w_out)

    flat = (2 * length, width)
    chunk = pl.BlockSpec((2 * length, width), lambda c: (0, c))
    joint = pl.pallas_call(
        functools.partial(feed_grad_kernel, small),
        grid=(hidden // width,),
        in_specs=[whole(flat), whole(flat), whole(flat), whole((length, width)), whole((length, width)), chunk, chunk],
        out_specs=anywhere,
        out_shape=struct((width, 2 * hidden + width), BF16),
        scratch_shapes=[
            pltpu.VMEM((width, 2 * length), BF16),
            pltpu.VMEM((2, width, width), BF16),
            pltpu.VMEM((2, width * width // hidden, hidden), BF16),
            pltpu.VMEM((width, width), BF16),
            pltpu.SemaphoreType.DMA((3, 2)),
        ],
        compiler_params=params(),
        name="feed_weight_grads",
    )(h3.reshape(flat), a2.reshape(flat), e2.reshape(flat), g1, g2, du.reshape(2 * length, hidden), r.reshape(2 * length, hidden))
    share = lax.psum_scatter(joint, "wide", scatter_dimension=0, tiled=True)

    dy1, do1, d_query, d_self, d_kv, d_mem, dnorm1 = call_cross_back(bounds, q2, kv, a1, a2, stat2, do2, y1, dy2, mem_turned, norms, w_query, w_self, w_kv)

    low = call_self_back(bounds, qkv, a1, stat1, do1)

    def split(item):
        return item.reshape(lines, 2, small, item.shape[1])

    scratch = [
        pltpu.VMEM((2, length, 3 * width), BF16),
        pltpu.VMEM((2, length, width), BF16),
        pltpu.VMEM((2, length, width), F32),
        pltpu.VMEM((width, 2 * length), BF16),
        pltpu.VMEM((3, lines, 2, small, width), BF16),
        pltpu.VMEM((2 + 4 + lines + 2 * max(1, members // 4 - 1), 8, width), F32),
    ]
    for cols in (2 * width, width, width, width, width, width):
        scratch += reduced_scratch(sizes, small, cols, True)
    for cols in (hidden, hidden, width):
        scratch += reduced_scratch(sizes, small, cols, False)
    slots = reduce_slots(sizes, 9)
    scratch += [
        pltpu.SemaphoreType.DMA((slots,)),
        pltpu.SemaphoreType.DMA((slots,)),
        pltpu.SemaphoreType.DMA((4 + 2 * tiles,)),
    ]
    results = pl.pallas_call(
        functools.partial(finish_kernel, sizes),
        in_specs=[anywhere] * 4 + [vmem] * 8,
        out_specs=[anywhere] * 2 + [vmem] * 8,
        out_shape=[
            struct((length, width), F32),
            struct((length, width), F32),
            struct((small, 3 * width), BF16),
            struct((small, width), BF16),
            struct((small, width), BF16),
            struct((small, 2 * width), BF16),
            struct((small, hidden), BF16),
            struct((small, hidden), BF16),
            struct((small, width), BF16),
            struct((8, width), F32),
        ],
        scratch_shapes=scratch,
        compiler_params=pltpu.CompilerParams(
            vmem_limit_bytes=VMEM_LIMIT, collective_id=1, has_side_effects=True
        ),
        name="finish_reduce",
    )(low, h1_turned, xs, dy1, norms, w_qkv, split(d_self), split(d_query), split(d_kv), share, dnorm1, dnorm2)
    group = hidden // width
    shapes = [
        (3, small), (3, small), (small, 3 * width), (small, width), (small, width), (small, 2 * width),
        (small, hidden), (group * small, width), (small, width),
    ]
    gi1, gi2, t_gain, t_shift, *grads = pl.pallas_call(
        functools.partial(emit_kernel, wides),
        grid=(tiles,),
        in_specs=[pl.BlockSpec((TILE, width), lambda i: (i, 0))] * 2 + [whole(item.shape) for item in results[2:]],
        out_specs=[pl.BlockSpec((TILE, width), lambda i: (i, 0))] * 2 + [fixed(item) for item in shapes],
        out_shape=[struct((length, width), F32)] * 2 + [struct(item, F32) for item in shapes],
        compiler_params=params(),
        name="emit",
    )(*results)
    return o1, o2, gi1, gi2, d_mem, t_gain, t_shift, grads


def body(
    sizes, inputs_one, inputs_two, memory, cotangent_one, cotangent_two, target_ids, memory_ids,
    norm_gain, norm_shift, self_qkv, self_out, cross_query, cross_kv, cross_out, ffn_in, ffn_out,
):
    shape = inputs_one.shape
    length, width = shape[1:]
    small = width // sizes[1]
    at = lax.axis_index("wide") * small
    norm = jnp.concatenate([norm_gain, norm_shift]).astype(F32)
    norm = lax.dynamic_update_slice(jnp.zeros((8, width), F32), norm, (0, at))
    o1, o2, gi1, gi2, d_mem, t_gain, t_shift, grads = local_step(
        sizes,
        inputs_one.reshape(length, width),
        inputs_two.reshape(length, width),
        memory.reshape(length, width),
        cotangent_one.reshape(length, width),
        cotangent_two.reshape(length, width),
        target_ids,
        memory_ids,
        norm,
        (self_qkv, cross_kv, self_out, cross_query, cross_out, ffn_in, ffn_out),
    )
    d_qkv, d_self, d_query, d_kv, d_in, d_out, d_cross = grads
    return (
        o1.reshape(shape), o2.reshape(shape), gi1.reshape(shape), gi2.reshape(shape), d_mem.reshape(shape),
        t_gain, t_shift, d_qkv, d_self, d_query, d_kv, d_cross, d_in, d_out,
    )


def solution(mesh):
    rows = P(("narrow", "wide"), None, None)
    ids = P(("narrow", "wide"), None)
    norm, weight = P(None, "wide"), P("wide", None)
    return jax.shard_map(
        functools.partial(body, (mesh.shape["narrow"], mesh.shape["wide"])),
        mesh=mesh,
        in_specs=(rows,) * 5 + (ids,) * 2 + (norm,) * 2 + (weight,) * 7,
        out_specs=(rows,) * 5 + (norm,) * 2 + (weight,) * 7,
        check_vma=False,
    )
```

```python
import functools

import jax
import jax.numpy as jnp
from jax import lax
from jax.experimental import pallas as pl
from jax.experimental.pallas import tpu as pltpu
from jax.sharding import PartitionSpec as P

HEAD_DIM = 64
TILE = 256
SMALL = 128
FEED = 512
SEGMENTS = 5
MASKED = -1e30
VMEM_LIMIT = 60 * 1024 * 1024
BF16 = jnp.bfloat16
F32 = jnp.float32
MESH = pl.DeviceIdType.MESH


def lower(values):
    return values.astype(BF16)


def dot(left, right):
    return lax.dot_general(left, right, (((1,), (0,)), ((), ())), preferred_element_type=F32)


def dot_bt(left, right):
    return lax.dot_general(left, right, (((1,), (1,)), ((), ())), preferred_element_type=F32)


def dot_at(left, right):
    return lax.dot_general(left, right, (((0,), (0,)), ((), ())), preferred_element_type=F32)


def standardise(values):
    centred = values - jnp.mean(values, -1, keepdims=True)
    inverse = lax.rsqrt(jnp.mean(centred * centred, -1, keepdims=True) + 1e-05)
    return centred * inverse, inverse


def norm_back(xhat, inverse, gain, incoming):
    dz = incoming * gain
    inner = jnp.mean(dz * xhat, -1, keepdims=True)
    return (dz - jnp.mean(dz, -1, keepdims=True) - xhat * inner) * inverse


def fold_rows(values):
    rows, width = values.shape
    return jnp.sum(values.reshape(rows // 8, 8, width), axis=0)


def segment_bounds(ids):
    order = jnp.where(ids < 0, SEGMENTS - 1, ids).reshape(1, -1)
    level = lax.broadcasted_iota(jnp.int32, (8, 1), 0)
    return jnp.sum((order < level).astype(jnp.int32), axis=1)


def lane_index(rows):
    return lax.broadcasted_iota(jnp.int32, (rows, 128), 1)


def row_index(rows):
    return lax.broadcasted_iota(jnp.int32, (rows, 128), 0)


def stack_heads(pair, first):
    zero = jnp.zeros_like(pair)
    return jnp.concatenate([jnp.where(first, pair, zero), jnp.where(first, zero, pair)], axis=0)


def tiles_of(low, high, length, visit):
    base = (low // 16) * 16
    span = high - base
    whole_tiles = (span + TILE - 1 - SMALL) // TILE
    rest = span - whole_tiles * TILE

    def per_tile(i, carry):
        begin = base + i * TILE
        visit(TILE, pl.multiple_of(jnp.minimum(begin, length - TILE), 16), jnp.maximum(low, begin))
        return carry

    lax.fori_loop(0, whole_tiles, per_tile, 0)

    @pl.when(rest > 0)
    def _():
        begin = base + whole_tiles * TILE
        visit(SMALL, pl.multiple_of(jnp.minimum(begin, length - SMALL), 16), jnp.maximum(low, begin))


def each_segment(bounds, q_row, k_row, visit):
    def per_segment(s, carry):
        visit(bounds[q_row, s], bounds[q_row, s + 1], bounds[k_row, s], bounds[k_row, s + 1])
        return carry

    lax.fori_loop(0, SEGMENTS, per_segment, 0)


def pair_lanes(offset, p):
    if isinstance(p, int):
        return slice(offset + p * 128, offset + p * 128 + 128)
    return pl.ds(pl.multiple_of(offset + p * 128, 128), 128)


def inside_rows(size, start, low, high):
    rows = row_index(size) + start
    return (rows >= low) & (rows < high)


def attend(bounds, q_row, k_row, query, keys, values, out_ref, tail_ref):
    (q_ref, q_col), (k_ref, k_col), (v_ref, v_col) = query, keys, values
    length, width = out_ref.shape
    pairs = range(width // 128)

    def visit(size, start, low, high, k_low, k_high):
        lanes = lane_index(size)
        first = lanes < HEAD_DIM
        owner, place = lanes // 4, lanes % 4
        unit = jnp.where(lane_index(2 * size) == 0, 1.0, 0.0).astype(BF16)
        keep = inside_rows(size, start, low, high)
        span = pl.ds(start, size)
        k_base = (k_low // 16) * 16
        k_tiles = (k_high - k_base + TILE - 1) // TILE

        def piece(p, k_size, k_start, low_k):
            inside = inside_rows(k_size, k_start, low_k, k_high)
            shut = (lane_index(k_size) == 0) & jnp.logical_not(inside)
            bias = jnp.where(shut, MASKED, 0.0).astype(BF16)
            queries = stack_heads(q_ref[span, pair_lanes(q_col, p)], first)
            k_span = pl.ds(k_start, k_size)
            pair_k = k_ref[k_span, pair_lanes(k_col, p)]
            pair_v = v_ref[k_span, pair_lanes(v_col, p)]
            scores = dot_bt(
                jnp.concatenate([queries, unit], axis=1), jnp.concatenate([pair_k, bias], axis=1)
            )
            ones = jnp.ones((k_size, 128), BF16)
            return scores, jnp.concatenate([pair_v, ones], axis=1)

        def finish(p, highest, total, stats):
            cols = pair_lanes(0, p)
            top, bottom = total[:size], total[size:]
            mass = jnp.where(first, top[:, 128:], bottom[:, 128:])
            merged = lower(jnp.where(first, top[:, :128], bottom[:, :128]) / mass)
            out_ref[span, cols] = jnp.where(keep, merged, out_ref[span, cols])
            peak, sums = stats
            for h, half in ((0, slice(0, size)), (1, slice(size, 2 * size))):
                here = owner == 2 * p + h
                peak = jnp.where(here, highest[half], peak)
                sums = jnp.where(here, total[half, 128:], sums)
            return peak, sums

        empty = (jnp.zeros((size, 128), F32), jnp.ones((size, 128), F32))

        def close(stats):
            peak, sums = stats
            tail = split_lanes(peak + jnp.log(sums), place, 1.0)
            tail_ref[span, :] = jnp.where(keep, tail, tail_ref[span, :])

        def rolled(one):
            close(lax.fori_loop(0, len(pairs), lambda p, stats: finish(p, *one(p), stats), empty))

        def direct(k_size):
            k_start = pl.multiple_of(jnp.minimum(k_base, length - k_size), 16)

            items = [piece(p, k_size, k_start, k_low) for p in pairs]
            tops = [jnp.max(item[0], -1, keepdims=True) for item in items]
            probs = [lower(jnp.exp(item[0] - top)) for item, top in zip(items, tops)]
            totals = [dot(prob, item[1]) for prob, item in zip(probs, items)]
            stats = empty
            for p in pairs:
                stats = finish(p, tops[p], totals[p], stats)
            close(stats)

        if size < TILE:

            @pl.when(k_tiles <= 2)
            def _():
                direct(2 * TILE)

        else:

            @pl.when(k_tiles == 1)
            def _():
                direct(TILE)

            @pl.when(k_tiles == 2)
            def _():
                direct(2 * TILE)

        @pl.when(k_tiles > 2)
        def _():
            def one(p):
                def per_key(j, carry):
                    highest, total = carry
                    begin = k_base + j * TILE
                    k_start = pl.multiple_of(jnp.minimum(begin, length - TILE), 16)
                    scores, wide_v = piece(p, TILE, k_start, jnp.maximum(k_low, begin))
                    newest = jnp.maximum(highest, jnp.max(scores, -1, keepdims=True))
                    expon = lower(jnp.exp(scores - newest))
                    return newest, total * jnp.exp(highest - newest) + dot(expon, wide_v)

                start_at = (jnp.full((2 * size, 1), MASKED, F32), jnp.zeros((2 * size, 256), F32))
                return lax.fori_loop(0, k_tiles, per_key, start_at)

            rolled(one)

    def segment(q_low, q_high, k_low, k_high):
        tiles_of(
            q_low, q_high, length, lambda size, start, low: visit(size, start, low, q_high, k_low, k_high)
        )

    each_segment(bounds, q_row, k_row, segment)


def split_lanes(values, place, lead):
    high = lower(values).astype(F32)
    rest = values - high
    middle = lower(rest).astype(F32)
    spread = jnp.where(place == 1, high, jnp.where(place == 2, middle, rest - middle))
    return lower(jnp.where(place == 0, lead, -spread))


def attend_back(bounds, q_row, k_row, query, keys, values, do_ref, out_ref, tail_ref, dq, dk, dv):
    (q_ref, q_col), (k_ref, k_col), (v_ref, v_col) = query, keys, values
    (dq_ref, dq_col), (dk_ref, dk_col), (dv_ref, dv_col) = dq, dk, dv
    length, width = do_ref.shape
    pairs = width // 128
    zero = jnp.zeros((), BF16)
    lane = lane_index(width)
    collect = (lane % 4 > 0) & (lane // 4 == row_index(width) // HEAD_DIM)
    collect = jnp.where(collect, 1.0, 0.0).astype(BF16)

    def visit(size, start, low, high, k_low, k_high):
        lanes = lane_index(size)
        first = lanes < HEAD_DIM
        owner, place = lanes // 4, lanes % 4
        closed = lower(jnp.where(place == 0, 1.0, jnp.where(place == 1, MASKED, 0.0)))
        keep = inside_rows(size, start, low, high)
        span = pl.ds(start, size)
        tail_q = jnp.where(keep, tail_ref[span, :], closed)
        centre = jnp.zeros((size, 128), F32)
        for p in range(pairs):
            cols = slice(p * 128, (p + 1) * 128)
            grad = jnp.where(keep, do_ref[span, cols], zero)
            inner = grad.astype(F32) * out_ref[span, cols].astype(F32)
            coarse = lower(inner)
            fine = lower(inner - coarse.astype(F32))
            centre = centre + dot(
                jnp.concatenate([coarse, fine], axis=1),
                jnp.concatenate([collect[cols], collect[cols]], axis=0),
            )
        tail_g = split_lanes(centre, place, 0.0)

        def per_key(k_size, k_start, low_k):
            k_span = pl.ds(k_start, k_size)
            inside = inside_rows(k_size, k_start, low_k, k_high)
            lead = lane_index(k_size) % 4 == 0
            tail = lower(jnp.where(lead, jnp.where(inside, 0.0, MASKED), 1.0))

            def load(p):
                pair_q = q_ref[span, pair_lanes(q_col, p)]
                pair_k = k_ref[k_span, pair_lanes(k_col, p)]
                pair_v = v_ref[k_span, pair_lanes(v_col, p)]
                pair_do = jnp.where(keep, do_ref[span, pair_lanes(0, p)], zero)
                queries = stack_heads(pair_q, first)
                grads = stack_heads(pair_do, first)
                ends = [
                    jnp.concatenate(
                        [jnp.where(owner == 2 * p, item, zero), jnp.where(owner == 2 * p + 1, item, zero)],
                        axis=0,
                    )
                    for item in (tail_q, tail_g)
                ]
                scores = dot_bt(
                    jnp.concatenate([pair_k, tail], axis=1),
                    jnp.concatenate([queries, ends[0]], axis=1),
                )
                slope = dot_bt(
                    jnp.concatenate([pair_v, tail], axis=1),
                    jnp.concatenate([grads, ends[1]], axis=1),
                )
                return pair_k, queries, grads, scores, slope

            def middle(item):
                pair_k, queries, grads, scores, slope = item
                probs = jnp.exp(scores)
                return pair_k, queries, grads, lower(probs), lower(probs * slope)

            def store(p, pair_k, queries, grads, probs, ds):
                dv_ref[k_span, pair_lanes(dv_col, p)] += dot(probs, grads)
                dk_ref[k_span, pair_lanes(dk_col, p)] += dot(ds, queries)
                turned = [dot_at(ds[:, :size], pair_k), dot_at(ds[:, size:], pair_k)]
                dq_ref[span, pair_lanes(dq_col, p)] += jnp.where(first, turned[0], turned[1])

            ahead = load(0)
            for p in range(pairs):
                item = ahead
                if p + 1 < pairs:
                    ahead = load(p + 1)
                store(p, *middle(item))

        tiles_of(k_low, k_high, length, per_key)

    def segment(q_low, q_high, k_low, k_high):
        tiles_of(
            q_low, q_high, length, lambda size, start, low: visit(size, start, low, q_high, k_low, k_high)
        )

    each_segment(bounds, q_row, k_row, segment)


def forward_kernel(bounds, xs, block, norms, w_self, w_query, attended, tail, y1, q2, queries):
    phase = pl.program_id(1)
    length, width = queries.shape

    @pl.when(phase == 0)
    def _():
        queries[...] = block[0, :, :width]

    attend(
        bounds, 0, phase, (queries, 0), (block.at[0], width), (block.at[0], 2 * width),
        attended.at[0, 0], tail.at[0, 0],
    )

    @pl.when(phase == 0)
    def _():
        for i in range(length // TILE):
            span = slice(i * TILE, (i + 1) * TILE)
            after = xs[0, span, :].astype(F32) + dot(attended[0, 0, span, :], w_self[...])
            y1[0, span, :] = after
            xhat, _ = standardise(after)
            h2 = lower(xhat * norms[1:2, :] + norms[4:5, :])
            asked = lower(dot(h2, w_query[...]) * HEAD_DIM ** (-0.5))
            queries[span, :] = asked
            q2[0, span, :] = asked


def feed_kernel(
    per_step, y1, a2, g1, g2, norms, w_cross, w_in, w_out,
    o1, o2, h3, r, du, e2, dy2, do2, dnorm,
):
    i = pl.program_id(0)
    width = w_cross.shape[0]
    is_first = i < per_step
    grad = jnp.where(is_first, g1[...], g2[...])
    after = y1[0] + dot(a2[0, 0], w_cross[...])
    xhat, inverse = standardise(after)
    normed = lower(xhat * norms[2:3, :] + norms[5:6, :])
    h3[0] = normed
    result = after
    dh3 = jnp.zeros_like(after)
    slope = (2.0 / jnp.pi) ** 0.5
    chunks = w_in.shape[1] // width

    def enter(c):
        cols = slice(c * width, (c + 1) * width)
        return dot(normed, w_in[:, cols]), dot_bt(grad, w_out[cols, :])

    ahead = enter(0)
    for c in range(chunks):
        cols = slice(c * width, (c + 1) * width)
        u, dr = ahead
        if c + 1 < chunks:
            ahead = enter(c + 1)
        square = u * u
        half = 0.5 + 0.5 * jnp.tanh(u * (slope + slope * 0.044715 * square))
        hidden = lower(u * half)
        r[0, :, cols] = hidden
        bend = u * (2 * slope + 6 * slope * 0.044715 * square)
        pre = lower(dr * (half * (1.0 + (1.0 - half) * bend)))
        du[0, :, cols] = pre
        result = result + dot(hidden, w_out[cols, :])
        dh3 = dh3 + dot_bt(pre, w_in[:, cols])

    @pl.when(is_first)
    def _():
        o1[...] = lower(result)

    @pl.when(jnp.logical_not(is_first))
    def _():
        o2[...] = lower(result)

    @pl.when(i == 0)
    def _():
        dnorm[...] = jnp.zeros_like(dnorm)

    dnorm[0] += fold_rows(dh3 * xhat)
    dnorm[1] += fold_rows(dh3)
    back = grad.astype(F32) + norm_back(xhat, inverse, norms[2:3, :], dh3)
    dy2[0] = back
    low = lower(back)
    e2[0] = low
    do2[0] = lower(dot_bt(low, w_cross[...]))


def feed_grad_kernel(
    small, h3, g1, g2, du, r, a2_hbm, e2_hbm, joint,
    turned, turned_g, a2, e2, d_in, d_out, d_cross, sem,
):
    c = pl.program_id(0)
    last = pl.num_programs(0) - 1
    half, width = g1.shape
    hidden = d_out.shape[2]
    group = hidden // width
    rows = width // group
    slot = lax.rem(c, 2)

    def copies(at, chunk):
        return (
            pltpu.make_async_copy(
                d_in.at[at], joint.at[:, pl.ds(pl.multiple_of(chunk * width, width), width)], sem.at[0, at]
            ),
            pltpu.make_async_copy(
                d_out.at[at],
                joint.at[pl.ds(pl.multiple_of(chunk * rows, rows), rows), hidden + width :],
                sem.at[1, at],
            ),
        )

    loads = [
        pltpu.make_async_copy(a2_hbm.at[:, 1], a2, sem.at[2, 1]),
        pltpu.make_async_copy(e2_hbm, e2, sem.at[3, 0]),
    ]
    cross = pltpu.make_async_copy(d_cross, joint.at[:, hidden : hidden + width], sem.at[2, 0])

    @pl.when(c >= 2)
    def _():
        for copy in copies(slot, c - 2):
            copy.wait()

    @pl.when(c == 0)
    def _():
        for copy in loads:
            copy.start()
        turned[...] = h3[...].T
        turned_g[:, :half] = g1[...].T
        turned_g[:, half:] = g2[...].T

    d_in[slot] = lower(dot(turned[...], du[...]))
    part = lower(dot(turned_g[...], r[...])).T
    for w in range(width // (group * small)):
        for j in range(group):
            at = (w * group + j) * small
            d_out[slot, w * small : (w + 1) * small, j * width : (j + 1) * width] = part[at : at + small]
    for copy in copies(slot, c):
        copy.start()

    @pl.when(c == last)
    def _():
        wait_all(loads)
        d_cross[...] = lower(dot(a2[0].T, e2[0]) + dot(a2[1].T, e2[1]))
        cross.start()
        for copy in copies(1 - slot, c - 1) + copies(slot, c):
            copy.wait()
        cross.wait()


def cross_back_kernel(
    bounds, q2, keys, values, a1, a2, stat2, do2, y1, dy2, mem_turned, norms, w_query, w_self, w_kv,
    dy1, do1, d_query, d_self, d_kv, d_mem, dnorm,
    dq_sum, dkv_sum, h2, low_q, low_e,
):
    step = pl.program_id(0)
    length, width = q2.shape[1:]

    @pl.when(step == 0)
    def _():
        dkv_sum[...] = jnp.zeros_like(dkv_sum)
        dnorm[...] = jnp.zeros_like(dnorm)

    dq_sum[...] = jnp.zeros_like(dq_sum)
    attend_back(
        bounds, 0, 1, (q2.at[0], 0), (keys.at[0], 0), (values.at[0], 0), do2.at[0], a2.at[0, 0], stat2.at[0, 0],
        (dq_sum, 0), (dkv_sum, 0), (dkv_sum, width),
    )

    def rows(i):
        span = slice(i * TILE, (i + 1) * TILE)
        grad_q = lower(dq_sum[span, :] * HEAD_DIM ** (-0.5))
        low_q[step, span, :] = grad_q
        xhat, inverse = standardise(y1[0, span, :])
        h2[step, span, :] = lower(xhat * norms[1:2, :] + norms[4:5, :])
        dh2 = dot_bt(grad_q, w_query[...])
        dnorm[0] += fold_rows(dh2 * xhat)
        dnorm[1] += fold_rows(dh2)
        back = dy2[0, span, :] + norm_back(xhat, inverse, norms[1:2, :], dh2)
        dy1[0, span, :] = back
        low = lower(back)
        low_e[step, span, :] = low
        do1[0, span, :] = lower(dot_bt(low, w_self[...]))

    for i in range(length // TILE):
        rows(i)

    @pl.when(step == 1)
    def _():
        d_query[...] = lower(dot(h2[0].T, low_q[0]) + dot(h2[1].T, low_q[1]))
        d_self[...] = lower(dot(a1[0, 0].T, low_e[0]) + dot(a1[1, 0].T, low_e[1]))
        pair = lower(dkv_sum[...])
        d_kv[...] = lower(dot(mem_turned[...], pair))
        d_mem[...] = dot_bt(pair, w_kv[...])


def self_back_kernel(bounds, qkv, a1, stat1, do1, low, sums):
    width = do1.shape[2]
    sums[...] = jnp.zeros_like(sums)
    attend_back(
        bounds, 0, 0, (qkv.at[0], 0), (qkv.at[0], width), (qkv.at[0], 2 * width),
        do1.at[0], a1.at[0, 0], stat1.at[0, 0], (sums, 0), (sums, width), (sums, 2 * width),
    )
    low[0, :, :width] = lower(sums[:, :width] * HEAD_DIM ** (-0.5))
    low[0, :, width:] = lower(sums[:, width:])


def flip(index, mask):
    out, bit = index, 1
    while bit <= mask:
        if mask & bit:
            out = out + bit - 2 * bit * lax.rem(lax.div(index, bit), 2)
        bit *= 2
    return out


class Links:
    def __init__(self, sizes, send, recv):
        self.members, wides = sizes
        self.lines = wides // 2
        self.group = min(4, self.members)
        self.narrow, self.wide = lax.axis_index("narrow"), lax.axis_index("wide")
        self.line, self.core = lax.div(self.wide, 2), lax.rem(self.wide, 2)
        self.part = lax.rem(self.narrow, self.group)
        self.send, self.recv, self.used = send, recv, 0

    def core_peer(self):
        return (self.narrow, flip(self.wide, 1))

    def plane_peer(self, mask):
        return (flip(self.narrow, mask), self.wide)

    def line_peer(self, mask):
        return (self.narrow, 2 * flip(self.line, mask) + self.core)

    def far_masks(self):
        masks, mask = [], self.group
        while mask < self.members:
            masks.append(mask)
            mask *= 2
        return masks

    def barrier(self, far):
        semaphore = pltpu.get_barrier_semaphore()
        peers = [self.core_peer()]
        peers += [self.plane_peer(m) for m in range(1, self.group)]
        peers += [self.line_peer(m) for m in range(1, self.lines)]
        if far:
            peers += [self.plane_peer(m) for m in self.far_masks()]
        for peer in peers:
            pl.semaphore_signal(semaphore, inc=1, device_id=peer, device_id_type=MESH)
        pl.semaphore_wait(semaphore, len(peers))

    def push(self, src, dst, peer):
        slot = self.used
        self.used += 1
        copy = pltpu.make_async_remote_copy(
            src_ref=src,
            dst_ref=dst,
            send_sem=self.send.at[slot],
            recv_sem=self.recv.at[slot],
            device_id=peer,
            device_id_type=MESH,
        )
        copy.start()
        return copy

    def quarter(self, part, cols):
        size = cols // self.group
        return pl.ds(pl.multiple_of(part * size, size), size)


def wait_all(copies):
    for copy in copies:
        copy.wait()


class Gathered:
    def __init__(self, links, shard, full):
        self.links, self.shard, self.full = links, shard, full
        self.cols = shard.shape[-1]

    def start_line(self):
        links = self.links
        self.full[links.line, links.core] = self.shard[...]
        mine = links.quarter(links.part, self.cols)
        self.copies = [
            links.push(
                self.shard.at[:, mine], self.full.at[links.line, links.core, :, mine], links.line_peer(m)
            )
            for m in range(1, links.lines)
        ]

    def start_plane(self):
        links = self.links
        wait_all(self.copies)
        mine = links.quarter(links.part, self.cols)
        self.copies = []
        for k in range(1, links.lines):
            place = self.full.at[flip(links.line, k), links.core, :, mine]
            for m in range(1, links.group):
                self.copies.append(links.push(place, place, links.plane_peer(m)))

    def start_core(self):
        links = self.links
        wait_all(self.copies)
        place = self.full.at[:, links.core]
        self.copies = [links.push(place, place, links.core_peer())]

    def finish(self):
        wait_all(self.copies)


def gather_slots(sizes, pieces):
    lines, group = sizes[1] // 2, min(4, sizes[0])
    return pieces * (lines - 1 + (lines - 1) * (group - 1) + 1) + lines


def gather_kernel(
    sizes, x1, x2, mem, norm, s_qkv, s_kv, s_self, s_query, s_cross, s_in,
    xs, blocks, norms, h1_turned, mem_turned, f_qkv, f_kv, f_self, f_query, f_cross, f_in,
    h1, turned, turned_mem, v_qkv, v_kv, v_self, v_query, v_cross, v_in, o_qkv, o_kv, norm_all, send, recv, local,
):
    links = Links(sizes, send, recv)
    length, width = x1.shape
    used = [0]

    def local_copy(src, dst):
        copy = pltpu.make_async_copy(src, dst, local.at[used[0]])
        used[0] += 1
        copy.start()
        return copy

    landing = []

    def piece(shard, full, out):
        landing.append((full, out))
        return Gathered(links, shard, full)

    links.barrier(False)
    pieces = []
    for c in range(3):
        cols = slice(c * width, (c + 1) * width)
        pieces.append(piece(s_qkv.at[:, cols], v_qkv.at[c], f_qkv.at[:, :, :, cols]))
    for c in range(2):
        cols = slice(c * width, (c + 1) * width)
        pieces.append(piece(s_kv.at[:, cols], v_kv.at[c], f_kv.at[:, :, :, cols]))
    pieces.append(piece(s_self, v_self, f_self))
    pieces.append(piece(s_query, v_query, f_query))
    pieces.append(piece(s_cross, v_cross, f_cross))
    half = s_in.shape[1] // 2
    for c in range(2):
        cols = slice(c * half, (c + 1) * half)
        pieces.append(piece(s_in.at[:, cols], v_in.at[c], f_in.at[:, :, :, cols]))

    norm_all[links.line, links.core] = norm[...]
    own = norm_all.at[links.line, links.core]
    norm_copies = [links.push(own, own, links.line_peer(m)) for m in range(1, links.lines)]
    for p in range(2):
        pieces[p].start_line()
    outgoing = [local_copy(x1, xs.at[0]), local_copy(x2, xs.at[1])]
    pieces[2].start_line()
    wait_all(norm_copies)
    place = norm_all.at[:, links.core]
    norm_copy = links.push(place, place, links.core_peer())
    pieces[0].start_plane()
    norm_copy.wait()
    every = norm_all[...]
    total = every[0, 0]
    for k in range(1, 2 * links.lines):
        total = total + every[k // 2, k % 2]
    norms[...] = total
    gain, shift = total[0:1, :], total[3:4, :]

    def normalise(t, x):
        for i in range(length // TILE):
            span = slice(i * TILE, (i + 1) * TILE)
            xhat, _ = standardise(x[span, :].astype(F32))
            h1[t, span, :] = lower(xhat * gain + shift)

    def turn():
        turned[:, :length] = h1[0].T
        turned[:, length:] = h1[1].T
        turned_mem[...] = mem[...].T
        outgoing.append(local_copy(turned, h1_turned))
        outgoing.append(local_copy(turned_mem, mem_turned))

    def project(c):
        def run():
            weight = v_qkv[c].reshape(width, width)
            scale = HEAD_DIM ** (-0.5) if c == 0 else 1.0
            for t in range(2):

                def rows(i, carry, t=t):
                    span = pl.ds(pl.multiple_of(i * 2 * TILE, 2 * TILE), 2 * TILE)
                    o_qkv[c, t, span, :] = lower(dot(h1[t, span, :], weight) * scale)
                    return carry

                lax.fori_loop(0, length // (2 * TILE), rows, 0)
            cols = slice(c * width, (c + 1) * width)
            outgoing.append(local_copy(o_qkv.at[c], blocks.at[0:2, :, cols]))

        return run

    def project_memory(c):
        def run():
            weight = v_kv[c].reshape(width, width)

            def rows(i, carry):
                span = pl.ds(pl.multiple_of(i * 2 * TILE, 2 * TILE), 2 * TILE)
                o_kv[c, span, :] = lower(dot(mem[span, :], weight))
                return carry

            lax.fori_loop(0, length // (2 * TILE), rows, 0)
            cols = slice((c + 1) * width, (c + 2) * width)
            outgoing.append(local_copy(o_kv.at[c], blocks.at[2, :, cols]))

        return run

    work = {c: project(c) for c in range(3)} | {3 + c: project_memory(c) for c in range(2)}
    count = len(pieces)
    for t in range(3, count + 6):
        if t < count:
            pieces[t].start_line()
        if 1 <= t - 2 < count:
            pieces[t - 2].start_plane()
        if t == 3:
            normalise(0, x1)
        if t == 4:
            normalise(1, x2)
        if 0 <= t - 4 < count:
            pieces[t - 4].start_core()
        if 0 <= t - 5 < count:
            pieces[t - 5].finish()
            outgoing.append(local_copy(*landing[t - 5]))
            if t - 5 in work:
                work[t - 5]()
            if t - 5 == 5:
                turn()
    wait_all(outgoing)


class Reduced:
    def __init__(self, links, bufs, out, source=None, shard=None):
        self.links, self.out, self.source, self.shard = links, out, source, shard
        self.crecv, self.chip, self.precv, self.plane, self.lrecv, self.mine, self.xrecv, self.full = bufs
        self.cols = self.full.shape[-1]

    def start_core(self):
        links = self.links
        self.copies = [links.push(self.source.at[:, 1 - links.core], self.crecv, links.core_peer())]

    def start_plane(self):
        links = self.links
        if self.source is not None:
            wait_all(self.copies)
            for k in range(links.lines):
                self.chip[k] = lower(
                    self.source[k, links.core].astype(F32) + self.crecv[k].astype(F32)
                )
        self.copies = [
            links.push(
                self.chip.at[:, :, links.quarter(flip(links.part, m), self.cols)],
                self.precv.at[m - 1],
                links.plane_peer(m),
            )
            for m in range(1, links.group)
        ]

    def start_line(self):
        links = self.links
        wait_all(self.copies)
        total = self.chip[:, :, links.quarter(links.part, self.cols)].astype(F32)
        for m in range(1, links.group):
            total = total + self.precv[m - 1].astype(F32)
        self.plane[...] = lower(total)
        if self.source is None:
            self.copies = []
            return
        self.copies = [
            links.push(self.plane.at[flip(links.line, m)], self.lrecv.at[m - 1], links.line_peer(m))
            for m in range(1, links.lines)
        ]

    def start_gather(self):
        links = self.links
        wait_all(self.copies)
        if self.source is None:
            total = self.plane[0].astype(F32)
        else:
            total = self.plane[links.line].astype(F32)
            for m in range(1, links.lines):
                total = total + self.lrecv[m - 1].astype(F32)
        for i, mask in enumerate(links.far_masks()):
            self.xrecv[2 * i] = lower(total)
            links.push(self.xrecv.at[2 * i], self.xrecv.at[2 * i + 1], links.plane_peer(mask)).wait()
            total = self.xrecv[2 * i].astype(F32) + self.xrecv[2 * i + 1].astype(F32)
        self.mine[...] = lower(total)
        place = self.full.at[:, links.quarter(links.part, self.cols)]
        place[...] = self.mine[...]
        self.copies = [links.push(self.mine, place, links.plane_peer(m)) for m in range(1, links.group)]

    def finish(self):
        wait_all(self.copies)
        self.out[...] = self.full[...]


class LineFirst:
    def __init__(self, links, bufs, source, then):
        self.links, self.source, self.then = links, source, then
        self.crecv, self.chip, self.lrecv = bufs

    def start_core(self):
        links = self.links
        self.copies = [links.push(self.source.at[:, 1 - links.core], self.crecv, links.core_peer())]

    def start_line(self):
        links = self.links
        wait_all(self.copies)
        for k in range(links.lines):
            self.chip[k] = lower(self.source[k, links.core].astype(F32) + self.crecv[k].astype(F32))
        self.copies = [
            links.push(self.chip.at[flip(links.line, m)], self.lrecv.at[m - 1], links.line_peer(m))
            for m in range(1, links.lines)
        ]

    def start_plane(self):
        links = self.links
        wait_all(self.copies)
        total = self.chip[links.line].astype(F32)
        for m in range(1, links.lines):
            total = total + self.lrecv[m - 1].astype(F32)
        self.then.chip[0] = lower(total)
        self.then.start_plane()


def reduced_scratch(sizes, rows, cols, wide_too):
    members, wides = sizes
    lines, group = wides // 2, min(4, members)
    part = cols // group
    depth = lines if wide_too else 1
    far = max(2, 2 * (members // group - 1))
    small = (1, 16, 128)
    return [
        pltpu.VMEM((lines, rows, cols) if wide_too else small, BF16),
        pltpu.VMEM((depth, rows, cols), BF16),
        pltpu.VMEM((group - 1, depth, rows, part), BF16),
        pltpu.VMEM((depth, rows, part), BF16),
        pltpu.VMEM((lines - 1, rows, part) if wide_too else small, BF16),
        pltpu.VMEM((rows, part), BF16),
        pltpu.VMEM((far, rows, part), BF16),
        pltpu.VMEM((rows, cols), BF16),
    ]


def reduce_slots(sizes, jobs):
    members, wides = sizes
    lines, group = wides // 2, min(4, members)
    return (jobs + 1) * (1 + 2 * (group - 1) + lines - 1 + members // group)


BUFS = 8


def finish_kernel(
    sizes, low_hbm, h1_hbm, xs_hbm, dy1_hbm, norms, w_qkv, d_self, d_query, d_kv, share, dnorm1, dnorm2,
    gi1, gi2, t_qkv, t_self, t_query, t_kv, t_in, t_out, t_cross, t_norm,
    low, xs, dy1, h1, grads, norm_slots, *rest,
):
    send, recv, local = rest[-3:]
    bufs, first_bufs = rest[:-12], rest[-12:-3]
    links = Links(sizes, send, recv)
    _, length, width = xs.shape
    loads = [
        pltpu.make_async_copy(h1_hbm, h1, local.at[0]),
        pltpu.make_async_copy(low_hbm, low, local.at[1]),
        pltpu.make_async_copy(xs_hbm, xs, local.at[2]),
        pltpu.make_async_copy(dy1_hbm, dy1, local.at[3]),
    ]
    for copy in loads:
        copy.start()
    links.barrier(True)

    taken = [0]

    def job(out, **kind):
        at = taken[0] * BUFS
        taken[0] += 1
        return Reduced(links, bufs[at : at + BUFS], out, **kind)

    others = [job(t_kv, shard=True), job(t_self, shard=True), job(t_query, shard=True)]
    before = [
        LineFirst(links, first_bufs[3 * i : 3 * i + 3], source, others[i])
        for i, source in enumerate((d_kv, d_self, d_query))
    ]
    heads = [job(t_qkv.at[:, c * width : (c + 1) * width], source=grads.at[c]) for c in range(3)]
    hidden = t_in.shape[1]
    shards = [
        job(t_in, shard=share.at[:, :hidden]),
        job(t_out, shard=share.at[:, hidden + width :]),
        job(t_cross, shard=share.at[:, hidden : hidden + width]),
    ]
    for one in before:
        one.start_core()
    for one in shards:
        one.chip[0] = one.shard[...]
        one.start_plane()
    gain = norms[0:1, :]
    loads[0].wait()
    loads[1].wait()
    for c in range(3):
        cols = slice(c * width, (c + 1) * width)
        value = dot(h1[:, :length], low[0, :, cols]) + dot(h1[:, length:], low[1, :, cols])
        grads[c] = lower(value).reshape(grads.shape[1:])
        heads[c].start_core()
        if c > 0:
            heads[c - 1].start_plane()
        if c == 0:
            for one in before:
                one.start_line()
    heads[2].start_plane()
    loads[2].wait()
    loads[3].wait()
    stores = []
    dgain = jnp.zeros((8, width), F32)
    dshift = jnp.zeros((8, width), F32)
    steps = [
        lambda: [one.start_line() for one in shards],
        lambda: [one.start_gather() for one in shards],
        lambda: heads[0].start_line(),
        lambda: heads[1].start_line(),
        lambda: heads[2].start_line(),
        lambda: [one.start_plane() for one in before],
        lambda: [one.finish() for one in shards],
    ]
    weight = w_qkv[...]
    for t in range(2):
        for i in range(length // TILE):
            span = slice(i * TILE, (i + 1) * TILE)
            xhat, inverse = standardise(xs[t, span, :].astype(F32))
            dh1 = dot_bt(low[t, span, :], weight)
            dgain = dgain + fold_rows(dh1 * xhat)
            dshift = dshift + fold_rows(dh1)
            dy1[t, span, :] = dy1[t, span, :] + norm_back(xhat, inverse, gain, dh1)
            out = (gi1, gi2)[t]
            number = t * (length // TILE) + i
            copy = pltpu.make_async_copy(dy1.at[t, span, :], out.at[span, :], local.at[4 + number])
            copy.start()
            stores.append(copy)
            if number < len(steps):
                steps[number]()
    rows = [jnp.sum(item, axis=0, keepdims=True) for item in (dgain, dnorm1[0], dnorm2[0], dshift, dnorm1[1], dnorm2[1])]
    total = jnp.concatenate(rows + [jnp.zeros((2, width), F32)], axis=0)

    def swap(first, count, own, peers, total):
        norm_slots[first + own] = total
        place = norm_slots.at[first + own]
        wait_all([links.push(place, place, peer) for peer in peers])
        out = norm_slots[first]
        for k in range(1, count):
            out = out + norm_slots[first + k]
        return out

    total = swap(0, 2, links.core, [links.core_peer()], total)
    for one in heads:
        one.start_gather()
    for one in others:
        one.start_line()
        one.start_gather()
    total = swap(2, links.group, links.part, [links.plane_peer(m) for m in range(1, links.group)], total)
    first = 2 + links.group
    total = swap(first, links.lines, links.line, [links.line_peer(m) for m in range(1, links.lines)], total)
    first += links.lines
    for mask in links.far_masks():
        side = lax.rem(lax.div(links.narrow, mask), 2)
        total = swap(first, 2, side, [links.plane_peer(mask)], total)
        first += 2
    t_norm[...] = total
    for one in heads + others:
        one.finish()
    wait_all(stores)


def emit_kernel(
    wides, f1, f2, b_qkv, b_self, b_query, b_kv, b_in, b_out, b_cross, t_norm,
    gi1, gi2, gain, shift, t_qkv, t_self, t_query, t_kv, t_in, t_out, t_cross,
):
    gi1[...] = f1[...]
    gi2[...] = f2[...]
    width = gi1.shape[1]
    small = b_out.shape[0]

    @pl.when(pl.program_id(0) == 0)
    def _():
        for src, dst in (
            (b_qkv, t_qkv), (b_self, t_self), (b_query, t_query), (b_kv, t_kv), (b_in, t_in), (b_cross, t_cross),
        ):
            dst[...] = src[...].astype(F32)
        for j in range(b_out.shape[1] // width):
            t_out[j * small : (j + 1) * small, :] = b_out[:, j * width : (j + 1) * width].astype(F32)
        at = lax.axis_index("wide") * small
        mine = pltpu.roll(t_norm[...], lax.rem(width - at, width), 1)
        gain[...] = mine[:3, :small]
        shift[...] = mine[3:6, :small]


def whole(shape):
    zeros = (0,) * len(shape)
    return pl.BlockSpec(shape, lambda *_: zeros, pipeline_mode=pl.Buffered(1))


def fixed(shape):
    zeros = (0,) * len(shape)
    return pl.BlockSpec(shape, lambda *_: zeros)


def by_step(shape):
    return pl.BlockSpec((1,) + shape, lambda t, *_: (t, 0, 0))


def params():
    return pltpu.CompilerParams(
        vmem_limit_bytes=VMEM_LIMIT, dimension_semantics=("arbitrary",)
    )


def struct(shape, dtype):
    return jax.ShapeDtypeStruct(shape, dtype)


def call_forward(bounds, xs, blocks, norms, w_self, w_query):
    length, width = xs.shape[1:]
    each = pl.BlockSpec((1, length, width), lambda t, p, *_: (t, 0, 0))
    return pl.pallas_call(
        forward_kernel,
        grid_spec=pltpu.PrefetchScalarGridSpec(
            num_scalar_prefetch=1,
            grid=(2, 2),
            in_specs=[
                each,
                pl.BlockSpec((1, length, 3 * width), lambda t, p, *_: (t + p * (2 - t), 0, 0)),
                whole((8, width)), whole(w_self.shape), whole(w_query.shape),
            ],
            out_specs=[
                pl.BlockSpec((1, 1, length, width), lambda t, p, *_: (t, p, 0, 0)),
                pl.BlockSpec((1, 1, length, 128), lambda t, p, *_: (t, p, 0, 0)),
                each, each,
            ],
            scratch_shapes=[pltpu.VMEM((length, width), BF16)],
        ),
        out_shape=[
            struct((2, 2, length, width), BF16),
            struct((2, 2, length, 128), BF16),
            struct((2, length, width), F32),
            struct((2, length, width), BF16),
        ],
        compiler_params=pltpu.CompilerParams(
            vmem_limit_bytes=VMEM_LIMIT, dimension_semantics=("arbitrary", "arbitrary")
        ),
        name="attend_forward",
    )(bounds, xs, blocks, norms, w_self, w_query)


def call_cross_back(bounds, q2, blocks, attended, tail, do2, y1, dy2, mem_turned, norms, w_query, w_self, w_kv):
    length, width = q2.shape[1:]
    norm_spec = whole((8, width))
    step_low = by_step((length, width))
    return pl.pallas_call(
        cross_back_kernel,
        grid_spec=pltpu.PrefetchScalarGridSpec(
            num_scalar_prefetch=1,
            grid=(2,),
            in_specs=[
                step_low,
                pl.BlockSpec((1, length, width), lambda *_: (2, 0, 1), pipeline_mode=pl.Buffered(1)),
                pl.BlockSpec((1, length, width), lambda *_: (2, 0, 2), pipeline_mode=pl.Buffered(1)),
                pl.BlockSpec((2, 1, length, width), lambda *_: (0, 0, 0, 0), pipeline_mode=pl.Buffered(1)),
                pl.BlockSpec((1, 1, length, width), lambda t, *_: (t, 1, 0, 0)),
                pl.BlockSpec((1, 1, length, 128), lambda t, *_: (t, 1, 0, 0)),
                step_low,
                step_low, step_low, whole(mem_turned.shape), norm_spec,
                whole(w_query.shape), whole(w_self.shape), whole(w_kv.shape),
            ],
            out_specs=[
                step_low, step_low, fixed((width, width)), fixed((width, width)), fixed((width, 2 * width)),
                fixed((length, width)), fixed((2, 8, width)),
            ],
            scratch_shapes=[
                pltpu.VMEM((length, width), F32),
                pltpu.VMEM((length, 2 * width), F32),
                pltpu.VMEM((2, length, width), BF16),
                pltpu.VMEM((2, length, width), BF16),
                pltpu.VMEM((2, length, width), BF16),
            ],
        ),
        out_shape=[
            struct((2, length, width), F32),
            struct((2, length, width), BF16),
            struct((width, width), BF16),
            struct((width, width), BF16),
            struct((width, 2 * width), BF16),
            struct((length, width), F32),
            struct((2, 8, width), F32),
        ],
        compiler_params=params(),
        name="cross_back",
    )(bounds, q2, blocks, blocks, attended, attended, tail, do2, y1, dy2, mem_turned, norms, w_query, w_self, w_kv)


def call_self_back(bounds, blocks, attended, tail, do1):
    length, width = do1.shape[1:]
    norm_spec = whole((8, width))
    step_low = by_step((length, width))
    return pl.pallas_call(
        self_back_kernel,
        grid_spec=pltpu.PrefetchScalarGridSpec(
            num_scalar_prefetch=1,
            grid=(2,),
            in_specs=[
                by_step((length, 3 * width)),
                pl.BlockSpec((1, 1, length, width), lambda t, *_: (t, 0, 0, 0)),
                pl.BlockSpec((1, 1, length, 128), lambda t, *_: (t, 0, 0, 0)),
                step_low,
            ],
            out_specs=by_step((length, 3 * width)),
            scratch_shapes=[pltpu.VMEM((length, 3 * width), F32)],
        ),
        out_shape=struct((2, length, 3 * width), BF16),
        compiler_params=params(),
        name="self_back",
    )(bounds, blocks, attended, tail, do1)


def call_gather(sizes, x1, x2, mem, norm, shards):
    length, width = x1.shape
    lines = sizes[1] // 2
    small = width // sizes[1]
    vmem = pl.BlockSpec(memory_space=pltpu.VMEM)
    anywhere = pl.BlockSpec(memory_space=pl.ANY)

    def full(shape):
        return struct((lines, 2, shape[0], shape[1]), BF16)

    pieces = 10
    slots = gather_slots(sizes, pieces)
    return pl.pallas_call(
        functools.partial(gather_kernel, sizes),
        in_specs=[vmem] * 10,
        out_specs=[anywhere] * 2 + [vmem] + [anywhere] * 8,
        out_shape=[
            struct((2, length, width), BF16),
            struct((3, length, 3 * width), BF16),
            struct((8, width), F32),
            struct((width, 2 * length), BF16),
            struct((width, length), BF16),
        ]
        + [full(item.shape) for item in shards],
        scratch_shapes=[
            pltpu.VMEM((2, length, width), BF16),
            pltpu.VMEM((width, 2 * length), BF16),
            pltpu.VMEM((width, length), BF16),
            pltpu.VMEM((3, lines, 2, small, width), BF16),
            pltpu.VMEM((2, lines, 2, small, width), BF16),
            pltpu.VMEM((lines, 2, small, width), BF16),
            pltpu.VMEM((lines, 2, small, width), BF16),
            pltpu.VMEM((lines, 2, small, width), BF16),
            pltpu.VMEM((2, lines, 2, small, shards[5].shape[1] // 2), BF16),
            pltpu.VMEM((3, 2, length, width), BF16),
            pltpu.VMEM((2, length, width), BF16),
            pltpu.VMEM((lines, 2, 8, width), F32),
            pltpu.SemaphoreType.DMA((slots,)),
            pltpu.SemaphoreType.DMA((slots,)),
            pltpu.SemaphoreType.DMA((pieces + 14,)),
        ],
        compiler_params=pltpu.CompilerParams(
            vmem_limit_bytes=VMEM_LIMIT, collective_id=0, has_side_effects=True
        ),
        name="gather_project",
    )(x1, x2, mem, norm, *shards)


def call_feed(y1, a2, g1, g2, norms, w_cross, w_in, w_out):
    length, width = g1.shape
    hidden = w_in.shape[1]
    tiles = length // FEED
    norm_spec = whole((8, width))
    step_tile = pl.BlockSpec((1, FEED, width), lambda i: (i // tiles, i % tiles, 0))
    step_wide = pl.BlockSpec((1, FEED, hidden), lambda i: (i // tiles, i % tiles, 0))
    early = pl.BlockSpec((FEED, width), lambda i: (jnp.minimum(i, tiles - 1), 0))
    late = pl.BlockSpec((FEED, width), lambda i: (jnp.maximum(i - tiles, 0), 0))
    return pl.pallas_call(
        functools.partial(feed_kernel, tiles),
        grid=(2 * tiles,),
        in_specs=[
            step_tile,
            pl.BlockSpec((1, 1, FEED, width), lambda i: (i // tiles, 1, i % tiles, 0)),
            early, late, norm_spec,
            whole(w_cross.shape), whole(w_in.shape), whole(w_out.shape),
        ],
        out_specs=[
            early, late, step_tile, step_wide, step_wide, step_tile, step_tile, step_tile,
            fixed((2, 8, width)),
        ],
        out_shape=[
            struct((length, width), BF16),
            struct((length, width), BF16),
            struct((2, length, width), BF16),
            struct((2, length, hidden), BF16),
            struct((2, length, hidden), BF16),
            struct((2, length, width), BF16),
            struct((2, length, width), F32),
            struct((2, length, width), BF16),
            struct((2, 8, width), F32),
        ],
        compiler_params=params(),
        name="feed_forward_back",
    )(y1, a2, g1, g2, norms, w_cross, w_in, w_out)


def call_feed_grads(small, h3, a2, e2, g1, g2, du, r):
    length, width = g1.shape
    hidden = r.shape[2]
    flat = (2 * length, width)
    chunk = pl.BlockSpec((2 * length, width), lambda c: (0, c))
    return pl.pallas_call(
        functools.partial(feed_grad_kernel, small),
        grid=(hidden // width,),
        in_specs=[whole(flat), whole((length, width)), whole((length, width)), chunk, chunk]
        + [pl.BlockSpec(memory_space=pl.ANY)] * 2,
        out_specs=pl.BlockSpec(memory_space=pl.ANY),
        out_shape=struct((width, 2 * hidden + width), BF16),
        scratch_shapes=[
            pltpu.VMEM((width, 2 * length), BF16),
            pltpu.VMEM((width, 2 * length), BF16),
            pltpu.VMEM((2, length, width), BF16),
            pltpu.VMEM((2, length, width), BF16),
            pltpu.VMEM((2, width, width), BF16),
            pltpu.VMEM((2, width * width // hidden, hidden), BF16),
            pltpu.VMEM((width, width), BF16),
            pltpu.SemaphoreType.DMA((4, 2)),
        ],
        compiler_params=params(),
        name="feed_weight_grads",
    )(h3.reshape(flat), g1, g2, du.reshape(2 * length, hidden), r.reshape(2 * length, hidden), a2, e2)


def call_finish(sizes, low, h1_turned, xs, dy1, norms, w_qkv, d_self, d_query, d_kv, share, dnorm1, dnorm2):
    members, wides = sizes
    _, length, width = xs.shape
    lines, small, tiles = wides // 2, width // wides, length // TILE
    hidden = (share.shape[1] - width) // 2
    vmem = pl.BlockSpec(memory_space=pltpu.VMEM)
    anywhere = pl.BlockSpec(memory_space=pl.ANY)

    def split(item):
        return item.reshape(lines, 2, small, item.shape[1])

    scratch = [
        pltpu.VMEM((2, length, 3 * width), BF16),
        pltpu.VMEM((2, length, width), BF16),
        pltpu.VMEM((2, length, width), F32),
        pltpu.VMEM((width, 2 * length), BF16),
        pltpu.VMEM((3, lines, 2, small, width), BF16),
        pltpu.VMEM((2 + 4 + lines + 2 * max(1, members // 4 - 1), 8, width), F32),
    ]
    for cols in (2 * width, width, width):
        scratch += reduced_scratch(sizes, small, cols, False)
    for cols in (width, width, width):
        scratch += reduced_scratch(sizes, small, cols, True)
    for cols in (hidden, hidden, width):
        scratch += reduced_scratch(sizes, small, cols, False)
    for cols in (2 * width, width, width):
        scratch += [
            pltpu.VMEM((lines, small, cols), BF16),
            pltpu.VMEM((lines, small, cols), BF16),
            pltpu.VMEM((max(1, lines - 1), small, cols), BF16),
        ]
    slots = reduce_slots(sizes, 9)
    scratch += [
        pltpu.SemaphoreType.DMA((slots,)),
        pltpu.SemaphoreType.DMA((slots,)),
        pltpu.SemaphoreType.DMA((4 + 2 * tiles,)),
    ]
    return pl.pallas_call(
        functools.partial(finish_kernel, sizes),
        in_specs=[anywhere] * 4 + [vmem] * 8,
        out_specs=[anywhere] * 2 + [vmem] * 8,
        out_shape=[
            struct((length, width), F32),
            struct((length, width), F32),
            struct((small, 3 * width), BF16),
            struct((small, width), BF16),
            struct((small, width), BF16),
            struct((small, 2 * width), BF16),
            struct((small, hidden), BF16),
            struct((small, hidden), BF16),
            struct((small, width), BF16),
            struct((8, width), F32),
        ],
        scratch_shapes=scratch,
        compiler_params=pltpu.CompilerParams(
            vmem_limit_bytes=VMEM_LIMIT, collective_id=1, has_side_effects=True
        ),
        name="finish_reduce",
    )(low, h1_turned, xs, dy1, norms, w_qkv, split(d_self), split(d_query), split(d_kv), share, dnorm1, dnorm2)


def call_emit(sizes, *results):
    length, width = results[0].shape
    wides = sizes[1]
    small, tiles = width // wides, length // TILE
    hidden = results[6].shape[1]
    group = hidden // width
    shapes = [
        (3, small), (3, small), (small, 3 * width), (small, width), (small, width), (small, 2 * width),
        (small, hidden), (group * small, width), (small, width),
    ]
    return pl.pallas_call(
        functools.partial(emit_kernel, wides),
        grid=(tiles,),
        in_specs=[pl.BlockSpec((TILE, width), lambda i: (i, 0))] * 2 + [whole(item.shape) for item in results[2:]],
        out_specs=[pl.BlockSpec((TILE, width), lambda i: (i, 0))] * 2 + [fixed(item) for item in shapes],
        out_shape=[struct((length, width), F32)] * 2 + [struct(item, F32) for item in shapes],
        compiler_params=params(),
        name="emit",
    )(*results)


def local_step(sizes, x1, x2, mem, g1, g2, target_ids, memory_ids, norm, shards):
    length, width = x1.shape
    members, wides = sizes
    lines = wides // 2
    small = width // wides
    hidden = shards[5].shape[1]
    w_out = lax.all_gather(shards[6], "wide", axis=0, tiled=True)
    shards = shards[:6]
    tiles = length // TILE
    bounds = jnp.stack([segment_bounds(target_ids), segment_bounds(memory_ids)])
    results = call_gather(sizes, x1, x2, mem, norm, shards)
    xs, blocks, norms, h1_turned, mem_turned = results[:5]
    w_qkv, w_kv, w_self, w_query, w_cross, w_in = (
        item.reshape(-1, item.shape[-1]) for item in results[5:]
    )
    attended, tail, y1, q2 = call_forward(bounds, xs, blocks, norms, w_self, w_query)

    o1, o2, h3, r, du, e2, dy2, do2, dnorm2 = call_feed(y1, attended, g1, g2, norms, w_cross, w_in, w_out)
    joint = call_feed_grads(small, h3, attended, e2, g1, g2, du, r)
    share = lax.psum_scatter(joint, "wide", scatter_dimension=0, tiled=True)

    dy1, do1, d_query, d_self, d_kv, d_mem, dnorm1 = call_cross_back(bounds, q2, blocks, attended, tail, do2, y1, dy2, mem_turned, norms, w_query, w_self, w_kv)

    low = call_self_back(bounds, blocks, attended, tail, do1)

    results = call_finish(sizes, low, h1_turned, xs, dy1, norms, w_qkv, d_self, d_query, d_kv, share, dnorm1, dnorm2)
    gi1, gi2, t_gain, t_shift, *grads = call_emit(sizes, *results)
    return o1, o2, gi1, gi2, d_mem, t_gain, t_shift, grads


def body(
    sizes, inputs_one, inputs_two, memory, cotangent_one, cotangent_two, target_ids, memory_ids,
    norm_gain, norm_shift, self_qkv, self_out, cross_query, cross_kv, cross_out, ffn_in, ffn_out,
):
    shape = inputs_one.shape
    length, width = shape[1:]
    small = width // sizes[1]
    at = lax.axis_index("wide") * small
    norm = jnp.concatenate([norm_gain, norm_shift]).astype(F32)
    norm = lax.dynamic_update_slice(jnp.zeros((8, width), F32), norm, (0, at))
    o1, o2, gi1, gi2, d_mem, t_gain, t_shift, grads = local_step(
        sizes,
        inputs_one.reshape(length, width),
        inputs_two.reshape(length, width),
        memory.reshape(length, width),
        cotangent_one.reshape(length, width),
        cotangent_two.reshape(length, width),
        target_ids,
        memory_ids,
        norm,
        (self_qkv, cross_kv, self_out, cross_query, cross_out, ffn_in, ffn_out),
    )
    d_qkv, d_self, d_query, d_kv, d_in, d_out, d_cross = grads
    return (
        o1.reshape(shape), o2.reshape(shape), gi1.reshape(shape), gi2.reshape(shape), d_mem.reshape(shape),
        t_gain, t_shift, d_qkv, d_self, d_query, d_kv, d_cross, d_in, d_out,
    )


def solution(mesh):
    rows = P(("narrow", "wide"), None, None)
    ids = P(("narrow", "wide"), None)
    norm, weight = P(None, "wide"), P("wide", None)
    return jax.shard_map(
        functools.partial(body, (mesh.shape["narrow"], mesh.shape["wide"])),
        mesh=mesh,
        in_specs=(rows,) * 5 + (ids,) * 2 + (norm,) * 2 + (weight,) * 7,
        out_specs=(rows,) * 5 + (norm,) * 2 + (weight,) * 7,
        check_vma=False,
    )
```

```python
import functools

import jax
import jax.numpy as jnp
from jax import lax
from jax.experimental import pallas as pl
from jax.experimental.pallas import tpu as pltpu
from jax.sharding import PartitionSpec as P

HEAD_DIM = 64
TILE = 256
SMALL = 128
FEED = 512
SEGMENTS = 5
MASKED = -1e30
VMEM_LIMIT = 60 * 1024 * 1024
BF16 = jnp.bfloat16
F32 = jnp.float32
MESH = pl.DeviceIdType.MESH


def lower(values):
    return values.astype(BF16)


def dot(left, right):
    return lax.dot_general(left, right, (((1,), (0,)), ((), ())), preferred_element_type=F32)


def dot_bt(left, right):
    return lax.dot_general(left, right, (((1,), (1,)), ((), ())), preferred_element_type=F32)


def dot_at(left, right):
    return lax.dot_general(left, right, (((0,), (0,)), ((), ())), preferred_element_type=F32)


def standardise(values):
    centred = values - jnp.mean(values, -1, keepdims=True)
    inverse = lax.rsqrt(jnp.mean(centred * centred, -1, keepdims=True) + 1e-05)
    return centred * inverse, inverse


def norm_back(xhat, inverse, gain, incoming):
    dz = incoming * gain
    inner = jnp.mean(dz * xhat, -1, keepdims=True)
    return (dz - jnp.mean(dz, -1, keepdims=True) - xhat * inner) * inverse


def fold_rows(values):
    rows, width = values.shape
    return jnp.sum(values.reshape(rows // 8, 8, width), axis=0)


def segment_bounds(ids):
    order = jnp.where(ids < 0, SEGMENTS - 1, ids).reshape(1, -1)
    level = lax.broadcasted_iota(jnp.int32, (8, 1), 0)
    return jnp.sum((order < level).astype(jnp.int32), axis=1)


def lane_index(rows):
    return lax.broadcasted_iota(jnp.int32, (rows, 128), 1)


def row_index(rows):
    return lax.broadcasted_iota(jnp.int32, (rows, 128), 0)


def stack_heads(pair, first):
    zero = jnp.zeros_like(pair)
    return jnp.concatenate([jnp.where(first, pair, zero), jnp.where(first, zero, pair)], axis=0)


def tiles_of(low, high, length, visit):
    base = (low // 16) * 16
    span = high - base
    whole_tiles = (span + TILE - 1 - SMALL) // TILE
    rest = span - whole_tiles * TILE

    def per_tile(i, carry):
        begin = base + i * TILE
        visit(TILE, pl.multiple_of(jnp.minimum(begin, length - TILE), 16), jnp.maximum(low, begin))
        return carry

    lax.fori_loop(0, whole_tiles, per_tile, 0)

    @pl.when(rest > 0)
    def _():
        begin = base + whole_tiles * TILE
        visit(SMALL, pl.multiple_of(jnp.minimum(begin, length - SMALL), 16), jnp.maximum(low, begin))


def each_segment(bounds, q_row, k_row, visit):
    def per_segment(s, carry):
        visit(bounds[q_row, s], bounds[q_row, s + 1], bounds[k_row, s], bounds[k_row, s + 1])
        return carry

    lax.fori_loop(0, SEGMENTS, per_segment, 0)


def pair_lanes(offset, p):
    if isinstance(p, int):
        return slice(offset + p * 128, offset + p * 128 + 128)
    return pl.ds(pl.multiple_of(offset + p * 128, 128), 128)


def inside_rows(size, start, low, high):
    rows = row_index(size) + start
    return (rows >= low) & (rows < high)


def attend(bounds, q_row, k_row, query, keys, values, out_ref, tail_ref):
    (q_ref, q_col), (k_ref, k_col), (v_ref, v_col) = query, keys, values
    length, width = out_ref.shape
    pairs = range(width // 128)

    def visit(size, start, low, high, k_low, k_high):
        lanes = lane_index(size)
        first = lanes < HEAD_DIM
        owner, place = lanes // 4, lanes % 4
        unit = jnp.where(lane_index(2 * size) == 0, 1.0, 0.0).astype(BF16)
        keep = inside_rows(size, start, low, high)
        span = pl.ds(start, size)
        k_base = (k_low // 16) * 16
        k_tiles = (k_high - k_base + TILE - 1) // TILE

        def piece(p, k_size, k_start, low_k):
            inside = inside_rows(k_size, k_start, low_k, k_high)
            shut = (lane_index(k_size) == 0) & jnp.logical_not(inside)
            bias = jnp.where(shut, MASKED, 0.0).astype(BF16)
            queries = stack_heads(q_ref[span, pair_lanes(q_col, p)], first)
            k_span = pl.ds(k_start, k_size)
            pair_k = k_ref[k_span, pair_lanes(k_col, p)]
            pair_v = v_ref[k_span, pair_lanes(v_col, p)]
            scores = dot_bt(
                jnp.concatenate([queries, unit], axis=1), jnp.concatenate([pair_k, bias], axis=1)
            )
            ones = jnp.ones((k_size, 128), BF16)
            return scores, jnp.concatenate([pair_v, ones], axis=1)

        def finish(p, highest, total, stats):
            cols = pair_lanes(0, p)
            top, bottom = total[:size], total[size:]
            mass = jnp.where(first, top[:, 128:], bottom[:, 128:])
            merged = lower(jnp.where(first, top[:, :128], bottom[:, :128]) / mass)
            out_ref[span, cols] = jnp.where(keep, merged, out_ref[span, cols])
            peak, sums = stats
            for h, half in ((0, slice(0, size)), (1, slice(size, 2 * size))):
                here = owner == 2 * p + h
                peak = jnp.where(here, highest[half], peak)
                sums = jnp.where(here, total[half, 128:], sums)
            return peak, sums

        empty = (jnp.zeros((size, 128), F32), jnp.ones((size, 128), F32))

        def close(stats):
            peak, sums = stats
            tail = split_lanes(peak + jnp.log(sums), place, 1.0)
            tail_ref[span, :] = jnp.where(keep, tail, tail_ref[span, :])

        def rolled(one):
            close(lax.fori_loop(0, len(pairs), lambda p, stats: finish(p, *one(p), stats), empty))

        def direct(k_size):
            k_start = pl.multiple_of(jnp.minimum(k_base, length - k_size), 16)

            items = [piece(p, k_size, k_start, k_low) for p in pairs]
            tops = [jnp.max(item[0], -1, keepdims=True) for item in items]
            probs = [lower(jnp.exp(item[0] - top)) for item, top in zip(items, tops)]
            totals = [dot(prob, item[1]) for prob, item in zip(probs, items)]
            stats = empty
            for p in pairs:
                stats = finish(p, tops[p], totals[p], stats)
            close(stats)

        if size < TILE:

            @pl.when(k_tiles <= 2)
            def _():
                direct(2 * TILE)

        else:

            @pl.when(k_tiles == 1)
            def _():
                direct(TILE)

            @pl.when(k_tiles == 2)
            def _():
                direct(2 * TILE)

        @pl.when(k_tiles > 2)
        def _():
            def one(p):
                def per_key(j, carry):
                    highest, total = carry
                    begin = k_base + j * TILE
                    k_start = pl.multiple_of(jnp.minimum(begin, length - TILE), 16)
                    scores, wide_v = piece(p, TILE, k_start, jnp.maximum(k_low, begin))
                    newest = jnp.maximum(highest, jnp.max(scores, -1, keepdims=True))
                    expon = lower(jnp.exp(scores - newest))
                    return newest, total * jnp.exp(highest - newest) + dot(expon, wide_v)

                start_at = (jnp.full((2 * size, 1), MASKED, F32), jnp.zeros((2 * size, 256), F32))
                return lax.fori_loop(0, k_tiles, per_key, start_at)

            rolled(one)

    def segment(q_low, q_high, k_low, k_high):
        tiles_of(
            q_low, q_high, length, lambda size, start, low: visit(size, start, low, q_high, k_low, k_high)
        )

    each_segment(bounds, q_row, k_row, segment)


def split_lanes(values, place, lead):
    high = lower(values).astype(F32)
    rest = values - high
    middle = lower(rest).astype(F32)
    spread = jnp.where(place == 1, high, jnp.where(place == 2, middle, rest - middle))
    return lower(jnp.where(place == 0, lead, -spread))


def attend_back(bounds, q_row, k_row, query, keys, values, do_ref, out_ref, tail_ref, dq, dk, dv):
    (q_ref, q_col), (k_ref, k_col), (v_ref, v_col) = query, keys, values
    (dq_ref, dq_col), (dk_ref, dk_col), (dv_ref, dv_col) = dq, dk, dv
    length, width = do_ref.shape
    pairs = width // 128
    zero = jnp.zeros((), BF16)
    lane = lane_index(width)
    collect = (lane % 4 > 0) & (lane // 4 == row_index(width) // HEAD_DIM)
    collect = jnp.where(collect, 1.0, 0.0).astype(BF16)

    def visit(size, start, low, high, k_low, k_high):
        lanes = lane_index(size)
        first = lanes < HEAD_DIM
        owner, place = lanes // 4, lanes % 4
        closed = lower(jnp.where(place == 0, 1.0, jnp.where(place == 1, MASKED, 0.0)))
        keep = inside_rows(size, start, low, high)
        span = pl.ds(start, size)
        tail_q = jnp.where(keep, tail_ref[span, :], closed)
        centre = jnp.zeros((size, 128), F32)
        for p in range(pairs):
            cols = slice(p * 128, (p + 1) * 128)
            grad = jnp.where(keep, do_ref[span, cols], zero)
            inner = grad.astype(F32) * out_ref[span, cols].astype(F32)
            coarse = lower(inner)
            fine = lower(inner - coarse.astype(F32))
            centre = centre + dot(
                jnp.concatenate([coarse, fine], axis=1),
                jnp.concatenate([collect[cols], collect[cols]], axis=0),
            )
        tail_g = split_lanes(centre, place, 0.0)

        def per_key(k_size, k_start, low_k):
            k_span = pl.ds(k_start, k_size)
            inside = inside_rows(k_size, k_start, low_k, k_high)
            lead = lane_index(k_size) % 4 == 0
            tail = lower(jnp.where(lead, jnp.where(inside, 0.0, MASKED), 1.0))

            def load(p):
                pair_q = q_ref[span, pair_lanes(q_col, p)]
                pair_k = k_ref[k_span, pair_lanes(k_col, p)]
                pair_v = v_ref[k_span, pair_lanes(v_col, p)]
                pair_do = jnp.where(keep, do_ref[span, pair_lanes(0, p)], zero)
                queries = stack_heads(pair_q, first)
                grads = stack_heads(pair_do, first)
                ends = [
                    jnp.concatenate(
                        [jnp.where(owner == 2 * p, item, zero), jnp.where(owner == 2 * p + 1, item, zero)],
                        axis=0,
                    )
                    for item in (tail_q, tail_g)
                ]
                scores = dot_bt(
                    jnp.concatenate([pair_k, tail], axis=1),
                    jnp.concatenate([queries, ends[0]], axis=1),
                )
                slope = dot_bt(
                    jnp.concatenate([pair_v, tail], axis=1),
                    jnp.concatenate([grads, ends[1]], axis=1),
                )
                return pair_k, queries, grads, scores, slope

            def middle(item):
                pair_k, queries, grads, scores, slope = item
                probs = jnp.exp(scores)
                return pair_k, queries, grads, lower(probs), lower(probs * slope)

            def store(p, pair_k, queries, grads, probs, ds):
                dv_ref[k_span, pair_lanes(dv_col, p)] += dot(probs, grads)
                dk_ref[k_span, pair_lanes(dk_col, p)] += dot(ds, queries)
                turned = [dot_at(ds[:, :size], pair_k), dot_at(ds[:, size:], pair_k)]
                dq_ref[span, pair_lanes(dq_col, p)] += jnp.where(first, turned[0], turned[1])

            ahead = load(0)
            for p in range(pairs):
                item = ahead
                if p + 1 < pairs:
                    ahead = load(p + 1)
                store(p, *middle(item))

        tiles_of(k_low, k_high, length, per_key)

    def segment(q_low, q_high, k_low, k_high):
        tiles_of(
            q_low, q_high, length, lambda size, start, low: visit(size, start, low, q_high, k_low, k_high)
        )

    each_segment(bounds, q_row, k_row, segment)


def forward_kernel(bounds, xs, block, norms, w_self, w_query, attended, tail, y1, q2, queries):
    phase = pl.program_id(1)
    length, width = queries.shape

    @pl.when(phase == 0)
    def _():
        queries[...] = block[0, :, :width]

    attend(
        bounds, 0, phase, (queries, 0), (block.at[0], width), (block.at[0], 2 * width),
        attended.at[0, 0], tail.at[0, 0],
    )

    @pl.when(phase == 0)
    def _():
        for i in range(length // TILE):
            span = slice(i * TILE, (i + 1) * TILE)
            after = xs[0, span, :].astype(F32) + dot(attended[0, 0, span, :], w_self[...])
            y1[0, span, :] = after
            xhat, _ = standardise(after)
            h2 = lower(xhat * norms[1:2, :] + norms[4:5, :])
            asked = lower(dot(h2, w_query[...]) * HEAD_DIM ** (-0.5))
            queries[span, :] = asked
            q2[0, span, :] = asked


def feed_kernel(
    per_step, y1, a2, g1, g2, norms, w_cross, w_in, w_out,
    o1, o2, h3, r, du, e2, dy2, do2, dnorm,
):
    i = pl.program_id(0)
    width = w_cross.shape[0]
    is_first = i < per_step
    grad = jnp.where(is_first, g1[...], g2[...])
    after = y1[0] + dot(a2[0, 0], w_cross[...])
    xhat, inverse = standardise(after)
    normed = lower(xhat * norms[2:3, :] + norms[5:6, :])
    h3[0] = normed
    result = after
    dh3 = jnp.zeros_like(after)
    slope = (2.0 / jnp.pi) ** 0.5
    chunks = w_in.shape[1] // width

    def enter(c):
        cols = slice(c * width, (c + 1) * width)
        return dot(normed, w_in[:, cols]), dot_bt(grad, w_out[cols, :])

    ahead = enter(0)
    for c in range(chunks):
        cols = slice(c * width, (c + 1) * width)
        u, dr = ahead
        if c + 1 < chunks:
            ahead = enter(c + 1)
        square = u * u
        half = 0.5 + 0.5 * jnp.tanh(u * (slope + slope * 0.044715 * square))
        hidden = lower(u * half)
        r[0, :, cols] = hidden
        bend = u * (2 * slope + 6 * slope * 0.044715 * square)
        pre = lower(dr * (half * (1.0 + (1.0 - half) * bend)))
        du[0, :, cols] = pre
        result = result + dot(hidden, w_out[cols, :])
        dh3 = dh3 + dot_bt(pre, w_in[:, cols])

    @pl.when(is_first)
    def _():
        o1[...] = lower(result)

    @pl.when(jnp.logical_not(is_first))
    def _():
        o2[...] = lower(result)

    @pl.when(i == 0)
    def _():
        dnorm[...] = jnp.zeros_like(dnorm)

    dnorm[0] += fold_rows(dh3 * xhat)
    dnorm[1] += fold_rows(dh3)
    back = grad.astype(F32) + norm_back(xhat, inverse, norms[2:3, :], dh3)
    dy2[0] = back
    low = lower(back)
    e2[0] = low
    do2[0] = lower(dot_bt(low, w_cross[...]))


def feed_grad_kernel(
    small, h3, g1, g2, du, r, a2_hbm, e2_hbm, mine, theirs,
    turned, turned_g, a2, e2, d_in, d_out, d_cross, sem,
):
    c = pl.program_id(0)
    last = pl.num_programs(0) - 1
    half, width = g1.shape
    hidden = d_out.shape[4]
    group = hidden // width
    rows = width // group
    slot = lax.rem(c, 2)

    core = lax.rem(lax.axis_index("wide"), 2)
    lines = width // (2 * small)
    depth = rows // (2 * small)

    def copies(at, chunk):
        cols = pl.ds(pl.multiple_of(chunk * width, width), width)
        deep = pl.ds(chunk * depth, depth)
        found = []
        for k, (out, side) in enumerate(((mine, core), (theirs, 1 - core))):
            found.append(
                pltpu.make_async_copy(d_in.at[at, :, side], out.at[:, :, cols], sem.at[2 * k, at])
            )
            found.append(
                pltpu.make_async_copy(
                    d_out.at[at, :, side], out.at[deep, :, hidden + width :], sem.at[2 * k + 1, at]
                )
            )
        return found

    loads = [
        pltpu.make_async_copy(a2_hbm.at[:, 1], a2, sem.at[4, 0]),
        pltpu.make_async_copy(e2_hbm, e2, sem.at[4, 1]),
    ]
    cross = [
        pltpu.make_async_copy(
            d_cross.at[:, side], out.at[:, :, hidden : hidden + width], sem.at[5, k]
        )
        for k, (out, side) in enumerate(((mine, core), (theirs, 1 - core)))
    ]

    @pl.when(c >= 2)
    def _():
        for copy in copies(slot, c - 2):
            copy.wait()

    @pl.when(c == 0)
    def _():
        for copy in loads:
            copy.start()
        turned[...] = h3[...].T
        turned_g[:, :half] = g1[...].T
        turned_g[:, half:] = g2[...].T

    d_in[slot] = lower(dot(turned[...], du[...])).reshape(d_in.shape[1:])
    part = lower(dot(turned_g[...], r[...])).T
    for w in range(width // (group * small)):
        for j in range(group):
            at = (w * group + j) * small
            d_out[slot, w // 2, w % 2, :, j * width : (j + 1) * width] = part[at : at + small]
    for copy in copies(slot, c):
        copy.start()

    @pl.when(c == last)
    def _():
        wait_all(loads)
        d_cross[...] = lower(dot(a2[0].T, e2[0]) + dot(a2[1].T, e2[1])).reshape(d_cross.shape)
        for copy in cross:
            copy.start()
        for copy in copies(1 - slot, c - 1) + copies(slot, c):
            copy.wait()
        wait_all(cross)


def cross_back_kernel(
    bounds, q2, keys, values, a1, a2, stat2, do2, y1, dy2, mem_turned, norms, w_query, w_self, w_kv,
    dy1, do1, d_query, d_self, d_kv, d_mem, dnorm,
    dq_sum, dkv_sum, h2, low_q, low_e,
):
    step = pl.program_id(0)
    length, width = q2.shape[1:]

    @pl.when(step == 0)
    def _():
        dkv_sum[...] = jnp.zeros_like(dkv_sum)
        dnorm[...] = jnp.zeros_like(dnorm)

    dq_sum[...] = jnp.zeros_like(dq_sum)
    attend_back(
        bounds, 0, 1, (q2.at[0], 0), (keys.at[0], 0), (values.at[0], 0), do2.at[0], a2.at[0, 0], stat2.at[0, 0],
        (dq_sum, 0), (dkv_sum, 0), (dkv_sum, width),
    )

    def rows(i):
        span = slice(i * TILE, (i + 1) * TILE)
        grad_q = lower(dq_sum[span, :] * HEAD_DIM ** (-0.5))
        low_q[step, span, :] = grad_q
        xhat, inverse = standardise(y1[0, span, :])
        h2[step, span, :] = lower(xhat * norms[1:2, :] + norms[4:5, :])
        dh2 = dot_bt(grad_q, w_query[...])
        dnorm[0] += fold_rows(dh2 * xhat)
        dnorm[1] += fold_rows(dh2)
        back = dy2[0, span, :] + norm_back(xhat, inverse, norms[1:2, :], dh2)
        dy1[0, span, :] = back
        low = lower(back)
        low_e[step, span, :] = low
        do1[0, span, :] = lower(dot_bt(low, w_self[...]))

    for i in range(length // TILE):
        rows(i)

    @pl.when(step == 1)
    def _():
        d_query[...] = lower(dot(h2[0].T, low_q[0]) + dot(h2[1].T, low_q[1]))
        d_self[...] = lower(dot(a1[0, 0].T, low_e[0]) + dot(a1[1, 0].T, low_e[1]))
        pair = lower(dkv_sum[...])
        d_kv[...] = lower(dot(mem_turned[...], pair))
        d_mem[...] = dot_bt(pair, w_kv[...])


def self_back_kernel(bounds, qkv, a1, stat1, do1, low, sums):
    width = do1.shape[2]
    sums[...] = jnp.zeros_like(sums)
    attend_back(
        bounds, 0, 0, (qkv.at[0], 0), (qkv.at[0], width), (qkv.at[0], 2 * width),
        do1.at[0], a1.at[0, 0], stat1.at[0, 0], (sums, 0), (sums, width), (sums, 2 * width),
    )
    low[0, :, :width] = lower(sums[:, :width] * HEAD_DIM ** (-0.5))
    low[0, :, width:] = lower(sums[:, width:])


def flip(index, mask):
    out, bit = index, 1
    while bit <= mask:
        if mask & bit:
            out = out + bit - 2 * bit * lax.rem(lax.div(index, bit), 2)
        bit *= 2
    return out


class Links:
    def __init__(self, sizes, send, recv):
        self.members, wides = sizes
        self.lines = wides // 2
        self.group = min(4, self.members)
        self.narrow, self.wide = lax.axis_index("narrow"), lax.axis_index("wide")
        self.line, self.core = lax.div(self.wide, 2), lax.rem(self.wide, 2)
        self.part = lax.rem(self.narrow, self.group)
        self.send, self.recv, self.used = send, recv, 0

    def core_peer(self):
        return (self.narrow, flip(self.wide, 1))

    def plane_peer(self, mask):
        return (flip(self.narrow, mask), self.wide)

    def line_peer(self, mask):
        return (self.narrow, 2 * flip(self.line, mask) + self.core)

    def far_masks(self):
        masks, mask = [], self.group
        while mask < self.members:
            masks.append(mask)
            mask *= 2
        return masks

    def barrier(self, far):
        semaphore = pltpu.get_barrier_semaphore()
        peers = [self.core_peer()]
        peers += [self.plane_peer(m) for m in range(1, self.group)]
        peers += [self.line_peer(m) for m in range(1, self.lines)]
        if far:
            peers += [self.plane_peer(m) for m in self.far_masks()]
        for peer in peers:
            pl.semaphore_signal(semaphore, inc=1, device_id=peer, device_id_type=MESH)
        pl.semaphore_wait(semaphore, len(peers))

    def push(self, src, dst, peer):
        slot = self.used
        self.used += 1
        copy = pltpu.make_async_remote_copy(
            src_ref=src,
            dst_ref=dst,
            send_sem=self.send.at[slot],
            recv_sem=self.recv.at[slot],
            device_id=peer,
            device_id_type=MESH,
        )
        copy.start()
        return copy

    def quarter(self, part, cols):
        size = cols // self.group
        return pl.ds(pl.multiple_of(part * size, size), size)


def wait_all(copies):
    for copy in copies:
        copy.wait()


class Gathered:
    def __init__(self, links, shard, full):
        self.links, self.shard, self.full = links, shard, full
        self.cols = shard.shape[-1]

    def start_line(self):
        links = self.links
        self.full[links.line, links.core] = self.shard[...]
        mine = links.quarter(links.part, self.cols)
        self.copies = [
            links.push(
                self.shard.at[:, mine], self.full.at[links.line, links.core, :, mine], links.line_peer(m)
            )
            for m in range(1, links.lines)
        ]

    def start_plane(self):
        links = self.links
        wait_all(self.copies)
        mine = links.quarter(links.part, self.cols)
        self.copies = []
        for k in range(1, links.lines):
            place = self.full.at[flip(links.line, k), links.core, :, mine]
            for m in range(1, links.group):
                self.copies.append(links.push(place, place, links.plane_peer(m)))

    def start_core(self):
        links = self.links
        wait_all(self.copies)
        place = self.full.at[:, links.core]
        self.copies = [links.push(place, place, links.core_peer())]

    def finish(self):
        wait_all(self.copies)


def gather_slots(sizes, pieces):
    lines, group = sizes[1] // 2, min(4, sizes[0])
    return pieces * (lines - 1 + (lines - 1) * (group - 1) + 1) + lines


def gather_kernel(
    sizes, x1, x2, mem, norm, s_qkv, s_kv, s_self, s_query, s_cross, s_in, s_out,
    xs, blocks, norms, h1_turned, mem_turned, f_qkv, f_kv, f_self, f_query, f_cross, f_in, f_out,
    h1, turned, turned_mem, v_qkv, v_kv, v_self, v_query, v_cross, v_in, v_out, o_qkv, o_kv, norm_all, send, recv, local,
):
    links = Links(sizes, send, recv)
    length, width = x1.shape
    used = [0]

    def local_copy(src, dst):
        copy = pltpu.make_async_copy(src, dst, local.at[used[0]])
        used[0] += 1
        copy.start()
        return copy

    landing = []

    def piece(shard, full, out):
        landing.append((full, out))
        return Gathered(links, shard, full)

    links.barrier(False)
    pieces = []
    for c in range(3):
        cols = slice(c * width, (c + 1) * width)
        pieces.append(piece(s_qkv.at[:, cols], v_qkv.at[c], f_qkv.at[:, :, :, cols]))
    for c in range(2):
        cols = slice(c * width, (c + 1) * width)
        pieces.append(piece(s_kv.at[:, cols], v_kv.at[c], f_kv.at[:, :, :, cols]))
    pieces.append(piece(s_self, v_self, f_self))
    pieces.append(piece(s_query, v_query, f_query))
    pieces.append(piece(s_cross, v_cross, f_cross))
    half = s_in.shape[1] // 2
    for c in range(2):
        cols = slice(c * half, (c + 1) * half)
        pieces.append(piece(s_in.at[:, cols], v_in.at[c], f_in.at[:, :, :, cols]))
    half = s_out.shape[0] // 2
    for c in range(2):
        rows = slice(c * half, (c + 1) * half)
        pieces.append(piece(s_out.at[rows], v_out.at[c], f_out.at[:, :, rows]))

    norm_all[links.line, links.core] = norm[...]
    own = norm_all.at[links.line, links.core]
    norm_copies = [links.push(own, own, links.line_peer(m)) for m in range(1, links.lines)]
    for p in range(2):
        pieces[p].start_line()
    outgoing = [local_copy(x1, xs.at[0]), local_copy(x2, xs.at[1])]
    pieces[2].start_line()
    wait_all(norm_copies)
    place = norm_all.at[:, links.core]
    norm_copy = links.push(place, place, links.core_peer())
    pieces[0].start_plane()
    norm_copy.wait()
    every = norm_all[...]
    total = every[0, 0]
    for k in range(1, 2 * links.lines):
        total = total + every[k // 2, k % 2]
    norms[...] = total
    gain, shift = total[0:1, :], total[3:4, :]

    def normalise(t, x):
        for i in range(length // TILE):
            span = slice(i * TILE, (i + 1) * TILE)
            xhat, _ = standardise(x[span, :].astype(F32))
            h1[t, span, :] = lower(xhat * gain + shift)

    def turn():
        turned[:, :length] = h1[0].T
        turned[:, length:] = h1[1].T
        turned_mem[...] = mem[...].T
        outgoing.append(local_copy(turned, h1_turned))
        outgoing.append(local_copy(turned_mem, mem_turned))

    def project(c):
        def run():
            weight = v_qkv[c].reshape(width, width)
            scale = HEAD_DIM ** (-0.5) if c == 0 else 1.0
            for t in range(2):

                def rows(i, carry, t=t):
                    span = pl.ds(pl.multiple_of(i * 2 * TILE, 2 * TILE), 2 * TILE)
                    o_qkv[c, t, span, :] = lower(dot(h1[t, span, :], weight) * scale)
                    return carry

                lax.fori_loop(0, length // (2 * TILE), rows, 0)
            cols = slice(c * width, (c + 1) * width)
            outgoing.append(local_copy(o_qkv.at[c], blocks.at[0:2, :, cols]))

        return run

    def project_memory(c):
        def run():
            weight = v_kv[c].reshape(width, width)

            def rows(i, carry):
                span = pl.ds(pl.multiple_of(i * 2 * TILE, 2 * TILE), 2 * TILE)
                o_kv[c, span, :] = lower(dot(mem[span, :], weight))
                return carry

            lax.fori_loop(0, length // (2 * TILE), rows, 0)
            cols = slice((c + 1) * width, (c + 2) * width)
            outgoing.append(local_copy(o_kv.at[c], blocks.at[2, :, cols]))

        return run

    work = {c: project(c) for c in range(3)} | {3 + c: project_memory(c) for c in range(2)}
    count = len(pieces)
    for t in range(3, count + 6):
        if t < count:
            pieces[t].start_line()
        if 1 <= t - 2 < count:
            pieces[t - 2].start_plane()
        if t == 3:
            normalise(0, x1)
        if t == 4:
            normalise(1, x2)
        if 0 <= t - 4 < count:
            pieces[t - 4].start_core()
        if 0 <= t - 5 < count:
            pieces[t - 5].finish()
            outgoing.append(local_copy(*landing[t - 5]))
            if t - 5 in work:
                work[t - 5]()
            if t - 5 == 5:
                turn()
    wait_all(outgoing)


class Reduced:
    def __init__(self, links, bufs, out, source=None, ready=None):
        self.links, self.out, self.source, self.ready = links, out, source, ready
        self.lined = source is not None or ready is not None
        self.crecv, self.chip, self.precv, self.plane, self.lrecv, self.mine, self.xrecv, self.full = bufs
        self.cols = self.full.shape[-1]

    def start_core(self):
        links = self.links
        self.copies = [links.push(self.source.at[:, 1 - links.core], self.crecv, links.core_peer())]

    def start_plane(self):
        links = self.links
        if self.source is not None:
            wait_all(self.copies)
            for k in range(links.lines):
                self.chip[k] = lower(
                    self.source[k, links.core].astype(F32) + self.crecv[k].astype(F32)
                )
        self.copies = [
            links.push(
                self.chip.at[:, :, links.quarter(flip(links.part, m), self.cols)],
                self.precv.at[m - 1],
                links.plane_peer(m),
            )
            for m in range(1, links.group)
        ]

    def start_line(self):
        links = self.links
        if self.ready is not None:
            total = self.ready[0][...].astype(F32)
            for item in self.ready[1:]:
                total = total + item[...].astype(F32)
        else:
            wait_all(self.copies)
            total = self.chip[:, :, links.quarter(links.part, self.cols)].astype(F32)
            for m in range(1, links.group):
                total = total + self.precv[m - 1].astype(F32)
        self.plane[...] = lower(total)
        if not self.lined:
            self.copies = []
            return
        self.copies = [
            links.push(self.plane.at[flip(links.line, m)], self.lrecv.at[m - 1], links.line_peer(m))
            for m in range(1, links.lines)
        ]

    def start_gather(self):
        links = self.links
        wait_all(self.copies)
        if not self.lined:
            total = self.plane[0].astype(F32)
        else:
            total = self.plane[links.line].astype(F32)
            for m in range(1, links.lines):
                total = total + self.lrecv[m - 1].astype(F32)
        for i, mask in enumerate(links.far_masks()):
            self.xrecv[2 * i] = lower(total)
            links.push(self.xrecv.at[2 * i], self.xrecv.at[2 * i + 1], links.plane_peer(mask)).wait()
            total = self.xrecv[2 * i].astype(F32) + self.xrecv[2 * i + 1].astype(F32)
        self.mine[...] = lower(total)
        place = self.full.at[:, links.quarter(links.part, self.cols)]
        place[...] = self.mine[...]
        self.copies = [links.push(self.mine, place, links.plane_peer(m)) for m in range(1, links.group)]

    def finish(self):
        wait_all(self.copies)
        self.out[...] = self.full[...]


class LineFirst:
    def __init__(self, links, bufs, source, then):
        self.links, self.source, self.then = links, source, then
        self.crecv, self.chip, self.lrecv = bufs

    def start_core(self):
        links = self.links
        self.copies = [links.push(self.source.at[:, 1 - links.core], self.crecv, links.core_peer())]

    def start_line(self):
        links = self.links
        wait_all(self.copies)
        for k in range(links.lines):
            self.chip[k] = lower(self.source[k, links.core].astype(F32) + self.crecv[k].astype(F32))
        self.copies = [
            links.push(self.chip.at[flip(links.line, m)], self.lrecv.at[m - 1], links.line_peer(m))
            for m in range(1, links.lines)
        ]

    def start_plane(self):
        links = self.links
        wait_all(self.copies)
        total = self.chip[links.line].astype(F32)
        for m in range(1, links.lines):
            total = total + self.lrecv[m - 1].astype(F32)
        self.then.chip[0] = lower(total)
        self.then.start_plane()


def reduced_scratch(sizes, rows, cols, kind):
    members, wides = sizes
    lines, group = wides // 2, min(4, members)
    part = cols // group
    depth = 1 if kind == "shard" else lines
    far = max(2, 2 * (members // group - 1))
    small = (1, 16, 128)
    return [
        pltpu.VMEM((lines, rows, cols) if kind == "whole" else small, BF16),
        pltpu.VMEM(small if kind == "ready" else (depth, rows, cols), BF16),
        pltpu.VMEM(small if kind == "ready" else (group - 1, depth, rows, part), BF16),
        pltpu.VMEM((depth, rows, part), BF16),
        pltpu.VMEM(small if kind == "shard" else (lines - 1, rows, part), BF16),
        pltpu.VMEM((rows, part), BF16),
        pltpu.VMEM((far, rows, part), BF16),
        pltpu.VMEM((rows, cols), BF16),
    ]


def reduce_slots(sizes, jobs):
    members, wides = sizes
    lines, group = wides // 2, min(4, members)
    return (jobs + 1) * (1 + 2 * (group - 1) + lines - 1 + members // group)


BUFS = 8


def finish_kernel(
    sizes, low_hbm, h1_hbm, xs_hbm, dy1_hbm, w_hbm, norms, d_self, d_query, d_kv, dnorm1, dnorm2, *rest,
):
    group = min(4, sizes[0])
    ready, rest = rest[:group], rest[group:]
    gi1, gi2, t_qkv, t_self, t_query, t_kv, t_joint, t_norm = rest[:8]
    low, xs, dy1, w_qkv, h1, grads, norm_slots = rest[8:15]
    bufs, first_bufs = rest[15:-6], rest[-6:-3]
    send, recv, local = rest[-3:]
    links = Links(sizes, send, recv)
    _, length, width = xs.shape
    loads = [
        pltpu.make_async_copy(h1_hbm, h1, local.at[0]),
        pltpu.make_async_copy(low_hbm, low, local.at[1]),
        pltpu.make_async_copy(xs_hbm, xs, local.at[2]),
        pltpu.make_async_copy(dy1_hbm, dy1, local.at[3]),
        pltpu.make_async_copy(w_hbm, w_qkv, local.at[4]),
    ]
    for copy in loads:
        copy.start()
    links.barrier(True)

    taken = [0]

    def job(out, **kind):
        at = taken[0] * BUFS
        taken[0] += 1
        return Reduced(links, bufs[at : at + BUFS], out, **kind)

    others = [job(t_kv, source=d_kv), job(t_query, source=d_query)]
    heads = [job(t_qkv.at[:, c * width : (c + 1) * width], source=grads.at[c]) for c in range(3)]
    joint = job(t_joint, ready=ready)
    late = job(t_self)
    before = LineFirst(links, first_bufs, d_self, late)
    for one in others + [before]:
        one.start_core()
    joint.start_line()
    gain = norms[0:1, :]
    loads[0].wait()
    loads[1].wait()
    for c in range(3):
        cols = slice(c * width, (c + 1) * width)
        value = dot(h1[:, :length], low[0, :, cols]) + dot(h1[:, length:], low[1, :, cols])
        grads[c] = lower(value).reshape(grads.shape[1:])
        heads[c].start_core()
        if c > 0:
            heads[c - 1].start_plane()
        if c == 0:
            for one in others:
                one.start_plane()
            before.start_line()
    heads[2].start_plane()
    wait_all(loads[2:])
    stores = []
    dgain = jnp.zeros((8, width), F32)
    dshift = jnp.zeros((8, width), F32)
    steps = [
        lambda: [one.start_line() for one in others],
        lambda: joint.start_gather(),
        lambda: heads[0].start_line(),
        lambda: before.start_plane(),
        lambda: heads[1].start_line(),
        lambda: heads[2].start_line(),
        lambda: [one.start_gather() for one in others],
        lambda: joint.finish(),
    ]
    weight = w_qkv[...]
    for t in range(2):
        for i in range(length // TILE):
            span = slice(i * TILE, (i + 1) * TILE)
            xhat, inverse = standardise(xs[t, span, :].astype(F32))
            dh1 = dot_bt(low[t, span, :], weight)
            dgain = dgain + fold_rows(dh1 * xhat)
            dshift = dshift + fold_rows(dh1)
            dy1[t, span, :] = dy1[t, span, :] + norm_back(xhat, inverse, gain, dh1)
            out = (gi1, gi2)[t]
            number = t * (length // TILE) + i
            copy = pltpu.make_async_copy(dy1.at[t, span, :], out.at[span, :], local.at[5 + number])
            copy.start()
            stores.append(copy)
            if number < len(steps):
                steps[number]()
    rows = [jnp.sum(item, axis=0, keepdims=True) for item in (dgain, dnorm1[0], dnorm2[0], dshift, dnorm1[1], dnorm2[1])]
    total = jnp.concatenate(rows + [jnp.zeros((2, width), F32)], axis=0)

    def swap(first, count, own, peers, total):
        norm_slots[first + own] = total
        place = norm_slots.at[first + own]
        wait_all([links.push(place, place, peer) for peer in peers])
        out = norm_slots[first]
        for k in range(1, count):
            out = out + norm_slots[first + k]
        return out

    total = swap(0, 2, links.core, [links.core_peer()], total)
    for one in heads:
        one.start_gather()
    late.start_line()
    late.start_gather()
    total = swap(2, links.group, links.part, [links.plane_peer(m) for m in range(1, links.group)], total)
    first = 2 + links.group
    total = swap(first, links.lines, links.line, [links.line_peer(m) for m in range(1, links.lines)], total)
    first += links.lines
    for mask in links.far_masks():
        side = lax.rem(lax.div(links.narrow, mask), 2)
        total = swap(first, 2, side, [links.plane_peer(mask)], total)
        first += 2
    t_norm[...] = total
    for one in heads + others + [late]:
        one.finish()
    wait_all(stores)


def emit_kernel(
    wides, f1, f2, b_qkv, b_self, b_query, b_kv, b_joint, t_norm,
    gi1, gi2, gain, shift, t_qkv, t_self, t_query, t_kv, t_in, t_out, t_cross,
):
    gi1[...] = f1[...]
    gi2[...] = f2[...]
    width = gi1.shape[1]
    small, hidden = t_in.shape

    @pl.when(pl.program_id(0) == 0)
    def _():
        for src, dst in (
            (b_qkv, t_qkv), (b_self, t_self), (b_query, t_query), (b_kv, t_kv),
            (b_joint.at[:, :hidden], t_in), (b_joint.at[:, hidden : hidden + width], t_cross),
        ):
            dst[...] = src[...].astype(F32)
        for j in range(hidden // width):
            begin = hidden + width + j * width
            t_out[j * small : (j + 1) * small, :] = b_joint[:, begin : begin + width].astype(F32)
        at = lax.axis_index("wide") * small
        mine = pltpu.roll(t_norm[...], lax.rem(width - at, width), 1)
        gain[...] = mine[:3, :small]
        shift[...] = mine[3:6, :small]


def whole(shape):
    zeros = (0,) * len(shape)
    return pl.BlockSpec(shape, lambda *_: zeros, pipeline_mode=pl.Buffered(1))


def fixed(shape):
    zeros = (0,) * len(shape)
    return pl.BlockSpec(shape, lambda *_: zeros)


def by_step(shape):
    return pl.BlockSpec((1,) + shape, lambda t, *_: (t, 0, 0))


def params():
    return pltpu.CompilerParams(
        vmem_limit_bytes=VMEM_LIMIT, dimension_semantics=("arbitrary",)
    )


def struct(shape, dtype):
    return jax.ShapeDtypeStruct(shape, dtype)


def call_forward(bounds, xs, blocks, norms, w_self, w_query):
    length, width = xs.shape[1:]
    each = pl.BlockSpec((1, length, width), lambda t, p, *_: (t, 0, 0))
    return pl.pallas_call(
        forward_kernel,
        grid_spec=pltpu.PrefetchScalarGridSpec(
            num_scalar_prefetch=1,
            grid=(2, 2),
            in_specs=[
                each,
                pl.BlockSpec((1, length, 3 * width), lambda t, p, *_: (t + p * (2 - t), 0, 0)),
                whole((8, width)), whole(w_self.shape), whole(w_query.shape),
            ],
            out_specs=[
                pl.BlockSpec((1, 1, length, width), lambda t, p, *_: (t, p, 0, 0)),
                pl.BlockSpec((1, 1, length, 128), lambda t, p, *_: (t, p, 0, 0)),
                each, each,
            ],
            scratch_shapes=[pltpu.VMEM((length, width), BF16)],
        ),
        out_shape=[
            struct((2, 2, length, width), BF16),
            struct((2, 2, length, 128), BF16),
            struct((2, length, width), F32),
            struct((2, length, width), BF16),
        ],
        compiler_params=pltpu.CompilerParams(
            vmem_limit_bytes=VMEM_LIMIT, dimension_semantics=("arbitrary", "arbitrary")
        ),
        name="attend_forward",
    )(bounds, xs, blocks, norms, w_self, w_query)


def call_cross_back(bounds, q2, blocks, attended, tail, do2, y1, dy2, mem_turned, norms, w_query, w_self, w_kv):
    length, width = q2.shape[1:]
    norm_spec = whole((8, width))
    step_low = by_step((length, width))
    return pl.pallas_call(
        cross_back_kernel,
        grid_spec=pltpu.PrefetchScalarGridSpec(
            num_scalar_prefetch=1,
            grid=(2,),
            in_specs=[
                step_low,
                pl.BlockSpec((1, length, width), lambda *_: (2, 0, 1), pipeline_mode=pl.Buffered(1)),
                pl.BlockSpec((1, length, width), lambda *_: (2, 0, 2), pipeline_mode=pl.Buffered(1)),
                pl.BlockSpec((2, 1, length, width), lambda *_: (0, 0, 0, 0), pipeline_mode=pl.Buffered(1)),
                pl.BlockSpec((1, 1, length, width), lambda t, *_: (t, 1, 0, 0)),
                pl.BlockSpec((1, 1, length, 128), lambda t, *_: (t, 1, 0, 0)),
                step_low,
                step_low, step_low, whole(mem_turned.shape), norm_spec,
                whole(w_query.shape), whole(w_self.shape), whole(w_kv.shape),
            ],
            out_specs=[
                step_low, step_low, fixed((width, width)), fixed((width, width)), fixed((width, 2 * width)),
                fixed((length, width)), fixed((2, 8, width)),
            ],
            scratch_shapes=[
                pltpu.VMEM((length, width), F32),
                pltpu.VMEM((length, 2 * width), F32),
                pltpu.VMEM((2, length, width), BF16),
                pltpu.VMEM((2, length, width), BF16),
                pltpu.VMEM((2, length, width), BF16),
            ],
        ),
        out_shape=[
            struct((2, length, width), F32),
            struct((2, length, width), BF16),
            struct((width, width), BF16),
            struct((width, width), BF16),
            struct((width, 2 * width), BF16),
            struct((length, width), F32),
            struct((2, 8, width), F32),
        ],
        compiler_params=params(),
        cost_estimate=pl.CostEstimate(flops=45000000000, bytes_accessed=20000000, transcendentals=0),
        name="cross_back",
    )(bounds, q2, blocks, blocks, attended, attended, tail, do2, y1, dy2, mem_turned, norms, w_query, w_self, w_kv)


def call_self_back(bounds, blocks, attended, tail, do1):
    length, width = do1.shape[1:]
    norm_spec = whole((8, width))
    step_low = by_step((length, width))
    return pl.pallas_call(
        self_back_kernel,
        grid_spec=pltpu.PrefetchScalarGridSpec(
            num_scalar_prefetch=1,
            grid=(2,),
            in_specs=[
                by_step((length, 3 * width)),
                pl.BlockSpec((1, 1, length, width), lambda t, *_: (t, 0, 0, 0)),
                pl.BlockSpec((1, 1, length, 128), lambda t, *_: (t, 0, 0, 0)),
                step_low,
            ],
            out_specs=by_step((length, 3 * width)),
            scratch_shapes=[pltpu.VMEM((length, 3 * width), F32)],
        ),
        out_shape=struct((2, length, 3 * width), BF16),
        compiler_params=params(),
        cost_estimate=pl.CostEstimate(flops=30000000000, bytes_accessed=20000000, transcendentals=0),
        name="self_back",
    )(bounds, blocks, attended, tail, do1)


def call_gather(sizes, x1, x2, mem, norm, shards):
    length, width = x1.shape
    lines = sizes[1] // 2
    small = width // sizes[1]
    vmem = pl.BlockSpec(memory_space=pltpu.VMEM)
    anywhere = pl.BlockSpec(memory_space=pl.ANY)

    def full(shape):
        return struct((lines, 2, shape[0], shape[1]), BF16)

    pieces = 12
    slots = gather_slots(sizes, pieces)
    return pl.pallas_call(
        functools.partial(gather_kernel, sizes),
        in_specs=[vmem] * 11,
        out_specs=[anywhere] * 2 + [vmem] + [anywhere] * 9,
        out_shape=[
            struct((2, length, width), BF16),
            struct((3, length, 3 * width), BF16),
            struct((8, width), F32),
            struct((width, 2 * length), BF16),
            struct((width, length), BF16),
        ]
        + [full(item.shape) for item in shards],
        scratch_shapes=[
            pltpu.VMEM((2, length, width), BF16),
            pltpu.VMEM((width, 2 * length), BF16),
            pltpu.VMEM((width, length), BF16),
            pltpu.VMEM((3, lines, 2, small, width), BF16),
            pltpu.VMEM((2, lines, 2, small, width), BF16),
            pltpu.VMEM((lines, 2, small, width), BF16),
            pltpu.VMEM((lines, 2, small, width), BF16),
            pltpu.VMEM((lines, 2, small, width), BF16),
            pltpu.VMEM((2, lines, 2, small, shards[5].shape[1] // 2), BF16),
            pltpu.VMEM((2, lines, 2, shards[6].shape[0] // 2, width), BF16),
            pltpu.VMEM((3, 2, length, width), BF16),
            pltpu.VMEM((2, length, width), BF16),
            pltpu.VMEM((lines, 2, 8, width), F32),
            pltpu.SemaphoreType.DMA((slots,)),
            pltpu.SemaphoreType.DMA((slots,)),
            pltpu.SemaphoreType.DMA((pieces + 14,)),
        ],
        compiler_params=pltpu.CompilerParams(
            vmem_limit_bytes=VMEM_LIMIT, collective_id=0, has_side_effects=True
        ),
        name="gather_project",
    )(x1, x2, mem, norm, *shards)


def call_feed(y1, a2, g1, g2, norms, w_cross, w_in, w_out):
    length, width = g1.shape
    hidden = w_in.shape[1]
    tiles = length // FEED
    norm_spec = whole((8, width))
    step_tile = pl.BlockSpec((1, FEED, width), lambda i: (i // tiles, i % tiles, 0))
    step_wide = pl.BlockSpec((1, FEED, hidden), lambda i: (i // tiles, i % tiles, 0))
    early = pl.BlockSpec((FEED, width), lambda i: (jnp.minimum(i, tiles - 1), 0))
    late = pl.BlockSpec((FEED, width), lambda i: (jnp.maximum(i - tiles, 0), 0))
    return pl.pallas_call(
        functools.partial(feed_kernel, tiles),
        grid=(2 * tiles,),
        in_specs=[
            step_tile,
            pl.BlockSpec((1, 1, FEED, width), lambda i: (i // tiles, 1, i % tiles, 0)),
            early, late, norm_spec,
            whole(w_cross.shape), whole(w_in.shape), whole(w_out.shape),
        ],
        out_specs=[
            early, late, step_tile, step_wide, step_wide, step_tile, step_tile, step_tile,
            fixed((2, 8, width)),
        ],
        out_shape=[
            struct((length, width), BF16),
            struct((length, width), BF16),
            struct((2, length, width), BF16),
            struct((2, length, hidden), BF16),
            struct((2, length, hidden), BF16),
            struct((2, length, width), BF16),
            struct((2, length, width), F32),
            struct((2, length, width), BF16),
            struct((2, 8, width), F32),
        ],
        compiler_params=params(),
        name="feed_forward_back",
    )(y1, a2, g1, g2, norms, w_cross, w_in, w_out)


def call_feed_grads(small, h3, a2, e2, g1, g2, du, r):
    length, width = g1.shape
    hidden = r.shape[2]
    lines = width // (2 * small)
    flat = (2 * length, width)
    chunk = pl.BlockSpec((2 * length, width), lambda c: (0, c))
    return pl.pallas_call(
        functools.partial(feed_grad_kernel, small),
        grid=(hidden // width,),
        in_specs=[whole(flat), whole((length, width)), whole((length, width)), chunk, chunk]
        + [pl.BlockSpec(memory_space=pl.ANY)] * 2,
        out_specs=[pl.BlockSpec(memory_space=pl.ANY)] * 2,
        out_shape=[struct((lines, small, 2 * hidden + width), BF16)] * 2,
        scratch_shapes=[
            pltpu.VMEM((width, 2 * length), BF16),
            pltpu.VMEM((width, 2 * length), BF16),
            pltpu.VMEM((2, length, width), BF16),
            pltpu.VMEM((2, length, width), BF16),
            pltpu.VMEM((2, lines, 2, small, width), BF16),
            pltpu.VMEM((2, width * width // hidden // (2 * small), 2, small, hidden), BF16),
            pltpu.VMEM((lines, 2, small, width), BF16),
            pltpu.SemaphoreType.DMA((6, 2)),
        ],
        compiler_params=params(),
        name="feed_weight_grads",
    )(h3.reshape(flat), g1, g2, du.reshape(2 * length, hidden), r.reshape(2 * length, hidden), a2, e2)


def call_finish(sizes, low, h1_turned, xs, dy1, norms, w_qkv, d_self, d_query, d_kv, ready, dnorm1, dnorm2):
    members, wides = sizes
    _, length, width = xs.shape
    lines, small, tiles = wides // 2, width // wides, length // TILE
    total = ready[0].shape[2] * len(ready)
    vmem = pl.BlockSpec(memory_space=pltpu.VMEM)
    anywhere = pl.BlockSpec(memory_space=pl.ANY)

    def split(item):
        return item.reshape(lines, 2, small, item.shape[1])

    scratch = [
        pltpu.VMEM((2, length, 3 * width), BF16),
        pltpu.VMEM((2, length, width), BF16),
        pltpu.VMEM((2, length, width), F32),
        pltpu.VMEM((width, 3 * width), BF16),
        pltpu.VMEM((width, 2 * length), BF16),
        pltpu.VMEM((3, lines, 2, small, width), BF16),
        pltpu.VMEM((2 + 4 + lines + 2 * max(1, members // 4 - 1), 8, width), F32),
    ]
    for cols in (2 * width, width, width, width, width):
        scratch += reduced_scratch(sizes, small, cols, "whole")
    scratch += reduced_scratch(sizes, small, total, "ready")
    scratch += reduced_scratch(sizes, small, width, "shard")
    scratch += [
        pltpu.VMEM((lines, small, width), BF16),
        pltpu.VMEM((lines, small, width), BF16),
        pltpu.VMEM((max(1, lines - 1), small, width), BF16),
    ]
    slots = reduce_slots(sizes, 7)
    scratch += [
        pltpu.SemaphoreType.DMA((slots,)),
        pltpu.SemaphoreType.DMA((slots,)),
        pltpu.SemaphoreType.DMA((5 + 2 * tiles,)),
    ]
    return pl.pallas_call(
        functools.partial(finish_kernel, sizes),
        in_specs=[anywhere] * 5 + [vmem] * (6 + len(ready)),
        out_specs=[anywhere] * 2 + [vmem] * 6,
        out_shape=[
            struct((length, width), F32),
            struct((length, width), F32),
            struct((small, 3 * width), BF16),
            struct((small, width), BF16),
            struct((small, width), BF16),
            struct((small, 2 * width), BF16),
            struct((small, total), BF16),
            struct((8, width), F32),
        ],
        scratch_shapes=scratch,
        compiler_params=pltpu.CompilerParams(
            vmem_limit_bytes=VMEM_LIMIT, collective_id=1, has_side_effects=True
        ),
        name="finish_reduce",
    )(low, h1_turned, xs, dy1, w_qkv, norms, split(d_self), split(d_query), split(d_kv), dnorm1, dnorm2, *ready)


def call_emit(sizes, *results):
    length, width = results[0].shape
    wides = sizes[1]
    small, tiles = width // wides, length // TILE
    hidden = (results[6].shape[1] - width) // 2
    group = hidden // width
    shapes = [
        (3, small), (3, small), (small, 3 * width), (small, width), (small, width), (small, 2 * width),
        (small, hidden), (group * small, width), (small, width),
    ]
    return pl.pallas_call(
        functools.partial(emit_kernel, wides),
        grid=(tiles,),
        in_specs=[pl.BlockSpec((TILE, width), lambda i: (i, 0))] * 2 + [whole(item.shape) for item in results[2:]],
        out_specs=[pl.BlockSpec((TILE, width), lambda i: (i, 0))] * 2 + [fixed(item) for item in shapes],
        out_shape=[struct((length, width), F32)] * 2 + [struct(item, F32) for item in shapes],
        compiler_params=params(),
        name="emit",
    )(*results)


def local_step(sizes, x1, x2, mem, g1, g2, target_ids, memory_ids, norm, shards):
    length, width = x1.shape
    members, wides = sizes
    lines = wides // 2
    small = width // wides
    hidden = shards[5].shape[1]
    tiles = length // TILE
    bounds = jnp.stack([segment_bounds(target_ids), segment_bounds(memory_ids)])
    results = call_gather(sizes, x1, x2, mem, norm, shards)
    xs, blocks, norms, h1_turned, mem_turned = results[:5]
    w_qkv, w_kv, w_self, w_query, w_cross, w_in, w_out = (
        item.reshape(-1, item.shape[-1]) for item in results[5:]
    )
    attended, tail, y1, q2 = call_forward(bounds, xs, blocks, norms, w_self, w_query)

    o1, o2, h3, r, du, e2, dy2, do2, dnorm2 = call_feed(y1, attended, g1, g2, norms, w_cross, w_in, w_out)
    mine, theirs = call_feed_grads(small, h3, attended, e2, g1, g2, du, r)
    swapped = lax.ppermute(theirs, "wide", [(i, i ^ 1) for i in range(wides)])
    dy1, do1, d_query, d_self, d_kv, d_mem, dnorm1 = call_cross_back(
        bounds, q2, blocks, attended, tail, do2, y1, dy2, mem_turned, norms, w_query, w_self, w_kv
    )
    swapped, do1 = lax.optimization_barrier((swapped, do1))
    group = min(4, members)
    part = lax.rem(lax.axis_index("narrow"), group)
    cols = mine.shape[2] // group

    def chip_sum(which):
        pair = [lax.dynamic_slice_in_dim(item, which * cols, cols, 2).astype(F32) for item in (mine, swapped)]
        return lower(pair[0] + pair[1])

    sums = [chip_sum(flip(part, m)) for m in range(group)]
    *sums, do1 = lax.optimization_barrier((*sums, do1))
    ready = [sums[0]]
    for m in range(1, group):
        ready.append(lax.ppermute(sums[m], "narrow", [(i, i ^ m) for i in range(members)]))
    low = call_self_back(bounds, blocks, attended, tail, do1)
    results = call_finish(
        sizes, low, h1_turned, xs, dy1, norms, w_qkv, d_self, d_query, d_kv, ready, dnorm1, dnorm2
    )
    gi1, gi2, t_gain, t_shift, *grads = call_emit(sizes, *results)
    return o1, o2, gi1, gi2, d_mem, t_gain, t_shift, grads


def body(
    sizes, inputs_one, inputs_two, memory, cotangent_one, cotangent_two, target_ids, memory_ids,
    norm_gain, norm_shift, self_qkv, self_out, cross_query, cross_kv, cross_out, ffn_in, ffn_out,
):
    shape = inputs_one.shape
    length, width = shape[1:]
    small = width // sizes[1]
    at = lax.axis_index("wide") * small
    norm = jnp.concatenate([norm_gain, norm_shift]).astype(F32)
    norm = lax.dynamic_update_slice(jnp.zeros((8, width), F32), norm, (0, at))
    o1, o2, gi1, gi2, d_mem, t_gain, t_shift, grads = local_step(
        sizes,
        inputs_one.reshape(length, width),
        inputs_two.reshape(length, width),
        memory.reshape(length, width),
        cotangent_one.reshape(length, width),
        cotangent_two.reshape(length, width),
        target_ids,
        memory_ids,
        norm,
        (self_qkv, cross_kv, self_out, cross_query, cross_out, ffn_in, ffn_out),
    )
    d_qkv, d_self, d_query, d_kv, d_in, d_out, d_cross = grads
    return (
        o1.reshape(shape), o2.reshape(shape), gi1.reshape(shape), gi2.reshape(shape), d_mem.reshape(shape),
        t_gain, t_shift, d_qkv, d_self, d_query, d_kv, d_cross, d_in, d_out,
    )


def solution(mesh):
    rows = P(("narrow", "wide"), None, None)
    ids = P(("narrow", "wide"), None)
    norm, weight = P(None, "wide"), P("wide", None)
    return jax.shard_map(
        functools.partial(body, (mesh.shape["narrow"], mesh.shape["wide"])),
        mesh=mesh,
        in_specs=(rows,) * 5 + (ids,) * 2 + (norm,) * 2 + (weight,) * 7,
        out_specs=(rows,) * 5 + (norm,) * 2 + (weight,) * 7,
        check_vma=False,
    )
```

```python
import functools

import jax
import jax.numpy as jnp
from jax import lax
from jax.experimental import pallas as pl
from jax.experimental.pallas import tpu as pltpu
from jax.sharding import PartitionSpec as P

HEAD_DIM = 64
TILE = 256
SMALL = 128
FEED = 512
SEGMENTS = 5
MASKED = -1e30
MIB = 1024 * 1024
BF16 = jnp.bfloat16
F32 = jnp.float32
MESH = pl.DeviceIdType.MESH


def lower(values):
    return values.astype(BF16)


def dot(left, right):
    return lax.dot_general(left, right, (((1,), (0,)), ((), ())), preferred_element_type=F32)


def dot_bt(left, right):
    return lax.dot_general(left, right, (((1,), (1,)), ((), ())), preferred_element_type=F32)


def dot_at(left, right):
    return lax.dot_general(left, right, (((0,), (0,)), ((), ())), preferred_element_type=F32)


def standardise(values):
    centred = values - jnp.mean(values, -1, keepdims=True)
    inverse = lax.rsqrt(jnp.mean(centred * centred, -1, keepdims=True) + 1e-05)
    return centred * inverse, inverse


def norm_back(xhat, inverse, gain, incoming):
    dz = incoming * gain
    inner = jnp.mean(dz * xhat, -1, keepdims=True)
    return (dz - jnp.mean(dz, -1, keepdims=True) - xhat * inner) * inverse


def fold_rows(values):
    rows, width = values.shape
    return jnp.sum(values.reshape(rows // 8, 8, width), axis=0)


def lane_index(rows):
    return lax.broadcasted_iota(jnp.int32, (rows, 128), 1)


def row_index(rows):
    return lax.broadcasted_iota(jnp.int32, (rows, 128), 0)


def stack_heads(pair, first):
    zero = jnp.zeros_like(pair)
    return jnp.concatenate([jnp.where(first, pair, zero), jnp.where(first, zero, pair)], axis=0)


def tiles_of(low, high, length, visit):
    base = (low // 16) * 16
    span = high - base
    whole_tiles = (span + TILE - 1 - SMALL) // TILE
    rest = span - whole_tiles * TILE

    def per_tile(i, carry):
        begin = base + i * TILE
        visit(TILE, pl.multiple_of(jnp.minimum(begin, length - TILE), 16), jnp.maximum(low, begin))
        return carry

    lax.fori_loop(0, whole_tiles, per_tile, 0)

    @pl.when(rest > 0)
    def _():
        begin = base + whole_tiles * TILE
        visit(SMALL, pl.multiple_of(jnp.minimum(begin, length - SMALL), 16), jnp.maximum(low, begin))


def each_segment(bounds, q_row, k_row, visit):
    def per_segment(s, carry):
        visit(
            bounds[q_row, s, 0], bounds[q_row, s + 1, 0], bounds[k_row, s, 0], bounds[k_row, s + 1, 0]
        )
        return carry

    lax.fori_loop(0, SEGMENTS, per_segment, 0)


def pair_lanes(offset, p):
    if isinstance(p, int):
        return slice(offset + p * 128, offset + p * 128 + 128)
    return pl.ds(pl.multiple_of(offset + p * 128, 128), 128)


def inside_rows(size, start, low, high):
    rows = row_index(size) + start
    return (rows >= low) & (rows < high)


def attend(bounds, q_row, k_row, query, keys, values, out_ref, tail_ref):
    (q_ref, q_col), (k_ref, k_col), (v_ref, v_col) = query, keys, values
    length, width = out_ref.shape
    pairs = range(width // 128)

    def visit(size, start, low, high, k_low, k_high):
        lanes = lane_index(size)
        first = lanes < HEAD_DIM
        owner, place = lanes // 4, lanes % 4
        unit = jnp.where(lane_index(2 * size) == 0, 1.0, 0.0).astype(BF16)
        keep = inside_rows(size, start, low, high)
        span = pl.ds(start, size)
        k_base = (k_low // 16) * 16
        k_tiles = (k_high - k_base + TILE - 1) // TILE

        def piece(p, k_size, k_start, low_k):
            inside = inside_rows(k_size, k_start, low_k, k_high)
            shut = (lane_index(k_size) == 0) & jnp.logical_not(inside)
            bias = jnp.where(shut, MASKED, 0.0).astype(BF16)
            queries = stack_heads(q_ref[span, pair_lanes(q_col, p)], first)
            k_span = pl.ds(k_start, k_size)
            pair_k = k_ref[k_span, pair_lanes(k_col, p)]
            pair_v = v_ref[k_span, pair_lanes(v_col, p)]
            scores = dot_bt(
                jnp.concatenate([queries, unit], axis=1), jnp.concatenate([pair_k, bias], axis=1)
            )
            ones = jnp.ones((k_size, 128), BF16)
            return scores, jnp.concatenate([pair_v, ones], axis=1)

        def finish(p, highest, total, stats):
            cols = pair_lanes(0, p)
            top, bottom = total[:size], total[size:]
            mass = jnp.where(first, top[:, 128:], bottom[:, 128:])
            merged = lower(jnp.where(first, top[:, :128], bottom[:, :128]) / mass)
            out_ref[span, cols] = jnp.where(keep, merged, out_ref[span, cols])
            peak, sums = stats
            for h, half in ((0, slice(0, size)), (1, slice(size, 2 * size))):
                here = owner == 2 * p + h
                peak = jnp.where(here, highest[half], peak)
                sums = jnp.where(here, total[half, 128:], sums)
            return peak, sums

        empty = (jnp.zeros((size, 128), F32), jnp.ones((size, 128), F32))

        def close(stats):
            peak, sums = stats
            tail = split_lanes(peak + jnp.log(sums), place, 1.0)
            tail_ref[span, :] = jnp.where(keep, tail, tail_ref[span, :])

        def rolled(one):
            close(lax.fori_loop(0, len(pairs), lambda p, stats: finish(p, *one(p), stats), empty))

        def direct(k_size):
            k_start = pl.multiple_of(jnp.minimum(k_base, length - k_size), 16)

            items = [piece(p, k_size, k_start, k_low) for p in pairs]
            tops = [jnp.max(item[0], -1, keepdims=True) for item in items]
            probs = [lower(jnp.exp(item[0] - top)) for item, top in zip(items, tops)]
            totals = [dot(prob, item[1]) for prob, item in zip(probs, items)]
            stats = empty
            for p in pairs:
                stats = finish(p, tops[p], totals[p], stats)
            close(stats)

        if size < TILE:

            @pl.when(k_tiles <= 2)
            def _():
                direct(2 * TILE)

        else:

            @pl.when(k_tiles == 1)
            def _():
                direct(TILE)

            @pl.when(k_tiles == 2)
            def _():
                direct(2 * TILE)

        @pl.when(k_tiles > 2)
        def _():
            def one(p):
                def per_key(j, carry):
                    highest, total = carry
                    begin = k_base + j * TILE
                    k_start = pl.multiple_of(jnp.minimum(begin, length - TILE), 16)
                    scores, wide_v = piece(p, TILE, k_start, jnp.maximum(k_low, begin))
                    newest = jnp.maximum(highest, jnp.max(scores, -1, keepdims=True))
                    expon = lower(jnp.exp(scores - newest))
                    return newest, total * jnp.exp(highest - newest) + dot(expon, wide_v)

                start_at = (jnp.full((2 * size, 1), MASKED, F32), jnp.zeros((2 * size, 256), F32))
                return lax.fori_loop(0, k_tiles, per_key, start_at)

            rolled(one)

    def segment(q_low, q_high, k_low, k_high):
        tiles_of(
            q_low, q_high, length, lambda size, start, low: visit(size, start, low, q_high, k_low, k_high)
        )

    each_segment(bounds, q_row, k_row, segment)


def split_lanes(values, place, lead):
    high = lower(values).astype(F32)
    rest = values - high
    middle = lower(rest).astype(F32)
    spread = jnp.where(place == 1, high, jnp.where(place == 2, middle, rest - middle))
    return lower(jnp.where(place == 0, lead, -spread))


def attend_back(bounds, q_row, k_row, query, keys, values, do_ref, out_ref, tail_ref, dq, dk, dv):
    (q_ref, q_col), (k_ref, k_col), (v_ref, v_col) = query, keys, values
    (dq_ref, dq_col), (dk_ref, dk_col), (dv_ref, dv_col) = dq, dk, dv
    length, width = do_ref.shape
    pairs = width // 128
    zero = jnp.zeros((), BF16)
    lane = lane_index(width)
    collect = (lane % 4 > 0) & (lane // 4 == row_index(width) // HEAD_DIM)
    collect = jnp.where(collect, 1.0, 0.0).astype(BF16)

    def visit(size, start, low, high, k_low, k_high):
        lanes = lane_index(size)
        first = lanes < HEAD_DIM
        owner, place = lanes // 4, lanes % 4
        closed = lower(jnp.where(place == 0, 1.0, jnp.where(place == 1, MASKED, 0.0)))
        keep = inside_rows(size, start, low, high)
        span = pl.ds(start, size)
        tail_q = jnp.where(keep, tail_ref[span, :], closed)
        centre = jnp.zeros((size, 128), F32)
        for p in range(pairs):
            cols = slice(p * 128, (p + 1) * 128)
            grad = jnp.where(keep, do_ref[span, cols], zero)
            inner = grad.astype(F32) * out_ref[span, cols].astype(F32)
            coarse = lower(inner)
            fine = lower(inner - coarse.astype(F32))
            centre = centre + dot(
                jnp.concatenate([coarse, fine], axis=1),
                jnp.concatenate([collect[cols], collect[cols]], axis=0),
            )
        tail_g = split_lanes(centre, place, 0.0)

        def per_key(k_size, k_start, low_k):
            k_span = pl.ds(k_start, k_size)
            inside = inside_rows(k_size, k_start, low_k, k_high)
            lead = lane_index(k_size) % 4 == 0
            tail = lower(jnp.where(lead, jnp.where(inside, 0.0, MASKED), 1.0))

            def load(p):
                pair_q = q_ref[span, pair_lanes(q_col, p)]
                pair_k = k_ref[k_span, pair_lanes(k_col, p)]
                pair_v = v_ref[k_span, pair_lanes(v_col, p)]
                pair_do = jnp.where(keep, do_ref[span, pair_lanes(0, p)], zero)
                queries = stack_heads(pair_q, first)
                grads = stack_heads(pair_do, first)
                ends = [
                    jnp.concatenate(
                        [jnp.where(owner == 2 * p, item, zero), jnp.where(owner == 2 * p + 1, item, zero)],
                        axis=0,
                    )
                    for item in (tail_q, tail_g)
                ]
                scores = dot_bt(
                    jnp.concatenate([pair_k, tail], axis=1),
                    jnp.concatenate([queries, ends[0]], axis=1),
                )
                slope = dot_bt(
                    jnp.concatenate([pair_v, tail], axis=1),
                    jnp.concatenate([grads, ends[1]], axis=1),
                )
                return pair_k, queries, grads, scores, slope

            def middle(item):
                pair_k, queries, grads, scores, slope = item
                probs = jnp.exp(scores)
                return pair_k, queries, grads, lower(probs), lower(probs * slope)

            def store(p, pair_k, queries, grads, probs, ds):
                dv_ref[k_span, pair_lanes(dv_col, p)] += dot(probs, grads)
                dk_ref[k_span, pair_lanes(dk_col, p)] += dot(ds, queries)
                turned = [dot_at(ds[:, :size], pair_k), dot_at(ds[:, size:], pair_k)]
                dq_ref[span, pair_lanes(dq_col, p)] += jnp.where(first, turned[0], turned[1])

            ahead = load(0)
            for p in range(pairs):
                item = ahead
                if p + 1 < pairs:
                    ahead = load(p + 1)
                store(p, *middle(item))

        tiles_of(k_low, k_high, length, per_key)

    def segment(q_low, q_high, k_low, k_high):
        tiles_of(
            q_low, q_high, length, lambda size, start, low: visit(size, start, low, q_high, k_low, k_high)
        )

    each_segment(bounds, q_row, k_row, segment)


def forward_kernel(bounds, xs, block, norms, w_self, w_query, attended, tail, y1, q2, queries):
    phase = pl.program_id(1)
    length, width = queries.shape

    @pl.when(phase == 0)
    def _():
        queries[...] = block[0, :, :width]

    attend(
        bounds, 0, phase, (queries, 0), (block.at[0], width), (block.at[0], 2 * width),
        attended.at[0, 0], tail.at[0, 0],
    )

    @pl.when(phase == 0)
    def _():
        for i in range(length // TILE):
            span = slice(i * TILE, (i + 1) * TILE)
            after = xs[0, span, :].astype(F32) + dot(attended[0, 0, span, :], w_self[...])
            y1[0, span, :] = after
            xhat, _ = standardise(after)
            h2 = lower(xhat * norms[1:2, :] + norms[4:5, :])
            asked = lower(dot(h2, w_query[...]) * HEAD_DIM ** (-0.5))
            queries[span, :] = asked
            q2[0, span, :] = asked


def feed_kernel(
    per_step, y1, a2, g1, g2, norms, w_cross, w_in, w_out,
    o1, o2, h3, r, du, e2, dy2, do2, dnorm,
):
    i = pl.program_id(0)
    width = w_cross.shape[0]
    is_first = i < per_step
    grad = jnp.where(is_first, g1[...], g2[...])
    after = y1[0] + dot(a2[0, 0], w_cross[...])
    xhat, inverse = standardise(after)
    normed = lower(xhat * norms[2:3, :] + norms[5:6, :])
    h3[0] = normed
    result = after
    dh3 = jnp.zeros_like(after)
    slope = (2.0 / jnp.pi) ** 0.5
    chunks = w_in.shape[1] // width

    def enter(c):
        cols = slice(c * width, (c + 1) * width)
        return dot(normed, w_in[:, cols]), dot_bt(grad, w_out[cols, :])

    ahead = enter(0)
    for c in range(chunks):
        cols = slice(c * width, (c + 1) * width)
        u, dr = ahead
        if c + 1 < chunks:
            ahead = enter(c + 1)
        square = u * u
        half = 0.5 + 0.5 * jnp.tanh(u * (slope + slope * 0.044715 * square))
        hidden = lower(u * half)
        r[0, :, cols] = hidden
        bend = u * (2 * slope + 6 * slope * 0.044715 * square)
        pre = lower(dr * (half * (1.0 + (1.0 - half) * bend)))
        du[0, :, cols] = pre
        result = result + dot(hidden, w_out[cols, :])
        dh3 = dh3 + dot_bt(pre, w_in[:, cols])

    @pl.when(is_first)
    def _():
        o1[...] = lower(result)

    @pl.when(jnp.logical_not(is_first))
    def _():
        o2[...] = lower(result)

    @pl.when(i == 0)
    def _():
        dnorm[...] = jnp.zeros_like(dnorm)

    dnorm[0] += fold_rows(dh3 * xhat)
    dnorm[1] += fold_rows(dh3)
    back = grad.astype(F32) + norm_back(xhat, inverse, norms[2:3, :], dh3)
    dy2[0] = back
    low = lower(back)
    e2[0] = low
    do2[0] = lower(dot_bt(low, w_cross[...]))


def feed_grad_kernel(
    small, h3, g1, g2, du, r, a2_hbm, e2_hbm, mine, theirs,
    turned, turned_g, a2, e2, d_in, d_out, d_cross, sem,
):
    c = pl.program_id(0)
    last = pl.num_programs(0) - 1
    half, width = g1.shape
    hidden = d_out.shape[4]
    group = hidden // width
    rows = width // group
    slot = lax.rem(c, 2)

    core = lax.rem(lax.axis_index("wide"), 2)
    lines = width // (2 * small)
    depth = rows // (2 * small)

    def copies(at, chunk):
        cols = pl.ds(pl.multiple_of(chunk * width, width), width)
        deep = pl.ds(chunk * depth, depth)
        found = []
        for k, (out, side) in enumerate(((mine, core), (theirs, 1 - core))):
            found.append(
                pltpu.make_async_copy(d_in.at[at, :, side], out.at[:, :, cols], sem.at[2 * k, at])
            )
            found.append(
                pltpu.make_async_copy(
                    d_out.at[at, :, side], out.at[deep, :, hidden + width :], sem.at[2 * k + 1, at]
                )
            )
        return found

    loads = [
        pltpu.make_async_copy(a2_hbm.at[:, 1], a2, sem.at[4, 0]),
        pltpu.make_async_copy(e2_hbm, e2, sem.at[4, 1]),
    ]
    cross = [
        pltpu.make_async_copy(
            d_cross.at[:, side], out.at[:, :, hidden : hidden + width], sem.at[5, k]
        )
        for k, (out, side) in enumerate(((mine, core), (theirs, 1 - core)))
    ]

    @pl.when(c >= 2)
    def _():
        for copy in copies(slot, c - 2):
            copy.wait()

    @pl.when(c == 0)
    def _():
        for copy in loads:
            copy.start()
        turned[...] = h3[...].T
        turned_g[:, :half] = g1[...].T
        turned_g[:, half:] = g2[...].T

    d_in[slot] = lower(dot(turned[...], du[...])).reshape(d_in.shape[1:])
    part = lower(dot(turned_g[...], r[...])).T
    for w in range(width // (group * small)):
        for j in range(group):
            at = (w * group + j) * small
            d_out[slot, w // 2, w % 2, :, j * width : (j + 1) * width] = part[at : at + small]
    for copy in copies(slot, c):
        copy.start()

    @pl.when(c == last)
    def _():
        wait_all(loads)
        d_cross[...] = lower(dot(a2[0].T, e2[0]) + dot(a2[1].T, e2[1])).reshape(d_cross.shape)
        for copy in cross:
            copy.start()
        for copy in copies(1 - slot, c - 1) + copies(slot, c):
            copy.wait()
        wait_all(cross)


def cross_back_kernel(
    bounds, q2, keys, values, a1, a2, stat2, do2, y1, dy2, mem_turned, norms, w_query, w_self, w_kv,
    dy1, do1, d_query, d_self, d_kv, d_mem, dnorm,
    dq_sum, dkv_sum, h2, low_q, low_e,
):
    step = pl.program_id(0)
    length, width = q2.shape[1:]

    @pl.when(step == 0)
    def _():
        dkv_sum[...] = jnp.zeros_like(dkv_sum)
        dnorm[...] = jnp.zeros_like(dnorm)

    dq_sum[...] = jnp.zeros_like(dq_sum)
    attend_back(
        bounds, 0, 1, (q2.at[0], 0), (keys.at[0], 0), (values.at[0], 0), do2.at[0], a2.at[0, 0], stat2.at[0, 0],
        (dq_sum, 0), (dkv_sum, 0), (dkv_sum, width),
    )

    def rows(i):
        span = slice(i * TILE, (i + 1) * TILE)
        grad_q = lower(dq_sum[span, :] * HEAD_DIM ** (-0.5))
        low_q[step, span, :] = grad_q
        xhat, inverse = standardise(y1[0, span, :])
        h2[step, span, :] = lower(xhat * norms[1:2, :] + norms[4:5, :])
        dh2 = dot_bt(grad_q, w_query[...])
        dnorm[0] += fold_rows(dh2 * xhat)
        dnorm[1] += fold_rows(dh2)
        back = dy2[0, span, :] + norm_back(xhat, inverse, norms[1:2, :], dh2)
        dy1[0, span, :] = back
        low = lower(back)
        low_e[step, span, :] = low
        do1[0, span, :] = lower(dot_bt(low, w_self[...]))

    for i in range(length // TILE):
        rows(i)

    @pl.when(step == 1)
    def _():
        d_query[...] = lower(dot(h2[0].T, low_q[0]) + dot(h2[1].T, low_q[1]))
        d_self[...] = lower(dot(a1[0, 0].T, low_e[0]) + dot(a1[1, 0].T, low_e[1]))
        pair = lower(dkv_sum[...])
        d_kv[...] = lower(dot(mem_turned[...], pair))
        d_mem[...] = dot_bt(pair, w_kv[...])


def self_back_kernel(bounds, qkv, a1, stat1, do1, low, sums):
    width = do1.shape[2]
    sums[...] = jnp.zeros_like(sums)
    attend_back(
        bounds, 0, 0, (qkv.at[0], 0), (qkv.at[0], width), (qkv.at[0], 2 * width),
        do1.at[0], a1.at[0, 0], stat1.at[0, 0], (sums, 0), (sums, width), (sums, 2 * width),
    )
    low[0, :, :width] = lower(sums[:, :width] * HEAD_DIM ** (-0.5))
    low[0, :, width:] = lower(sums[:, width:])


def flip(index, mask):
    out, bit = index, 1
    while bit <= mask:
        if mask & bit:
            out = out + bit - 2 * bit * lax.rem(lax.div(index, bit), 2)
        bit *= 2
    return out


class Links:
    def __init__(self, sizes, send, recv):
        self.members, wides = sizes
        self.lines = wides // 2
        self.group = min(4, self.members)
        self.narrow, self.wide = lax.axis_index("narrow"), lax.axis_index("wide")
        self.line, self.core = lax.div(self.wide, 2), lax.rem(self.wide, 2)
        self.part = lax.rem(self.narrow, self.group)
        self.send, self.recv, self.used = send, recv, 0

    def core_peer(self):
        return (self.narrow, flip(self.wide, 1))

    def plane_peer(self, mask):
        return (flip(self.narrow, mask), self.wide)

    def line_peer(self, mask):
        return (self.narrow, 2 * flip(self.line, mask) + self.core)

    def far_masks(self):
        masks, mask = [], self.group
        while mask < self.members:
            masks.append(mask)
            mask *= 2
        return masks

    def barrier(self, far):
        semaphore = pltpu.get_barrier_semaphore()
        peers = [self.core_peer()]
        peers += [self.plane_peer(m) for m in range(1, self.group)]
        peers += [self.line_peer(m) for m in range(1, self.lines)]
        if far:
            peers += [self.plane_peer(m) for m in self.far_masks()]
        for peer in peers:
            pl.semaphore_signal(semaphore, inc=1, device_id=peer, device_id_type=MESH)
        pl.semaphore_wait(semaphore, len(peers))

    def push(self, src, dst, peer):
        slot = self.used
        self.used += 1
        copy = pltpu.make_async_remote_copy(
            src_ref=src,
            dst_ref=dst,
            send_sem=self.send.at[slot],
            recv_sem=self.recv.at[slot],
            device_id=peer,
            device_id_type=MESH,
        )
        copy.start()
        return copy

    def quarter(self, part, cols):
        size = cols // self.group
        return pl.ds(pl.multiple_of(part * size, size), size)


def wait_all(copies):
    for copy in copies:
        copy.wait()


class Gathered:
    def __init__(self, links, shard, full, masks):
        self.links, self.shard, self.full, self.masks = links, shard, full, masks
        self.cols = shard.shape[-1]

    def start_line(self):
        links = self.links
        self.full[links.line, links.core] = self.shard[...]
        mine = links.quarter(links.part, self.cols)
        self.copies = [
            links.push(
                self.shard.at[:, mine], self.full.at[links.line, links.core, :, mine], links.line_peer(m)
            )
            for m in range(1, links.lines)
        ]

    def spread(self, parts, mask):
        links = self.links
        wait_all(self.copies)
        self.copies = []
        for k in range(1, links.lines):
            for part in parts:
                cols = links.quarter(part, self.cols)
                place = self.full.at[flip(links.line, k), links.core, :, cols]
                self.copies.append(links.push(place, place, links.plane_peer(mask)))

    def start_plane(self):
        self.spread([self.links.part], self.masks[0])

    def cross_plane(self):
        self.spread([self.links.part, flip(self.links.part, self.masks[0])], self.masks[1])

    def start_core(self):
        links = self.links
        wait_all(self.copies)
        place = self.full.at[:, links.core]
        self.copies = [links.push(place, place, links.core_peer())]

    def finish(self):
        wait_all(self.copies)


def gather_slots(sizes, pieces):
    lines, group = sizes[1] // 2, min(4, sizes[0])
    return pieces * (lines - 1 + (lines - 1) * (group - 1) + 1) + lines


def gather_kernel(
    sizes, norm_gain, norm_shift, target_ids, memory_ids, x1_hbm, x2_hbm, mem_hbm,
    g_qkv, g_kv, g_self, g_query, g_cross, g_in, g_out,
    xs, blocks, bounds, norms, h1_turned, mem_turned, f_qkv, f_kv, f_self, f_query, f_cross, f_in, f_out,
    rows_in, placed, s_qkv, s_kv, s_self, s_query, s_cross, s_in, s_out,
    h1, turned, turned_mem, v_qkv, v_kv, v_self, v_query, v_cross, v_in, v_out, o_qkv, o_kv, norm_all, send, recv, local,
):
    links = Links(sizes, send, recv)
    _, length, width = rows_in.shape
    x1, x2, mem = rows_in.at[0], rows_in.at[1], rows_in.at[2]
    small = width // sizes[1]
    used = [0]

    def local_copy(src, dst):
        copy = pltpu.make_async_copy(src, dst, local.at[used[0]])
        used[0] += 1
        copy.start()
        return copy

    landing = []

    def piece(shard, full, out):
        landing.append((full, out))
        return Gathered(links, shard, full, (len(landing) % 2 + 1, 2 - len(landing) % 2))

    shards = [
        local_copy(src, dst)
        for src, dst in (
            (g_qkv, s_qkv), (g_kv, s_kv), (g_self, s_self), (g_query, s_query), (g_cross, s_cross),
            (g_in, s_in), (g_out, s_out),
        )
    ]
    loads = [local_copy(src, dst) for src, dst in ((x1_hbm, x1), (x2_hbm, x2), (mem_hbm, mem))]
    links.barrier(False)
    placed[...] = jnp.zeros_like(placed)
    placed[0:3, :] = norm_gain[...].astype(F32)
    placed[3:6, :] = norm_shift[...].astype(F32)
    column = lax.broadcasted_iota(jnp.int32, (small, width), 1)
    row = lax.broadcasted_iota(jnp.int32, (small, width), 0)
    spot = jnp.where(column == row + links.wide * small, 1.0, 0.0).astype(BF16)
    norm_all[links.line, links.core] = dot(lower(placed[...]), spot)
    level = lax.broadcasted_iota(jnp.int32, (8, length), 0)
    for k, ids in enumerate((target_ids, memory_ids)):
        order = jnp.where(ids[...] < 0, SEGMENTS - 1, ids[...])
        below = jnp.where(order < level, 1.0, 0.0)
        starts = jnp.sum(below, axis=1, keepdims=True).astype(jnp.int32)
        bounds[k] = jnp.broadcast_to(starts, (8, 128))
    wait_all(shards)
    pieces = []
    for c in range(3):
        cols = slice(c * width, (c + 1) * width)
        pieces.append(piece(s_qkv.at[:, cols], v_qkv.at[c], f_qkv.at[:, :, :, cols]))
    for c in range(2):
        cols = slice(c * width, (c + 1) * width)
        pieces.append(piece(s_kv.at[:, cols], v_kv.at[c], f_kv.at[:, :, :, cols]))
    pieces.append(piece(s_self, v_self, f_self))
    pieces.append(piece(s_query, v_query, f_query))
    pieces.append(piece(s_cross, v_cross, f_cross))
    half = s_in.shape[1] // 2
    for c in range(2):
        cols = slice(c * half, (c + 1) * half)
        pieces.append(piece(s_in.at[:, cols], v_in.at[c], f_in.at[:, :, :, cols]))
    half = s_out.shape[0] // 2
    for c in range(2):
        rows = slice(c * half, (c + 1) * half)
        pieces.append(piece(s_out.at[rows], v_out.at[c], f_out.at[:, :, rows]))

    own = norm_all.at[links.line, links.core]
    norm_copies = [links.push(own, own, links.line_peer(m)) for m in range(1, links.lines)]
    for p in range(4):
        pieces[p].start_line()
    wait_all(loads)
    outgoing = [local_copy(x1, xs.at[0]), local_copy(x2, xs.at[1])]
    wait_all(norm_copies)
    place = norm_all.at[:, links.core]
    norm_copy = links.push(place, place, links.core_peer())
    pieces[0].start_plane()
    norm_copy.wait()
    every = norm_all[...]
    total = every[0, 0]
    for k in range(1, 2 * links.lines):
        total = total + every[k // 2, k % 2]
    norms[...] = total
    gain, shift = total[0:1, :], total[3:4, :]

    def normalise(t, x):
        for i in range(length // TILE):
            span = slice(i * TILE, (i + 1) * TILE)
            xhat, _ = standardise(x[span, :].astype(F32))
            h1[t, span, :] = lower(xhat * gain + shift)

    def turn():
        turned[:, :length] = h1[0].T
        turned[:, length:] = h1[1].T
        turned_mem[...] = mem[...].T
        outgoing.append(local_copy(turned, h1_turned))
        outgoing.append(local_copy(turned_mem, mem_turned))

    def project(c):
        def run():
            weight = v_qkv[c].reshape(width, width)
            scale = HEAD_DIM ** (-0.5) if c == 0 else 1.0
            for t in range(2):

                def rows(i, carry, t=t):
                    span = pl.ds(pl.multiple_of(i * 2 * TILE, 2 * TILE), 2 * TILE)
                    o_qkv[c, t, span, :] = lower(dot(h1[t, span, :], weight) * scale)
                    return carry

                lax.fori_loop(0, length // (2 * TILE), rows, 0)
            cols = slice(c * width, (c + 1) * width)
            outgoing.append(local_copy(o_qkv.at[c], blocks.at[0:2, :, cols]))

        return run

    def project_memory(c):
        def run():
            weight = v_kv[c].reshape(width, width)

            def rows(i, carry):
                span = pl.ds(pl.multiple_of(i * 2 * TILE, 2 * TILE), 2 * TILE)
                o_kv[c, span, :] = lower(dot(mem[span, :], weight))
                return carry

            lax.fori_loop(0, length // (2 * TILE), rows, 0)
            cols = slice((c + 1) * width, (c + 2) * width)
            outgoing.append(local_copy(o_kv.at[c], blocks.at[2, :, cols]))

        return run

    work = {c: project(c) for c in range(3)} | {3 + c: project_memory(c) for c in range(2)}
    count = len(pieces)
    for t in range(1, count + 6):
        if 3 + t < count:
            pieces[3 + t].start_line()
        if t < count:
            pieces[t].start_plane()
        if t == 1:
            normalise(0, x1)
        if t == 2:
            normalise(1, x2)
        if 0 <= t - 2 < count:
            pieces[t - 2].cross_plane()
        if 0 <= t - 4 < count:
            pieces[t - 4].start_core()
        if 0 <= t - 5 < count:
            one = t - 5
            pieces[one].finish()
            outgoing.append(local_copy(*landing[one]))
            if one in work:
                work[one]()
            if one == 5:
                turn()
    wait_all(outgoing)


class Reduced:
    def __init__(self, links, bufs, out, masks, source=None, ready=None):
        self.links, self.out, self.masks, self.source, self.ready = links, out, masks, source, ready
        self.lined = source is not None or ready is not None
        self.crecv, self.chip, self.precv, self.plane, self.lrecv, self.mine, self.xrecv, self.full, self.half = bufs
        self.cols = self.full.shape[-1]

    def start_core(self):
        links = self.links
        self.copies = [links.push(self.source.at[:, 1 - links.core], self.crecv, links.core_peer())]

    def start_plane(self):
        links = self.links
        if self.source is not None:
            wait_all(self.copies)
            for k in range(links.lines):
                self.chip[k] = lower(
                    self.source[k, links.core].astype(F32) + self.crecv[k].astype(F32)
                )
        first, second = self.masks
        near = flip(links.part, first)
        self.copies = [
            links.push(
                self.chip.at[:, :, links.quarter(part, self.cols)], self.precv.at[k], links.plane_peer(first)
            )
            for k, part in enumerate((near, flip(near, second)))
        ]

    def cross_plane(self):
        links = self.links
        wait_all(self.copies)
        second = self.masks[1]
        far = self.chip[:, :, links.quarter(flip(links.part, second), self.cols)].astype(F32)
        self.half[...] = lower(far + self.precv[1].astype(F32))
        self.copies = [links.push(self.half, self.precv.at[2], links.plane_peer(second))]

    def start_line(self):
        links = self.links
        if self.ready is not None:
            total = self.ready[0][...].astype(F32)
            for item in self.ready[1:]:
                total = total + item[...].astype(F32)
        else:
            wait_all(self.copies)
            total = self.chip[:, :, links.quarter(links.part, self.cols)].astype(F32)
            total = total + self.precv[0].astype(F32) + self.precv[2].astype(F32)
        self.plane[...] = lower(total)
        if not self.lined:
            self.copies = []
            return
        self.copies = [
            links.push(self.plane.at[flip(links.line, m)], self.lrecv.at[m - 1], links.line_peer(m))
            for m in range(1, links.lines)
        ]

    def start_gather(self):
        links = self.links
        wait_all(self.copies)
        if not self.lined:
            total = self.plane[0].astype(F32)
        else:
            total = self.plane[links.line].astype(F32)
            for m in range(1, links.lines):
                total = total + self.lrecv[m - 1].astype(F32)
        for i, mask in enumerate(links.far_masks()):
            self.xrecv[2 * i] = lower(total)
            links.push(self.xrecv.at[2 * i], self.xrecv.at[2 * i + 1], links.plane_peer(mask)).wait()
            total = self.xrecv[2 * i].astype(F32) + self.xrecv[2 * i + 1].astype(F32)
        self.mine[...] = lower(total)
        place = self.full.at[:, links.quarter(links.part, self.cols)]
        place[...] = self.mine[...]
        self.copies = [links.push(self.mine, place, links.plane_peer(self.masks[0]))]

    def cross_gather(self):
        links = self.links
        wait_all(self.copies)
        self.copies = []
        for part in (links.part, flip(links.part, self.masks[0])):
            place = self.full.at[:, links.quarter(part, self.cols)]
            self.copies.append(links.push(place, place, links.plane_peer(self.masks[1])))

    def finish(self):
        wait_all(self.copies)
        self.out[...] = self.full[...]


class LineFirst:
    def __init__(self, links, bufs, source, then):
        self.links, self.source, self.then = links, source, then
        self.crecv, self.chip, self.lrecv = bufs

    def start_core(self):
        links = self.links
        self.copies = [links.push(self.source.at[:, 1 - links.core], self.crecv, links.core_peer())]

    def start_line(self):
        links = self.links
        wait_all(self.copies)
        for k in range(links.lines):
            self.chip[k] = lower(self.source[k, links.core].astype(F32) + self.crecv[k].astype(F32))
        self.copies = [
            links.push(self.chip.at[flip(links.line, m)], self.lrecv.at[m - 1], links.line_peer(m))
            for m in range(1, links.lines)
        ]

    def start_plane(self):
        links = self.links
        wait_all(self.copies)
        total = self.chip[links.line].astype(F32)
        for m in range(1, links.lines):
            total = total + self.lrecv[m - 1].astype(F32)
        self.then.chip[0] = lower(total)
        self.then.start_plane()


def reduced_scratch(sizes, rows, cols, kind):
    members, wides = sizes
    lines, group = wides // 2, min(4, members)
    part = cols // group
    depth = 1 if kind == "shard" else lines
    far = max(2, 2 * (members // group - 1))
    small = (1, 16, 128)
    return [
        pltpu.VMEM((lines, rows, cols) if kind == "whole" else small, BF16),
        pltpu.VMEM(small if kind == "ready" else (depth, rows, cols), BF16),
        pltpu.VMEM(small if kind == "ready" else (group - 1, depth, rows, part), BF16),
        pltpu.VMEM((depth, rows, part), BF16),
        pltpu.VMEM(small if kind == "shard" else (lines - 1, rows, part), BF16),
        pltpu.VMEM((rows, part), BF16),
        pltpu.VMEM((far, rows, part), BF16),
        pltpu.VMEM((rows, cols), BF16),
        pltpu.VMEM(small if kind == "ready" else (depth, rows, part), BF16),
    ]


def reduce_slots(sizes, jobs):
    members, wides = sizes
    lines, group = wides // 2, min(4, members)
    return (jobs + 1) * (1 + 2 * (group - 1) + lines - 1 + members // group)


BUFS = 9


def finish_kernel(
    sizes, low_hbm, h1_hbm, xs_hbm, dy1_hbm, w_hbm, self_hbm, query_hbm, kv_hbm, norms, dnorm1, dnorm2, *rest,
):
    group = min(4, sizes[0])
    ready, rest = rest[:group], rest[group:]
    gi1, gi2, t_qkv, t_self, t_query, t_kv, t_joint, t_norm = rest[:8]
    low, xs, dy1, w_qkv, h1, grads, norm_slots, d_self, d_query, d_kv = rest[8:18]
    bufs, first_bufs = rest[18:-9], rest[-9:-3]
    send, recv, local = rest[-3:]
    links = Links(sizes, send, recv)
    _, length, width = xs.shape
    early = [
        pltpu.make_async_copy(kv_hbm, d_kv, local.at[5]),
        pltpu.make_async_copy(query_hbm, d_query, local.at[6]),
        pltpu.make_async_copy(self_hbm, d_self, local.at[7]),
    ]
    loads = [
        pltpu.make_async_copy(h1_hbm, h1, local.at[0]),
        pltpu.make_async_copy(low_hbm, low, local.at[1]),
        pltpu.make_async_copy(xs_hbm, xs, local.at[2]),
        pltpu.make_async_copy(dy1_hbm, dy1, local.at[3]),
        pltpu.make_async_copy(w_hbm, w_qkv, local.at[4]),
    ]
    for copy in early + loads:
        copy.start()
    links.barrier(True)
    wait_all(early)

    taken = [0]

    def job(out, **kind):
        at = taken[0] * BUFS
        taken[0] += 1
        masks = (2 - taken[0] % 2, 1 + taken[0] % 2)
        return Reduced(links, bufs[at : at + BUFS], out, masks, **kind)

    other = job(t_kv, source=d_kv)
    heads = [job(t_qkv.at[:, c * width : (c + 1) * width], source=grads.at[c]) for c in range(3)]
    joint = job(t_joint, ready=ready)
    late = [job(t_query), job(t_self)]
    before = [
        LineFirst(links, first_bufs[3 * k : 3 * k + 3], source, late[k])
        for k, source in enumerate((d_query, d_self))
    ]
    for one in [other] + before:
        one.start_core()
    joint.start_line()
    gain = norms[0:1, :]
    loads[0].wait()
    loads[1].wait()
    for c in range(3):
        cols = slice(c * width, (c + 1) * width)
        value = dot(h1[:, :length], low[0, :, cols]) + dot(h1[:, length:], low[1, :, cols])
        grads[c] = lower(value).reshape(grads.shape[1:])
        heads[c].start_core()
        if c > 0:
            heads[c - 1].start_plane()
        if c == 0:
            other.start_plane()
            for one in before:
                one.start_line()
    other.cross_plane()
    heads[2].start_plane()
    wait_all(loads[2:])
    stores = []
    dgain = jnp.zeros((8, width), F32)
    dshift = jnp.zeros((8, width), F32)
    steps = [
        lambda: (joint.start_gather(), heads[0].cross_plane()),
        lambda: (heads[1].cross_plane(), other.start_line()),
        lambda: (heads[2].cross_plane(), joint.cross_gather()),
        lambda: (heads[0].start_line(), [one.start_plane() for one in before]),
        lambda: heads[1].start_line(),
        lambda: (heads[2].start_line(), other.start_gather()),
        lambda: ([one.cross_plane() for one in late], heads[0].start_gather()),
        lambda: (heads[1].start_gather(), other.cross_gather(), joint.finish()),
    ]
    weight = w_qkv[...]
    for t in range(2):
        for i in range(length // TILE):
            span = slice(i * TILE, (i + 1) * TILE)
            xhat, inverse = standardise(xs[t, span, :].astype(F32))
            dh1 = dot_bt(low[t, span, :], weight)
            dgain = dgain + fold_rows(dh1 * xhat)
            dshift = dshift + fold_rows(dh1)
            dy1[t, span, :] = dy1[t, span, :] + norm_back(xhat, inverse, gain, dh1)
            number = t * (length // TILE) + i
            copy = pltpu.make_async_copy(
                dy1.at[t, span, :], (gi1, gi2)[t].at[span, :], local.at[8 + number]
            )
            copy.start()
            stores.append(copy)
            if number < len(steps):
                steps[number]()
    rows = [jnp.sum(item, axis=0, keepdims=True) for item in (dgain, dnorm1[0], dnorm2[0], dshift, dnorm1[1], dnorm2[1])]
    total = jnp.concatenate(rows + [jnp.zeros((2, width), F32)], axis=0)

    def swap(first, count, own, peers, total):
        norm_slots[first + own] = total
        place = norm_slots.at[first + own]
        wait_all([links.push(place, place, peer) for peer in peers])
        out = norm_slots[first]
        for k in range(1, count):
            out = out + norm_slots[first + k]
        return out

    total = swap(0, 2, links.core, [links.core_peer()], total)
    heads[2].start_gather()
    for one in late:
        one.start_line()
        one.start_gather()
    for one in heads[:2]:
        one.cross_gather()
    total = swap(2, links.group, links.part, [links.plane_peer(m) for m in range(1, links.group)], total)
    first = 2 + links.group
    for one in heads[2:] + late:
        one.cross_gather()
    total = swap(first, links.lines, links.line, [links.line_peer(m) for m in range(1, links.lines)], total)
    first += links.lines
    for mask in links.far_masks():
        side = lax.rem(lax.div(links.narrow, mask), 2)
        total = swap(first, 2, side, [links.plane_peer(mask)], total)
        first += 2
    t_norm[...] = total
    for one in heads + [other] + late:
        one.finish()
    wait_all(stores)


def emit_kernel(
    wides, f1, f2, b_qkv, b_self, b_query, b_kv, b_joint, t_norm,
    gi1, gi2, gain, shift, t_qkv, t_self, t_query, t_kv, t_in, t_out, t_cross,
):
    gi1[...] = f1[...]
    gi2[...] = f2[...]
    width = gi1.shape[1]
    small, hidden = t_in.shape

    @pl.when(pl.program_id(0) == 0)
    def _():
        for src, dst in (
            (b_qkv, t_qkv), (b_self, t_self), (b_query, t_query), (b_kv, t_kv),
            (b_joint.at[:, :hidden], t_in), (b_joint.at[:, hidden : hidden + width], t_cross),
        ):
            dst[...] = src[...].astype(F32)
        for j in range(hidden // width):
            begin = hidden + width + j * width
            t_out[j * small : (j + 1) * small, :] = b_joint[:, begin : begin + width].astype(F32)
        at = lax.axis_index("wide") * small
        mine = pltpu.roll(t_norm[...], lax.rem(width - at, width), 1)
        gain[...] = mine[:3, :small]
        shift[...] = mine[3:6, :small]


def whole(shape):
    zeros = (0,) * len(shape)
    return pl.BlockSpec(shape, lambda *_: zeros, pipeline_mode=pl.Buffered(1))


def fixed(shape):
    zeros = (0,) * len(shape)
    return pl.BlockSpec(shape, lambda *_: zeros)


def by_step(shape):
    return pl.BlockSpec((1,) + shape, lambda t, *_: (t, 0, 0))


def params(limit):
    return pltpu.CompilerParams(
        vmem_limit_bytes=limit * MIB, dimension_semantics=("arbitrary",)
    )


def struct(shape, dtype):
    return jax.ShapeDtypeStruct(shape, dtype)


def call_forward(bounds, xs, blocks, norms, w_self, w_query):
    length, width = xs.shape[1:]
    each = pl.BlockSpec((1, length, width), lambda t, p, *_: (t, 0, 0))
    return pl.pallas_call(
        forward_kernel,
        grid_spec=pltpu.PrefetchScalarGridSpec(
            num_scalar_prefetch=1,
            grid=(2, 2),
            in_specs=[
                each,
                pl.BlockSpec((1, length, 3 * width), lambda t, p, *_: (t + p * (2 - t), 0, 0)),
                whole((8, width)), whole(w_self.shape), whole(w_query.shape),
            ],
            out_specs=[
                pl.BlockSpec((1, 1, length, width), lambda t, p, *_: (t, p, 0, 0)),
                pl.BlockSpec((1, 1, length, 128), lambda t, p, *_: (t, p, 0, 0)),
                each, each,
            ],
            scratch_shapes=[pltpu.VMEM((length, width), BF16)],
        ),
        out_shape=[
            struct((2, 2, length, width), BF16),
            struct((2, 2, length, 128), BF16),
            struct((2, length, width), F32),
            struct((2, length, width), BF16),
        ],
        compiler_params=pltpu.CompilerParams(
            vmem_limit_bytes=60 * MIB, dimension_semantics=("arbitrary", "arbitrary")
        ),
        name="attend_forward",
    )(bounds, xs, blocks, norms, w_self, w_query)


def call_cross_back(bounds, q2, blocks, attended, tail, do2, y1, dy2, mem_turned, norms, w_query, w_self, w_kv):
    length, width = q2.shape[1:]
    norm_spec = whole((8, width))
    step_low = by_step((length, width))
    return pl.pallas_call(
        cross_back_kernel,
        grid_spec=pltpu.PrefetchScalarGridSpec(
            num_scalar_prefetch=1,
            grid=(2,),
            in_specs=[
                step_low,
                pl.BlockSpec((1, length, width), lambda *_: (2, 0, 1), pipeline_mode=pl.Buffered(1)),
                pl.BlockSpec((1, length, width), lambda *_: (2, 0, 2), pipeline_mode=pl.Buffered(1)),
                pl.BlockSpec((2, 1, length, width), lambda *_: (0, 0, 0, 0), pipeline_mode=pl.Buffered(1)),
                pl.BlockSpec((1, 1, length, width), lambda t, *_: (t, 1, 0, 0)),
                pl.BlockSpec((1, 1, length, 128), lambda t, *_: (t, 1, 0, 0)),
                step_low,
                step_low, step_low, whole(mem_turned.shape), norm_spec,
                whole(w_query.shape), whole(w_self.shape), whole(w_kv.shape),
            ],
            out_specs=[
                step_low, step_low, fixed((width, width)), fixed((width, width)), fixed((width, 2 * width)),
                fixed((length, width)), fixed((2, 8, width)),
            ],
            scratch_shapes=[
                pltpu.VMEM((length, width), F32),
                pltpu.VMEM((length, 2 * width), F32),
                pltpu.VMEM((2, length, width), BF16),
                pltpu.VMEM((2, length, width), BF16),
                pltpu.VMEM((2, length, width), BF16),
            ],
        ),
        out_shape=[
            struct((2, length, width), F32),
            struct((2, length, width), BF16),
            struct((width, width), BF16),
            struct((width, width), BF16),
            struct((width, 2 * width), BF16),
            struct((length, width), F32),
            struct((2, 8, width), F32),
        ],
        compiler_params=params(60),
        cost_estimate=pl.CostEstimate(flops=45000000000, bytes_accessed=20000000, transcendentals=0),
        name="cross_back",
    )(bounds, q2, blocks, blocks, attended, attended, tail, do2, y1, dy2, mem_turned, norms, w_query, w_self, w_kv)


def call_self_back(bounds, blocks, attended, tail, do1):
    length, width = do1.shape[1:]
    norm_spec = whole((8, width))
    step_low = by_step((length, width))
    return pl.pallas_call(
        self_back_kernel,
        grid_spec=pltpu.PrefetchScalarGridSpec(
            num_scalar_prefetch=1,
            grid=(2,),
            in_specs=[
                by_step((length, 3 * width)),
                pl.BlockSpec((1, 1, length, width), lambda t, *_: (t, 0, 0, 0)),
                pl.BlockSpec((1, 1, length, 128), lambda t, *_: (t, 0, 0, 0)),
                step_low,
            ],
            out_specs=by_step((length, 3 * width)),
            scratch_shapes=[pltpu.VMEM((length, 3 * width), F32)],
        ),
        out_shape=struct((2, length, 3 * width), BF16),
        compiler_params=params(60),
        cost_estimate=pl.CostEstimate(flops=30000000000, bytes_accessed=20000000, transcendentals=0),
        name="self_back",
    )(bounds, blocks, attended, tail, do1)


def call_gather(sizes, norm_gain, norm_shift, target_ids, memory_ids, x1, x2, mem, shards):
    length, width = x1.shape
    lines = sizes[1] // 2
    small = width // sizes[1]
    vmem = pl.BlockSpec(memory_space=pltpu.VMEM)
    anywhere = pl.BlockSpec(memory_space=pl.ANY)

    def full(shape):
        return struct((lines, 2, shape[0], shape[1]), BF16)

    pieces = 12
    slots = gather_slots(sizes, pieces)
    return pl.pallas_call(
        functools.partial(gather_kernel, sizes),
        in_specs=[vmem] * 4 + [pl.BlockSpec(memory_space=pltpu.HBM)] * 10,
        out_specs=[anywhere] * 2 + [vmem] * 2 + [anywhere] * 9,
        out_shape=[
            struct((2, length, width), BF16),
            struct((3, length, 3 * width), BF16),
            struct((2, 8, 128), jnp.int32),
            struct((8, width), F32),
            struct((width, 2 * length), BF16),
            struct((width, length), BF16),
        ]
        + [full(item.shape) for item in shards],
        scratch_shapes=[pltpu.VMEM((3, length, width), BF16), pltpu.VMEM((8, small), F32)]
        + [pltpu.VMEM(item.shape, BF16) for item in shards]
        + [
            pltpu.VMEM((2, length, width), BF16),
            pltpu.VMEM((width, 2 * length), BF16),
            pltpu.VMEM((width, length), BF16),
            pltpu.VMEM((3, lines, 2, small, width), BF16),
            pltpu.VMEM((2, lines, 2, small, width), BF16),
            pltpu.VMEM((lines, 2, small, width), BF16),
            pltpu.VMEM((lines, 2, small, width), BF16),
            pltpu.VMEM((lines, 2, small, width), BF16),
            pltpu.VMEM((2, lines, 2, small, shards[5].shape[1] // 2), BF16),
            pltpu.VMEM((2, lines, 2, shards[6].shape[0] // 2, width), BF16),
            pltpu.VMEM((3, 2, length, width), BF16),
            pltpu.VMEM((2, length, width), BF16),
            pltpu.VMEM((lines, 2, 8, width), F32),
            pltpu.SemaphoreType.DMA((slots,)),
            pltpu.SemaphoreType.DMA((slots,)),
            pltpu.SemaphoreType.DMA((pieces + 26,)),
        ],
        compiler_params=pltpu.CompilerParams(
            vmem_limit_bytes=60 * MIB, collective_id=0, has_side_effects=True
        ),
        name="gather_project",
    )(norm_gain, norm_shift, target_ids, memory_ids, x1, x2, mem, *shards)


def call_feed(y1, a2, g1, g2, norms, w_cross, w_in, w_out):
    length, width = g1.shape
    hidden = w_in.shape[1]
    tiles = length // FEED
    norm_spec = whole((8, width))
    step_tile = pl.BlockSpec((1, FEED, width), lambda i: (i // tiles, i % tiles, 0))
    step_wide = pl.BlockSpec((1, FEED, hidden), lambda i: (i // tiles, i % tiles, 0))
    early = pl.BlockSpec((FEED, width), lambda i: (jnp.minimum(i, tiles - 1), 0))
    late = pl.BlockSpec((FEED, width), lambda i: (jnp.maximum(i - tiles, 0), 0))
    return pl.pallas_call(
        functools.partial(feed_kernel, tiles),
        grid=(2 * tiles,),
        in_specs=[
            step_tile,
            pl.BlockSpec((1, 1, FEED, width), lambda i: (i // tiles, 1, i % tiles, 0)),
            early, late, norm_spec,
            whole(w_cross.shape), whole(w_in.shape), whole(w_out.shape),
        ],
        out_specs=[
            early, late, step_tile, step_wide, step_wide, step_tile, step_tile, step_tile,
            fixed((2, 8, width)),
        ],
        out_shape=[
            struct((length, width), BF16),
            struct((length, width), BF16),
            struct((2, length, width), BF16),
            struct((2, length, hidden), BF16),
            struct((2, length, hidden), BF16),
            struct((2, length, width), BF16),
            struct((2, length, width), F32),
            struct((2, length, width), BF16),
            struct((2, 8, width), F32),
        ],
        compiler_params=params(60),
        name="feed_forward_back",
    )(y1, a2, g1, g2, norms, w_cross, w_in, w_out)


def call_feed_grads(small, h3, a2, e2, g1, g2, du, r):
    length, width = g1.shape
    hidden = r.shape[2]
    lines = width // (2 * small)
    flat = (2 * length, width)
    chunk = pl.BlockSpec((2 * length, width), lambda c: (0, c))
    return pl.pallas_call(
        functools.partial(feed_grad_kernel, small),
        grid=(hidden // width,),
        in_specs=[whole(flat), whole((length, width)), whole((length, width)), chunk, chunk]
        + [pl.BlockSpec(memory_space=pl.ANY)] * 2,
        out_specs=[pl.BlockSpec(memory_space=pl.ANY)] * 2,
        out_shape=[struct((lines, small, 2 * hidden + width), BF16)] * 2,
        scratch_shapes=[
            pltpu.VMEM((width, 2 * length), BF16),
            pltpu.VMEM((width, 2 * length), BF16),
            pltpu.VMEM((2, length, width), BF16),
            pltpu.VMEM((2, length, width), BF16),
            pltpu.VMEM((2, lines, 2, small, width), BF16),
            pltpu.VMEM((2, width * width // hidden // (2 * small), 2, small, hidden), BF16),
            pltpu.VMEM((lines, 2, small, width), BF16),
            pltpu.SemaphoreType.DMA((6, 2)),
        ],
        compiler_params=params(60),
        name="feed_weight_grads",
    )(h3.reshape(flat), g1, g2, du.reshape(2 * length, hidden), r.reshape(2 * length, hidden), a2, e2)


def call_finish(sizes, low, h1_turned, xs, dy1, norms, w_qkv, d_self, d_query, d_kv, ready, dnorm1, dnorm2):
    members, wides = sizes
    _, length, width = xs.shape
    lines, small = wides // 2, width // wides
    total = ready[0].shape[2] * len(ready)
    vmem = pl.BlockSpec(memory_space=pltpu.VMEM)

    def split(item):
        return item.reshape(lines, 2, small, item.shape[1])

    scratch = [
        pltpu.VMEM((2, length, 3 * width), BF16),
        pltpu.VMEM((2, length, width), BF16),
        pltpu.VMEM((2, length, width), F32),
        pltpu.VMEM((width, 3 * width), BF16),
        pltpu.VMEM((width, 2 * length), BF16),
        pltpu.VMEM((3, lines, 2, small, width), BF16),
        pltpu.VMEM((2 + 4 + lines + 2 * max(1, members // 4 - 1), 8, width), F32),
        pltpu.VMEM((lines, 2, small, width), BF16),
        pltpu.VMEM((lines, 2, small, width), BF16),
        pltpu.VMEM((lines, 2, small, 2 * width), BF16),
    ]
    for cols in (2 * width, width, width, width):
        scratch += reduced_scratch(sizes, small, cols, "whole")
    scratch += reduced_scratch(sizes, small, total, "ready")
    for _ in range(2):
        scratch += reduced_scratch(sizes, small, width, "shard")
    for _ in range(2):
        scratch += [
            pltpu.VMEM((lines, small, width), BF16),
            pltpu.VMEM((lines, small, width), BF16),
            pltpu.VMEM((max(1, lines - 1), small, width), BF16),
        ]
    slots = reduce_slots(sizes, 7)
    scratch += [
        pltpu.SemaphoreType.DMA((slots,)),
        pltpu.SemaphoreType.DMA((slots,)),
        pltpu.SemaphoreType.DMA((8 + 2 * length // TILE,)),
    ]
    return pl.pallas_call(
        functools.partial(finish_kernel, sizes),
        in_specs=[pl.BlockSpec(memory_space=pltpu.HBM)] * 8 + [vmem] * (3 + len(ready)),
        out_specs=[pl.BlockSpec(memory_space=pl.ANY)] * 2 + [vmem] * 6,
        out_shape=[
            struct((length, width), F32),
            struct((length, width), F32),
            struct((small, 3 * width), BF16),
            struct((small, width), BF16),
            struct((small, width), BF16),
            struct((small, 2 * width), BF16),
            struct((small, total), BF16),
            struct((8, width), F32),
        ],
        scratch_shapes=scratch,
        compiler_params=pltpu.CompilerParams(
            vmem_limit_bytes=60 * MIB, collective_id=1, has_side_effects=True
        ),
        name="finish_reduce",
    )(low, h1_turned, xs, dy1, w_qkv, split(d_self), split(d_query), split(d_kv), norms, dnorm1, dnorm2, *ready)


def call_emit(sizes, *results):
    length, width = results[0].shape
    wides = sizes[1]
    small, tiles = width // wides, length // TILE
    hidden = (results[6].shape[1] - width) // 2
    group = hidden // width
    shapes = [
        (3, small), (3, small), (small, 3 * width), (small, width), (small, width), (small, 2 * width),
        (small, hidden), (group * small, width), (small, width),
    ]
    return pl.pallas_call(
        functools.partial(emit_kernel, wides),
        grid=(tiles,),
        in_specs=[pl.BlockSpec((TILE, width), lambda i: (i, 0))] * 2 + [whole(item.shape) for item in results[2:]],
        out_specs=[pl.BlockSpec((TILE, width), lambda i: (i, 0))] * 2 + [fixed(item) for item in shapes],
        out_shape=[struct((length, width), F32)] * 2 + [struct(item, F32) for item in shapes],
        compiler_params=params(60),
        name="emit",
    )(*results)


def local_step(sizes, x1, x2, mem, g1, g2, target_ids, memory_ids, norm_gain, norm_shift, shards):
    length, width = x1.shape
    members, wides = sizes
    lines = wides // 2
    small = width // wides
    hidden = shards[5].shape[1]
    tiles = length // TILE
    results = call_gather(sizes, norm_gain, norm_shift, target_ids, memory_ids, x1, x2, mem, shards)
    xs, blocks, bounds, norms, h1_turned, mem_turned = results[:6]
    w_qkv, w_kv, w_self, w_query, w_cross, w_in, w_out = (
        item.reshape(-1, item.shape[-1]) for item in results[6:]
    )
    attended, tail, y1, q2 = call_forward(bounds, xs, blocks, norms, w_self, w_query)

    o1, o2, h3, r, du, e2, dy2, do2, dnorm2 = call_feed(y1, attended, g1, g2, norms, w_cross, w_in, w_out)
    mine, theirs = call_feed_grads(small, h3, attended, e2, g1, g2, du, r)
    swapped = lax.ppermute(theirs, "wide", [(i, i ^ 1) for i in range(wides)])
    dy1, do1, d_query, d_self, d_kv, d_mem, dnorm1 = call_cross_back(
        bounds, q2, blocks, attended, tail, do2, y1, dy2, mem_turned, norms, w_query, w_self, w_kv
    )
    swapped, do1 = lax.optimization_barrier((swapped, do1))
    group = min(4, members)
    part = lax.rem(lax.axis_index("narrow"), group)
    cols = mine.shape[2] // group

    def chip_sum(which):
        pair = [lax.dynamic_slice_in_dim(item, which * cols, cols, 2).astype(F32) for item in (mine, swapped)]
        return lower(pair[0] + pair[1])

    sums = [chip_sum(flip(part, m)) for m in range(group)]
    *sums, do1 = lax.optimization_barrier((*sums, do1))
    ready = [sums[0]]
    for m in range(1, group):
        ready.append(lax.ppermute(sums[m], "narrow", [(i, i ^ m) for i in range(members)]))
    low = call_self_back(bounds, blocks, attended, tail, do1)
    results = call_finish(
        sizes, low, h1_turned, xs, dy1, norms, w_qkv, d_self, d_query, d_kv, ready, dnorm1, dnorm2
    )
    gi1, gi2, t_gain, t_shift, *grads = call_emit(sizes, *results)
    return o1, o2, gi1, gi2, d_mem, t_gain, t_shift, grads


def body(
    sizes, inputs_one, inputs_two, memory, cotangent_one, cotangent_two, target_ids, memory_ids,
    norm_gain, norm_shift, self_qkv, self_out, cross_query, cross_kv, cross_out, ffn_in, ffn_out,
):
    shape = inputs_one.shape
    length, width = shape[1:]
    o1, o2, gi1, gi2, d_mem, t_gain, t_shift, grads = local_step(
        sizes,
        inputs_one.reshape(length, width),
        inputs_two.reshape(length, width),
        memory.reshape(length, width),
        cotangent_one.reshape(length, width),
        cotangent_two.reshape(length, width),
        target_ids,
        memory_ids,
        norm_gain,
        norm_shift,
        (self_qkv, cross_kv, self_out, cross_query, cross_out, ffn_in, ffn_out),
    )
    d_qkv, d_self, d_query, d_kv, d_in, d_out, d_cross = grads
    return (
        o1.reshape(shape), o2.reshape(shape), gi1.reshape(shape), gi2.reshape(shape), d_mem.reshape(shape),
        t_gain, t_shift, d_qkv, d_self, d_query, d_kv, d_cross, d_in, d_out,
    )


def solution(mesh):
    rows = P(("narrow", "wide"), None, None)
    ids = P(("narrow", "wide"), None)
    norm, weight = P(None, "wide"), P("wide", None)
    return jax.shard_map(
        functools.partial(body, (mesh.shape["narrow"], mesh.shape["wide"])),
        mesh=mesh,
        in_specs=(rows,) * 5 + (ids,) * 2 + (norm,) * 2 + (weight,) * 7,
        out_specs=(rows,) * 5 + (norm,) * 2 + (weight,) * 7,
        check_vma=False,
    )
```

```python
import functools

import jax
import jax.numpy as jnp
from jax import lax
from jax.experimental import pallas as pl
from jax.experimental.pallas import tpu as pltpu
from jax.sharding import PartitionSpec as P

HEAD_DIM = 64
TILE = 256
SMALL = 128
FEED = 512
SEGMENTS = 5
MASKED = -1e30
MIB = 1024 * 1024
BF16 = jnp.bfloat16
F32 = jnp.float32
MESH = pl.DeviceIdType.MESH


def lower(values):
    return values.astype(BF16)


def dot(left, right):
    return lax.dot_general(left, right, (((1,), (0,)), ((), ())), preferred_element_type=F32)


def dot_bt(left, right):
    return lax.dot_general(left, right, (((1,), (1,)), ((), ())), preferred_element_type=F32)


def dot_at(left, right):
    return lax.dot_general(left, right, (((0,), (0,)), ((), ())), preferred_element_type=F32)


def standardise(values):
    centred = values - jnp.mean(values, -1, keepdims=True)
    inverse = lax.rsqrt(jnp.mean(centred * centred, -1, keepdims=True) + 1e-05)
    return centred * inverse, inverse


def norm_back(xhat, inverse, gain, incoming):
    dz = incoming * gain
    inner = jnp.mean(dz * xhat, -1, keepdims=True)
    return (dz - jnp.mean(dz, -1, keepdims=True) - xhat * inner) * inverse


def fold_rows(values):
    rows, width = values.shape
    return jnp.sum(values.reshape(rows // 8, 8, width), axis=0)


def lane_index(rows):
    return lax.broadcasted_iota(jnp.int32, (rows, 128), 1)


def row_index(rows):
    return lax.broadcasted_iota(jnp.int32, (rows, 128), 0)


def stack_heads(pair, first):
    zero = jnp.zeros_like(pair)
    return jnp.concatenate([jnp.where(first, pair, zero), jnp.where(first, zero, pair)], axis=0)


def tiles_of(low, high, length, small, visit):
    base = (low // 16) * 16
    span = high - base
    whole_tiles = (span + TILE - 1 - small) // TILE
    rest = span - whole_tiles * TILE

    def per_tile(i, carry):
        begin = base + i * TILE
        visit(TILE, pl.multiple_of(jnp.minimum(begin, length - TILE), 16), jnp.maximum(low, begin))
        return carry

    lax.fori_loop(0, whole_tiles, per_tile, 0)

    @pl.when(rest > 0)
    def _():
        begin = base + whole_tiles * TILE
        visit(small, pl.multiple_of(jnp.minimum(begin, length - small), 16), jnp.maximum(low, begin))


def each_segment(bounds, q_row, k_row, visit):
    def per_segment(s, carry):
        visit(
            bounds[q_row, s, 0], bounds[q_row, s + 1, 0], bounds[k_row, s, 0], bounds[k_row, s + 1, 0]
        )
        return carry

    lax.fori_loop(0, SEGMENTS, per_segment, 0)


def pair_lanes(offset, p):
    if isinstance(p, int):
        return slice(offset + p * 128, offset + p * 128 + 128)
    return pl.ds(pl.multiple_of(offset + p * 128, 128), 128)


def inside_rows(size, start, low, high):
    rows = row_index(size) + start
    return (rows >= low) & (rows < high)


def attend(bounds, q_row, k_row, query, keys, values, out_ref, tail_ref):
    (q_ref, q_col), (k_ref, k_col), (v_ref, v_col) = query, keys, values
    length, width = out_ref.shape
    pairs = range(width // 128)

    def visit(size, start, low, high, k_low, k_high):
        lanes = lane_index(size)
        first = lanes < HEAD_DIM
        owner, place = lanes // 4, lanes % 4
        unit = jnp.where(lane_index(2 * size) == 0, 1.0, 0.0).astype(BF16)
        keep = inside_rows(size, start, low, high)
        span = pl.ds(start, size)
        k_base = (k_low // 16) * 16
        k_tiles = (k_high - k_base + TILE - 1) // TILE

        def piece(p, k_size, k_start, low_k):
            inside = inside_rows(k_size, k_start, low_k, k_high)
            shut = (lane_index(k_size) == 0) & jnp.logical_not(inside)
            bias = jnp.where(shut, MASKED, 0.0).astype(BF16)
            queries = stack_heads(q_ref[span, pair_lanes(q_col, p)], first)
            k_span = pl.ds(k_start, k_size)
            pair_k = k_ref[k_span, pair_lanes(k_col, p)]
            pair_v = v_ref[k_span, pair_lanes(v_col, p)]
            scores = dot_bt(
                jnp.concatenate([queries, unit], axis=1), jnp.concatenate([pair_k, bias], axis=1)
            )
            ones = jnp.ones((k_size, 128), BF16)
            return scores, jnp.concatenate([pair_v, ones], axis=1)

        def finish(p, highest, total, stats):
            cols = pair_lanes(0, p)
            top, bottom = total[:size], total[size:]
            mass = jnp.where(first, top[:, 128:], bottom[:, 128:])
            merged = lower(jnp.where(first, top[:, :128], bottom[:, :128]) / mass)
            out_ref[span, cols] = jnp.where(keep, merged, out_ref[span, cols])
            peak, sums = stats
            for h, half in ((0, slice(0, size)), (1, slice(size, 2 * size))):
                here = owner == 2 * p + h
                peak = jnp.where(here, highest[half], peak)
                sums = jnp.where(here, total[half, 128:], sums)
            return peak, sums

        empty = (jnp.zeros((size, 128), F32), jnp.ones((size, 128), F32))

        def close(stats):
            peak, sums = stats
            tail = split_lanes(peak + jnp.log(sums), place, 1.0)
            tail_ref[span, :] = jnp.where(keep, tail, tail_ref[span, :])

        def rolled(one):
            close(lax.fori_loop(0, len(pairs), lambda p, stats: finish(p, *one(p), stats), empty))

        def direct(k_size):
            k_start = pl.multiple_of(jnp.minimum(k_base, length - k_size), 16)

            items = [piece(p, k_size, k_start, k_low) for p in pairs]
            tops = [jnp.max(item[0], -1, keepdims=True) for item in items]
            probs = [lower(jnp.exp(item[0] - top)) for item, top in zip(items, tops)]
            totals = [dot(prob, item[1]) for prob, item in zip(probs, items)]
            stats = empty
            for p in pairs:
                stats = finish(p, tops[p], totals[p], stats)
            close(stats)

        if size < TILE:

            @pl.when(k_tiles <= 2)
            def _():
                direct(2 * TILE)

        else:

            @pl.when(k_tiles == 1)
            def _():
                direct(TILE)

            @pl.when(k_tiles == 2)
            def _():
                direct(2 * TILE)

        @pl.when(k_tiles > 2)
        def _():
            def one(p):
                def per_key(j, carry):
                    highest, total = carry
                    begin = k_base + j * TILE
                    k_start = pl.multiple_of(jnp.minimum(begin, length - TILE), 16)
                    scores, wide_v = piece(p, TILE, k_start, jnp.maximum(k_low, begin))
                    newest = jnp.maximum(highest, jnp.max(scores, -1, keepdims=True))
                    expon = lower(jnp.exp(scores - newest))
                    return newest, total * jnp.exp(highest - newest) + dot(expon, wide_v)

                start_at = (jnp.full((2 * size, 1), MASKED, F32), jnp.zeros((2 * size, 256), F32))
                return lax.fori_loop(0, k_tiles, per_key, start_at)

            rolled(one)

    def segment(q_low, q_high, k_low, k_high):
        tiles_of(
            q_low, q_high, length, SMALL // 2, lambda size, start, low: visit(size, start, low, q_high, k_low, k_high)
        )

    each_segment(bounds, q_row, k_row, segment)


def split_lanes(values, place, lead):
    high = lower(values).astype(F32)
    rest = values - high
    middle = lower(rest).astype(F32)
    spread = jnp.where(place == 1, high, jnp.where(place == 2, middle, rest - middle))
    return lower(jnp.where(place == 0, lead, -spread))


def attend_back(bounds, q_row, k_row, query, keys, values, do_ref, out_ref, tail_ref, dq, dk, dv):
    (q_ref, q_col), (k_ref, k_col), (v_ref, v_col) = query, keys, values
    (dq_ref, dq_col), (dk_ref, dk_col), (dv_ref, dv_col) = dq, dk, dv
    length, width = do_ref.shape
    pairs = width // 128
    zero = jnp.zeros((), BF16)
    lane = lane_index(width)
    collect = (lane % 4 > 0) & (lane // 4 == row_index(width) // HEAD_DIM)
    collect = jnp.where(collect, 1.0, 0.0).astype(BF16)

    def visit(size, start, low, high, k_low, k_high):
        lanes = lane_index(size)
        first = lanes < HEAD_DIM
        owner, place = lanes // 4, lanes % 4
        closed = lower(jnp.where(place == 0, 1.0, jnp.where(place == 1, MASKED, 0.0)))
        keep = inside_rows(size, start, low, high)
        span = pl.ds(start, size)
        tail_q = jnp.where(keep, tail_ref[span, :], closed)
        centre = jnp.zeros((size, 128), F32)
        for p in range(pairs):
            cols = slice(p * 128, (p + 1) * 128)
            grad = jnp.where(keep, do_ref[span, cols], zero)
            inner = grad.astype(F32) * out_ref[span, cols].astype(F32)
            coarse = lower(inner)
            fine = lower(inner - coarse.astype(F32))
            centre = centre + dot(
                jnp.concatenate([coarse, fine], axis=1),
                jnp.concatenate([collect[cols], collect[cols]], axis=0),
            )
        tail_g = split_lanes(centre, place, 0.0)

        def per_key(k_size, k_start, low_k):
            k_span = pl.ds(k_start, k_size)
            inside = inside_rows(k_size, k_start, low_k, k_high)
            lead = lane_index(k_size) % 4 == 0
            tail = lower(jnp.where(lead, jnp.where(inside, 0.0, MASKED), 1.0))

            def load(p):
                pair_q = q_ref[span, pair_lanes(q_col, p)]
                pair_k = k_ref[k_span, pair_lanes(k_col, p)]
                pair_v = v_ref[k_span, pair_lanes(v_col, p)]
                pair_do = jnp.where(keep, do_ref[span, pair_lanes(0, p)], zero)
                queries = stack_heads(pair_q, first)
                grads = stack_heads(pair_do, first)
                ends = [
                    jnp.concatenate(
                        [jnp.where(owner == 2 * p, item, zero), jnp.where(owner == 2 * p + 1, item, zero)],
                        axis=0,
                    )
                    for item in (tail_q, tail_g)
                ]
                scores = dot_bt(
                    jnp.concatenate([pair_k, tail], axis=1),
                    jnp.concatenate([queries, ends[0]], axis=1),
                )
                slope = dot_bt(
                    jnp.concatenate([pair_v, tail], axis=1),
                    jnp.concatenate([grads, ends[1]], axis=1),
                )
                return pair_k, queries, grads, scores, slope

            def middle(item):
                pair_k, queries, grads, scores, slope = item
                probs = jnp.exp(scores)
                return pair_k, queries, grads, lower(probs), lower(probs * slope)

            def store(p, pair_k, queries, grads, probs, ds):
                dv_ref[k_span, pair_lanes(dv_col, p)] += dot(probs, grads)
                dk_ref[k_span, pair_lanes(dk_col, p)] += dot(ds, queries)
                turned = [dot_at(ds[:, :size], pair_k), dot_at(ds[:, size:], pair_k)]
                dq_ref[span, pair_lanes(dq_col, p)] += jnp.where(first, turned[0], turned[1])

            ahead = load(0)
            for p in range(pairs):
                item = ahead
                if p + 1 < pairs:
                    ahead = load(p + 1)
                store(p, *middle(item))

        tiles_of(k_low, k_high, length, SMALL // 2, per_key)

    def segment(q_low, q_high, k_low, k_high):
        tiles_of(
            q_low, q_high, length, SMALL, lambda size, start, low: visit(size, start, low, q_high, k_low, k_high)
        )

    each_segment(bounds, q_row, k_row, segment)


def forward_kernel(bounds, xs, block, norms, w_self, w_query, attended, tail, y1, q2, queries):
    phase = pl.program_id(1)
    length, width = queries.shape

    @pl.when(phase == 0)
    def _():
        queries[...] = block[0, :, :width]

    attend(
        bounds, 0, phase, (queries, 0), (block.at[0], width), (block.at[0], 2 * width),
        attended.at[0, 0], tail.at[0, 0],
    )

    @pl.when(phase == 0)
    def _():
        for i in range(length // TILE):
            span = slice(i * TILE, (i + 1) * TILE)
            after = xs[0, span, :].astype(F32) + dot(attended[0, 0, span, :], w_self[...])
            y1[0, span, :] = after
            xhat, _ = standardise(after)
            h2 = lower(xhat * norms[1:2, :] + norms[4:5, :])
            asked = lower(dot(h2, w_query[...]) * HEAD_DIM ** (-0.5))
            queries[span, :] = asked
            q2[0, span, :] = asked


def feed_kernel(
    per_step, y1, a2, g1, g2, norms, w_cross, w_in, w_out,
    o1, o2, h3, r, du, e2, dy2, do2, dnorm,
):
    i = pl.program_id(0)
    width = w_cross.shape[0]
    is_first = i < per_step
    grad = jnp.where(is_first, g1[...], g2[...])
    after = y1[0] + dot(a2[0, 0], w_cross[...])
    xhat, inverse = standardise(after)
    normed = lower(xhat * norms[2:3, :] + norms[5:6, :])
    h3[0] = normed
    result = after
    dh3 = jnp.zeros_like(after)
    slope = (2.0 / jnp.pi) ** 0.5
    chunks = w_in.shape[1] // width

    def enter(c):
        cols = slice(c * width, (c + 1) * width)
        return dot(normed, w_in[:, cols]), dot_bt(grad, w_out[cols, :])

    ahead = enter(0)
    for c in range(chunks):
        cols = slice(c * width, (c + 1) * width)
        u, dr = ahead
        if c + 1 < chunks:
            ahead = enter(c + 1)
        square = u * u
        half = 0.5 + 0.5 * jnp.tanh(u * (slope + slope * 0.044715 * square))
        hidden = lower(u * half)
        r[0, :, cols] = hidden
        bend = u * (2 * slope + 6 * slope * 0.044715 * square)
        pre = lower(dr * (half * (1.0 + (1.0 - half) * bend)))
        du[0, :, cols] = pre
        result = result + dot(hidden, w_out[cols, :])
        dh3 = dh3 + dot_bt(pre, w_in[:, cols])

    @pl.when(is_first)
    def _():
        o1[...] = lower(result)

    @pl.when(jnp.logical_not(is_first))
    def _():
        o2[...] = lower(result)

    @pl.when(i == 0)
    def _():
        dnorm[...] = jnp.zeros_like(dnorm)

    dnorm[0] += fold_rows(dh3 * xhat)
    dnorm[1] += fold_rows(dh3)
    back = grad.astype(F32) + norm_back(xhat, inverse, norms[2:3, :], dh3)
    dy2[0] = back
    low = lower(back)
    e2[0] = low
    do2[0] = lower(dot_bt(low, w_cross[...]))


def feed_grad_kernel(
    small, h3, g1, g2, du, r, a2_hbm, e2_hbm, mine, theirs,
    turned, turned_g, a2, e2, d_in, d_out, d_cross, sem,
):
    c = pl.program_id(0)
    last = pl.num_programs(0) - 1
    half, width = g1.shape
    hidden = d_out.shape[4]
    group = hidden // width
    rows = width // group
    slot = lax.rem(c, 2)

    core = lax.rem(lax.axis_index("wide"), 2)
    lines = width // (2 * small)
    depth = rows // (2 * small)

    def copies(at, chunk):
        cols = pl.ds(pl.multiple_of(chunk * width, width), width)
        deep = pl.ds(chunk * depth, depth)
        found = []
        for k, (out, side) in enumerate(((mine, core), (theirs, 1 - core))):
            found.append(
                pltpu.make_async_copy(d_in.at[at, :, side], out.at[:, :, cols], sem.at[2 * k, at])
            )
            found.append(
                pltpu.make_async_copy(
                    d_out.at[at, :, side], out.at[deep, :, hidden + width :], sem.at[2 * k + 1, at]
                )
            )
        return found

    loads = [
        pltpu.make_async_copy(a2_hbm.at[:, 1], a2, sem.at[4, 0]),
        pltpu.make_async_copy(e2_hbm, e2, sem.at[4, 1]),
    ]
    cross = [
        pltpu.make_async_copy(
            d_cross.at[:, side], out.at[:, :, hidden : hidden + width], sem.at[5, k]
        )
        for k, (out, side) in enumerate(((mine, core), (theirs, 1 - core)))
    ]

    @pl.when(c >= 2)
    def _():
        for copy in copies(slot, c - 2):
            copy.wait()

    @pl.when(c == 0)
    def _():
        for copy in loads:
            copy.start()
        turned[...] = h3[...].T
        turned_g[:, :half] = g1[...].T
        turned_g[:, half:] = g2[...].T

    d_in[slot] = lower(dot(turned[...], du[...])).reshape(d_in.shape[1:])
    part = lower(dot(turned_g[...], r[...])).T
    for w in range(width // (group * small)):
        for j in range(group):
            at = (w * group + j) * small
            d_out[slot, w // 2, w % 2, :, j * width : (j + 1) * width] = part[at : at + small]
    for copy in copies(slot, c):
        copy.start()

    @pl.when(c == last)
    def _():
        wait_all(loads)
        d_cross[...] = lower(dot(a2[0].T, e2[0]) + dot(a2[1].T, e2[1])).reshape(d_cross.shape)
        for copy in cross:
            copy.start()
        for copy in copies(1 - slot, c - 1) + copies(slot, c):
            copy.wait()
        wait_all(cross)


def cross_back_kernel(
    bounds, q2, keys, values, a1, a2, stat2, do2, y1, dy2, mem_turned, norms, w_query, w_self, w_kv,
    dy1, do1, d_query, d_self, d_kv, d_mem, dnorm,
    dq_sum, dkv_sum, h2, low_q, low_e,
):
    step = pl.program_id(0)
    length, width = q2.shape[1:]

    @pl.when(step == 0)
    def _():
        dkv_sum[...] = jnp.zeros_like(dkv_sum)
        dnorm[...] = jnp.zeros_like(dnorm)

    dq_sum[...] = jnp.zeros_like(dq_sum)
    attend_back(
        bounds, 0, 1, (q2.at[0], 0), (keys.at[0], 0), (values.at[0], 0), do2.at[0], a2.at[0, 0], stat2.at[0, 0],
        (dq_sum, 0), (dkv_sum, 0), (dkv_sum, width),
    )

    def rows(i):
        span = slice(i * TILE, (i + 1) * TILE)
        grad_q = lower(dq_sum[span, :] * HEAD_DIM ** (-0.5))
        low_q[step, span, :] = grad_q
        xhat, inverse = standardise(y1[0, span, :])
        h2[step, span, :] = lower(xhat * norms[1:2, :] + norms[4:5, :])
        dh2 = dot_bt(grad_q, w_query[...])
        dnorm[0] += fold_rows(dh2 * xhat)
        dnorm[1] += fold_rows(dh2)
        back = dy2[0, span, :] + norm_back(xhat, inverse, norms[1:2, :], dh2)
        dy1[0, span, :] = back
        low = lower(back)
        low_e[step, span, :] = low
        do1[0, span, :] = lower(dot_bt(low, w_self[...]))

    for i in range(length // TILE):
        rows(i)

    @pl.when(step == 1)
    def _():
        d_query[...] = lower(dot(h2[0].T, low_q[0]) + dot(h2[1].T, low_q[1]))
        d_self[...] = lower(dot(a1[0, 0].T, low_e[0]) + dot(a1[1, 0].T, low_e[1]))
        pair = lower(dkv_sum[...])
        d_kv[...] = lower(dot(mem_turned[...], pair))
        d_mem[...] = dot_bt(pair, w_kv[...])


def self_back_kernel(bounds, qkv, a1, stat1, do1, low, sums):
    width = do1.shape[2]
    sums[...] = jnp.zeros_like(sums)
    attend_back(
        bounds, 0, 0, (qkv.at[0], 0), (qkv.at[0], width), (qkv.at[0], 2 * width),
        do1.at[0], a1.at[0, 0], stat1.at[0, 0], (sums, 0), (sums, width), (sums, 2 * width),
    )
    low[0, :, :width] = lower(sums[:, :width] * HEAD_DIM ** (-0.5))
    low[0, :, width:] = lower(sums[:, width:])


def flip(index, mask):
    out, bit = index, 1
    while bit <= mask:
        if mask & bit:
            out = out + bit - 2 * bit * lax.rem(lax.div(index, bit), 2)
        bit *= 2
    return out


class Links:
    def __init__(self, sizes, send, recv):
        self.members, wides = sizes
        self.lines = wides // 2
        self.group = min(4, self.members)
        self.narrow, self.wide = lax.axis_index("narrow"), lax.axis_index("wide")
        self.line, self.core = lax.div(self.wide, 2), lax.rem(self.wide, 2)
        self.part = lax.rem(self.narrow, self.group)
        self.send, self.recv, self.used = send, recv, 0

    def core_peer(self):
        return (self.narrow, flip(self.wide, 1))

    def plane_peer(self, mask):
        return (flip(self.narrow, mask), self.wide)

    def line_peer(self, mask):
        return (self.narrow, 2 * flip(self.line, mask) + self.core)

    def far_masks(self):
        masks, mask = [], self.group
        while mask < self.members:
            masks.append(mask)
            mask *= 2
        return masks

    def barrier(self, far):
        semaphore = pltpu.get_barrier_semaphore()
        peers = [self.core_peer()]
        peers += [self.plane_peer(m) for m in range(1, self.group)]
        peers += [self.line_peer(m) for m in range(1, self.lines)]
        if far:
            peers += [self.plane_peer(m) for m in self.far_masks()]
        for peer in peers:
            pl.semaphore_signal(semaphore, inc=1, device_id=peer, device_id_type=MESH)
        pl.semaphore_wait(semaphore, len(peers))

    def push(self, src, dst, peer):
        slot = self.used
        self.used += 1
        copy = pltpu.make_async_remote_copy(
            src_ref=src,
            dst_ref=dst,
            send_sem=self.send.at[slot],
            recv_sem=self.recv.at[slot],
            device_id=peer,
            device_id_type=MESH,
        )
        copy.start()
        return copy

    def quarter(self, part, cols):
        size = cols // self.group
        return pl.ds(pl.multiple_of(part * size, size), size)


def wait_all(copies):
    for copy in copies:
        copy.wait()


class Gathered:
    def __init__(self, links, shard, full, masks):
        self.links, self.shard, self.full, self.masks = links, shard, full, masks
        self.cols = shard.shape[-1]

    def start_line(self):
        links = self.links
        self.full[links.line, links.core] = self.shard[...]
        mine = links.quarter(links.part, self.cols)
        self.copies = [
            links.push(
                self.shard.at[:, mine], self.full.at[links.line, links.core, :, mine], links.line_peer(m)
            )
            for m in range(1, links.lines)
        ]

    def spread(self, parts, mask):
        links = self.links
        wait_all(self.copies)
        self.copies = []
        for k in range(1, links.lines):
            for part in parts:
                cols = links.quarter(part, self.cols)
                place = self.full.at[flip(links.line, k), links.core, :, cols]
                self.copies.append(links.push(place, place, links.plane_peer(mask)))

    def start_plane(self):
        self.spread([self.links.part], self.masks[0])

    def cross_plane(self):
        self.spread([self.links.part, flip(self.links.part, self.masks[0])], self.masks[1])

    def start_core(self):
        links = self.links
        wait_all(self.copies)
        place = self.full.at[:, links.core]
        self.copies = [links.push(place, place, links.core_peer())]

    def finish(self):
        wait_all(self.copies)


def gather_slots(sizes, pieces):
    lines, group = sizes[1] // 2, min(4, sizes[0])
    return pieces * (lines - 1 + (lines - 1) * (group - 1) + 1) + lines


def gather_kernel(
    sizes, norm_gain, norm_shift, target_ids, memory_ids, x1_hbm, x2_hbm, mem_hbm,
    g_qkv, g_kv, g_self, g_query, g_cross, g_in, g_out,
    xs, blocks, bounds, norms, h1_turned, mem_turned, f_qkv, f_kv, f_self, f_query, f_cross, f_in, f_out,
    rows_in, placed, s_qkv, s_kv, s_self, s_query, s_cross, s_in, s_out,
    h1, turned, turned_mem, v_qkv, v_kv, v_self, v_query, v_cross, v_in, v_out, o_qkv, o_kv, norm_all, send, recv, local,
):
    links = Links(sizes, send, recv)
    _, length, width = rows_in.shape
    x1, x2, mem = rows_in.at[0], rows_in.at[1], rows_in.at[2]
    small = width // sizes[1]
    used = [0]

    def local_copy(src, dst):
        copy = pltpu.make_async_copy(src, dst, local.at[used[0]])
        used[0] += 1
        copy.start()
        return copy

    landing = []

    def piece(shard, full, out):
        landing.append((full, out))
        return Gathered(links, shard, full, (len(landing) % 2 + 1, 2 - len(landing) % 2))

    shards = [
        local_copy(src, dst)
        for src, dst in (
            (g_qkv, s_qkv), (g_kv, s_kv), (g_self, s_self), (g_query, s_query), (g_cross, s_cross),
            (g_in, s_in), (g_out, s_out),
        )
    ]
    loads = [local_copy(src, dst) for src, dst in ((x1_hbm, x1), (x2_hbm, x2), (mem_hbm, mem))]
    links.barrier(False)
    placed[...] = jnp.zeros_like(placed)
    placed[0:3, :] = norm_gain[...].astype(F32)
    placed[3:6, :] = norm_shift[...].astype(F32)
    column = lax.broadcasted_iota(jnp.int32, (small, width), 1)
    row = lax.broadcasted_iota(jnp.int32, (small, width), 0)
    spot = jnp.where(column == row + links.wide * small, 1.0, 0.0).astype(BF16)
    norm_all[links.line, links.core] = dot(lower(placed[...]), spot)
    level = lax.broadcasted_iota(jnp.int32, (8, length), 0)
    for k, ids in enumerate((target_ids, memory_ids)):
        order = jnp.where(ids[...] < 0, SEGMENTS - 1, ids[...])
        below = jnp.where(order < level, 1.0, 0.0)
        starts = jnp.sum(below, axis=1, keepdims=True).astype(jnp.int32)
        bounds[k] = jnp.broadcast_to(starts, (8, 128))
    wait_all(shards)
    pieces = []
    for c in range(3):
        cols = slice(c * width, (c + 1) * width)
        pieces.append(piece(s_qkv.at[:, cols], v_qkv.at[c], f_qkv.at[:, :, :, cols]))
    for c in range(2):
        cols = slice(c * width, (c + 1) * width)
        pieces.append(piece(s_kv.at[:, cols], v_kv.at[c], f_kv.at[:, :, :, cols]))
    pieces.append(piece(s_self, v_self, f_self))
    pieces.append(piece(s_query, v_query, f_query))
    pieces.append(piece(s_cross, v_cross, f_cross))
    half = s_in.shape[1] // 2
    for c in range(2):
        cols = slice(c * half, (c + 1) * half)
        pieces.append(piece(s_in.at[:, cols], v_in.at[c], f_in.at[:, :, :, cols]))
    half = s_out.shape[0] // 2
    for c in range(2):
        rows = slice(c * half, (c + 1) * half)
        pieces.append(piece(s_out.at[rows], v_out.at[c], f_out.at[:, :, rows]))

    own = norm_all.at[links.line, links.core]
    norm_copies = [links.push(own, own, links.line_peer(m)) for m in range(1, links.lines)]
    for p in range(4):
        pieces[p].start_line()
    wait_all(loads)
    outgoing = [local_copy(x1, xs.at[0]), local_copy(x2, xs.at[1])]
    wait_all(norm_copies)
    place = norm_all.at[:, links.core]
    norm_copy = links.push(place, place, links.core_peer())
    pieces[0].start_plane()
    norm_copy.wait()
    every = norm_all[...]
    total = every[0, 0]
    for k in range(1, 2 * links.lines):
        total = total + every[k // 2, k % 2]
    norms[...] = total
    gain, shift = total[0:1, :], total[3:4, :]

    def normalise(t, x):
        for i in range(length // TILE):
            span = slice(i * TILE, (i + 1) * TILE)
            xhat, _ = standardise(x[span, :].astype(F32))
            h1[t, span, :] = lower(xhat * gain + shift)

    def turn():
        turned[:, :length] = h1[0].T
        turned[:, length:] = h1[1].T
        turned_mem[...] = mem[...].T
        outgoing.append(local_copy(turned, h1_turned))
        outgoing.append(local_copy(turned_mem, mem_turned))

    def project(c):
        def run():
            weight = v_qkv[c].reshape(width, width)
            scale = HEAD_DIM ** (-0.5) if c == 0 else 1.0
            for t in range(2):

                def rows(i, carry, t=t):
                    span = pl.ds(pl.multiple_of(i * 2 * TILE, 2 * TILE), 2 * TILE)
                    o_qkv[c, t, span, :] = lower(dot(h1[t, span, :], weight) * scale)
                    return carry

                lax.fori_loop(0, length // (2 * TILE), rows, 0)
            cols = slice(c * width, (c + 1) * width)
            outgoing.append(local_copy(o_qkv.at[c], blocks.at[0:2, :, cols]))

        return run

    def project_memory(c):
        def run():
            weight = v_kv[c].reshape(width, width)

            def rows(i, carry):
                span = pl.ds(pl.multiple_of(i * 2 * TILE, 2 * TILE), 2 * TILE)
                o_kv[c, span, :] = lower(dot(mem[span, :], weight))
                return carry

            lax.fori_loop(0, length // (2 * TILE), rows, 0)
            cols = slice((c + 1) * width, (c + 2) * width)
            outgoing.append(local_copy(o_kv.at[c], blocks.at[2, :, cols]))

        return run

    work = {c: project(c) for c in range(3)} | {3 + c: project_memory(c) for c in range(2)}
    count = len(pieces)
    for t in range(1, count + 6):
        if 3 + t < count:
            pieces[3 + t].start_line()
        if t < count:
            pieces[t].start_plane()
        if t == 1:
            normalise(0, x1)
        if t == 2:
            normalise(1, x2)
        if 0 <= t - 2 < count:
            pieces[t - 2].cross_plane()
        if 0 <= t - 4 < count:
            pieces[t - 4].start_core()
        if 0 <= t - 5 < count:
            one = t - 5
            pieces[one].finish()
            outgoing.append(local_copy(*landing[one]))
            if one in work:
                work[one]()
            if one == 5:
                turn()
    wait_all(outgoing)


class Reduced:
    def __init__(self, links, bufs, out, masks, source=None, ready=None):
        self.links, self.out, self.masks, self.source, self.ready = links, out, masks, source, ready
        self.lined = source is not None or ready is not None
        self.crecv, self.chip, self.precv, self.plane, self.lrecv, self.mine, self.xrecv, self.full, self.half = bufs
        self.cols = self.full.shape[-1]

    def start_core(self):
        links = self.links
        self.copies = [links.push(self.source.at[:, 1 - links.core], self.crecv, links.core_peer())]

    def start_plane(self):
        links = self.links
        if self.source is not None:
            wait_all(self.copies)
            for k in range(links.lines):
                self.chip[k] = lower(
                    self.source[k, links.core].astype(F32) + self.crecv[k].astype(F32)
                )
        first, second = self.masks
        near = flip(links.part, first)
        self.copies = [
            links.push(
                self.chip.at[:, :, links.quarter(part, self.cols)], self.precv.at[k], links.plane_peer(first)
            )
            for k, part in enumerate((near, flip(near, second)))
        ]

    def cross_plane(self):
        links = self.links
        wait_all(self.copies)
        second = self.masks[1]
        far = self.chip[:, :, links.quarter(flip(links.part, second), self.cols)].astype(F32)
        self.half[...] = lower(far + self.precv[1].astype(F32))
        self.copies = [links.push(self.half, self.precv.at[2], links.plane_peer(second))]

    def start_line(self):
        links = self.links
        if self.ready is not None:
            total = self.ready[0][...].astype(F32)
            for item in self.ready[1:]:
                total = total + item[...].astype(F32)
        else:
            wait_all(self.copies)
            total = self.chip[:, :, links.quarter(links.part, self.cols)].astype(F32)
            total = total + self.precv[0].astype(F32) + self.precv[2].astype(F32)
        self.plane[...] = lower(total)
        if not self.lined:
            self.copies = []
            return
        self.copies = [
            links.push(self.plane.at[flip(links.line, m)], self.lrecv.at[m - 1], links.line_peer(m))
            for m in range(1, links.lines)
        ]

    def start_gather(self):
        links = self.links
        wait_all(self.copies)
        if not self.lined:
            total = self.plane[0].astype(F32)
        else:
            total = self.plane[links.line].astype(F32)
            for m in range(1, links.lines):
                total = total + self.lrecv[m - 1].astype(F32)
        for i, mask in enumerate(links.far_masks()):
            self.xrecv[2 * i] = lower(total)
            links.push(self.xrecv.at[2 * i], self.xrecv.at[2 * i + 1], links.plane_peer(mask)).wait()
            total = self.xrecv[2 * i].astype(F32) + self.xrecv[2 * i + 1].astype(F32)
        self.mine[...] = lower(total)
        place = self.full.at[:, links.quarter(links.part, self.cols)]
        place[...] = self.mine[...]
        self.copies = [links.push(self.mine, place, links.plane_peer(self.masks[0]))]

    def cross_gather(self):
        links = self.links
        wait_all(self.copies)
        self.copies = []
        for part in (links.part, flip(links.part, self.masks[0])):
            place = self.full.at[:, links.quarter(part, self.cols)]
            self.copies.append(links.push(place, place, links.plane_peer(self.masks[1])))

    def finish(self):
        wait_all(self.copies)
        self.out[...] = self.full[...]


def reduced_scratch(sizes, rows, cols, kind):
    members, wides = sizes
    lines, group = wides // 2, min(4, members)
    part = cols // group
    depth = 1 if kind == "shard" else lines
    far = max(2, 2 * (members // group - 1))
    small = (1, 16, 128)
    return [
        pltpu.VMEM((lines, rows, cols) if kind == "whole" else small, BF16),
        pltpu.VMEM(small if kind == "ready" else (depth, rows, cols), BF16),
        pltpu.VMEM(small if kind == "ready" else (group - 1, depth, rows, part), BF16),
        pltpu.VMEM((depth, rows, part), BF16),
        pltpu.VMEM(small if kind == "shard" else (lines - 1, rows, part), BF16),
        pltpu.VMEM((rows, part), BF16),
        pltpu.VMEM((far, rows, part), BF16),
        pltpu.VMEM((rows, cols), BF16),
        pltpu.VMEM(small if kind == "ready" else (depth, rows, part), BF16),
    ]


def reduce_slots(sizes, jobs):
    members, wides = sizes
    lines, group = wides // 2, min(4, members)
    return (jobs + 1) * (1 + 2 * (group - 1) + lines - 1 + members // group)


BUFS = 9


def finish_kernel(
    sizes, low_hbm, h1_hbm, xs_hbm, dy1_hbm, w_hbm, self_hbm, query_hbm, kv_hbm, norms, dnorm1, dnorm2, *rest,
):
    group = min(4, sizes[0])
    ready, rest = rest[:group], rest[group:]
    gi1, gi2, t_qkv, t_self, t_query, t_kv, t_joint, t_norm = rest[:8]
    low, xs, dy1, w_qkv, h1, grads, norm_slots, d_self, d_query, d_kv = rest[8:18]
    bufs = rest[18:-3]
    send, recv, local = rest[-3:]
    links = Links(sizes, send, recv)
    _, length, width = xs.shape
    early = [
        pltpu.make_async_copy(kv_hbm, d_kv, local.at[5]),
        pltpu.make_async_copy(query_hbm, d_query, local.at[6]),
        pltpu.make_async_copy(self_hbm, d_self, local.at[7]),
    ]
    loads = [
        pltpu.make_async_copy(xs_hbm, xs, local.at[2]),
        pltpu.make_async_copy(dy1_hbm, dy1, local.at[3]),
        pltpu.make_async_copy(w_hbm, w_qkv, local.at[4]),
    ]
    turned = pltpu.make_async_copy(h1_hbm, h1, local.at[0])
    bands = []
    for c in range(3):
        cols = slice(c * width, (c + 1) * width)
        at = 1 if c == 0 else 7 + c
        bands.append(pltpu.make_async_copy(low_hbm.at[:, :, cols], low.at[:, :, cols], local.at[at]))
    for copy in [turned] + bands[:1] + early + bands[1:]:
        copy.start()
    links.barrier(True)
    wait_all(early)

    taken = [0]

    def job(out, **kind):
        at = taken[0] * BUFS
        taken[0] += 1
        masks = (2 - taken[0] % 2, 1 + taken[0] % 2)
        return Reduced(links, bufs[at : at + BUFS], out, masks, **kind)

    others = [job(t_kv, source=d_kv), job(t_query, source=d_query), job(t_self, source=d_self)]
    heads = [job(t_qkv.at[:, c * width : (c + 1) * width], source=grads.at[c]) for c in range(3)]
    joint = job(t_joint, ready=ready)
    for one in others:
        one.start_core()
    joint.start_line()
    gain = norms[0:1, :]
    turned.wait()
    for c in range(3):
        cols = slice(c * width, (c + 1) * width)
        bands[c].wait()
        if c == 2:
            for copy in loads:
                copy.start()
        value = dot(h1[:, :length], low[0, :, cols]) + dot(h1[:, length:], low[1, :, cols])
        grads[c] = lower(value).reshape(grads.shape[1:])
        heads[c].start_core()
        if c > 0:
            heads[c - 1].start_plane()
        if c == 0:
            for one in others:
                one.start_plane()
    heads[2].start_plane()
    wait_all(loads)
    stores = []
    dgain = jnp.zeros((8, width), F32)
    dshift = jnp.zeros((8, width), F32)
    steps = [
        lambda: [one.cross_plane() for one in others],
        lambda: heads[0].cross_plane(),
        lambda: (heads[1].cross_plane(), joint.start_gather()),
        lambda: (heads[2].cross_plane(), heads[0].start_line()),
        lambda: (heads[1].start_line(), joint.cross_gather()),
        lambda: heads[2].start_line(),
        lambda: [one.start_line() for one in others],
    ]
    weight = w_qkv[...]
    for t in range(2):
        for i in range(length // TILE):
            span = slice(i * TILE, (i + 1) * TILE)
            xhat, inverse = standardise(xs[t, span, :].astype(F32))
            dh1 = dot_bt(low[t, span, :], weight)
            dgain = dgain + fold_rows(dh1 * xhat)
            dshift = dshift + fold_rows(dh1)
            dy1[t, span, :] = dy1[t, span, :] + norm_back(xhat, inverse, gain, dh1)
            number = t * (length // TILE) + i
            copy = pltpu.make_async_copy(
                dy1.at[t, span, :], (gi1, gi2)[t].at[span, :], local.at[10 + number]
            )
            copy.start()
            stores.append(copy)
            if number < len(steps):
                steps[number]()
    rows = [jnp.sum(item, axis=0, keepdims=True) for item in (dgain, dnorm1[0], dnorm2[0], dshift, dnorm1[1], dnorm2[1])]
    total = jnp.concatenate(rows + [jnp.zeros((2, width), F32)], axis=0)

    def send(first, own, peers, total):
        norm_slots[first + own] = total
        place = norm_slots.at[first + own]
        return [links.push(place, place, peer) for peer in peers]

    def receive(first, count, copies):
        wait_all(copies)
        out = norm_slots[first]
        for k in range(1, count):
            out = out + norm_slots[first + k]
        return out

    copies = send(0, links.core, [links.core_peer()], total)
    total = receive(0, 2, copies)
    copies = send(2, links.part, [links.plane_peer(m) for m in range(1, links.group)], total)
    heads[0].start_gather()
    heads[1].start_gather()
    total = receive(2, links.group, copies)
    first = 2 + links.group
    copies = send(first, links.line, [links.line_peer(m) for m in range(1, links.lines)], total)
    heads[2].start_gather()
    for one in others:
        one.start_gather()
    for one in heads:
        one.cross_gather()
    total = receive(first, links.lines, copies)
    first += links.lines
    for mask in links.far_masks():
        side = lax.rem(lax.div(links.narrow, mask), 2)
        total = receive(first, 2, send(first, side, [links.plane_peer(mask)], total))
        first += 2
    t_norm[...] = total
    for one in others:
        one.cross_gather()
    joint.finish()
    for one in heads + others:
        one.finish()
    wait_all(stores)


def emit_kernel(
    wides, f1, f2, b_qkv, b_self, b_query, b_kv, b_joint, t_norm,
    gi1, gi2, gain, shift, t_qkv, t_self, t_query, t_kv, t_in, t_out, t_cross,
):
    gi1[...] = f1[...]
    gi2[...] = f2[...]
    width = gi1.shape[1]
    small, hidden = t_in.shape

    @pl.when(pl.program_id(0) == 0)
    def _():
        for src, dst in (
            (b_qkv, t_qkv), (b_self, t_self), (b_query, t_query), (b_kv, t_kv),
            (b_joint.at[:, :hidden], t_in), (b_joint.at[:, hidden : hidden + width], t_cross),
        ):
            dst[...] = src[...].astype(F32)
        for j in range(hidden // width):
            begin = hidden + width + j * width
            t_out[j * small : (j + 1) * small, :] = b_joint[:, begin : begin + width].astype(F32)
        at = lax.axis_index("wide") * small
        mine = pltpu.roll(t_norm[...], lax.rem(width - at, width), 1)
        gain[...] = mine[:3, :small]
        shift[...] = mine[3:6, :small]


def whole(shape):
    zeros = (0,) * len(shape)
    return pl.BlockSpec(shape, lambda *_: zeros, pipeline_mode=pl.Buffered(1))


def fixed(shape):
    zeros = (0,) * len(shape)
    return pl.BlockSpec(shape, lambda *_: zeros)


def by_step(shape):
    return pl.BlockSpec((1,) + shape, lambda t, *_: (t, 0, 0))


def params(limit):
    return pltpu.CompilerParams(
        vmem_limit_bytes=limit * MIB, dimension_semantics=("arbitrary",)
    )


def struct(shape, dtype):
    return jax.ShapeDtypeStruct(shape, dtype)


def call_forward(bounds, xs, blocks, norms, w_self, w_query):
    length, width = xs.shape[1:]
    each = pl.BlockSpec((1, length, width), lambda t, p, *_: (t, 0, 0))
    return pl.pallas_call(
        forward_kernel,
        grid_spec=pltpu.PrefetchScalarGridSpec(
            num_scalar_prefetch=1,
            grid=(2, 2),
            in_specs=[
                each,
                pl.BlockSpec((1, length, 3 * width), lambda t, p, *_: (t + p * (2 - t), 0, 0)),
                whole((8, width)), whole(w_self.shape), whole(w_query.shape),
            ],
            out_specs=[
                pl.BlockSpec((1, 1, length, width), lambda t, p, *_: (t, p, 0, 0)),
                pl.BlockSpec((1, 1, length, 128), lambda t, p, *_: (t, p, 0, 0)),
                each, each,
            ],
            scratch_shapes=[pltpu.VMEM((length, width), BF16)],
        ),
        out_shape=[
            struct((2, 2, length, width), BF16),
            struct((2, 2, length, 128), BF16),
            struct((2, length, width), F32),
            struct((2, length, width), BF16),
        ],
        compiler_params=pltpu.CompilerParams(
            vmem_limit_bytes=60 * MIB, dimension_semantics=("arbitrary", "arbitrary")
        ),
        name="attend_forward",
    )(bounds, xs, blocks, norms, w_self, w_query)


def call_cross_back(bounds, q2, blocks, attended, tail, do2, y1, dy2, mem_turned, norms, w_query, w_self, w_kv):
    length, width = q2.shape[1:]
    norm_spec = whole((8, width))
    step_low = by_step((length, width))
    return pl.pallas_call(
        cross_back_kernel,
        grid_spec=pltpu.PrefetchScalarGridSpec(
            num_scalar_prefetch=1,
            grid=(2,),
            in_specs=[
                step_low,
                pl.BlockSpec((1, length, width), lambda *_: (2, 0, 1), pipeline_mode=pl.Buffered(1)),
                pl.BlockSpec((1, length, width), lambda *_: (2, 0, 2), pipeline_mode=pl.Buffered(1)),
                pl.BlockSpec((2, 1, length, width), lambda *_: (0, 0, 0, 0), pipeline_mode=pl.Buffered(1)),
                pl.BlockSpec((1, 1, length, width), lambda t, *_: (t, 1, 0, 0)),
                pl.BlockSpec((1, 1, length, 128), lambda t, *_: (t, 1, 0, 0)),
                step_low,
                step_low, step_low, whole(mem_turned.shape), norm_spec,
                whole(w_query.shape), whole(w_self.shape), whole(w_kv.shape),
            ],
            out_specs=[
                step_low, step_low, fixed((width, width)), fixed((width, width)), fixed((width, 2 * width)),
                fixed((length, width)), fixed((2, 8, width)),
            ],
            scratch_shapes=[
                pltpu.VMEM((length, width), F32),
                pltpu.VMEM((length, 2 * width), F32),
                pltpu.VMEM((2, length, width), BF16),
                pltpu.VMEM((2, length, width), BF16),
                pltpu.VMEM((2, length, width), BF16),
            ],
        ),
        out_shape=[
            struct((2, length, width), F32),
            struct((2, length, width), BF16),
            struct((width, width), BF16),
            struct((width, width), BF16),
            struct((width, 2 * width), BF16),
            struct((length, width), F32),
            struct((2, 8, width), F32),
        ],
        compiler_params=params(60),
        cost_estimate=pl.CostEstimate(flops=45000000000, bytes_accessed=20000000, transcendentals=0),
        name="cross_back",
    )(bounds, q2, blocks, blocks, attended, attended, tail, do2, y1, dy2, mem_turned, norms, w_query, w_self, w_kv)


def call_self_back(bounds, blocks, attended, tail, do1):
    length, width = do1.shape[1:]
    norm_spec = whole((8, width))
    step_low = by_step((length, width))
    return pl.pallas_call(
        self_back_kernel,
        grid_spec=pltpu.PrefetchScalarGridSpec(
            num_scalar_prefetch=1,
            grid=(2,),
            in_specs=[
                by_step((length, 3 * width)),
                pl.BlockSpec((1, 1, length, width), lambda t, *_: (t, 0, 0, 0)),
                pl.BlockSpec((1, 1, length, 128), lambda t, *_: (t, 0, 0, 0)),
                step_low,
            ],
            out_specs=by_step((length, 3 * width)),
            scratch_shapes=[pltpu.VMEM((length, 3 * width), F32)],
        ),
        out_shape=struct((2, length, 3 * width), BF16),
        compiler_params=params(60),
        cost_estimate=pl.CostEstimate(flops=30000000000, bytes_accessed=20000000, transcendentals=0),
        name="self_back",
    )(bounds, blocks, attended, tail, do1)


def call_gather(sizes, norm_gain, norm_shift, target_ids, memory_ids, x1, x2, mem, shards):
    length, width = x1.shape
    lines = sizes[1] // 2
    small = width // sizes[1]
    vmem = pl.BlockSpec(memory_space=pltpu.VMEM)
    anywhere = pl.BlockSpec(memory_space=pl.ANY)

    def full(shape):
        return struct((lines, 2, shape[0], shape[1]), BF16)

    pieces = 12
    slots = gather_slots(sizes, pieces)
    return pl.pallas_call(
        functools.partial(gather_kernel, sizes),
        in_specs=[vmem] * 4 + [pl.BlockSpec(memory_space=pltpu.HBM)] * 10,
        out_specs=[anywhere] * 2 + [vmem] * 2 + [anywhere] * 9,
        out_shape=[
            struct((2, length, width), BF16),
            struct((3, length, 3 * width), BF16),
            struct((2, 8, 128), jnp.int32),
            struct((8, width), F32),
            struct((width, 2 * length), BF16),
            struct((width, length), BF16),
        ]
        + [full(item.shape) for item in shards],
        scratch_shapes=[pltpu.VMEM((3, length, width), BF16), pltpu.VMEM((8, small), F32)]
        + [pltpu.VMEM(item.shape, BF16) for item in shards]
        + [
            pltpu.VMEM((2, length, width), BF16),
            pltpu.VMEM((width, 2 * length), BF16),
            pltpu.VMEM((width, length), BF16),
            pltpu.VMEM((3, lines, 2, small, width), BF16),
            pltpu.VMEM((2, lines, 2, small, width), BF16),
            pltpu.VMEM((lines, 2, small, width), BF16),
            pltpu.VMEM((lines, 2, small, width), BF16),
            pltpu.VMEM((lines, 2, small, width), BF16),
            pltpu.VMEM((2, lines, 2, small, shards[5].shape[1] // 2), BF16),
            pltpu.VMEM((2, lines, 2, shards[6].shape[0] // 2, width), BF16),
            pltpu.VMEM((3, 2, length, width), BF16),
            pltpu.VMEM((2, length, width), BF16),
            pltpu.VMEM((lines, 2, 8, width), F32),
            pltpu.SemaphoreType.DMA((slots,)),
            pltpu.SemaphoreType.DMA((slots,)),
            pltpu.SemaphoreType.DMA((pieces + 26,)),
        ],
        compiler_params=pltpu.CompilerParams(
            vmem_limit_bytes=60 * MIB, collective_id=0, has_side_effects=True
        ),
        name="gather_project",
    )(norm_gain, norm_shift, target_ids, memory_ids, x1, x2, mem, *shards)


def call_feed(y1, a2, g1, g2, norms, w_cross, w_in, w_out):
    length, width = g1.shape
    hidden = w_in.shape[1]
    tiles = length // FEED
    norm_spec = whole((8, width))
    step_tile = pl.BlockSpec((1, FEED, width), lambda i: (i // tiles, i % tiles, 0))
    step_wide = pl.BlockSpec((1, FEED, hidden), lambda i: (i // tiles, i % tiles, 0))
    early = pl.BlockSpec((FEED, width), lambda i: (jnp.minimum(i, tiles - 1), 0))
    late = pl.BlockSpec((FEED, width), lambda i: (jnp.maximum(i - tiles, 0), 0))
    return pl.pallas_call(
        functools.partial(feed_kernel, tiles),
        grid=(2 * tiles,),
        in_specs=[
            step_tile,
            pl.BlockSpec((1, 1, FEED, width), lambda i: (i // tiles, 1, i % tiles, 0)),
            early, late, norm_spec,
            whole(w_cross.shape), whole(w_in.shape), whole(w_out.shape),
        ],
        out_specs=[
            early, late, step_tile, step_wide, step_wide, step_tile, step_tile, step_tile,
            fixed((2, 8, width)),
        ],
        out_shape=[
            struct((length, width), BF16),
            struct((length, width), BF16),
            struct((2, length, width), BF16),
            struct((2, length, hidden), BF16),
            struct((2, length, hidden), BF16),
            struct((2, length, width), BF16),
            struct((2, length, width), F32),
            struct((2, length, width), BF16),
            struct((2, 8, width), F32),
        ],
        compiler_params=params(60),
        name="feed_forward_back",
    )(y1, a2, g1, g2, norms, w_cross, w_in, w_out)


def call_feed_grads(small, h3, a2, e2, g1, g2, du, r):
    length, width = g1.shape
    hidden = r.shape[2]
    lines = width // (2 * small)
    flat = (2 * length, width)
    chunk = pl.BlockSpec((2 * length, width), lambda c: (0, c))
    return pl.pallas_call(
        functools.partial(feed_grad_kernel, small),
        grid=(hidden // width,),
        in_specs=[whole(flat), whole((length, width)), whole((length, width)), chunk, chunk]
        + [pl.BlockSpec(memory_space=pl.ANY)] * 2,
        out_specs=[pl.BlockSpec(memory_space=pl.ANY)] * 2,
        out_shape=[struct((lines, small, 2 * hidden + width), BF16)] * 2,
        scratch_shapes=[
            pltpu.VMEM((width, 2 * length), BF16),
            pltpu.VMEM((width, 2 * length), BF16),
            pltpu.VMEM((2, length, width), BF16),
            pltpu.VMEM((2, length, width), BF16),
            pltpu.VMEM((2, lines, 2, small, width), BF16),
            pltpu.VMEM((2, width * width // hidden // (2 * small), 2, small, hidden), BF16),
            pltpu.VMEM((lines, 2, small, width), BF16),
            pltpu.SemaphoreType.DMA((6, 2)),
        ],
        compiler_params=params(60),
        name="feed_weight_grads",
    )(h3.reshape(flat), g1, g2, du.reshape(2 * length, hidden), r.reshape(2 * length, hidden), a2, e2)


def call_finish(sizes, low, h1_turned, xs, dy1, norms, w_qkv, d_self, d_query, d_kv, ready, dnorm1, dnorm2):
    members, wides = sizes
    _, length, width = xs.shape
    lines, small = wides // 2, width // wides
    total = ready[0].shape[2] * len(ready)
    vmem = pl.BlockSpec(memory_space=pltpu.VMEM)

    def split(item):
        return item.reshape(lines, 2, small, item.shape[1])

    scratch = [
        pltpu.VMEM((2, length, 3 * width), BF16),
        pltpu.VMEM((2, length, width), BF16),
        pltpu.VMEM((2, length, width), F32),
        pltpu.VMEM((width, 3 * width), BF16),
        pltpu.VMEM((width, 2 * length), BF16),
        pltpu.VMEM((3, lines, 2, small, width), BF16),
        pltpu.VMEM((2 + 4 + lines + 2 * max(1, members // 4 - 1), 8, width), F32),
        pltpu.VMEM((lines, 2, small, width), BF16),
        pltpu.VMEM((lines, 2, small, width), BF16),
        pltpu.VMEM((lines, 2, small, 2 * width), BF16),
    ]
    for cols in (2 * width, width, width, width, width, width):
        scratch += reduced_scratch(sizes, small, cols, "whole")
    scratch += reduced_scratch(sizes, small, total, "ready")
    slots = reduce_slots(sizes, 7)
    scratch += [
        pltpu.SemaphoreType.DMA((slots,)),
        pltpu.SemaphoreType.DMA((slots,)),
        pltpu.SemaphoreType.DMA((10 + 2 * length // TILE,)),
    ]
    return pl.pallas_call(
        functools.partial(finish_kernel, sizes),
        in_specs=[pl.BlockSpec(memory_space=pltpu.HBM)] * 8 + [vmem] * (3 + len(ready)),
        out_specs=[pl.BlockSpec(memory_space=pl.ANY)] * 2 + [vmem] * 6,
        out_shape=[
            struct((length, width), F32),
            struct((length, width), F32),
            struct((small, 3 * width), BF16),
            struct((small, width), BF16),
            struct((small, width), BF16),
            struct((small, 2 * width), BF16),
            struct((small, total), BF16),
            struct((8, width), F32),
        ],
        scratch_shapes=scratch,
        compiler_params=pltpu.CompilerParams(
            vmem_limit_bytes=60 * MIB, collective_id=1, has_side_effects=True
        ),
        name="finish_reduce",
    )(low, h1_turned, xs, dy1, w_qkv, split(d_self), split(d_query), split(d_kv), norms, dnorm1, dnorm2, *ready)


def call_emit(sizes, *results):
    length, width = results[0].shape
    wides = sizes[1]
    small, tiles = width // wides, length // TILE
    hidden = (results[6].shape[1] - width) // 2
    group = hidden // width
    shapes = [
        (3, small), (3, small), (small, 3 * width), (small, width), (small, width), (small, 2 * width),
        (small, hidden), (group * small, width), (small, width),
    ]
    return pl.pallas_call(
        functools.partial(emit_kernel, wides),
        grid=(tiles,),
        in_specs=[pl.BlockSpec((TILE, width), lambda i: (i, 0))] * 2 + [whole(item.shape) for item in results[2:]],
        out_specs=[pl.BlockSpec((TILE, width), lambda i: (i, 0))] * 2 + [fixed(item) for item in shapes],
        out_shape=[struct((length, width), F32)] * 2 + [struct(item, F32) for item in shapes],
        compiler_params=params(60),
        name="emit",
    )(*results)


def local_step(sizes, x1, x2, mem, g1, g2, target_ids, memory_ids, norm_gain, norm_shift, shards):
    length, width = x1.shape
    members, wides = sizes
    lines = wides // 2
    small = width // wides
    hidden = shards[5].shape[1]
    tiles = length // TILE
    results = call_gather(sizes, norm_gain, norm_shift, target_ids, memory_ids, x1, x2, mem, shards)
    xs, blocks, bounds, norms, h1_turned, mem_turned = results[:6]
    w_qkv, w_kv, w_self, w_query, w_cross, w_in, w_out = (
        item.reshape(-1, item.shape[-1]) for item in results[6:]
    )
    attended, tail, y1, q2 = call_forward(bounds, xs, blocks, norms, w_self, w_query)

    o1, o2, h3, r, du, e2, dy2, do2, dnorm2 = call_feed(y1, attended, g1, g2, norms, w_cross, w_in, w_out)
    mine, theirs = call_feed_grads(small, h3, attended, e2, g1, g2, du, r)
    swapped = lax.ppermute(theirs, "wide", [(i, i ^ 1) for i in range(wides)])
    dy1, do1, d_query, d_self, d_kv, d_mem, dnorm1 = call_cross_back(
        bounds, q2, blocks, attended, tail, do2, y1, dy2, mem_turned, norms, w_query, w_self, w_kv
    )
    swapped, do1 = lax.optimization_barrier((swapped, do1))
    group = min(4, members)
    part = lax.rem(lax.axis_index("narrow"), group)
    cols = mine.shape[2] // group

    def chip_sum(which):
        pair = [lax.dynamic_slice_in_dim(item, which * cols, cols, 2).astype(F32) for item in (mine, swapped)]
        return lower(pair[0] + pair[1])

    sums = [chip_sum(flip(part, m)) for m in range(group)]
    *sums, do1 = lax.optimization_barrier((*sums, do1))
    ready = [sums[0]]
    for m in range(1, group):
        ready.append(lax.ppermute(sums[m], "narrow", [(i, i ^ m) for i in range(members)]))
    low = call_self_back(bounds, blocks, attended, tail, do1)
    results = call_finish(
        sizes, low, h1_turned, xs, dy1, norms, w_qkv, d_self, d_query, d_kv, ready, dnorm1, dnorm2
    )
    gi1, gi2, t_gain, t_shift, *grads = call_emit(sizes, *results)
    return o1, o2, gi1, gi2, d_mem, t_gain, t_shift, grads


def body(
    sizes, inputs_one, inputs_two, memory, cotangent_one, cotangent_two, target_ids, memory_ids,
    norm_gain, norm_shift, self_qkv, self_out, cross_query, cross_kv, cross_out, ffn_in, ffn_out,
):
    shape = inputs_one.shape
    length, width = shape[1:]
    o1, o2, gi1, gi2, d_mem, t_gain, t_shift, grads = local_step(
        sizes,
        inputs_one.reshape(length, width),
        inputs_two.reshape(length, width),
        memory.reshape(length, width),
        cotangent_one.reshape(length, width),
        cotangent_two.reshape(length, width),
        target_ids,
        memory_ids,
        norm_gain,
        norm_shift,
        (self_qkv, cross_kv, self_out, cross_query, cross_out, ffn_in, ffn_out),
    )
    d_qkv, d_self, d_query, d_kv, d_in, d_out, d_cross = grads
    return (
        o1.reshape(shape), o2.reshape(shape), gi1.reshape(shape), gi2.reshape(shape), d_mem.reshape(shape),
        t_gain, t_shift, d_qkv, d_self, d_query, d_kv, d_cross, d_in, d_out,
    )


def solution(mesh):
    rows = P(("narrow", "wide"), None, None)
    ids = P(("narrow", "wide"), None)
    norm, weight = P(None, "wide"), P("wide", None)
    return jax.shard_map(
        functools.partial(body, (mesh.shape["narrow"], mesh.shape["wide"])),
        mesh=mesh,
        in_specs=(rows,) * 5 + (ids,) * 2 + (norm,) * 2 + (weight,) * 7,
        out_specs=(rows,) * 5 + (norm,) * 2 + (weight,) * 7,
        check_vma=False,
    )
```

```python
import functools

import jax
import jax.numpy as jnp
from jax import lax
from jax.experimental import pallas as pl
from jax.experimental.pallas import tpu as pltpu
from jax.sharding import PartitionSpec as P

HEAD_DIM = 64
TILE = 256
SMALL = 128
FEED = 512
SEGMENTS = 5
MASKED = -1e30
MIB = 1024 * 1024
BF16 = jnp.bfloat16
F32 = jnp.float32
MESH = pl.DeviceIdType.MESH


def lower(values):
    return values.astype(BF16)


def dot(left, right):
    return lax.dot_general(left, right, (((1,), (0,)), ((), ())), preferred_element_type=F32)


def dot_bt(left, right):
    return lax.dot_general(left, right, (((1,), (1,)), ((), ())), preferred_element_type=F32)


def dot_at(left, right):
    return lax.dot_general(left, right, (((0,), (0,)), ((), ())), preferred_element_type=F32)


def standardise(values):
    centred = values - jnp.mean(values, -1, keepdims=True)
    inverse = lax.rsqrt(jnp.mean(centred * centred, -1, keepdims=True) + 1e-05)
    return centred * inverse, inverse


def norm_back(xhat, inverse, gain, incoming):
    dz = incoming * gain
    inner = jnp.mean(dz * xhat, -1, keepdims=True)
    return (dz - jnp.mean(dz, -1, keepdims=True) - xhat * inner) * inverse


def fold_rows(values):
    rows, width = values.shape
    return jnp.sum(values.reshape(rows // 8, 8, width), axis=0)


def lane_index(rows):
    return lax.broadcasted_iota(jnp.int32, (rows, 128), 1)


def row_index(rows):
    return lax.broadcasted_iota(jnp.int32, (rows, 128), 0)


def stack_heads(pair, first):
    zero = jnp.zeros_like(pair)
    return jnp.concatenate([jnp.where(first, pair, zero), jnp.where(first, zero, pair)], axis=0)


def tiles_of(low, high, length, small, visit):
    base = (low // 16) * 16
    span = high - base
    whole_tiles = (span + TILE - 1 - small) // TILE
    rest = span - whole_tiles * TILE

    def per_tile(i, carry):
        begin = base + i * TILE
        visit(TILE, pl.multiple_of(jnp.minimum(begin, length - TILE), 16), jnp.maximum(low, begin))
        return carry

    lax.fori_loop(0, whole_tiles, per_tile, 0)

    @pl.when(rest > 0)
    def _():
        begin = base + whole_tiles * TILE
        visit(small, pl.multiple_of(jnp.minimum(begin, length - small), 16), jnp.maximum(low, begin))


def each_segment(bounds, q_row, k_row, visit):
    def per_segment(s, carry):
        visit(
            bounds[q_row, s, 0], bounds[q_row, s + 1, 0], bounds[k_row, s, 0], bounds[k_row, s + 1, 0]
        )
        return carry

    lax.fori_loop(0, SEGMENTS, per_segment, 0)


def pair_lanes(offset, p):
    if isinstance(p, int):
        return slice(offset + p * 128, offset + p * 128 + 128)
    return pl.ds(pl.multiple_of(offset + p * 128, 128), 128)


def inside_rows(size, start, low, high):
    rows = row_index(size) + start
    return (rows >= low) & (rows < high)


def attend(bounds, q_row, k_row, query, keys, values, out_ref, tail_ref):
    (q_ref, q_col), (k_ref, k_col), (v_ref, v_col) = query, keys, values
    length, width = out_ref.shape
    pairs = range(width // 128)

    def visit(size, start, low, high, k_low, k_high):
        lanes = lane_index(size)
        first = lanes < HEAD_DIM
        owner, place = lanes // 4, lanes % 4
        unit = jnp.where(lane_index(2 * size) == 0, 1.0, 0.0).astype(BF16)
        keep = inside_rows(size, start, low, high)
        span = pl.ds(start, size)
        k_base = (k_low // 16) * 16
        k_tiles = (k_high - k_base + TILE - 1) // TILE

        def piece(p, k_size, k_start, low_k):
            inside = inside_rows(k_size, k_start, low_k, k_high)
            shut = (lane_index(k_size) == 0) & jnp.logical_not(inside)
            bias = jnp.where(shut, MASKED, 0.0).astype(BF16)
            queries = stack_heads(q_ref[span, pair_lanes(q_col, p)], first)
            k_span = pl.ds(k_start, k_size)
            pair_k = k_ref[k_span, pair_lanes(k_col, p)]
            pair_v = v_ref[k_span, pair_lanes(v_col, p)]
            scores = dot_bt(
                jnp.concatenate([queries, unit], axis=1), jnp.concatenate([pair_k, bias], axis=1)
            )
            ones = jnp.ones((k_size, 128), BF16)
            return scores, jnp.concatenate([pair_v, ones], axis=1)

        def finish(p, highest, total, stats):
            cols = pair_lanes(0, p)
            top, bottom = total[:size], total[size:]
            mass = jnp.where(first, top[:, 128:], bottom[:, 128:])
            merged = lower(jnp.where(first, top[:, :128], bottom[:, :128]) / mass)
            out_ref[span, cols] = jnp.where(keep, merged, out_ref[span, cols])
            peak, sums = stats
            for h, half in ((0, slice(0, size)), (1, slice(size, 2 * size))):
                here = owner == 2 * p + h
                peak = jnp.where(here, highest[half], peak)
                sums = jnp.where(here, total[half, 128:], sums)
            return peak, sums

        empty = (jnp.zeros((size, 128), F32), jnp.ones((size, 128), F32))

        def close(stats):
            peak, sums = stats
            tail = split_lanes(peak + jnp.log(sums), place, 1.0)
            tail_ref[span, :] = jnp.where(keep, tail, tail_ref[span, :])

        def rolled(one):
            close(lax.fori_loop(0, len(pairs), lambda p, stats: finish(p, *one(p), stats), empty))

        def direct(k_size):
            k_start = pl.multiple_of(jnp.minimum(k_base, length - k_size), 16)

            items = [piece(p, k_size, k_start, k_low) for p in pairs]
            tops = [jnp.max(item[0], -1, keepdims=True) for item in items]
            probs = [lower(jnp.exp(item[0] - top)) for item, top in zip(items, tops)]
            totals = [dot(prob, item[1]) for prob, item in zip(probs, items)]
            stats = empty
            for p in pairs:
                stats = finish(p, tops[p], totals[p], stats)
            close(stats)

        if size < TILE:

            @pl.when(k_tiles <= 2)
            def _():
                direct(2 * TILE)

        else:

            @pl.when(k_tiles == 1)
            def _():
                direct(TILE)

            @pl.when(k_tiles == 2)
            def _():
                direct(2 * TILE)

        @pl.when(k_tiles > 2)
        def _():
            def one(p):
                def per_key(j, carry):
                    highest, total = carry
                    begin = k_base + j * TILE
                    k_start = pl.multiple_of(jnp.minimum(begin, length - TILE), 16)
                    scores, wide_v = piece(p, TILE, k_start, jnp.maximum(k_low, begin))
                    newest = jnp.maximum(highest, jnp.max(scores, -1, keepdims=True))
                    expon = lower(jnp.exp(scores - newest))
                    return newest, total * jnp.exp(highest - newest) + dot(expon, wide_v)

                start_at = (jnp.full((2 * size, 1), MASKED, F32), jnp.zeros((2 * size, 256), F32))
                return lax.fori_loop(0, k_tiles, per_key, start_at)

            rolled(one)

    def segment(q_low, q_high, k_low, k_high):
        tiles_of(
            q_low, q_high, length, SMALL // 2, lambda size, start, low: visit(size, start, low, q_high, k_low, k_high)
        )

    each_segment(bounds, q_row, k_row, segment)


def split_lanes(values, place, lead):
    high = lower(values).astype(F32)
    rest = values - high
    middle = lower(rest).astype(F32)
    spread = jnp.where(place == 1, high, jnp.where(place == 2, middle, rest - middle))
    return lower(jnp.where(place == 0, lead, -spread))


def attend_back(bounds, q_row, k_row, query, keys, values, do_ref, out_ref, tail_ref, dq, dk, dv):
    (q_ref, q_col), (k_ref, k_col), (v_ref, v_col) = query, keys, values
    (dq_ref, dq_col), (dk_ref, dk_col), (dv_ref, dv_col) = dq, dk, dv
    length, width = do_ref.shape
    pairs = width // 128
    zero = jnp.zeros((), BF16)
    lane = lane_index(width)
    collect = (lane % 4 > 0) & (lane // 4 == row_index(width) // HEAD_DIM)
    collect = jnp.where(collect, 1.0, 0.0).astype(BF16)

    def visit(size, start, low, high, k_low, k_high):
        lanes = lane_index(size)
        first = lanes < HEAD_DIM
        owner, place = lanes // 4, lanes % 4
        closed = lower(jnp.where(place == 0, 1.0, jnp.where(place == 1, MASKED, 0.0)))
        keep = inside_rows(size, start, low, high)
        span = pl.ds(start, size)
        tail_q = jnp.where(keep, tail_ref[span, :], closed)
        centre = jnp.zeros((size, 128), F32)
        for p in range(pairs):
            cols = slice(p * 128, (p + 1) * 128)
            grad = jnp.where(keep, do_ref[span, cols], zero)
            inner = grad.astype(F32) * out_ref[span, cols].astype(F32)
            coarse = lower(inner)
            fine = lower(inner - coarse.astype(F32))
            centre = centre + dot(
                jnp.concatenate([coarse, fine], axis=1),
                jnp.concatenate([collect[cols], collect[cols]], axis=0),
            )
        tail_g = split_lanes(centre, place, 0.0)

        def per_key(k_size, k_start, low_k):
            k_span = pl.ds(k_start, k_size)
            inside = inside_rows(k_size, k_start, low_k, k_high)
            lead = lane_index(k_size) % 4 == 0
            tail = lower(jnp.where(lead, jnp.where(inside, 0.0, MASKED), 1.0))

            def load(p):
                pair_q = q_ref[span, pair_lanes(q_col, p)]
                pair_k = k_ref[k_span, pair_lanes(k_col, p)]
                pair_v = v_ref[k_span, pair_lanes(v_col, p)]
                pair_do = jnp.where(keep, do_ref[span, pair_lanes(0, p)], zero)
                queries = stack_heads(pair_q, first)
                grads = stack_heads(pair_do, first)
                ends = [
                    jnp.concatenate(
                        [jnp.where(owner == 2 * p, item, zero), jnp.where(owner == 2 * p + 1, item, zero)],
                        axis=0,
                    )
                    for item in (tail_q, tail_g)
                ]
                scores = dot_bt(
                    jnp.concatenate([pair_k, tail], axis=1),
                    jnp.concatenate([queries, ends[0]], axis=1),
                )
                slope = dot_bt(
                    jnp.concatenate([pair_v, tail], axis=1),
                    jnp.concatenate([grads, ends[1]], axis=1),
                )
                return pair_k, queries, grads, scores, slope

            def middle(item):
                pair_k, queries, grads, scores, slope = item
                probs = jnp.exp(scores)
                return pair_k, queries, grads, lower(probs), lower(probs * slope)

            def store(p, pair_k, queries, grads, probs, ds):
                dv_ref[k_span, pair_lanes(dv_col, p)] += dot(probs, grads)
                dk_ref[k_span, pair_lanes(dk_col, p)] += dot(ds, queries)
                turned = [dot_at(ds[:, :size], pair_k), dot_at(ds[:, size:], pair_k)]
                dq_ref[span, pair_lanes(dq_col, p)] += jnp.where(first, turned[0], turned[1])

            ahead = load(0)
            for p in range(pairs):
                item = ahead
                if p + 1 < pairs:
                    ahead = load(p + 1)
                store(p, *middle(item))

        tiles_of(k_low, k_high, length, SMALL // 2, per_key)

    def segment(q_low, q_high, k_low, k_high):
        tiles_of(
            q_low, q_high, length, SMALL, lambda size, start, low: visit(size, start, low, q_high, k_low, k_high)
        )

    each_segment(bounds, q_row, k_row, segment)


def forward_kernel(bounds, xs, block, norms, w_self, w_query, attended, tail, y1, q2, queries):
    phase = pl.program_id(1)
    length, width = queries.shape

    @pl.when(phase == 0)
    def _():
        queries[...] = block[0, :, :width]

    attend(
        bounds, 0, phase, (queries, 0), (block.at[0], width), (block.at[0], 2 * width),
        attended.at[0, 0], tail.at[0, 0],
    )

    @pl.when(phase == 0)
    def _():
        for i in range(length // TILE):
            span = slice(i * TILE, (i + 1) * TILE)
            after = xs[0, span, :].astype(F32) + dot(attended[0, 0, span, :], w_self[...])
            y1[0, span, :] = after
            xhat, _ = standardise(after)
            h2 = lower(xhat * norms[1:2, :] + norms[4:5, :])
            asked = lower(dot(h2, w_query[...]) * HEAD_DIM ** (-0.5))
            queries[span, :] = asked
            q2[0, span, :] = asked


def feed_kernel(
    per_step, y1, a2, g1, g2, norms, w_cross, w_in, w_out,
    o1, o2, h3, r, du, e2, dy2, do2, dnorm,
):
    i = pl.program_id(0)
    width = w_cross.shape[0]
    is_first = i < per_step
    grad = jnp.where(is_first, g1[...], g2[...])
    after = y1[0] + dot(a2[0, 0], w_cross[...])
    xhat, inverse = standardise(after)
    normed = lower(xhat * norms[2:3, :] + norms[5:6, :])
    h3[0] = normed
    result = after
    dh3 = jnp.zeros_like(after)
    slope = (2.0 / jnp.pi) ** 0.5
    chunks = w_in.shape[1] // width

    def enter(c):
        cols = slice(c * width, (c + 1) * width)
        return dot(normed, w_in[:, cols]), dot_bt(grad, w_out[cols, :])

    ahead = enter(0)
    for c in range(chunks):
        cols = slice(c * width, (c + 1) * width)
        u, dr = ahead
        if c + 1 < chunks:
            ahead = enter(c + 1)
        square = u * u
        half = 0.5 + 0.5 * jnp.tanh(u * (slope + slope * 0.044715 * square))
        hidden = lower(u * half)
        r[0, :, cols] = hidden
        bend = u * (2 * slope + 6 * slope * 0.044715 * square)
        pre = lower(dr * (half * (1.0 + (1.0 - half) * bend)))
        du[0, :, cols] = pre
        result = result + dot(hidden, w_out[cols, :])
        dh3 = dh3 + dot_bt(pre, w_in[:, cols])

    @pl.when(is_first)
    def _():
        o1[...] = lower(result)

    @pl.when(jnp.logical_not(is_first))
    def _():
        o2[...] = lower(result)

    @pl.when(i == 0)
    def _():
        dnorm[...] = jnp.zeros_like(dnorm)

    dnorm[0] += fold_rows(dh3 * xhat)
    dnorm[1] += fold_rows(dh3)
    back = grad.astype(F32) + norm_back(xhat, inverse, norms[2:3, :], dh3)
    dy2[0] = back
    low = lower(back)
    e2[0] = low
    do2[0] = lower(dot_bt(low, w_cross[...]))


def feed_grad_kernel(
    small, h3, g1, g2, du, r, a2_hbm, e2_hbm, mine, theirs,
    turned, turned_g, a2, e2, d_in, d_out, d_cross, sem,
):
    c = pl.program_id(0)
    last = pl.num_programs(0) - 1
    half, width = g1.shape
    hidden = d_out.shape[4]
    group = hidden // width
    rows = width // group
    slot = lax.rem(c, 2)

    core = lax.rem(lax.axis_index("wide"), 2)
    lines = width // (2 * small)
    depth = rows // (2 * small)

    def copies(at, chunk):
        cols = pl.ds(pl.multiple_of(chunk * width, width), width)
        deep = pl.ds(chunk * depth, depth)
        found = []
        for k, (out, side) in enumerate(((mine, core), (theirs, 1 - core))):
            found.append(
                pltpu.make_async_copy(d_in.at[at, :, side], out.at[:, :, cols], sem.at[2 * k, at])
            )
            found.append(
                pltpu.make_async_copy(
                    d_out.at[at, :, side], out.at[deep, :, hidden + width :], sem.at[2 * k + 1, at]
                )
            )
        return found

    loads = [
        pltpu.make_async_copy(a2_hbm.at[:, 1], a2, sem.at[4, 0]),
        pltpu.make_async_copy(e2_hbm, e2, sem.at[4, 1]),
    ]
    cross = [
        pltpu.make_async_copy(
            d_cross.at[:, side], out.at[:, :, hidden : hidden + width], sem.at[5, k]
        )
        for k, (out, side) in enumerate(((mine, core), (theirs, 1 - core)))
    ]

    @pl.when(c >= 2)
    def _():
        for copy in copies(slot, c - 2):
            copy.wait()

    @pl.when(c == 0)
    def _():
        for copy in loads:
            copy.start()
        turned[...] = h3[...].T
        turned_g[:, :half] = g1[...].T
        turned_g[:, half:] = g2[...].T

    d_in[slot] = lower(dot(turned[...], du[...])).reshape(d_in.shape[1:])
    part = lower(dot(turned_g[...], r[...])).T
    for w in range(width // (group * small)):
        for j in range(group):
            at = (w * group + j) * small
            d_out[slot, w // 2, w % 2, :, j * width : (j + 1) * width] = part[at : at + small]
    for copy in copies(slot, c):
        copy.start()

    @pl.when(c == last)
    def _():
        wait_all(loads)
        d_cross[...] = lower(dot(a2[0].T, e2[0]) + dot(a2[1].T, e2[1])).reshape(d_cross.shape)
        for copy in cross:
            copy.start()
        for copy in copies(1 - slot, c - 1) + copies(slot, c):
            copy.wait()
        wait_all(cross)


def cross_back_kernel(
    bounds, q2, keys, values, a1, a2, stat2, do2, y1, dy2, mem_turned, norms, w_query, w_self, w_kv,
    dy1, do1, d_query, d_self, d_kv, d_mem, dnorm,
    dq_sum, dkv_sum, h2, low_q, low_e,
):
    step = pl.program_id(0)
    length, width = q2.shape[1:]

    @pl.when(step == 0)
    def _():
        dkv_sum[...] = jnp.zeros_like(dkv_sum)
        dnorm[...] = jnp.zeros_like(dnorm)

    dq_sum[...] = jnp.zeros_like(dq_sum)
    attend_back(
        bounds, 0, 1, (q2.at[0], 0), (keys.at[0], 0), (values.at[0], 0), do2.at[0], a2.at[0, 0], stat2.at[0, 0],
        (dq_sum, 0), (dkv_sum, 0), (dkv_sum, width),
    )

    def rows(i):
        span = slice(i * FEED, (i + 1) * FEED)
        grad_q = lower(dq_sum[span, :] * HEAD_DIM ** (-0.5))
        low_q[step, span, :] = grad_q
        xhat, inverse = standardise(y1[0, span, :])
        h2[step, span, :] = lower(xhat * norms[1:2, :] + norms[4:5, :])
        dh2 = dot_bt(grad_q, w_query[...])
        dnorm[0] += fold_rows(dh2 * xhat)
        dnorm[1] += fold_rows(dh2)
        back = dy2[0, span, :] + norm_back(xhat, inverse, norms[1:2, :], dh2)
        dy1[0, span, :] = back
        low = lower(back)
        low_e[step, span, :] = low
        do1[0, span, :] = lower(dot_bt(low, w_self[...]))

    for i in range(length // FEED):
        rows(i)

    @pl.when(step == 1)
    def _():
        d_query[...] = lower(dot_at(h2[0], low_q[0]) + dot_at(h2[1], low_q[1]))
        d_self[...] = lower(dot_at(a1[0, 0], low_e[0]) + dot_at(a1[1, 0], low_e[1]))
        pair = lower(dkv_sum[...])
        d_kv[...] = lower(dot(mem_turned[...], pair))
        d_mem[...] = dot_bt(pair, w_kv[...])


def self_back_kernel(bounds, qkv, a1, stat1, do1, low, sums):
    width = do1.shape[2]
    sums[...] = jnp.zeros_like(sums)
    attend_back(
        bounds, 0, 0, (qkv.at[0], 0), (qkv.at[0], width), (qkv.at[0], 2 * width),
        do1.at[0], a1.at[0, 0], stat1.at[0, 0], (sums, 0), (sums, width), (sums, 2 * width),
    )
    low[0, :, :width] = lower(sums[:, :width] * HEAD_DIM ** (-0.5))
    low[0, :, width:] = lower(sums[:, width:])


def flip(index, mask):
    out, bit = index, 1
    while bit <= mask:
        if mask & bit:
            out = out + bit - 2 * bit * lax.rem(lax.div(index, bit), 2)
        bit *= 2
    return out


class Links:
    def __init__(self, sizes, send, recv):
        self.members, wides = sizes
        self.lines = wides // 2
        self.group = min(4, self.members)
        self.narrow, self.wide = lax.axis_index("narrow"), lax.axis_index("wide")
        self.line, self.core = lax.div(self.wide, 2), lax.rem(self.wide, 2)
        self.part = lax.rem(self.narrow, self.group)
        self.send, self.recv, self.used = send, recv, 0

    def core_peer(self):
        return (self.narrow, flip(self.wide, 1))

    def plane_peer(self, mask):
        return (flip(self.narrow, mask), self.wide)

    def line_peer(self, mask):
        return (self.narrow, 2 * flip(self.line, mask) + self.core)

    def far_masks(self):
        masks, mask = [], self.group
        while mask < self.members:
            masks.append(mask)
            mask *= 2
        return masks

    def barrier(self, far):
        semaphore = pltpu.get_barrier_semaphore()
        peers = [self.core_peer()]
        peers += [self.plane_peer(m) for m in range(1, self.group)]
        peers += [self.line_peer(m) for m in range(1, self.lines)]
        if far:
            peers += [self.plane_peer(m) for m in self.far_masks()]
        for peer in peers:
            pl.semaphore_signal(semaphore, inc=1, device_id=peer, device_id_type=MESH)
        pl.semaphore_wait(semaphore, len(peers))

    def push(self, src, dst, peer):
        slot = self.used
        self.used += 1
        copy = pltpu.make_async_remote_copy(
            src_ref=src,
            dst_ref=dst,
            send_sem=self.send.at[slot],
            recv_sem=self.recv.at[slot],
            device_id=peer,
            device_id_type=MESH,
        )
        copy.start()
        return copy

    def quarter(self, part, cols):
        size = cols // self.group
        return pl.ds(pl.multiple_of(part * size, size), size)


def wait_all(copies):
    for copy in copies:
        copy.wait()


class Gathered:
    def __init__(self, links, shard, full, masks):
        self.links, self.shard, self.full, self.masks = links, shard, full, masks
        self.cols = shard.shape[-1]

    def start_line(self):
        links = self.links
        self.full[links.line, links.core] = self.shard[...]
        mine = links.quarter(links.part, self.cols)
        self.copies = [
            links.push(
                self.shard.at[:, mine], self.full.at[links.line, links.core, :, mine], links.line_peer(m)
            )
            for m in range(1, links.lines)
        ]

    def spread(self, parts, mask):
        links = self.links
        wait_all(self.copies)
        self.copies = []
        for k in range(1, links.lines):
            for part in parts:
                cols = links.quarter(part, self.cols)
                place = self.full.at[flip(links.line, k), links.core, :, cols]
                self.copies.append(links.push(place, place, links.plane_peer(mask)))

    def start_plane(self):
        self.spread([self.links.part], self.masks[0])

    def cross_plane(self):
        self.spread([self.links.part, flip(self.links.part, self.masks[0])], self.masks[1])

    def start_core(self):
        links = self.links
        wait_all(self.copies)
        place = self.full.at[:, links.core]
        self.copies = [links.push(place, place, links.core_peer())]

    def finish(self):
        wait_all(self.copies)


def gather_slots(sizes, pieces):
    lines, group = sizes[1] // 2, min(4, sizes[0])
    return pieces * (lines - 1 + (lines - 1) * (group - 1) + 1) + lines


def gather_kernel(
    sizes, norm_gain, norm_shift, target_ids, memory_ids, x1_hbm, x2_hbm, mem_hbm,
    g_qkv, g_kv, g_self, g_query, g_cross, g_in, g_out,
    xs, blocks, bounds, norms, h1_turned, mem_turned, f_qkv, f_kv, f_self, f_query, f_cross, f_in, f_out,
    rows_in, placed, s_qkv, s_kv, s_self, s_query, s_cross, s_in, s_out,
    h1, turned, turned_mem, v_qkv, v_kv, v_self, v_query, v_cross, v_in, v_out, o_qkv, o_kv, norm_all, send, recv, local,
):
    links = Links(sizes, send, recv)
    _, length, width = rows_in.shape
    x1, x2, mem = rows_in.at[0], rows_in.at[1], rows_in.at[2]
    small = width // sizes[1]
    used = [0]

    def local_copy(src, dst):
        copy = pltpu.make_async_copy(src, dst, local.at[used[0]])
        used[0] += 1
        copy.start()
        return copy

    landing = []

    def piece(shard, full, out):
        landing.append((full, out))
        return Gathered(links, shard, full, (len(landing) % 2 + 1, 2 - len(landing) % 2))

    shards = [
        local_copy(src, dst)
        for src, dst in (
            (g_qkv, s_qkv), (g_kv, s_kv), (g_self, s_self), (g_query, s_query), (g_cross, s_cross),
            (g_in, s_in), (g_out, s_out),
        )
    ]
    loads = [local_copy(src, dst) for src, dst in ((x1_hbm, x1), (x2_hbm, x2), (mem_hbm, mem))]
    links.barrier(False)
    placed[...] = jnp.zeros_like(placed)
    placed[0:3, :] = norm_gain[...].astype(F32)
    placed[3:6, :] = norm_shift[...].astype(F32)
    column = lax.broadcasted_iota(jnp.int32, (small, width), 1)
    row = lax.broadcasted_iota(jnp.int32, (small, width), 0)
    spot = jnp.where(column == row + links.wide * small, 1.0, 0.0).astype(BF16)
    norm_all[links.line, links.core] = dot(lower(placed[...]), spot)
    level = lax.broadcasted_iota(jnp.int32, (8, length), 0)
    for k, ids in enumerate((target_ids, memory_ids)):
        order = jnp.where(ids[...] < 0, SEGMENTS - 1, ids[...])
        below = jnp.where(order < level, 1.0, 0.0)
        starts = jnp.sum(below, axis=1, keepdims=True).astype(jnp.int32)
        bounds[k] = jnp.broadcast_to(starts, (8, 128))
    wait_all(shards)
    pieces = []
    for c in range(3):
        cols = slice(c * width, (c + 1) * width)
        pieces.append(piece(s_qkv.at[:, cols], v_qkv.at[c], f_qkv.at[:, :, :, cols]))
    for c in range(2):
        cols = slice(c * width, (c + 1) * width)
        pieces.append(piece(s_kv.at[:, cols], v_kv.at[c], f_kv.at[:, :, :, cols]))
    pieces.append(piece(s_self, v_self, f_self))
    pieces.append(piece(s_query, v_query, f_query))
    pieces.append(piece(s_cross, v_cross, f_cross))
    half = s_in.shape[1] // 2
    for c in range(2):
        cols = slice(c * half, (c + 1) * half)
        pieces.append(piece(s_in.at[:, cols], v_in.at[c], f_in.at[:, :, :, cols]))
    half = s_out.shape[0] // 2
    for c in range(2):
        rows = slice(c * half, (c + 1) * half)
        pieces.append(piece(s_out.at[rows], v_out.at[c], f_out.at[:, :, rows]))

    own = norm_all.at[links.line, links.core]
    norm_copies = [links.push(own, own, links.line_peer(m)) for m in range(1, links.lines)]
    for p in range(4):
        pieces[p].start_line()
    wait_all(loads)
    outgoing = [local_copy(x1, xs.at[0]), local_copy(x2, xs.at[1])]
    wait_all(norm_copies)
    place = norm_all.at[:, links.core]
    norm_copy = links.push(place, place, links.core_peer())
    pieces[0].start_plane()
    norm_copy.wait()
    every = norm_all[...]
    total = every[0, 0]
    for k in range(1, 2 * links.lines):
        total = total + every[k // 2, k % 2]
    norms[...] = total
    gain, shift = total[0:1, :], total[3:4, :]

    def normalise(t, x):
        for i in range(length // TILE):
            span = slice(i * TILE, (i + 1) * TILE)
            xhat, _ = standardise(x[span, :].astype(F32))
            h1[t, span, :] = lower(xhat * gain + shift)

    def turn():
        turned[:, :length] = h1[0].T
        turned[:, length:] = h1[1].T
        turned_mem[...] = mem[...].T
        outgoing.append(local_copy(turned, h1_turned))
        outgoing.append(local_copy(turned_mem, mem_turned))

    def project(c):
        def run():
            weight = v_qkv[c].reshape(width, width)
            scale = HEAD_DIM ** (-0.5) if c == 0 else 1.0
            for t in range(2):

                def rows(i, carry, t=t):
                    span = pl.ds(pl.multiple_of(i * 2 * TILE, 2 * TILE), 2 * TILE)
                    o_qkv[c, t, span, :] = lower(dot(h1[t, span, :], weight) * scale)
                    return carry

                lax.fori_loop(0, length // (2 * TILE), rows, 0)
            cols = slice(c * width, (c + 1) * width)
            outgoing.append(local_copy(o_qkv.at[c], blocks.at[0:2, :, cols]))

        return run

    def project_memory(c):
        def run():
            weight = v_kv[c].reshape(width, width)

            def rows(i, carry):
                span = pl.ds(pl.multiple_of(i * 2 * TILE, 2 * TILE), 2 * TILE)
                o_kv[c, span, :] = lower(dot(mem[span, :], weight))
                return carry

            lax.fori_loop(0, length // (2 * TILE), rows, 0)
            cols = slice((c + 1) * width, (c + 2) * width)
            outgoing.append(local_copy(o_kv.at[c], blocks.at[2, :, cols]))

        return run

    work = {c: project(c) for c in range(3)} | {3 + c: project_memory(c) for c in range(2)}
    count = len(pieces)
    for t in range(1, count + 6):
        if 3 + t < count:
            pieces[3 + t].start_line()
        if t < count:
            pieces[t].start_plane()
        if t == 1:
            normalise(0, x1)
        if t == 2:
            normalise(1, x2)
        if 0 <= t - 2 < count:
            pieces[t - 2].cross_plane()
        if 0 <= t - 4 < count:
            pieces[t - 4].start_core()
        if 0 <= t - 5 < count:
            one = t - 5
            pieces[one].finish()
            outgoing.append(local_copy(*landing[one]))
            if one in work:
                work[one]()
            if one == 5:
                turn()
    wait_all(outgoing)


class Reduced:
    def __init__(self, links, bufs, out, masks, source=None, ready=None):
        self.links, self.out, self.masks, self.source, self.ready = links, out, masks, source, ready
        self.lined = source is not None or ready is not None
        self.crecv, self.chip, self.precv, self.plane, self.lrecv, self.mine, self.xrecv, self.full, self.half = bufs
        self.cols = self.full.shape[-1]

    def start_core(self):
        links = self.links
        self.copies = [links.push(self.source.at[:, 1 - links.core], self.crecv, links.core_peer())]

    def start_plane(self):
        links = self.links
        if self.source is not None:
            wait_all(self.copies)
            for k in range(links.lines):
                self.chip[k] = lower(
                    self.source[k, links.core].astype(F32) + self.crecv[k].astype(F32)
                )
        first, second = self.masks
        near = flip(links.part, first)
        self.copies = [
            links.push(
                self.chip.at[:, :, links.quarter(part, self.cols)], self.precv.at[k], links.plane_peer(first)
            )
            for k, part in enumerate((near, flip(near, second)))
        ]

    def cross_plane(self):
        links = self.links
        wait_all(self.copies)
        second = self.masks[1]
        far = self.chip[:, :, links.quarter(flip(links.part, second), self.cols)].astype(F32)
        self.half[...] = lower(far + self.precv[1].astype(F32))
        self.copies = [links.push(self.half, self.precv.at[2], links.plane_peer(second))]

    def start_line(self):
        links = self.links
        if self.ready is not None:
            total = self.ready[0][...].astype(F32)
            for item in self.ready[1:]:
                total = total + item[...].astype(F32)
        else:
            wait_all(self.copies)
            total = self.chip[:, :, links.quarter(links.part, self.cols)].astype(F32)
            total = total + self.precv[0].astype(F32) + self.precv[2].astype(F32)
        self.plane[...] = lower(total)
        if not self.lined:
            self.copies = []
            return
        self.copies = [
            links.push(self.plane.at[flip(links.line, m)], self.lrecv.at[m - 1], links.line_peer(m))
            for m in range(1, links.lines)
        ]

    def start_gather(self):
        links = self.links
        wait_all(self.copies)
        if not self.lined:
            total = self.plane[0].astype(F32)
        else:
            total = self.plane[links.line].astype(F32)
            for m in range(1, links.lines):
                total = total + self.lrecv[m - 1].astype(F32)
        for i, mask in enumerate(links.far_masks()):
            self.xrecv[2 * i] = lower(total)
            links.push(self.xrecv.at[2 * i], self.xrecv.at[2 * i + 1], links.plane_peer(mask)).wait()
            total = self.xrecv[2 * i].astype(F32) + self.xrecv[2 * i + 1].astype(F32)
        self.mine[...] = lower(total)
        place = self.full.at[:, links.quarter(links.part, self.cols)]
        place[...] = self.mine[...]
        self.copies = [links.push(self.mine, place, links.plane_peer(self.masks[0]))]

    def cross_gather(self):
        links = self.links
        wait_all(self.copies)
        self.copies = []
        for part in (links.part, flip(links.part, self.masks[0])):
            place = self.full.at[:, links.quarter(part, self.cols)]
            self.copies.append(links.push(place, place, links.plane_peer(self.masks[1])))

    def finish(self):
        wait_all(self.copies)
        self.out[...] = self.full[...]


def reduced_scratch(sizes, rows, cols, kind):
    members, wides = sizes
    lines, group = wides // 2, min(4, members)
    part = cols // group
    depth = 1 if kind == "shard" else lines
    far = max(2, 2 * (members // group - 1))
    small = (1, 16, 128)
    return [
        pltpu.VMEM((lines, rows, cols) if kind == "whole" else small, BF16),
        pltpu.VMEM(small if kind == "ready" else (depth, rows, cols), BF16),
        pltpu.VMEM(small if kind == "ready" else (group - 1, depth, rows, part), BF16),
        pltpu.VMEM((depth, rows, part), BF16),
        pltpu.VMEM(small if kind == "shard" else (lines - 1, rows, part), BF16),
        pltpu.VMEM((rows, part), BF16),
        pltpu.VMEM((far, rows, part), BF16),
        pltpu.VMEM((rows, cols), BF16),
        pltpu.VMEM(small if kind == "ready" else (depth, rows, part), BF16),
    ]


def reduce_slots(sizes, jobs):
    members, wides = sizes
    lines, group = wides // 2, min(4, members)
    return (jobs + 1) * (1 + 2 * (group - 1) + lines - 1 + members // group)


BUFS = 9


def finish_kernel(
    sizes, low_hbm, h1_hbm, xs_hbm, dy1_hbm, w_hbm, self_hbm, query_hbm, kv_hbm, norms, dnorm1, dnorm2, *rest,
):
    group = min(4, sizes[0])
    ready, rest = rest[:group], rest[group:]
    gi1, gi2, t_qkv, t_self, t_query, t_kv, t_joint, t_norm = rest[:8]
    low, xs, dy1, w_qkv, h1, grads, norm_slots, d_self, d_query, d_kv = rest[8:18]
    bufs = rest[18:-3]
    send, recv, local = rest[-3:]
    links = Links(sizes, send, recv)
    _, length, width = xs.shape
    early = [
        pltpu.make_async_copy(kv_hbm, d_kv, local.at[5]),
        pltpu.make_async_copy(query_hbm, d_query, local.at[6]),
        pltpu.make_async_copy(self_hbm, d_self, local.at[7]),
    ]
    loads = [
        pltpu.make_async_copy(xs_hbm, xs, local.at[2]),
        pltpu.make_async_copy(dy1_hbm, dy1, local.at[3]),
        pltpu.make_async_copy(w_hbm, w_qkv, local.at[4]),
    ]
    turned = pltpu.make_async_copy(h1_hbm, h1, local.at[0])
    bands = []
    for c in range(3):
        cols = slice(c * width, (c + 1) * width)
        at = 1 if c == 0 else 7 + c
        bands.append(pltpu.make_async_copy(low_hbm.at[:, :, cols], low.at[:, :, cols], local.at[at]))
    for copy in [turned] + bands[:1] + early + bands[1:]:
        copy.start()
    links.barrier(True)
    wait_all(early)

    taken = [0]

    def job(out, **kind):
        at = taken[0] * BUFS
        taken[0] += 1
        masks = (2 - taken[0] % 2, 1 + taken[0] % 2)
        return Reduced(links, bufs[at : at + BUFS], out, masks, **kind)

    others = [job(t_kv, source=d_kv), job(t_query, source=d_query), job(t_self, source=d_self)]
    heads = [job(t_qkv.at[:, c * width : (c + 1) * width], source=grads.at[c]) for c in range(3)]
    joint = job(t_joint, ready=ready)
    for one in others:
        one.start_core()
    joint.start_line()
    gain = norms[0:1, :]
    turned.wait()
    for c in range(3):
        cols = slice(c * width, (c + 1) * width)
        bands[c].wait()
        if c == 2:
            for copy in loads:
                copy.start()
        value = dot(h1[:, :length], low[0, :, cols]) + dot(h1[:, length:], low[1, :, cols])
        grads[c] = lower(value).reshape(grads.shape[1:])
        heads[c].start_core()
        if c > 0:
            heads[c - 1].start_plane()
        if c == 0:
            for one in others:
                one.start_plane()
    heads[2].start_plane()
    wait_all(loads)
    stores = []
    dgain = jnp.zeros((8, width), F32)
    dshift = jnp.zeros((8, width), F32)
    steps = [
        lambda: [one.cross_plane() for one in others],
        lambda: heads[0].cross_plane(),
        lambda: (heads[1].cross_plane(), joint.start_gather()),
        lambda: (heads[2].cross_plane(), heads[0].start_line()),
        lambda: (heads[1].start_line(), joint.cross_gather()),
        lambda: heads[2].start_line(),
        lambda: [one.start_line() for one in others],
    ]
    weight = w_qkv[...]
    for t in range(2):
        for i in range(length // TILE):
            span = slice(i * TILE, (i + 1) * TILE)
            xhat, inverse = standardise(xs[t, span, :].astype(F32))
            dh1 = dot_bt(low[t, span, :], weight)
            dgain = dgain + fold_rows(dh1 * xhat)
            dshift = dshift + fold_rows(dh1)
            dy1[t, span, :] = dy1[t, span, :] + norm_back(xhat, inverse, gain, dh1)
            number = t * (length // TILE) + i
            copy = pltpu.make_async_copy(
                dy1.at[t, span, :], (gi1, gi2)[t].at[span, :], local.at[10 + number]
            )
            copy.start()
            stores.append(copy)
            if number < len(steps):
                steps[number]()
    rows = [jnp.sum(item, axis=0, keepdims=True) for item in (dgain, dnorm1[0], dnorm2[0], dshift, dnorm1[1], dnorm2[1])]
    total = jnp.concatenate(rows + [jnp.zeros((2, width), F32)], axis=0)

    def send(first, own, peers, total):
        norm_slots[first + own] = total
        place = norm_slots.at[first + own]
        return [links.push(place, place, peer) for peer in peers]

    def receive(first, count, copies):
        wait_all(copies)
        out = norm_slots[first]
        for k in range(1, count):
            out = out + norm_slots[first + k]
        return out

    copies = send(0, links.core, [links.core_peer()], total)
    total = receive(0, 2, copies)
    copies = send(2, links.part, [links.plane_peer(m) for m in range(1, links.group)], total)
    heads[0].start_gather()
    heads[1].start_gather()
    total = receive(2, links.group, copies)
    first = 2 + links.group
    copies = send(first, links.line, [links.line_peer(m) for m in range(1, links.lines)], total)
    heads[2].start_gather()
    for one in others:
        one.start_gather()
    for one in heads:
        one.cross_gather()
    total = receive(first, links.lines, copies)
    first += links.lines
    for mask in links.far_masks():
        side = lax.rem(lax.div(links.narrow, mask), 2)
        total = receive(first, 2, send(first, side, [links.plane_peer(mask)], total))
        first += 2
    t_norm[...] = total
    for one in others:
        one.cross_gather()
    joint.finish()
    for one in heads + others:
        one.finish()
    wait_all(stores)


def emit_kernel(
    wides, f1, f2, b_qkv, b_self, b_query, b_kv, b_joint, t_norm,
    gi1, gi2, gain, shift, o_qkv, o_self, o_query, o_kv, o_in, o_out, o_cross,
    t_qkv, t_self, t_query, t_kv, t_in, t_out, t_cross, sem,
):
    pairs = (
        (t_qkv, o_qkv), (t_self, o_self), (t_query, o_query), (t_kv, o_kv), (t_in, o_in), (t_out, o_out), (t_cross, o_cross),
    )
    stores = [pltpu.make_async_copy(src, dst, sem.at[k]) for k, (src, dst) in enumerate(pairs)]
    gi1[...] = f1[...]
    gi2[...] = f2[...]
    width = gi1.shape[1]
    small, hidden = t_in.shape

    @pl.when(pl.program_id(0) == 0)
    def _():
        for src, dst in (
            (b_qkv, t_qkv), (b_self, t_self), (b_query, t_query), (b_kv, t_kv),
            (b_joint.at[:, :hidden], t_in), (b_joint.at[:, hidden : hidden + width], t_cross),
        ):
            dst[...] = src[...].astype(F32)
        for j in range(hidden // width):
            begin = hidden + width + j * width
            t_out[j * small : (j + 1) * small, :] = b_joint[:, begin : begin + width].astype(F32)
        at = lax.axis_index("wide") * small
        mine = pltpu.roll(t_norm[...], lax.rem(width - at, width), 1)
        gain[...] = mine[:3, :small]
        shift[...] = mine[3:6, :small]
        for copy in stores:
            copy.start()

    @pl.when(pl.program_id(0) == pl.num_programs(0) - 1)
    def _():
        wait_all(stores)


def whole(shape):
    zeros = (0,) * len(shape)
    return pl.BlockSpec(shape, lambda *_: zeros, pipeline_mode=pl.Buffered(1))


def fixed(shape):
    zeros = (0,) * len(shape)
    return pl.BlockSpec(shape, lambda *_: zeros)


def by_step(shape):
    return pl.BlockSpec((1,) + shape, lambda t, *_: (t, 0, 0))


def params(limit):
    return pltpu.CompilerParams(
        vmem_limit_bytes=limit * MIB, dimension_semantics=("arbitrary",)
    )


def struct(shape, dtype):
    return jax.ShapeDtypeStruct(shape, dtype)


def call_forward(bounds, xs, blocks, norms, w_self, w_query):
    length, width = xs.shape[1:]
    each = pl.BlockSpec((1, length, width), lambda t, p, *_: (t, 0, 0))
    return pl.pallas_call(
        forward_kernel,
        grid_spec=pltpu.PrefetchScalarGridSpec(
            num_scalar_prefetch=1,
            grid=(2, 2),
            in_specs=[
                each,
                pl.BlockSpec((1, length, 3 * width), lambda t, p, *_: (t + p * (2 - t), 0, 0)),
                whole((8, width)), whole(w_self.shape), whole(w_query.shape),
            ],
            out_specs=[
                pl.BlockSpec((1, 1, length, width), lambda t, p, *_: (t, p, 0, 0)),
                pl.BlockSpec((1, 1, length, 128), lambda t, p, *_: (t, p, 0, 0)),
                each, each,
            ],
            scratch_shapes=[pltpu.VMEM((length, width), BF16)],
        ),
        out_shape=[
            struct((2, 2, length, width), BF16),
            struct((2, 2, length, 128), BF16),
            struct((2, length, width), F32),
            struct((2, length, width), BF16),
        ],
        compiler_params=pltpu.CompilerParams(
            vmem_limit_bytes=60 * MIB, dimension_semantics=("arbitrary", "arbitrary")
        ),
        name="attend_forward",
    )(bounds, xs, blocks, norms, w_self, w_query)


def call_cross_back(bounds, q2, blocks, attended, tail, do2, y1, dy2, mem_turned, norms, w_query, w_self, w_kv):
    length, width = q2.shape[1:]
    norm_spec = whole((8, width))
    step_low = by_step((length, width))
    return pl.pallas_call(
        cross_back_kernel,
        grid_spec=pltpu.PrefetchScalarGridSpec(
            num_scalar_prefetch=1,
            grid=(2,),
            in_specs=[
                step_low,
                pl.BlockSpec((1, length, width), lambda *_: (2, 0, 1), pipeline_mode=pl.Buffered(1)),
                pl.BlockSpec((1, length, width), lambda *_: (2, 0, 2), pipeline_mode=pl.Buffered(1)),
                pl.BlockSpec((2, 1, length, width), lambda *_: (0, 0, 0, 0), pipeline_mode=pl.Buffered(1)),
                pl.BlockSpec((1, 1, length, width), lambda t, *_: (t, 1, 0, 0)),
                pl.BlockSpec((1, 1, length, 128), lambda t, *_: (t, 1, 0, 0)),
                step_low,
                step_low, step_low, whole(mem_turned.shape), norm_spec,
                whole(w_query.shape), whole(w_self.shape), whole(w_kv.shape),
            ],
            out_specs=[
                step_low, step_low, fixed((width, width)), fixed((width, width)), fixed((width, 2 * width)),
                fixed((length, width)), fixed((2, 8, width)),
            ],
            scratch_shapes=[
                pltpu.VMEM((length, width), F32),
                pltpu.VMEM((length, 2 * width), F32),
                pltpu.VMEM((2, length, width), BF16),
                pltpu.VMEM((2, length, width), BF16),
                pltpu.VMEM((2, length, width), BF16),
            ],
        ),
        out_shape=[
            struct((2, length, width), F32),
            struct((2, length, width), BF16),
            struct((width, width), BF16),
            struct((width, width), BF16),
            struct((width, 2 * width), BF16),
            struct((length, width), F32),
            struct((2, 8, width), F32),
        ],
        compiler_params=params(60),
        cost_estimate=pl.CostEstimate(flops=45000000000, bytes_accessed=20000000, transcendentals=0),
        name="cross_back",
    )(bounds, q2, blocks, blocks, attended, attended, tail, do2, y1, dy2, mem_turned, norms, w_query, w_self, w_kv)


def call_self_back(bounds, blocks, attended, tail, do1):
    length, width = do1.shape[1:]
    norm_spec = whole((8, width))
    step_low = by_step((length, width))
    return pl.pallas_call(
        self_back_kernel,
        grid_spec=pltpu.PrefetchScalarGridSpec(
            num_scalar_prefetch=1,
            grid=(2,),
            in_specs=[
                by_step((length, 3 * width)),
                pl.BlockSpec((1, 1, length, width), lambda t, *_: (t, 0, 0, 0)),
                pl.BlockSpec((1, 1, length, 128), lambda t, *_: (t, 0, 0, 0)),
                step_low,
            ],
            out_specs=by_step((length, 3 * width)),
            scratch_shapes=[pltpu.VMEM((length, 3 * width), F32)],
        ),
        out_shape=struct((2, length, 3 * width), BF16),
        compiler_params=params(60),
        cost_estimate=pl.CostEstimate(flops=30000000000, bytes_accessed=20000000, transcendentals=0),
        name="self_back",
    )(bounds, blocks, attended, tail, do1)


def call_gather(sizes, norm_gain, norm_shift, target_ids, memory_ids, x1, x2, mem, shards):
    length, width = x1.shape
    lines = sizes[1] // 2
    small = width // sizes[1]
    vmem = pl.BlockSpec(memory_space=pltpu.VMEM)
    anywhere = pl.BlockSpec(memory_space=pl.ANY)

    def full(shape):
        return struct((lines, 2, shape[0], shape[1]), BF16)

    pieces = 12
    slots = gather_slots(sizes, pieces)
    return pl.pallas_call(
        functools.partial(gather_kernel, sizes),
        in_specs=[vmem] * 4 + [pl.BlockSpec(memory_space=pltpu.HBM)] * 10,
        out_specs=[anywhere] * 2 + [vmem] * 2 + [anywhere] * 9,
        out_shape=[
            struct((2, length, width), BF16),
            struct((3, length, 3 * width), BF16),
            struct((2, 8, 128), jnp.int32),
            struct((8, width), F32),
            struct((width, 2 * length), BF16),
            struct((width, length), BF16),
        ]
        + [full(item.shape) for item in shards],
        scratch_shapes=[pltpu.VMEM((3, length, width), BF16), pltpu.VMEM((8, small), F32)]
        + [pltpu.VMEM(item.shape, BF16) for item in shards]
        + [
            pltpu.VMEM((2, length, width), BF16),
            pltpu.VMEM((width, 2 * length), BF16),
            pltpu.VMEM((width, length), BF16),
            pltpu.VMEM((3, lines, 2, small, width), BF16),
            pltpu.VMEM((2, lines, 2, small, width), BF16),
            pltpu.VMEM((lines, 2, small, width), BF16),
            pltpu.VMEM((lines, 2, small, width), BF16),
            pltpu.VMEM((lines, 2, small, width), BF16),
            pltpu.VMEM((2, lines, 2, small, shards[5].shape[1] // 2), BF16),
            pltpu.VMEM((2, lines, 2, shards[6].shape[0] // 2, width), BF16),
            pltpu.VMEM((3, 2, length, width), BF16),
            pltpu.VMEM((2, length, width), BF16),
            pltpu.VMEM((lines, 2, 8, width), F32),
            pltpu.SemaphoreType.DMA((slots,)),
            pltpu.SemaphoreType.DMA((slots,)),
            pltpu.SemaphoreType.DMA((pieces + 26,)),
        ],
        compiler_params=pltpu.CompilerParams(
            vmem_limit_bytes=60 * MIB, collective_id=0, has_side_effects=True
        ),
        name="gather_project",
    )(norm_gain, norm_shift, target_ids, memory_ids, x1, x2, mem, *shards)


def call_feed(y1, a2, g1, g2, norms, w_cross, w_in, w_out):
    length, width = g1.shape
    hidden = w_in.shape[1]
    tiles = length // FEED
    norm_spec = whole((8, width))
    step_tile = pl.BlockSpec((1, FEED, width), lambda i: (i // tiles, i % tiles, 0))
    step_wide = pl.BlockSpec((1, FEED, hidden), lambda i: (i // tiles, i % tiles, 0))
    early = pl.BlockSpec((FEED, width), lambda i: (jnp.minimum(i, tiles - 1), 0))
    late = pl.BlockSpec((FEED, width), lambda i: (jnp.maximum(i - tiles, 0), 0))
    return pl.pallas_call(
        functools.partial(feed_kernel, tiles),
        grid=(2 * tiles,),
        in_specs=[
            step_tile,
            pl.BlockSpec((1, 1, FEED, width), lambda i: (i // tiles, 1, i % tiles, 0)),
            early, late, norm_spec,
            whole(w_cross.shape), whole(w_in.shape), whole(w_out.shape),
        ],
        out_specs=[
            early, late, step_tile, step_wide, step_wide, step_tile, step_tile, step_tile,
            fixed((2, 8, width)),
        ],
        out_shape=[
            struct((length, width), BF16),
            struct((length, width), BF16),
            struct((2, length, width), BF16),
            struct((2, length, hidden), BF16),
            struct((2, length, hidden), BF16),
            struct((2, length, width), BF16),
            struct((2, length, width), F32),
            struct((2, length, width), BF16),
            struct((2, 8, width), F32),
        ],
        compiler_params=params(60),
        name="feed_forward_back",
    )(y1, a2, g1, g2, norms, w_cross, w_in, w_out)


def call_feed_grads(small, h3, a2, e2, g1, g2, du, r):
    length, width = g1.shape
    hidden = r.shape[2]
    lines = width // (2 * small)
    flat = (2 * length, width)
    chunk = pl.BlockSpec((2 * length, width), lambda c: (0, c))
    return pl.pallas_call(
        functools.partial(feed_grad_kernel, small),
        grid=(hidden // width,),
        in_specs=[whole(flat), whole((length, width)), whole((length, width)), chunk, chunk]
        + [pl.BlockSpec(memory_space=pl.ANY)] * 2,
        out_specs=[pl.BlockSpec(memory_space=pl.ANY)] * 2,
        out_shape=[struct((lines, small, 2 * hidden + width), BF16)] * 2,
        scratch_shapes=[
            pltpu.VMEM((width, 2 * length), BF16),
            pltpu.VMEM((width, 2 * length), BF16),
            pltpu.VMEM((2, length, width), BF16),
            pltpu.VMEM((2, length, width), BF16),
            pltpu.VMEM((2, lines, 2, small, width), BF16),
            pltpu.VMEM((2, width * width // hidden // (2 * small), 2, small, hidden), BF16),
            pltpu.VMEM((lines, 2, small, width), BF16),
            pltpu.SemaphoreType.DMA((6, 2)),
        ],
        compiler_params=params(60),
        name="feed_weight_grads",
    )(h3.reshape(flat), g1, g2, du.reshape(2 * length, hidden), r.reshape(2 * length, hidden), a2, e2)


def call_finish(sizes, low, h1_turned, xs, dy1, norms, w_qkv, d_self, d_query, d_kv, ready, dnorm1, dnorm2):
    members, wides = sizes
    _, length, width = xs.shape
    lines, small = wides // 2, width // wides
    total = ready[0].shape[2] * len(ready)
    vmem = pl.BlockSpec(memory_space=pltpu.VMEM)

    def split(item):
        return item.reshape(lines, 2, small, item.shape[1])

    scratch = [
        pltpu.VMEM((2, length, 3 * width), BF16),
        pltpu.VMEM((2, length, width), BF16),
        pltpu.VMEM((2, length, width), F32),
        pltpu.VMEM((width, 3 * width), BF16),
        pltpu.VMEM((width, 2 * length), BF16),
        pltpu.VMEM((3, lines, 2, small, width), BF16),
        pltpu.VMEM((2 + 4 + lines + 2 * max(1, members // 4 - 1), 8, width), F32),
        pltpu.VMEM((lines, 2, small, width), BF16),
        pltpu.VMEM((lines, 2, small, width), BF16),
        pltpu.VMEM((lines, 2, small, 2 * width), BF16),
    ]
    for cols in (2 * width, width, width, width, width, width):
        scratch += reduced_scratch(sizes, small, cols, "whole")
    scratch += reduced_scratch(sizes, small, total, "ready")
    slots = reduce_slots(sizes, 7)
    scratch += [
        pltpu.SemaphoreType.DMA((slots,)),
        pltpu.SemaphoreType.DMA((slots,)),
        pltpu.SemaphoreType.DMA((10 + 2 * length // TILE,)),
    ]
    return pl.pallas_call(
        functools.partial(finish_kernel, sizes),
        in_specs=[pl.BlockSpec(memory_space=pltpu.HBM)] * 8 + [vmem] * (3 + len(ready)),
        out_specs=[pl.BlockSpec(memory_space=pl.ANY)] * 2 + [vmem] * 6,
        out_shape=[
            struct((length, width), F32),
            struct((length, width), F32),
            struct((small, 3 * width), BF16),
            struct((small, width), BF16),
            struct((small, width), BF16),
            struct((small, 2 * width), BF16),
            struct((small, total), BF16),
            struct((8, width), F32),
        ],
        scratch_shapes=scratch,
        compiler_params=pltpu.CompilerParams(
            vmem_limit_bytes=60 * MIB, collective_id=1, has_side_effects=True
        ),
        name="finish_reduce",
    )(low, h1_turned, xs, dy1, w_qkv, split(d_self), split(d_query), split(d_kv), norms, dnorm1, dnorm2, *ready)


def call_emit(sizes, *results):
    length, width = results[0].shape
    wides = sizes[1]
    small, tiles = width // wides, length // TILE
    hidden = (results[6].shape[1] - width) // 2
    group = hidden // width
    shapes = [
        (3, small), (3, small), (small, 3 * width), (small, width), (small, width), (small, 2 * width),
        (small, hidden), (group * small, width), (small, width),
    ]
    return pl.pallas_call(
        functools.partial(emit_kernel, wides),
        grid=(tiles,),
        in_specs=[pl.BlockSpec((TILE, width), lambda i: (i, 0))] * 2 + [whole(item.shape) for item in results[2:]],
        out_specs=[pl.BlockSpec((TILE, width), lambda i: (i, 0))] * 2 + [fixed(item) for item in shapes[:2]]
        + [pl.BlockSpec(memory_space=pl.ANY)] * 7,
        out_shape=[struct((length, width), F32)] * 2 + [struct(item, F32) for item in shapes],
        scratch_shapes=[pltpu.VMEM(item, F32) for item in shapes[2:]] + [pltpu.SemaphoreType.DMA((7,))],
        compiler_params=params(60),
        name="emit",
    )(*results)


def local_step(sizes, x1, x2, mem, g1, g2, target_ids, memory_ids, norm_gain, norm_shift, shards):
    length, width = x1.shape
    members, wides = sizes
    lines = wides // 2
    small = width // wides
    hidden = shards[5].shape[1]
    tiles = length // TILE
    results = call_gather(sizes, norm_gain, norm_shift, target_ids, memory_ids, x1, x2, mem, shards)
    xs, blocks, bounds, norms, h1_turned, mem_turned = results[:6]
    w_qkv, w_kv, w_self, w_query, w_cross, w_in, w_out = (
        item.reshape(-1, item.shape[-1]) for item in results[6:]
    )
    attended, tail, y1, q2 = call_forward(bounds, xs, blocks, norms, w_self, w_query)

    o1, o2, h3, r, du, e2, dy2, do2, dnorm2 = call_feed(y1, attended, g1, g2, norms, w_cross, w_in, w_out)
    mine, theirs = call_feed_grads(small, h3, attended, e2, g1, g2, du, r)
    swapped = lax.ppermute(theirs, "wide", [(i, i ^ 1) for i in range(wides)])
    dy1, do1, d_query, d_self, d_kv, d_mem, dnorm1 = call_cross_back(
        bounds, q2, blocks, attended, tail, do2, y1, dy2, mem_turned, norms, w_query, w_self, w_kv
    )
    swapped, do1 = lax.optimization_barrier((swapped, do1))
    group = min(4, members)
    part = lax.rem(lax.axis_index("narrow"), group)
    cols = mine.shape[2] // group

    def chip_sum(which):
        pair = [lax.dynamic_slice_in_dim(item, which * cols, cols, 2).astype(F32) for item in (mine, swapped)]
        return lower(pair[0] + pair[1])

    sums = [chip_sum(flip(part, m)) for m in range(group)]
    *sums, do1 = lax.optimization_barrier((*sums, do1))
    ready = [sums[0]]
    for m in range(1, group):
        ready.append(lax.ppermute(sums[m], "narrow", [(i, i ^ m) for i in range(members)]))
    low = call_self_back(bounds, blocks, attended, tail, do1)
    results = call_finish(
        sizes, low, h1_turned, xs, dy1, norms, w_qkv, d_self, d_query, d_kv, ready, dnorm1, dnorm2
    )
    gi1, gi2, t_gain, t_shift, *grads = call_emit(sizes, *results)
    return o1, o2, gi1, gi2, d_mem, t_gain, t_shift, grads


def body(
    sizes, inputs_one, inputs_two, memory, cotangent_one, cotangent_two, target_ids, memory_ids,
    norm_gain, norm_shift, self_qkv, self_out, cross_query, cross_kv, cross_out, ffn_in, ffn_out,
):
    shape = inputs_one.shape
    length, width = shape[1:]
    o1, o2, gi1, gi2, d_mem, t_gain, t_shift, grads = local_step(
        sizes,
        inputs_one.reshape(length, width),
        inputs_two.reshape(length, width),
        memory.reshape(length, width),
        cotangent_one.reshape(length, width),
        cotangent_two.reshape(length, width),
        target_ids,
        memory_ids,
        norm_gain,
        norm_shift,
        (self_qkv, cross_kv, self_out, cross_query, cross_out, ffn_in, ffn_out),
    )
    d_qkv, d_self, d_query, d_kv, d_in, d_out, d_cross = grads
    return (
        o1.reshape(shape), o2.reshape(shape), gi1.reshape(shape), gi2.reshape(shape), d_mem.reshape(shape),
        t_gain, t_shift, d_qkv, d_self, d_query, d_kv, d_cross, d_in, d_out,
    )


def solution(mesh):
    rows = P(("narrow", "wide"), None, None)
    ids = P(("narrow", "wide"), None)
    norm, weight = P(None, "wide"), P("wide", None)
    return jax.shard_map(
        functools.partial(body, (mesh.shape["narrow"], mesh.shape["wide"])),
        mesh=mesh,
        in_specs=(rows,) * 5 + (ids,) * 2 + (norm,) * 2 + (weight,) * 7,
        out_specs=(rows,) * 5 + (norm,) * 2 + (weight,) * 7,
        check_vma=False,
    )
```
